32 devices in a mesh: dp: 8 (over y, x, core), tensor: 4 (over z).
Axes of the slice: x: 2, y: 2, z: 4, core: 2. Of those that a mesh axis runs over, the one named last changes fastest.
Arguments:
- tokens: bfloat16 [16384, 768], P(('dp', 'tensor')), may hold values from -6 to 6
- teacher: bfloat16 [16384, 768], P(('dp', 'tensor')), may hold values from -6 to 6
- lengths: int32 [8], P('dp'), may hold values from 256 to 2048, as said below
- loss_mask: int32 [16384], P(('dp', 'tensor')), may hold values 0 or 1
- loss_scale: float32 [], replicated, may hold values from 1572864 to 6291456
- query_weight: bfloat16 [768, 768], P('dp', 'tensor'), may hold values from -0.21875 to 0.21875
- query_bias: bfloat16 [768], P('dp'), may hold values from -3 to 3
- key_weight: bfloat16 [768, 768], P('dp', 'tensor'), may hold values from -0.21875 to 0.21875
- value_weight: bfloat16 [768, 768], P('dp', 'tensor'), may hold values from -0.21875 to 0.21875
- value_bias: bfloat16 [768], P('dp'), may hold values from -3 to 3
- mixer_weight: bfloat16 [768, 768], P('tensor', 'dp'), may hold values from -6 to 6
- mixer_bias: bfloat16 [768], P('dp'), may hold values from -3 to 3
- first_gain: bfloat16 [768], P('dp'), may hold values from 0.5 to 1.5
- first_shift: bfloat16 [768], P('dp'), may hold values from -3 to 3
- inner_weight: bfloat16 [768, 3072], P('dp', 'tensor'), may hold values from -0.21875 to 0.21875
- inner_bias: bfloat16 [3072], P('dp'), may hold values from -3 to 3
- outer_weight: bfloat16 [3072, 768], P('tensor', 'dp'), may hold values from -0.15625 to 0.15625
- outer_bias: bfloat16 [768], P('dp'), may hold values from -3 to 3
- second_gain: bfloat16 [768], P('dp'), may hold values from 0.5 to 1.5
- second_shift: bfloat16 [768], P('dp'), may hold values from -3 to 3
Outputs:
- layer_output: bfloat16 [16384, 768], P(('dp', 'tensor'))
- loss_value: float32 [], replicated
- input_grad: float32 [16384, 768], P(('dp', 'tensor'))
- query_grad: float32 [768, 768], P('dp', 'tensor')
- querybias_grad: float32 [768], P('dp')
- key_grad: float32 [768, 768], P('dp', 'tensor')
- value_grad: float32 [768, 768], P('dp', 'tensor')
- valuebias_grad: float32 [768], P('dp')
- mixer_grad: float32 [768, 768], P('tensor', 'dp')
- mixerbias_grad: float32 [768], P('dp')
- firstgain_grad: float32 [768], P('dp')
- firstshift_grad: float32 [768], P('dp')
- inner_grad: float32 [768, 3072], P('dp', 'tensor')
- innerbias_grad: float32 [3072], P('dp')
- outer_grad: float32 [3072, 768], P('tensor', 'dp')
- outerbias_grad: float32 [768], P('dp')
- secondgain_grad: float32 [768], P('dp')
- secondshift_grad: float32 [768], P('dp')
The draws below stay inside these ranges and needn't reach their ends.
Inputs may be any that keep to these rules, and one draw needn't show every extreme that they name: lengths[s] is how many leading tokens of sequence s are valid; the rest are padding. Some sequence has exactly 2048 and another exactly one eighth of 2048.
All inputs are finite; a program needn't handle non-finite values. No bound on the sum of `loss_mask` on one device may be relied on, other than what follows from the above.
Results may differ from the reference program's by a relative error of at most 0.018.
Values may be sent and summed in bfloat16 or wider, within the bound.
A program may use at most 128 MiB of HBM per device.

```python
import math
import jax
import jax.numpy as jnp
from jax import lax

D = 768
HEADS = 12
HEAD_DIM = 64
FF = 3072
LEN = 2048
QBLOCK = 512
GROUPS = 4
SEQS = 8
TOKENS = 16384


def draw_lengths(key, part):
    places = jnp.arange(SEQS)
    low_end = LEN // 8
    rising = low_end + (LEN - low_end) * places // (SEQS - 1)
    jitter = jax.random.randint(jax.random.fold_in(key, 11), (SEQS,), -(LEN // 16), LEN // 16 + 1)
    base_lengths = jnp.clip(rising + jitter, low_end, LEN)
    base_lengths = jnp.where(places == 0, low_end, base_lengths)
    base_lengths = jnp.where(places == SEQS - 1, LEN, base_lengths)
    return base_lengths.astype(jnp.int32)


def place_ends(drawn, key, smallest, top_value):
    shape = drawn.shape
    index_at = [jax.random.randint(jax.random.fold_in(key, axis), (), 0, shape[axis]) for axis in range(len(shape))]
    drawn = drawn.at[tuple(index_at)].set(smallest)
    longest = shape.index(max(shape))
    index_at[longest] = (index_at[longest] + 1) % shape[longest]
    return drawn.at[tuple(index_at)].set(top_value)


def level_of(own_key, shape, split, smallest, high):
    loudness = 1.0
    for position, shards_of in split:
        heights = jax.random.uniform(jax.random.fold_in(jax.random.fold_in(own_key, 6), position), (shards_of,), jnp.float32, smallest / len(split), high / len(split))
        loudness = loudness * jnp.repeat(jnp.exp(heights), shape[position] // shards_of).reshape((-1,) + (1,) * (len(shape) - 1 - position))
    return loudness


def normal_values(rng, dims, width, bound, shards=(), kind=jnp.bfloat16):
    entries = jax.random.normal(rng, dims, jnp.float32) * width
    if len(shards) > 0:
        entries = level_of(rng, dims, shards, -0.22, 0.18) * entries
    return jnp.clip(entries, min=-bound, max=bound).astype(kind)


def setup_inputs(seed: int = 0) -> dict:
    keys = jax.random.split(jax.random.key(seed), 21)
    tokens = normal_values(keys[0], (TOKENS, D), 1.0, 6.0, ((0, 32),))
    teacher = normal_values(keys[1], (TOKENS, D), 1.0, 6.0, ((0, 32),))
    lengths = draw_lengths(jax.random.fold_in(keys[20], 71), 0)
    loss_mask = place_ends((jax.random.randint(keys[3], (TOKENS,), 0, 4) < 3).astype(jnp.int32), jax.random.fold_in(keys[3], 1), 0, 1)
    loss_scale = jnp.clip(jnp.exp(jax.random.uniform(keys[4], (), jnp.float32, math.log(1572864), math.log(6291456))), 1572864, 6291456)
    query_weight = normal_values(keys[5], (D, D), D ** -0.5, 0.21875, ((0, 8), (1, 4)))
    query_bias = normal_values(keys[6], (D,), 0.5, 3.0, ((0, 8),))
    key_weight = normal_values(keys[7], (D, D), D ** -0.5, 0.21875, ((0, 8), (1, 4)))
    value_weight = normal_values(keys[8], (D, D), D ** -0.5, 0.21875, ((0, 8), (1, 4)))
    value_bias = normal_values(keys[9], (D,), 0.5, 3.0, ((0, 8),))
    mixer_weight = normal_values(keys[10], (D, D), (max(1, 2 * D // LEN)) ** -0.5, 6.0, ((0, 4), (1, 8)))
    mixer_bias = normal_values(keys[11], (D,), 0.5, 3.0, ((0, 8),))
    first_gain = jnp.clip(1.0 + 0.1 * jax.random.normal(keys[12], (D,), jnp.float32), 0.5, 1.5).astype(jnp.bfloat16)
    first_shift = normal_values(keys[13], (D,), 0.5, 3.0, ((0, 8),))
    inner_weight = normal_values(keys[14], (D, FF), D ** -0.5, 0.21875, ((0, 8), (1, 4)))
    inner_bias = normal_values(keys[15], (FF,), 0.5, 3.0, ((0, 8),))
    outer_weight = normal_values(keys[16], (FF, D), (FF // 2) ** -0.5, 0.15625, ((0, 4), (1, 8)))
    outer_bias = normal_values(keys[17], (D,), 0.5, 3.0, ((0, 8),))
    second_gain = jnp.clip(1.0 + 0.1 * jax.random.normal(keys[18], (D,), jnp.float32), 0.5, 1.5).astype(jnp.bfloat16)
    second_shift = normal_values(keys[19], (D,), 0.5, 3.0, ((0, 8),))
    return dict(tokens=tokens, teacher=teacher, lengths=lengths, loss_mask=loss_mask, loss_scale=loss_scale, query_weight=query_weight, query_bias=query_bias, key_weight=key_weight, value_weight=value_weight, value_bias=value_bias, mixer_weight=mixer_weight, mixer_bias=mixer_bias, first_gain=first_gain, first_shift=first_shift, inner_weight=inner_weight, inner_bias=inner_bias, outer_weight=outer_weight, outer_bias=outer_bias, second_gain=second_gain, second_shift=second_shift)


norm_eps = 1e-05
masked_score = -1e+30
highest = lax.Precision.HIGHEST

@jax.custom_vjp
def low(v):
    return lax.optimization_barrier(v.astype(jnp.bfloat16)).astype(jnp.float32)

@jax.custom_vjp
def low_back(v):
    return v

def low_keep(v):
    return (low(v), None)

def low_pass(kept, grad):
    return (grad,)

def back_keep(v):
    return (v, None)

def back_low(kept, grad):
    return (low(grad),)
low.defvjp(low_keep, low_pass)
low_back.defvjp(back_keep, back_low)

def matmul(left_rows, right_rows):
    return jnp.dot(left_rows, right_rows, precision=highest, preferred_element_type=jnp.float32)

def layer_norm(values_in, gain_vec, shift_vec):
    centred = values_in - lax.optimization_barrier(jnp.mean(values_in, axis=-1, keepdims=True))
    inv_std = lax.rsqrt(lax.optimization_barrier(jnp.mean(centred * centred, axis=-1, keepdims=True)) + norm_eps)
    return centred * inv_std * gain_vec + shift_vec

def attend_block(query_block, keys_three, values_three, key_valid):
    scores = jnp.einsum('qhd,khd->hqk', query_block, keys_three, precision=highest) * HEAD_DIM ** (-0.5)
    scores = low_back(jnp.where(key_valid[None, None, :], scores, masked_score))
    probs = low(jax.nn.softmax(scores, axis=-1))
    return jnp.einsum('hqk,khd->qhd', probs, values_three, precision=highest)

def seq_forward(seq_tokens, params, length):
    query_weight, query_bias, key_weight, value_weight, value_bias, mixer_weight, mixer_bias, first_gain, first_shift, inner_weight, inner_bias, outer_weight, outer_bias, second_gain, second_shift = params
    head_width = D // GROUPS
    hidden_width = FF // GROUPS
    group_heads = HEADS // GROUPS
    key_valid = jnp.arange(LEN) < length
    token_low = low(seq_tokens)
    branch_parts = []
    for group_index in range(GROUPS):
        columns = slice(group_index * head_width, (group_index + 1) * head_width)
        group_rows = low_back(token_low)
        queries = low_back(low(matmul(group_rows, query_weight[:, columns]) + query_bias[columns]))
        keys_all = low_back(low(matmul(group_rows, key_weight[:, columns])))
        values_all = low_back(low(matmul(group_rows, value_weight[:, columns]) + value_bias[columns]))
        keys_three = keys_all.reshape(LEN, group_heads, HEAD_DIM)
        values_three = values_all.reshape(LEN, group_heads, HEAD_DIM)
        query_blocks = queries.reshape(LEN // QBLOCK, QBLOCK, group_heads, HEAD_DIM)
        attended = lax.map(jax.checkpoint(lambda query_block: attend_block(query_block, keys_three, values_three, key_valid)), query_blocks)
        attended = low_back(low(attended.reshape(LEN, head_width)))
        branch_parts.append(low(matmul(attended, mixer_weight[columns, :])))
    attn_out = low_back(sum(branch_parts))
    hidden_one = layer_norm(seq_tokens + attn_out + mixer_bias, first_gain, first_shift)
    hidden_low = low(hidden_one)
    ffn_parts = []
    for group_index in range(GROUPS):
        columns = slice(group_index * hidden_width, (group_index + 1) * hidden_width)
        group_rows = low_back(hidden_low)
        pre_act = low_back(matmul(group_rows, inner_weight[:, columns]) + inner_bias[columns])
        activated = low(jax.nn.gelu(pre_act, approximate=False))
        ffn_parts.append(low(matmul(activated, outer_weight[columns, :])))
    ffn_out = low_back(sum(ffn_parts))
    return layer_norm(hidden_one + ffn_out + outer_bias, second_gain, second_shift)

def reference(tokens, teacher, lengths, loss_mask, loss_scale, query_weight, query_bias, key_weight, value_weight, value_bias, mixer_weight, mixer_bias, first_gain, first_shift, inner_weight, inner_bias, outer_weight, outer_bias, second_gain, second_shift):
    params = tuple((member.astype(jnp.float32) for member in (query_weight, query_bias, key_weight, value_weight, value_bias, mixer_weight, mixer_bias, first_gain, first_shift, inner_weight, inner_bias, outer_weight, outer_bias, second_gain, second_shift)))
    positions = jnp.arange(LEN)
    valid_rows = positions[None, :] < lengths[:, None]
    counted = jnp.logical_and(valid_rows, loss_mask.reshape(SEQS, LEN) == 1).astype(jnp.float32)
    token_total = jnp.sum(counted)
    grad_scale = 2.0 * loss_scale / (token_total * D)
    seq_tokens = tokens.astype(jnp.float32).reshape(SEQS, LEN, D)
    seq_teacher = teacher.astype(jnp.float32).reshape(SEQS, LEN, D)

    def per_sequence(carried, seq_in):
        grads_sum, loss_sum = carried
        rows_in, target_rows, weight_rows, length = seq_in
        final_rows, pull_back = jax.vjp(lambda rows_x, params_x: seq_forward(rows_x, params_x, length), rows_in, params)
        diff_rows = final_rows - target_rows
        loss_part = jnp.sum(weight_rows * lax.optimization_barrier(jnp.sum(diff_rows * diff_rows, axis=1)))
        grad_rows, grad_params = pull_back(grad_scale * weight_rows[:, None] * diff_rows)
        grads_sum = jax.tree.map(jnp.add, grads_sum, grad_params)
        return ((grads_sum, loss_sum + loss_part), (final_rows.astype(jnp.bfloat16), grad_rows))
    zero_grads = jax.tree.map(jnp.zeros_like, params)
    (grads_sum, loss_sum), (outputs, input_grads) = lax.scan(per_sequence, (zero_grads, jnp.zeros((), jnp.float32)), (seq_tokens, seq_teacher, counted, lengths))
    loss_value = loss_sum / (token_total * D)
    return (outputs.reshape(TOKENS, D), loss_value, input_grads.reshape(TOKENS, D), grads_sum[0], grads_sum[1], grads_sum[2], grads_sum[3], grads_sum[4], grads_sum[5], grads_sum[6], grads_sum[7], grads_sum[8], grads_sum[9], grads_sum[10], grads_sum[11], grads_sum[12], grads_sum[13], grads_sum[14])
```

```python
import functools
import jax
import jax.numpy as jnp
from jax import lax
from jax.experimental import pallas as pl
from jax.experimental.pallas import tpu as pltpu
from jax.sharding import PartitionSpec as P

HEAD_DIM = 64
QBLOCK = 512
MESH = pl.DeviceIdType.MESH
F32 = jnp.float32
BF16 = jnp.bfloat16
norm_eps = 1e-05
masked_score = -1e30
VMEM_LIMIT = 60 * 1024 * 1024


def dot(left, right, left_dim, right_dim):
    return lax.dot_general(
        left, right, (((left_dim,), (right_dim,)), ((), ())), preferred_element_type=F32
    )


def remote(src, dst, send, recv, d, t):
    return pltpu.make_async_remote_copy(
        src_ref=src,
        dst_ref=dst,
        send_sem=send,
        recv_sem=recv,
        device_id={"dp": d, "tensor": t},
        device_id_type=MESH,
    )


def arrival(dst, recv):
    return pltpu.make_async_copy(dst, dst, recv)


class Place:
    def __init__(self):
        self.dp = lax.axis_size("dp")
        self.tp = lax.axis_size("tensor")
        self.d = lax.axis_index("dp")
        self.z = lax.axis_index("tensor")
        self.core = lax.rem(self.d, 2)
        self.chip = self.d // 2
        self.chips = self.dp // 2
        self.base = self.chip * 2
        self.sibling = self.base + 1 - self.core
        self.pair = self.z // 2
        self.low = lax.rem(self.z, 2)
        self.group = 2 * self.low + self.core
        self.buddy = 2 * self.pair + 1 - self.low
        self.owner = self.base + self.pair
        self.near_here = 1 + self.pair
        self.near_there = 2 - self.pair


def greet(place):
    barrier = pltpu.get_barrier_semaphore()
    count = 0
    for t in range(place.tp):
        for c in range(2):
            other = jnp.logical_not(jnp.logical_and(place.z == t, place.core == c))

            @pl.when(other)
            def _(t=t, c=c):
                pl.semaphore_signal(
                    barrier, inc=1, device_id={"dp": place.base + c, "tensor": t}, device_id_type=MESH
                )

            count += 1
    count -= 1

    def plane(i, _):
        chip = lax.rem(place.chip + 1 + i, place.chips)
        for c in range(2):
            pl.semaphore_signal(
                barrier, inc=1, device_id={"dp": chip * 2 + c, "tensor": place.z}, device_id_type=MESH
            )
        return 0

    lax.fori_loop(0, place.chips - 1, plane, 0)
    count += 2 * (place.chips - 1)
    pl.semaphore_wait(barrier, count)


def front_kernel(
    x_ref, wq_ref, wm_ref, sm_ref,
    oin_ref, wall_ref, smalls_ref, count_ref, xs_ref, wqf_ref, oT_ref, lse_ref, qT_ref, kA_ref, v_ref,
    wqz, counts, vT, scores, o_buf, wqT, wkp, wvp, wvT,
    sm_send, sm_recv, cn_send, cn_recv, wz_send, wz_recv, wp_send, wp_recv,
    x_send, x_recv, xr_send, xf_send, mz_send, mz_recv, mp_send, mp_recv, ms_send, ms_recv, o_send, o_recv,
):
    me = Place()
    dp, tp, chips = me.dp, me.tp, me.chips
    rows, width = x_ref.shape
    half = rows // 2
    length = rows * tp
    share = wq_ref.shape[0]
    heads = 3
    greet(me)

    def each_peer(f):
        def step(i, _):
            f(i, lax.rem(me.d + 1 + i, dp))
            return 0

        lax.fori_loop(0, dp - 1, step, 0)

    def small_copy(i, peer):
        return remote(sm_ref, smalls_ref.at[me.d], sm_send.at[i], sm_recv.at[me.d], peer, me.z)

    each_peer(lambda i, peer: small_copy(i, peer).start())
    smalls_ref[me.d] = sm_ref[...]

    for s in range(2):
        target = me.z // 2 + 2 * s
        src, dst = wq_ref, wqz.at[me.low]

        @pl.when(target == me.z)
        def _(s=s, dst=dst):
            pltpu.make_async_copy(wq_ref, dst, wz_recv.at[me.low]).start()

        @pl.when(target != me.z)
        def _(s=s, dst=dst, target=target):
            remote(wq_ref, dst, wz_send.at[s], wz_recv.at[me.low], me.d, target).start()

    is_owner = me.core == me.pair
    for h in range(2):
        part = pl.ds(h * half, half)

        @pl.when(is_owner)
        def _(h=h, part=part):
            pltpu.make_async_copy(x_ref.at[part], xs_ref.at[me.z, part], x_recv.at[me.z, h]).start()
            remote(x_ref.at[part], xs_ref.at[me.z, part], x_send.at[h], x_recv.at[me.z, h], me.base + h, me.buddy).start()
            remote(x_ref.at[part], xs_ref.at[me.z, part], xr_send.at[0, h], x_recv.at[me.z, h], me.sibling, me.z).start()

        @pl.when(jnp.logical_not(is_owner))
        def _(h=h, part=part):
            remote(x_ref.at[part], xs_ref.at[me.z, part], x_send.at[h], x_recv.at[me.z, h], me.base + h, me.near_there).start()

    pltpu.make_async_copy(wm_ref, wall_ref.at[me.z, me.d], mz_recv.at[me.z]).start()
    for s in range(1, tp):
        t = lax.rem(me.z + s, tp)
        remote(wm_ref, wall_ref.at[me.z, me.d], mz_send.at[s - 1], mz_recv.at[me.z], me.d, t).start()

    def wq_plane(s, k):
        dst = wqf_ref.at[me.d]
        return remote(wqz.at[s], dst, wp_send.at[s, k], wp_recv.at[me.d], 2 * k + s, me.z)

    for s in range(2):
        arrival(wqz.at[s], wz_recv.at[s]).wait()

        def step(i, _, s=s):
            k = lax.rem(me.chip + 1 + i, chips)
            here = 2 * k + s == me.d

            @pl.when(here)
            def _():
                pltpu.make_async_copy(wqz.at[s], wqf_ref.at[me.d], wp_recv.at[me.d]).start()

            @pl.when(jnp.logical_not(here))
            def _():
                wq_plane(s, k).start()

            return 0

        lax.fori_loop(0, chips, step, 0)

    def plane_units(t):
        def step(i, _):
            k = lax.rem(me.chip + 1 + i, chips)
            remote(
                wall_ref.at[t, me.d], wall_ref.at[t, me.d], mp_send.at[t, i], mp_recv.at[t, me.chip], 2 * k + me.core, me.z
            ).start()
            return 0

        lax.fori_loop(0, chips - 1, step, 0)

    arrival(wall_ref.at[me.z, me.d], mz_recv.at[me.z]).wait()
    plane_units(me.z)

    def small_wait(i, peer):
        arrival(smalls_ref.at[peer], sm_recv.at[peer]).wait()

    each_peer(small_wait)
    plane_count = smalls_ref[0][8:16]
    for k in range(1, dp):
        plane_count = plane_count + smalls_ref[k][8:16]
    counts[me.z] = plane_count
    for s in range(1, tp):
        remote(counts.at[me.z], counts.at[me.z], cn_send.at[s - 1], cn_recv.at[me.z], me.d, lax.rem(me.z + s, tp)).start()

    for k in range(dp):
        arrival(wqf_ref.at[k], wp_recv.at[k]).wait()
    zero = jnp.zeros((share, HEAD_DIM), BF16)
    gw = heads * HEAD_DIM
    for k in range(dp):
        w = wqf_ref[k]
        at = slice(k * share, (k + 1) * share)
        pads = []
        for m in range(3):
            cols = []
            for h in range(heads):
                cols += [w[:, m * gw + h * HEAD_DIM : m * gw + (h + 1) * HEAD_DIM], zero]
            pads.append(jnp.concatenate(cols, axis=1))
        wkp[at, :] = pads[1]
        wvp[at, :] = pads[2]
        scores[0, at, 0:384] = pads[0].astype(F32)
    wqT[...] = scores[0, 0:width, 0:384].T.astype(BF16)
    wvT[...] = wvp[...].astype(F32).T.astype(BF16)

    blocks = gw // share
    row_bias = jnp.zeros((8, 384), F32)
    col_bias = jnp.zeros((384, 8), F32)
    r_in = lax.broadcasted_iota(jnp.int32, (128, 384), 0)
    r_out = lax.broadcasted_iota(jnp.int32, (128, 384), 1)
    c_out = lax.broadcasted_iota(jnp.int32, (384, 128), 0)
    c_in = lax.broadcasted_iota(jnp.int32, (384, 128), 1)

    def padded(col):
        return (col // HEAD_DIM) * 128 + lax.rem(col, HEAD_DIM)

    for b in range(blocks):
        vecs = smalls_ref[me.group * blocks + b][0:8].astype(BF16)
        sel = jnp.logical_and(padded(r_in + b * share) == r_out, r_in < share)
        row_bias = row_bias + dot(vecs, jnp.where(sel, 1.0, 0.0).astype(BF16), 1, 0)
        sel = jnp.logical_and(padded(c_in + b * share) == c_out, c_in < share)
        col_bias = col_bias + dot(jnp.where(sel, 1.0, 0.0).astype(BF16), vecs, 1, 1)
    q_bias = col_bias[:, 0:1]
    v_bias_col = col_bias[:, 1:2]
    v_bias = row_bias[1:2, :]
    valid = smalls_ref[me.base + me.pair][12:13, 0:1]

    lane = lax.broadcasted_iota(jnp.int32, (rows, 128), 1)
    srow = lax.broadcasted_iota(jnp.int32, (128, rows), 0)

    def project(j):
        at = pl.ds(pl.multiple_of(j * rows, rows), rows)
        xb = xs_ref[j]
        keys = dot(xb, wkp[...], 1, 0)
        queries = dot(wqT[...], xb, 1, 1) + q_bias
        vals = dot(xb, wvp[...], 1, 0) + v_bias
        valsT = dot(wvT[...], xb, 1, 1) + v_bias_col
        pos = (j * rows + lax.broadcasted_iota(jnp.int32, (rows, 128), 0)).astype(F32)
        bias = jnp.where(pos < valid, 0.0, masked_score)
        for h in range(heads):
            span = slice(h * 128, (h + 1) * 128)
            vT[h * HEAD_DIM : (h + 1) * HEAD_DIM, at] = valsT[h * 128 : h * 128 + HEAD_DIM].astype(BF16)
            kA_ref[h, at, :] = jnp.where(lane == HEAD_DIM, bias, keys[:, span]).astype(BF16)
            qh = queries[span].astype(BF16) * BF16(HEAD_DIM**-0.5)
            qT_ref[h, :, at] = jnp.where(srow == HEAD_DIM, BF16(1), qh)
            v_ref[h, at, :] = vals[:, span].astype(BF16)

    def wait_half(j, h):
        arrival(xs_ref.at[j, pl.ds(h * half, half)], x_recv.at[j, h]).wait()

    mine = pl.ds(pl.multiple_of(me.core * half, half), half)

    def relay(j, slot):
        arrival(xs_ref.at[j, mine], x_recv.at[j, me.core]).wait()
        remote(xs_ref.at[j, mine], xs_ref.at[j, mine], xr_send.at[slot, 0], x_recv.at[j, me.core], me.sibling, me.z).start()

    wait_half(me.z, 0)
    wait_half(me.z, 1)
    project(me.z)
    relay(me.buddy, 1)
    wait_half(me.buddy, 0) if False else None
    far_first = 2 * (1 - me.pair) + me.pair
    far_second = 2 * (1 - me.pair) + 1 - me.pair

    is_near = me.z == me.near_here
    for n, j in enumerate((far_first, far_second)):
        relay(j, 2 + n)

        @pl.when(is_near)
        def _(n=n, j=j):
            remote(xs_ref.at[j, mine], xs_ref.at[j, mine], xf_send.at[n], x_recv.at[j, me.core], me.d, me.buddy).start()

        if n == 0:
            arrival(xs_ref.at[me.buddy, pl.ds(pl.multiple_of((1 - me.core) * half, half), half)], x_recv.at[me.buddy, 1 - me.core]).wait()
            project(me.buddy)
    for j in (far_first, far_second):
        arrival(xs_ref.at[j, pl.ds(pl.multiple_of((1 - me.core) * half, half), half)], x_recv.at[j, 1 - me.core]).wait()
        project(j)

    chunk = 256
    pieces = length // chunk

    def attend(i, _):
        j = lax.rem(me.z + 1 + i, tp)
        at = pl.ds(pl.multiple_of(j * rows, rows), rows)
        tops = []
        for h in range(heads):
            qt = qT_ref[h, :, at]
            top = None
            for c in range(pieces):
                s = dot(kA_ref[h, c * chunk : (c + 1) * chunk, :], qt, 1, 0)
                scores[h, c * chunk : (c + 1) * chunk, :] = s
                peak = jnp.max(s, axis=0, keepdims=True)
                top = peak if top is None else jnp.maximum(top, peak)
            tops.append(top)
        outs = []
        for h in range(heads):
            total, mixed = None, None
            for c in range(pieces):
                p = jnp.exp(scores[h, c * chunk : (c + 1) * chunk, :] - tops[h])
                part = jnp.sum(p, axis=0, keepdims=True)
                term = dot(vT[h * HEAD_DIM : (h + 1) * HEAD_DIM, c * chunk : (c + 1) * chunk], p.astype(BF16), 1, 0)
                total = part if total is None else total + part
                mixed = term if mixed is None else mixed + term
            mixed = mixed / total
            oT_ref[h * HEAD_DIM : (h + 1) * HEAD_DIM, at] = mixed
            lse_ref[h, :, at] = tops[h] + jnp.log(total)
            outs.append(mixed)
        o_buf[j] = jnp.concatenate(outs, axis=0).T.astype(BF16)
        here = jnp.logical_and(j == me.z, is_owner)

        @pl.when(here)
        def _():
            pltpu.make_async_copy(o_buf.at[j], oin_ref.at[me.group], o_recv.at[me.group]).start()

        @pl.when(jnp.logical_not(here))
        def _():
            remote(o_buf.at[j], oin_ref.at[me.group], o_send.at[i], o_recv.at[me.group], me.owner, j).start()

        @pl.when(i == 0)
        def _():
            for s in range(1, tp):
                t = lax.rem(me.z + s, tp)
                arrival(wall_ref.at[t, me.d], mz_recv.at[t]).wait()
                plane_units(t)

        return 0

    lax.fori_loop(0, tp, attend, 0)

    def to_sibling(t, k):
        unit = wall_ref.at[t, 2 * k + me.core]
        return remote(unit, unit, ms_send.at[t, k], ms_recv.at[t, k], me.sibling, me.z)

    def own_units(t, _):
        to_sibling(t, me.chip).start()
        return 0

    lax.fori_loop(0, tp, own_units, 0)

    def others(n, _):
        i, s = n // tp, lax.rem(n, tp)
        k = lax.rem(me.chip + 1 + i, chips)
        t = lax.rem(me.z + s, tp)
        arrival(wall_ref.at[t, 2 * k + me.core], mp_recv.at[t, k]).wait()
        to_sibling(t, k).start()
        return 0

    lax.fori_loop(0, (chips - 1) * tp, others, 0)

    for s in range(1, tp):
        t = lax.rem(me.z + s, tp)
        arrival(counts.at[t], cn_recv.at[t]).wait()
    total = counts[0]
    for t in range(1, tp):
        total = total + counts[t]
    count_ref[...] = total
    for g in range(4):
        arrival(oin_ref.at[g], o_recv.at[g]).wait()

    def sibling_units(n, _):
        t, k = n // chips, lax.rem(n, chips)
        arrival(wall_ref.at[t, 2 * k + 1 - me.core], ms_recv.at[t, k]).wait()
        to_sibling(t, k).wait_send()
        return 0

    lax.fori_loop(0, tp * chips, sibling_units, 0)

    def sent(n, _):
        t, i = n // (chips - 1), lax.rem(n, chips - 1)
        remote(wall_ref.at[t, me.d], wall_ref.at[t, me.d], mp_send.at[t, i], mp_recv.at[t, 0], me.sibling, me.z).wait_send()
        return 0

    lax.fori_loop(0, tp * (chips - 1), sent, 0)
    each_peer(lambda i, peer: small_copy(i, peer).wait_send())
    for s in range(2):

        @pl.when(me.z // 2 + 2 * s != me.z)
        def _(s=s):
            remote(wq_ref, wqz.at[0], wz_send.at[s], wz_recv.at[0], me.sibling, me.z).wait_send()

        def step(i, _, s=s):
            k = lax.rem(me.chip + 1 + i, chips)

            @pl.when(2 * k + s != me.d)
            def _():
                wq_plane(s, k).wait_send()

            return 0

        lax.fori_loop(0, chips, step, 0)
    for s in range(tp - 1):
        remote(counts.at[0], counts.at[0], cn_send.at[s], cn_recv.at[0], me.sibling, me.z).wait_send()
        remote(wm_ref, wall_ref.at[0, 0], mz_send.at[s], mz_recv.at[0], me.sibling, me.z).wait_send()

    def x_sent(sem):
        remote(x_ref.at[pl.ds(0, half)], xs_ref.at[0, pl.ds(0, half)], sem, x_recv.at[0, 0], me.sibling, me.z).wait_send()

    for h in range(2):
        x_sent(x_send.at[h])

        @pl.when(is_owner)
        def _(h=h):
            x_sent(xr_send.at[0, h])

    for n in range(3):
        x_sent(xr_send.at[1 + n, 0])

    @pl.when(is_near)
    def _():
        for n in range(2):
            x_sent(xf_send.at[n])

    def o_sent(i, _):
        j = lax.rem(me.z + 1 + i, tp)

        @pl.when(jnp.logical_not(jnp.logical_and(j == me.z, is_owner)))
        def _():
            remote(o_buf.at[0], oin_ref.at[0], o_send.at[i], o_recv.at[0], me.sibling, me.z).wait_send()

        return 0

    lax.fori_loop(0, tp, o_sent, 0)


def front(x, wq, wm, small, dp, tp):
    rows, width = x.shape
    length = rows * tp
    share = wq.shape[0]
    chips = dp // 2
    S = jax.ShapeDtypeStruct
    vmem = pl.BlockSpec(memory_space=pltpu.VMEM)
    anym = pl.BlockSpec(memory_space=pl.ANY)
    dma = pltpu.SemaphoreType.DMA
    return pl.pallas_call(
        front_kernel,
        name="front",
        out_shape=(
            S((4, rows, 192), BF16),
            S((tp, dp, share, wm.shape[1]), BF16),
            S((dp, 16, 128), F32),
            S((8, 128), F32),
            S((tp, rows, width), BF16),
            S((dp, share, wq.shape[1]), BF16),
            S((192, length), F32),
            S((3, 1, length), F32),
            S((3, 128, length), BF16),
            S((3, length, 128), BF16),
            S((3, length, 128), BF16),
        ),
        in_specs=[vmem, vmem, anym, vmem],
        out_specs=(anym, anym) + (vmem,) * 9,
        scratch_shapes=[
            pltpu.VMEM((2, share, wq.shape[1]), BF16),
            pltpu.VMEM((tp, 8, 128), F32),
            pltpu.VMEM((192, length), BF16),
            pltpu.VMEM((3, length, rows), F32),
            pltpu.VMEM((tp, rows, 192), BF16),
            pltpu.VMEM((384, width), BF16),
            pltpu.VMEM((width, 384), BF16),
            pltpu.VMEM((width, 384), BF16),
            pltpu.VMEM((384, width), BF16),
            dma((dp - 1,)), dma((dp,)), dma((tp - 1,)), dma((tp,)),
            dma((2,)), dma((2,)), dma((2, chips)), dma((dp,)),
            dma((2,)), dma((tp, 2)), dma((4, 2)), dma((2,)),
            dma((tp - 1,)), dma((tp,)), dma((tp, chips - 1)), dma((tp, chips)), dma((tp, chips)), dma((tp, chips)),
            dma((tp,)), dma((4,)),
        ],
        compiler_params=pltpu.CompilerParams(
            collective_id=0, has_side_effects=True, vmem_limit_bytes=VMEM_LIMIT
        ),
    )(x, wq, wm, small)


SQRT_HALF = 0.7071067811865476
INV_SQRT_2PI = 0.3989422804014327


def norm_forward(values, gain, shift):
    centred = values - jnp.mean(values, axis=1, keepdims=True)
    inv = lax.rsqrt(jnp.mean(centred * centred, axis=1, keepdims=True) + norm_eps)
    normed = centred * inv
    return normed * gain + shift, normed, inv


def norm_backward(grad_out, normed, inv, gain):
    g = grad_out * gain
    plain = jnp.mean(g, axis=1, keepdims=True)
    mixed = jnp.mean(g * normed, axis=1, keepdims=True)
    return inv * (g - plain - normed * mixed)


def column_sum(values):
    return jnp.sum(values, axis=0, keepdims=True)


def mid_kernel(
    x_ref, teacher_ref, counted_ref, scale_ref, oin_ref, wall_ref, vec_ref, ib_ref,
    out_ref, dr1_ref, do_ref, grad_ref, small_ref, ismall_ref,
    up_ref, act_ref, f_ref, n1_ref, acc_ref, hT_ref, dfT_ref,
):
    groups = wall_ref.shape[0]
    width = x_ref.shape[1]
    gw = oin_ref.shape[2]
    inner = slice(0, width)
    outer = slice(width, 2 * width)
    mixer = slice(2 * width, 2 * width + gw)
    vec = lambda i: vec_ref[i : i + 1, :]

    acc_ref[...] = x_ref[...].astype(F32) + vec(2)
    for g in range(groups):
        acc_ref[...] += dot(oin_ref[g], wall_ref[g, :, mixer], 1, 1)
    hidden, normed1, inv1 = norm_forward(acc_ref[...], vec(3), vec(4))
    n1_ref[...] = normed1
    low = hidden.astype(BF16)
    hT_ref[...] = hidden.T.astype(BF16)
    f_ref[...] = hidden + vec(5)

    def ffn_forward(g, _):
        up = dot(low, wall_ref[g, :, inner], 1, 0) + ib_ref[g]
        up_ref[g] = up
        act = (up * (0.5 * (1.0 + lax.erf(up * SQRT_HALF)))).astype(BF16)
        act_ref[g] = act
        f_ref[...] += dot(act, wall_ref[g, :, outer], 1, 1)
        return 0

    lax.fori_loop(0, groups, ffn_forward, 0)
    final, normed2, inv2 = norm_forward(f_ref[...], vec(6), vec(7))
    out_ref[...] = final.astype(BF16)
    diff = final - teacher_ref[...].astype(F32)
    counted = counted_ref[...]
    small_ref[...] = jnp.zeros_like(small_ref)
    small_ref[6:7, 0:1] = jnp.sum(counted * jnp.sum(diff * diff, axis=1, keepdims=True), axis=0, keepdims=True)
    grad = (scale_ref[0, 0] * counted) * diff
    small_ref[4:5, :] = column_sum(grad * normed2)
    small_ref[5:6, :] = column_sum(grad)
    dr2 = norm_backward(grad, normed2, inv2, vec(6))
    small_ref[3:4, :] = column_sum(dr2)
    acc_ref[...] = dr2
    df = dr2.astype(BF16)
    dfT_ref[...] = dr2.T.astype(BF16)

    def ffn_backward(g, _):
        up = up_ref[g]
        slope = 0.5 * (1.0 + lax.erf(up * SQRT_HALF)) + up * (INV_SQRT_2PI * jnp.exp(-0.5 * up * up))
        du = (dot(df, wall_ref[g, :, outer], 1, 0) * slope).astype(BF16)
        ismall_ref[g] = column_sum(du.astype(F32))
        acc_ref[...] += dot(du, wall_ref[g, :, inner], 1, 1)
        grad_ref[g, :, inner] = dot(hT_ref[...], du, 1, 0).astype(BF16)
        grad_ref[g, :, outer] = dot(dfT_ref[...], act_ref[g], 1, 0).astype(BF16)
        return 0

    lax.fori_loop(0, groups, ffn_backward, 0)
    dh1 = acc_ref[...]
    normed1 = n1_ref[...]
    small_ref[1:2, :] = column_sum(dh1 * normed1)
    small_ref[2:3, :] = column_sum(dh1)
    dr1 = norm_backward(dh1, normed1, inv1, vec(3))
    small_ref[0:1, :] = column_sum(dr1)
    dr1_ref[...] = dr1
    da = dr1.astype(BF16)
    daT = dr1.T.astype(BF16)
    for g in range(groups):
        do_ref[g] = dot(da, wall_ref[g, :, mixer], 1, 0).astype(BF16)
        grad_ref[g, :, mixer] = dot(daT, oin_ref[g], 1, 0).astype(BF16)


def mid(x, teacher, counted, scale, oin, wall, vecs, ib):
    rows, width = x.shape
    groups = wall.shape[0]
    S = jax.ShapeDtypeStruct
    vmem = pl.BlockSpec(memory_space=pltpu.VMEM)
    return pl.pallas_call(
        mid_kernel,
        name="mid",
        out_shape=(
            S((rows, width), BF16),
            S((rows, width), F32),
            S(oin.shape, BF16),
            S(wall.shape, BF16),
            S((8, width), F32),
            S(ib.shape, F32),
        ),
        in_specs=[vmem, vmem, vmem, pl.BlockSpec(memory_space=pltpu.SMEM)] + [vmem] * 4,
        out_specs=(vmem,) * 6,
        scratch_shapes=[
            pltpu.VMEM((groups, rows, ib.shape[2]), F32),
            pltpu.VMEM((groups, rows, ib.shape[2]), BF16),
            pltpu.VMEM((rows, width), F32),
            pltpu.VMEM((rows, width), F32),
            pltpu.VMEM((rows, width), F32),
            pltpu.VMEM((width, rows), BF16),
            pltpu.VMEM((width, rows), BF16),
        ],
        compiler_params=pltpu.CompilerParams(vmem_limit_bytes=VMEM_LIMIT),
    )(x, teacher, counted, scale, oin, wall, vecs, ib)


def back_kernel(
    do_ref, grad_ref, xs_ref, wqf_ref, oT_ref, lse_ref, qT_ref, kA_ref, v_ref, pack_ref, dr1_ref,
    dx_ref, gsum_ref, qgrad_ref, small_ref,
    dof, doT, delta, qs, kT, dk, dv, dqT, dqkv,
    sib, own, pln, zsrc, zrecv, parts, pr, sj, rr, fin, qsend, qr, qz, qf, spack, srecv, zpack,
    do_send, do_recv, sb_send, sb_recv, own_sem, pl_send, pl_recv, zz_send, zz_recv,
    pr_send, pr_recv, rr_send, rr_recv, fin_send, fin_recv, qr_send, qr_recv, qf_send, qf_recv,
    sm_send, sm_recv, sz_send, sz_recv,
):
    me = Place()
    dp, tp, chips = me.dp, me.tp, me.chips
    rows, width = dx_ref.shape
    half = rows // 2
    length = rows * tp
    heads = 3
    gw = heads * HEAD_DIM
    share = width // dp
    greet(me)

    for g in range(4):
        t = 2 * me.core + g // 2
        d = me.base + g % 2
        here = jnp.logical_and(t == me.z, g % 2 == me.core)

        @pl.when(here)
        def _(g=g):
            pltpu.make_async_copy(do_ref.at[g], dof.at[me.z], do_recv.at[me.z]).start()

        @pl.when(jnp.logical_not(here))
        def _(g=g, t=t, d=d):
            remote(do_ref.at[g], dof.at[me.z], do_send.at[g], do_recv.at[me.z], d, t).start()

    def sib_copy(t):
        return remote(grad_ref.at[t, :, 1 - me.core], sib.at[t], sb_send.at[t], sb_recv.at[t], me.sibling, me.z)

    for t in range(tp):
        sib_copy(t).start()
        pltpu.make_async_copy(grad_ref.at[t, :, me.core], own.at[t], own_sem.at[t]).start()

    def pair_sum(t, _):
        arrival(own.at[t], own_sem.at[t]).wait()
        arrival(sib.at[t], sb_recv.at[t]).wait()

        def unit(k, _):
            own[t, k] = (own[t, k].astype(F32) + sib[t, k].astype(F32)).astype(BF16)
            return 0

        lax.fori_loop(0, chips, unit, 0)
        return 0

    lax.fori_loop(0, tp, pair_sum, 0)

    def plane_copy(i, t):
        k = lax.rem(me.chip + 1 + i, chips)
        return remote(own.at[t, k], pln.at[t, i], pl_send.at[t, i], pl_recv.at[t, i], 2 * k + me.core, me.z)

    def plane_start(n, _):
        plane_copy(n // tp, lax.rem(n, tp)).start()
        return 0

    lax.fori_loop(0, (chips - 1) * tp, plane_start, 0)

    def prepare(i, _):
        j = lax.rem(me.z + i, tp)
        at = pl.ds(pl.multiple_of(j * rows, rows), rows)
        arrival(dof.at[j], do_recv.at[j]).wait()
        flipped = dof[j].astype(F32).T
        doT[:, at] = flipped.astype(BF16)
        for h in range(heads):
            span = slice(h * HEAD_DIM, (h + 1) * HEAD_DIM)
            delta[h, :, at] = jnp.sum(flipped[span] * oT_ref[span, at], axis=0, keepdims=True)
            qs[h, at, :] = qT_ref[h, :, at].astype(F32).T.astype(BF16)
            kT[h, :, at] = kA_ref[h, at, :].astype(F32).T[0:HEAD_DIM, :].astype(BF16)
        return 0

    lax.fori_loop(0, tp, prepare, 0)
    chunk = 256
    for h in range(heads):
        dk[...] = jnp.zeros_like(dk)
        dv[...] = jnp.zeros_like(dv)

        def attend(j, _, h=h):
            at = pl.ds(pl.multiple_of(j * rows, rows), rows)
            span = slice(h * HEAD_DIM, (h + 1) * HEAD_DIM)
            qt, gt = qT_ref[h, :, at], doT[span, at]
            q, go = qs[h, at, :], dof[j, :, span]
            lse, dl = lse_ref[h, :, at], delta[h, :, at]
            dq = None
            for c in range(length // chunk):
                r = slice(c * chunk, (c + 1) * chunk)
                p = jnp.exp(dot(kA_ref[h, r, :], qt, 1, 0) - lse)
                dp_ = dot(v_ref[h, r, 0:HEAD_DIM], gt, 1, 0)
                ds = (p * (dp_ - dl)).astype(BF16)
                dv[r, :] += dot(p.astype(BF16), go, 1, 0)
                dk[r, :] += dot(ds, q, 1, 0)
                term = dot(kT[h, :, r], ds, 1, 0)
                dq = term if dq is None else dq + term
            dqT[span, at] = dq * HEAD_DIM**-0.5
            return 0

        lax.fori_loop(0, tp, attend, 0)
        for j in range(tp):
            at = slice(j * rows, (j + 1) * rows)
            dqkv[j, :, gw + h * HEAD_DIM : gw + (h + 1) * HEAD_DIM] = dk[at, 0:HEAD_DIM].astype(BF16)
            dqkv[j, :, 2 * gw + h * HEAD_DIM : 2 * gw + (h + 1) * HEAD_DIM] = dv[at, :].astype(BF16)

    weights = wqf_ref[...].reshape(width, 3 * gw)
    ones = jnp.ones((8, rows), BF16)
    mine = pl.ds(pl.multiple_of(me.core * half, half), half)
    other = pl.ds(pl.multiple_of((1 - me.core) * half, half), half)
    far = 2 * (1 - me.pair)

    def block_at(i):
        return jnp.where(i < 2, far + i, jnp.where(i == 2, me.buddy, me.z))

    def pr_copy(j):
        return remote(parts.at[j, other], pr.at[j], pr_send.at[j], pr_recv.at[j], me.sibling, me.z)

    def token_grads(i, sums):
        j = block_at(i)
        at = pl.ds(pl.multiple_of(j * rows, rows), rows)
        dqkv[j, :, 0:gw] = dqT[:, at].T.astype(BF16)
        flat = dqkv[j]
        parts[j] = dot(flat, weights, 1, 1).astype(BF16)
        pr_copy(j).start()
        return sums + dot(ones, flat, 1, 0)

    sums = lax.fori_loop(0, tp, token_grads, jnp.zeros((8, 3 * gw), F32))

    spack[...] = pack_ref[...]
    blocks = gw // share
    for b in range(blocks):
        spack[me.group * blocks + b, 0:1, 0:share] = sums[0:1, b * share : (b + 1) * share]
        spack[me.group * blocks + b, 1:2, 0:share] = sums[0:1, 2 * gw + b * share : 2 * gw + (b + 1) * share]

    def small_copy(i):
        peer = lax.rem(me.d + 1 + i, dp)
        return remote(spack.at[peer], srecv.at[i], sm_send.at[i], sm_recv.at[i], peer, me.z)

    def small_start(i, _):
        small_copy(i).start()
        return 0

    lax.fori_loop(0, dp - 1, small_start, 0)

    def rr_copy(j):
        return remote(sj.at[j], rr.at[j], rr_send.at[j], rr_recv.at[j], me.d, me.buddy)

    def collects(j):
        return jnp.where(j // 2 == me.pair, j, me.near_here) == me.z

    def chip_sum(i, _):
        j = block_at(i)
        arrival(pr.at[j], pr_recv.at[j]).wait()
        sj[j] = (parts[j, mine, :].astype(F32) + pr[j].astype(F32)).astype(BF16)

        @pl.when(jnp.logical_not(collects(j)))
        def _():
            rr_copy(j).start()

        return 0

    lax.fori_loop(0, tp, chip_sum, 0)

    def fin_copy(j):
        return remote(pr.at[j], fin.at[me.core], fin_send.at[j], fin_recv.at[me.core], me.owner, j)

    def lands_here(j):
        return jnp.logical_and(me.core == me.pair, j == me.z)

    total = None
    for j in range(tp):
        term = dot(xs_ref[j], dqkv[j], 0, 0)
        total = term if total is None else total + term
    qsend[...] = total.astype(BF16).reshape(dp, share, 3 * gw)

    def q_copy(peer, i):
        return remote(qsend.at[peer], qr.at[me.core, me.chip], qr_send.at[i], qr_recv.at[me.core, me.chip], peer, me.z)

    def q_start(i, _):
        peer = lax.rem(me.d + i, dp)

        @pl.when(i == 0)
        def _():
            pltpu.make_async_copy(qsend.at[peer], qr.at[me.core, me.chip], qr_recv.at[me.core, me.chip]).start()

        @pl.when(i > 0)
        def _():
            q_copy(peer, i).start()

        return 0

    lax.fori_loop(0, dp, q_start, 0)

    def pair_total(i, _):
        j = block_at(i)

        @pl.when(collects(j))
        def _():
            arrival(rr.at[j], rr_recv.at[j]).wait()
            pr[j] = (sj[j].astype(F32) + rr[j].astype(F32)).astype(BF16)

            @pl.when(lands_here(j))
            def _():
                pltpu.make_async_copy(pr.at[j], fin.at[me.core], fin_recv.at[me.core]).start()

            @pl.when(jnp.logical_not(lands_here(j)))
            def _():
                fin_copy(j).start()

        return 0

    lax.fori_loop(0, tp, pair_total, 0)

    def plane_total(t, _):
        total = own[t, me.chip].astype(F32)
        for i in range(chips - 1):
            arrival(pln.at[t, i], pl_recv.at[t, i]).wait()
            total = total + pln[t, i].astype(F32)
        zsrc[t] = total.astype(BF16)
        return 0

    lax.fori_loop(0, tp, plane_total, 0)

    def z_copy(s):
        t = lax.rem(me.z + s, tp)
        return remote(zsrc.at[t], zrecv.at[s - 1], zz_send.at[s - 1], zz_recv.at[s - 1], me.d, t)

    for s in range(1, tp):
        z_copy(s).start()

    def q_pair(s):
        return me.z // 2, 2 * me.low + s

    for s in range(2):
        total = None
        for k in range(chips):
            arrival(qr.at[s, k], qr_recv.at[s, k]).wait()
            term = qr[s, k].astype(F32)
            total = term if total is None else total + term
        qz[s] = total.astype(BF16)
        p, t = q_pair(s)

        @pl.when(t == me.z)
        def _(s=s, p=p):
            pltpu.make_async_copy(qz.at[s], qf.at[p], qf_recv.at[p]).start()

        @pl.when(t != me.z)
        def _(s=s, p=p, t=t):
            remote(qz.at[s], qf.at[p], qf_send.at[s], qf_recv.at[p], me.d, t).start()

    total = spack[me.d]
    for i in range(dp - 1):
        arrival(srecv.at[i], sm_recv.at[i]).wait()
        total = total + srecv[i]
    zpack[me.z] = total

    def sz_copy(s):
        return remote(zpack.at[me.z], zpack.at[me.z], sz_send.at[s - 1], sz_recv.at[me.z], me.d, lax.rem(me.z + s, tp))

    for s in range(1, tp):
        sz_copy(s).start()

    for h in range(2):
        arrival(fin.at[h], fin_recv.at[h]).wait()
        at = slice(h * half, (h + 1) * half)
        dx_ref[at, :] = dr1_ref[at, :] + fin[h].astype(F32)
    for p in range(2):
        arrival(qf.at[p], qf_recv.at[p]).wait()
    qgrad_ref[...] = qf[0].astype(F32) + qf[1].astype(F32)
    for s in range(1, tp):
        t = lax.rem(me.z + s, tp)
        arrival(zpack.at[t], sz_recv.at[t]).wait()
    total = zpack[0]
    for t in range(1, tp):
        total = total + zpack[t]
    small_ref[...] = total
    total = zsrc[me.z].astype(F32)
    for s in range(tp - 1):
        arrival(zrecv.at[s], zz_recv.at[s]).wait()
        total = total + zrecv[s].astype(F32)
    gsum_ref[...] = total

    for g in range(4):

        @pl.when(jnp.logical_not(jnp.logical_and(2 * me.core + g // 2 == me.z, g % 2 == me.core)))
        def _(g=g):
            remote(do_ref.at[g], dof.at[0], do_send.at[g], do_recv.at[0], me.sibling, me.z).wait_send()

    for t in range(tp):
        sib_copy(t).wait_send()
        pr_copy(t).wait_send()

        @pl.when(jnp.logical_not(collects(t)))
        def _(t=t):
            rr_copy(t).wait_send()

        @pl.when(jnp.logical_and(collects(t), jnp.logical_not(lands_here(t))))
        def _(t=t):
            fin_copy(t).wait_send()

    def plane_sent(n, _):
        plane_copy(n // tp, lax.rem(n, tp)).wait_send()
        return 0

    lax.fori_loop(0, (chips - 1) * tp, plane_sent, 0)

    def peers_sent(i, _):
        small_copy(i).wait_send()
        q_copy(lax.rem(me.d + 1 + i, dp), i + 1).wait_send()
        return 0

    lax.fori_loop(0, dp - 1, peers_sent, 0)
    for s in range(1, tp):
        z_copy(s).wait_send()
        sz_copy(s).wait_send()
    for s in range(2):
        p, t = q_pair(s)

        @pl.when(t != me.z)
        def _(s=s, p=p, t=t):
            remote(qz.at[s], qf.at[p], qf_send.at[s], qf_recv.at[p], me.d, t).wait_send()


def back(do, grad, xs, wqf, oT, lse, qT, kA, v, pack, dr1):
    tp, rows, width = xs.shape
    dp, share, qwidth = wqf.shape
    chips = dp // 2
    length = rows * tp
    half = rows // 2
    cols = grad.shape[-1]
    S = jax.ShapeDtypeStruct
    vmem = pl.BlockSpec(memory_space=pltpu.VMEM)
    anym = pl.BlockSpec(memory_space=pl.ANY)
    dma = pltpu.SemaphoreType.DMA
    V = pltpu.VMEM
    return pl.pallas_call(
        back_kernel,
        name="back",
        out_shape=(
            S((rows, width), F32),
            S((share, cols), F32),
            S((share, qwidth), F32),
            S((16, 128), F32),
        ),
        in_specs=[anym, anym] + [vmem] * 9,
        out_specs=(vmem,) * 4,
        scratch_shapes=[
            V((tp, rows, 192), BF16), V((192, length), BF16), V((3, 1, length), F32),
            V((3, length, 128), BF16), V((3, HEAD_DIM, length), BF16),
            V((length, 128), F32), V((length, HEAD_DIM), F32), V((192, length), F32), V((tp, rows, qwidth), BF16),
            V((tp, chips, share, cols), BF16), V((tp, chips, share, cols), BF16), V((tp, chips - 1, share, cols), BF16),
            V((tp, share, cols), BF16), V((tp - 1, share, cols), BF16),
            V((tp, rows, width), BF16), V((tp, half, width), BF16), V((tp, half, width), BF16), V((tp, half, width), BF16),
            V((2, half, width), BF16),
            V((dp, share, qwidth), BF16), V((2, chips, share, qwidth), BF16), V((2, share, qwidth), BF16), V((2, share, qwidth), BF16),
            V((dp, 16, 128), F32), V((dp - 1, 16, 128), F32), V((tp, 16, 128), F32),
            dma((4,)), dma((tp,)), dma((tp,)), dma((tp,)), dma((tp,)), dma((tp, chips - 1)), dma((tp, chips - 1)), dma((tp - 1,)), dma((tp - 1,)),
            dma((tp,)), dma((tp,)), dma((tp,)), dma((tp,)), dma((tp,)), dma((2,)), dma((dp,)), dma((2, chips)), dma((2,)), dma((2,)),
            dma((dp - 1,)), dma((dp - 1,)), dma((tp - 1,)), dma((tp,)),
        ],
        compiler_params=pltpu.CompilerParams(
            collective_id=1, has_side_effects=True, vmem_limit_bytes=VMEM_LIMIT
        ),
    )(do, grad, xs, wqf, oT, lse, qT, kA, v, pack, dr1)


def shards(
    tokens, teacher, lengths, loss_mask, loss_scale,
    query_weight, query_bias, key_weight, value_weight, value_bias, mixer_weight, mixer_bias,
    first_gain, first_shift, inner_weight, inner_bias, outer_weight, outer_bias, second_gain, second_shift,
):
    dp, tp = lax.axis_size("dp"), lax.axis_size("tensor")
    if query_weight.shape[0] % 16 or tp != 4:
        return plain_shards(
            tokens, teacher, lengths, loss_mask, loss_scale,
            query_weight, query_bias, key_weight, value_weight, value_bias, mixer_weight, mixer_bias,
            first_gain, first_shift, inner_weight, inner_bias, outer_weight, outer_bias, second_gain, second_shift,
        )
    z = lax.axis_index("tensor")
    rows, width = tokens.shape
    share = query_weight.shape[0]
    gw = query_weight.shape[1]
    hidden = inner_weight.shape[1]
    hshare = inner_bias.shape[0]
    hrows = -(-hshare // 128)
    pos = z * rows + jnp.arange(rows)
    counted = jnp.logical_and(pos < lengths[0], loss_mask == 1).astype(F32)
    vectors = jnp.stack(
        [query_bias, value_bias, mixer_bias, first_gain, first_shift, outer_bias, second_gain, second_shift]
    ).astype(F32)
    small = jnp.concatenate(
        [
            jnp.pad(vectors, ((0, 0), (0, 128 - share))),
            jnp.full((1, 128), jnp.sum(counted)),
            jnp.pad(inner_bias.astype(F32), (0, hrows * 128 - hshare)).reshape(hrows, 128),
            jnp.zeros((3 - hrows, 128), F32),
            jnp.full((1, 128), lengths[0].astype(F32)),
            jnp.zeros((3, 128), F32),
        ],
        axis=0,
    )
    wq = jnp.concatenate([query_weight, key_weight, value_weight], axis=1)
    wm = jnp.concatenate([inner_weight, outer_weight.T, mixer_weight.T], axis=1)
    oin, wall, smalls, count, xs, wqf, oT, lse, qT, kA, v = front(tokens, wq, wm, small, dp, tp)
    token_total = count[0, 0]
    vecs = jnp.moveaxis(smalls[:, 0:8, 0:share], 0, 1).reshape(8, width)
    ib = smalls[:, 9 : 9 + hrows, :].reshape(dp, hrows * 128)[:, :hshare].reshape(tp, 1, hidden)
    scale = (2.0 * loss_scale / (token_total * width)).reshape(1, 1)
    wall = wall.reshape(tp, width, wm.shape[1])
    layer_output, dr1, do, grad, sums, isums = mid(tokens, teacher, counted[:, None], scale, oin, wall, vecs, ib)
    pack = jnp.concatenate(
        [
            jnp.zeros((dp, 2, 128), F32),
            jnp.pad(jnp.moveaxis(sums[0:6].reshape(6, dp, share), 1, 0), ((0, 0), (0, 0), (0, 128 - share))),
            jnp.broadcast_to(sums[6, 0], (dp, 1, 128)),
            jnp.pad(isums.reshape(dp, hshare), ((0, 0), (0, hrows * 128 - hshare))).reshape(dp, hrows, 128),
            jnp.zeros((dp, 7 - hrows, 128), F32),
        ],
        axis=1,
    )
    grad = grad.reshape(tp, dp // 2, 2, share, wm.shape[1])
    input_grad, gsum, qgrad, ssum = back(do, grad, xs, wqf, oT, lse, qT, kA, v, pack, dr1)
    loss_value = ssum[8, 0] / (token_total * width)
    line = lambda i: ssum[i, :share]
    innerbias_grad = ssum[9 : 9 + hrows].reshape(-1)[:hshare]
    return (
        layer_output,
        loss_value,
        input_grad,
        qgrad[:, 0:gw],
        line(0),
        qgrad[:, gw : 2 * gw],
        qgrad[:, 2 * gw :],
        line(1),
        gsum[:, 2 * hidden :].T,
        line(2),
        line(3),
        line(4),
        gsum[:, 0:hidden],
        innerbias_grad,
        gsum[:, hidden : 2 * hidden].T,
        line(5),
        line(6),
        line(7),
    )


def in_blocks(value, dim, size):
    before, after = (value.shape[:dim], value.shape[dim + 1 :])
    return jnp.moveaxis(value.reshape(*before, size, -1, *after), dim, 0)


def summed_on_arrival(value, axis, dim):
    size = lax.axis_size(axis)
    blocks = lax.all_to_all(in_blocks(value, dim, size), axis, 0, 0, tiled=True)
    return jnp.sum(blocks.astype(jnp.float32), axis=0)


def sent_together(arrays, axis, dim, along):
    both = jnp.concatenate(arrays, axis=along)
    out, at, gathered = (summed_on_arrival(both, axis, dim), 0, [])
    for a in arrays:
        gathered.append(lax.slice_in_dim(out, at, at + a.shape[along], axis=along))
        at += a.shape[along]
    return tuple(gathered)


def contract_last(left_rows, right_rows):
    return lax.dot_general(
        left_rows, right_rows, (((1,), (1,)), ((), ())), preferred_element_type=jnp.float32
    )


def contract_first(left_rows, right_rows):
    return lax.dot_general(
        left_rows, right_rows, (((0,), (0,)), ((), ())), preferred_element_type=jnp.float32
    )


def plain_dot(left_rows, right_rows):
    return jnp.dot(left_rows, right_rows, preferred_element_type=jnp.float32)


def gelu_exact(pre_values):
    return jax.nn.gelu(pre_values, approximate=False)


def plain_norm_forward(values_in, gain_vec, shift_vec):
    centred = values_in - jnp.mean(values_in, axis=1, keepdims=True)
    inv_std = lax.rsqrt(jnp.mean(centred * centred, axis=1, keepdims=True) + norm_eps)
    normed = centred * inv_std
    return (normed * gain_vec + shift_vec, normed, inv_std)


def plain_norm_backward(grad_out, normed, inv_std, gain_vec):
    grad_normed = grad_out * gain_vec
    mean_plain = jnp.mean(grad_normed, axis=1, keepdims=True)
    mean_mixed = jnp.mean(grad_normed * normed, axis=1, keepdims=True)
    grad_in = inv_std * (grad_normed - mean_plain - normed * mean_mixed)
    return (grad_in, jnp.sum(grad_out * normed, axis=0), jnp.sum(grad_out, axis=0))


def plain_shards(
    tokens,
    teacher,
    lengths,
    loss_mask,
    loss_scale,
    query_weight,
    query_bias,
    key_weight,
    value_weight,
    value_bias,
    mixer_weight,
    mixer_bias,
    first_gain,
    first_shift,
    inner_weight,
    inner_bias,
    outer_weight,
    outer_bias,
    second_gain,
    second_shift,
):
    tp_count = lax.axis_size("tensor")
    tp_index = lax.axis_index("tensor")
    dp_count = lax.axis_size("dp")
    dp_index = lax.axis_index("dp")
    local_rows = tokens.shape[0]
    seq_len = local_rows * tp_count
    model_width = tokens.shape[1]
    head_width = query_weight.shape[1]
    hidden_width = inner_weight.shape[1]
    head_count = head_width // HEAD_DIM
    block_count = seq_len // QBLOCK
    score_scale = HEAD_DIM ** (-0.5)
    length_here = lengths[0]
    local_pos = tp_index * local_rows + jnp.arange(local_rows)
    counted = jnp.logical_and(local_pos < length_here, loss_mask == 1).astype(jnp.float32)
    count_local = jnp.sum(counted)
    small_stack = jnp.stack(
        [
            query_bias,
            value_bias,
            mixer_bias,
            first_gain,
            first_shift,
            outer_bias,
            second_gain,
            second_shift,
        ]
    )

    def fetch_params():
        return (
            lax.all_gather(query_weight, "dp", axis=0, tiled=True),
            lax.all_gather(key_weight, "dp", axis=0, tiled=True),
            lax.all_gather(value_weight, "dp", axis=0, tiled=True),
            lax.all_gather(mixer_weight, "dp", axis=1, tiled=True),
            lax.all_gather(inner_weight, "dp", axis=0, tiled=True),
            lax.all_gather(outer_weight, "dp", axis=1, tiled=True),
            lax.all_gather(small_stack, "dp", axis=1, tiled=True),
            lax.all_gather(inner_bias, "dp", axis=0, tiled=True),
        )

    def attn_gather(values_in):
        return lax.all_gather(values_in, "tensor", axis=0, tiled=True)

    def ffn_gather(values_in):
        return lax.all_gather(values_in, "tensor", axis=0, tiled=True)

    (
        query_full,
        key_full,
        value_full,
        mixer_full,
        inner_full,
        outer_full,
        small_full,
        innerb_full,
    ) = fetch_params()
    small_wide = small_full.astype(jnp.float32)
    qbias_mine = lax.dynamic_slice_in_dim(small_wide[0], tp_index * head_width, head_width)
    vbias_mine = lax.dynamic_slice_in_dim(small_wide[1], tp_index * head_width, head_width)
    inner_mine = lax.dynamic_slice_in_dim(
        innerb_full.astype(jnp.float32), tp_index * hidden_width, hidden_width
    )
    seq_rows = attn_gather(tokens)
    queries = (plain_dot(seq_rows, query_full) + qbias_mine).astype(jnp.bfloat16)
    keys_all = plain_dot(seq_rows, key_full).astype(jnp.bfloat16)
    values_all = (plain_dot(seq_rows, value_full) + vbias_mine).astype(jnp.bfloat16)
    keys_three = keys_all.reshape(seq_len, head_count, HEAD_DIM)
    values_three = values_all.reshape(seq_len, head_count, HEAD_DIM)
    key_valid = jnp.arange(seq_len) < length_here

    def score_block(query_block):
        scores = (
            jnp.einsum("qhd,khd->hqk", query_block, keys_three, preferred_element_type=jnp.float32)
            * score_scale
        )
        return jnp.where(key_valid[None, None, :], scores, masked_score)

    def forward_block(query_block):
        scores = score_block(query_block)
        row_top = jnp.max(scores, axis=2, keepdims=True)
        exp_scores = jnp.exp(scores - row_top)
        row_total = jnp.sum(exp_scores, axis=2, keepdims=True)
        prob_low = (exp_scores / row_total).astype(jnp.bfloat16)
        mixed_rows = jnp.einsum(
            "hqk,khd->qhd", prob_low, values_three, preferred_element_type=jnp.float32
        )
        return (mixed_rows.astype(jnp.bfloat16), (row_top + jnp.log(row_total))[:, :, 0])

    query_blocks = queries.reshape(block_count, QBLOCK, head_count, HEAD_DIM)
    attended, log_sums = lax.map(forward_block, query_blocks)
    attended = attended.reshape(seq_len, head_width)
    attn_out = lax.psum_scatter(
        plain_dot(attended, mixer_full).astype(jnp.bfloat16),
        "tensor",
        scatter_dimension=0,
        tiled=True,
    ).astype(jnp.float32)
    first_sum = tokens.astype(jnp.float32) + attn_out + small_wide[2]
    hidden_one, normed_one, inv_one = plain_norm_forward(first_sum, small_wide[3], small_wide[4])
    hidden_low = hidden_one.astype(jnp.bfloat16)
    ffn_rows = ffn_gather(hidden_low)
    pre_act = plain_dot(ffn_rows, inner_full) + inner_mine
    act_full, gelu_pull = jax.vjp(gelu_exact, pre_act)
    activated = act_full.astype(jnp.bfloat16)
    ffn_out = lax.psum_scatter(
        plain_dot(activated, outer_full).astype(jnp.bfloat16),
        "tensor",
        scatter_dimension=0,
        tiled=True,
    ).astype(jnp.float32)
    second_sum = hidden_one + ffn_out + small_wide[5]
    final_rows, normed_two, inv_two = plain_norm_forward(second_sum, small_wide[6], small_wide[7])
    layer_output = final_rows.astype(jnp.bfloat16)
    diff_rows = final_rows - teacher.astype(jnp.float32)
    loss_local = jnp.sum(counted * jnp.sum(diff_rows * diff_rows, axis=1))
    loss_total, token_total = lax.psum((loss_local, count_local), ("dp", "tensor"))
    grad_scale = 2.0 * loss_scale / (token_total * model_width)
    grad_final = grad_scale * counted[:, None] * diff_rows
    (
        query_full,
        key_full,
        value_full,
        mixer_full,
        inner_full,
        outer_full,
        small_full,
        innerb_full,
    ) = fetch_params()
    ffn_rows = ffn_gather(hidden_low)
    grad_second, secondgain_part, secondshift_part = plain_norm_backward(
        grad_final, normed_two, inv_two, small_wide[6]
    )
    outerbias_part = jnp.sum(grad_second, axis=0)
    grad_ffn_rows = lax.all_gather(grad_second.astype(jnp.bfloat16), "tensor", axis=0, tiled=True)
    grad_act = contract_last(grad_ffn_rows, outer_full)
    outer_local = contract_first(activated, grad_ffn_rows)
    grad_pre = gelu_pull(grad_act)[0].astype(jnp.bfloat16)
    innerbias_part = jnp.sum(grad_pre, axis=0, dtype=jnp.float32)
    inner_local = contract_first(ffn_rows, grad_pre)
    grad_hidden = lax.psum_scatter(
        contract_last(grad_pre, inner_full).astype(jnp.bfloat16),
        "tensor",
        scatter_dimension=0,
        tiled=True,
    ).astype(jnp.float32)
    inner_grad, outer_grad = (
        lax.psum_scatter(inner_local, "dp", scatter_dimension=0, tiled=True),
        lax.psum_scatter(outer_local, "dp", scatter_dimension=1, tiled=True),
    )
    grad_first, firstgain_part, firstshift_part = plain_norm_backward(
        grad_second + grad_hidden, normed_one, inv_one, small_wide[3]
    )
    mixerbias_part = jnp.sum(grad_first, axis=0)
    grad_attn_rows = lax.all_gather(grad_first.astype(jnp.bfloat16), "tensor", axis=0, tiled=True)
    grad_attended = contract_last(grad_attn_rows, mixer_full).astype(jnp.bfloat16)
    mixer_local = contract_first(attended, grad_attn_rows)
    grad_blocks = grad_attended.reshape(block_count, QBLOCK, head_count, HEAD_DIM)

    def backward_block(carried, block_in):
        key_acc, value_acc = carried
        query_block, grad_block, lse_block = block_in
        scores = score_block(query_block)
        prob_full = jnp.exp(scores - lse_block[:, :, None])
        prob_low = prob_full.astype(jnp.bfloat16)
        grad_prob = jnp.einsum(
            "qhd,khd->hqk", grad_block, values_three, preferred_element_type=jnp.float32
        )
        row_dot = jnp.sum(prob_full * grad_prob, axis=2, keepdims=True)
        grad_scores = (prob_full * (grad_prob - row_dot)).astype(jnp.bfloat16)
        grad_query = (
            jnp.einsum("hqk,khd->qhd", grad_scores, keys_three, preferred_element_type=jnp.float32)
            * score_scale
        ).astype(jnp.bfloat16)
        key_acc = (
            key_acc
            + jnp.einsum(
                "hqk,qhd->khd", grad_scores, query_block, preferred_element_type=jnp.float32
            )
            * score_scale
        )
        value_acc = value_acc + jnp.einsum(
            "hqk,qhd->khd", prob_low, grad_block, preferred_element_type=jnp.float32
        )
        return ((key_acc, value_acc), grad_query)

    zero_acc = jnp.zeros((seq_len, head_count, HEAD_DIM), jnp.float32)
    (key_acc, value_acc), grad_queries = lax.scan(
        backward_block, (zero_acc, zero_acc), (query_blocks, grad_blocks, log_sums)
    )
    grad_queries = grad_queries.reshape(seq_len, head_width)
    grad_keys = key_acc.reshape(seq_len, head_width).astype(jnp.bfloat16)
    grad_values = value_acc.reshape(seq_len, head_width).astype(jnp.bfloat16)
    seq_rows = attn_gather(tokens)
    query_local = contract_first(seq_rows, grad_queries)
    key_local = contract_first(seq_rows, grad_keys)
    value_local = contract_first(seq_rows, grad_values)
    querybias_part = jnp.sum(grad_queries, axis=0, dtype=jnp.float32)
    valuebias_part = jnp.sum(grad_values, axis=0, dtype=jnp.float32)
    total_term = contract_last(grad_queries, query_full)
    total_term = total_term + contract_last(grad_keys, key_full)
    grad_tokens = lax.psum_scatter(
        (total_term + contract_last(grad_values, value_full)).astype(jnp.bfloat16),
        "tensor",
        scatter_dimension=0,
        tiled=True,
    ).astype(jnp.float32)
    input_grad = grad_first + grad_tokens
    query_grad, key_grad, value_grad, mixer_grad = (
        *sent_together(
            (
                query_local.astype(jnp.bfloat16),
                key_local.astype(jnp.bfloat16),
                value_local.astype(jnp.bfloat16),
            ),
            "dp",
            0,
            1,
        ),
        summed_on_arrival(mixer_local.astype(jnp.bfloat16), "dp", 1),
    )

    def spread_part(part_vec, full_width):
        return lax.dynamic_update_slice_in_dim(
            jnp.zeros((full_width,), jnp.float32), part_vec, tp_index * part_vec.shape[0], 0
        )

    small_terms = jnp.stack(
        [
            spread_part(querybias_part, model_width),
            spread_part(valuebias_part, model_width),
            mixerbias_part,
            firstgain_part,
            firstshift_part,
            outerbias_part,
            secondgain_part,
            secondshift_part,
        ]
    )
    inner_terms = spread_part(innerbias_part, hidden_width * tp_count)
    small_sum, inner_sum = lax.psum((small_terms, inner_terms), ("dp", "tensor"))
    loss_value = loss_total / (token_total * model_width)
    width_share = model_width // dp_count
    small_mine = lax.dynamic_slice_in_dim(small_sum, dp_index * width_share, width_share, 1)
    hidden_share = inner_sum.shape[0] // dp_count
    innerbias_grad = lax.dynamic_slice_in_dim(inner_sum, dp_index * hidden_share, hidden_share, 0)
    return (
        layer_output,
        loss_value,
        input_grad,
        query_grad,
        small_mine[0],
        key_grad,
        value_grad,
        small_mine[1],
        mixer_grad,
        small_mine[2],
        small_mine[3],
        small_mine[4],
        inner_grad,
        innerbias_grad,
        outer_grad,
        small_mine[5],
        small_mine[6],
        small_mine[7],
    )


def solution(mesh):
    return jax.shard_map(
        shards,
        mesh=mesh,
        in_specs=(
            P(("dp", "tensor"), None),
            P(("dp", "tensor"), None),
            P("dp"),
            P(("dp", "tensor")),
            P(),
            P("dp", "tensor"),
            P("dp"),
            P("dp", "tensor"),
            P("dp", "tensor"),
            P("dp"),
            P("tensor", "dp"),
            P("dp"),
            P("dp"),
            P("dp"),
            P("dp", "tensor"),
            P("dp"),
            P("tensor", "dp"),
            P("dp"),
            P("dp"),
            P("dp"),
        ),
        out_specs=(
            P(("dp", "tensor"), None),
            P(),
            P(("dp", "tensor"), None),
            P("dp", "tensor"),
            P("dp"),
            P("dp", "tensor"),
            P("dp", "tensor"),
            P("dp"),
            P("tensor", "dp"),
            P("dp"),
            P("dp"),
            P("dp"),
            P("dp", "tensor"),
            P("dp"),
            P("tensor", "dp"),
            P("dp"),
            P("dp"),
            P("dp"),
        ),
        check_vma=False,
    )
```

```python
import functools
import jax
import jax.numpy as jnp
from jax import lax
from jax.experimental import pallas as pl
from jax.experimental.pallas import tpu as pltpu
from jax.sharding import PartitionSpec as P

HEAD_DIM = 64
QBLOCK = 512
MESH = pl.DeviceIdType.MESH
F32 = jnp.float32
BF16 = jnp.bfloat16
norm_eps = 1e-05
masked_score = -1e30
VMEM_LIMIT = 60 * 1024 * 1024


def dot(left, right, left_dim, right_dim):
    return lax.dot_general(
        left, right, (((left_dim,), (right_dim,)), ((), ())), preferred_element_type=F32
    )


def remote(src, dst, send, recv, d, t):
    return pltpu.make_async_remote_copy(
        src_ref=src,
        dst_ref=dst,
        send_sem=send,
        recv_sem=recv,
        device_id={"dp": d, "tensor": t},
        device_id_type=MESH,
    )


def arrival(dst, recv):
    return pltpu.make_async_copy(dst, dst, recv)


class Place:
    def __init__(self):
        self.dp = lax.axis_size("dp")
        self.tp = lax.axis_size("tensor")
        self.d = lax.axis_index("dp")
        self.z = lax.axis_index("tensor")
        self.core = lax.rem(self.d, 2)
        self.chip = self.d // 2
        self.chips = self.dp // 2
        self.base = self.chip * 2
        self.sibling = self.base + 1 - self.core
        self.pair = self.z // 2
        self.low = lax.rem(self.z, 2)
        self.group = 2 * self.low + self.core
        self.buddy = 2 * self.pair + 1 - self.low
        self.owner = self.base + self.pair
        self.near_here = 1 + self.pair
        self.near_there = 2 - self.pair
        side = self.chip + 1 - 2 * lax.rem(self.chip, 2)
        across = lax.rem(self.chip + 2, 4)
        self.first = jnp.where(self.core == 0, side, across)
        self.second = jnp.where(self.core == 0, across, side)
        self.diagonal = 3 - self.chip
        self.around = (self.buddy, self.near_there, 3 * (1 - self.pair))


def greet(place):
    barrier = pltpu.get_barrier_semaphore()
    count = 0
    for t in range(place.tp):
        for c in range(2):
            other = jnp.logical_not(jnp.logical_and(place.z == t, place.core == c))

            @pl.when(other)
            def _(t=t, c=c):
                pl.semaphore_signal(
                    barrier, inc=1, device_id={"dp": place.base + c, "tensor": t}, device_id_type=MESH
                )

            count += 1
    count -= 1

    def plane(i, _):
        chip = lax.rem(place.chip + 1 + i, place.chips)
        for c in range(2):
            pl.semaphore_signal(
                barrier, inc=1, device_id={"dp": chip * 2 + c, "tensor": place.z}, device_id_type=MESH
            )
        return 0

    lax.fori_loop(0, place.chips - 1, plane, 0)
    count += 2 * (place.chips - 1)
    pl.semaphore_wait(barrier, count)


def front_kernel(
    x_ref, wq_ref, wm_ref, sm_ref,
    oin_ref, wall_ref, smalls_ref, count_ref, xs_ref, wqf_ref, oT_ref, lse_ref, qT_ref, kA_ref, v_ref,
    wqz, counts, vT, scores, o_buf, wqT, wkp, wvp, wvT,
    sm_send, sm_recv, cn_send, cn_recv, wz_send, wz_recv, wp_send, wp_recv,
    x_send, x_recv, xr_send, xf_send, mz_send, mz_recv, mp_send, mp_recv, ms_send, ms_recv, o_send, o_recv,
):
    me = Place()
    dp, tp, chips = me.dp, me.tp, me.chips
    rows, width = x_ref.shape
    half = rows // 2
    length = rows * tp
    share = wq_ref.shape[0]
    heads = 3
    greet(me)

    def each_peer(f):
        def step(i, _):
            f(i, lax.rem(me.d + 1 + i, dp))
            return 0

        lax.fori_loop(0, dp - 1, step, 0)

    def small_copy(i, peer):
        return remote(sm_ref, smalls_ref.at[me.d], sm_send.at[i], sm_recv.at[me.d], peer, me.z)

    each_peer(lambda i, peer: small_copy(i, peer).start())
    smalls_ref[me.d] = sm_ref[...]

    for s in range(2):
        target = me.z // 2 + 2 * s
        src, dst = wq_ref, wqz.at[me.low]

        @pl.when(target == me.z)
        def _(s=s, dst=dst):
            pltpu.make_async_copy(wq_ref, dst, wz_recv.at[me.low]).start()

        @pl.when(target != me.z)
        def _(s=s, dst=dst, target=target):
            remote(wq_ref, dst, wz_send.at[s], wz_recv.at[me.low], me.d, target).start()

    is_near = me.z == me.near_here
    is_end = jnp.logical_not(is_near)
    pltpu.make_async_copy(wm_ref, wall_ref.at[me.z, me.d], mz_recv.at[me.z]).start()

    def along_z(unit, t, sem, to):
        return remote(unit, wall_ref.at[t, me.d], mz_send.at[sem], mz_recv.at[t], me.d, to)

    pl.when(me.z > 0)(lambda: along_z(wm_ref, me.z, 0, me.z - 1).start())
    pl.when(me.z < tp - 1)(lambda: along_z(wm_ref, me.z, 1, me.z + 1).start())

    def goes_up(t):
        return jnp.logical_and(t < me.z, me.z < tp - 1)

    def goes_down(t):
        return jnp.logical_and(t > me.z, me.z > 0)

    is_owner = me.core == me.pair
    for h in range(2):
        part = pl.ds(h * half, half)

        @pl.when(is_owner)
        def _(h=h, part=part):
            pltpu.make_async_copy(x_ref.at[part], xs_ref.at[me.z, part], x_recv.at[me.z, h]).start()
            remote(x_ref.at[part], xs_ref.at[me.z, part], x_send.at[h], x_recv.at[me.z, h], me.base + h, me.buddy).start()
            remote(x_ref.at[part], xs_ref.at[me.z, part], xr_send.at[0, h], x_recv.at[me.z, h], me.sibling, me.z).start()

        @pl.when(jnp.logical_not(is_owner))
        def _(h=h, part=part):
            remote(x_ref.at[part], xs_ref.at[me.z, part], x_send.at[h], x_recv.at[me.z, h], me.base + h, me.near_there).start()

    def wq_plane(s, k):
        dst = wqf_ref.at[me.d]
        return remote(wqz.at[s], dst, wp_send.at[s, k], wp_recv.at[me.d], 2 * k + s, me.z)

    for s in range(2):
        arrival(wqz.at[s], wz_recv.at[s]).wait()

        def step(i, _, s=s):
            k = lax.rem(me.chip + 1 + i, chips)
            here = 2 * k + s == me.d

            @pl.when(here)
            def _():
                pltpu.make_async_copy(wqz.at[s], wqf_ref.at[me.d], wp_recv.at[me.d]).start()

            @pl.when(jnp.logical_not(here))
            def _():
                wq_plane(s, k).start()

            return 0

        lax.fori_loop(0, chips, step, 0)

    def in_plane(unit, t, k, sem, to):
        return remote(unit, wall_ref.at[t, 2 * k + me.core], mp_send.at[t, sem], mp_recv.at[t, k], 2 * to + me.core, me.z)

    def plane_units(t, unit):
        in_plane(unit, t, me.chip, 0, me.first).start()
        in_plane(unit, t, me.chip, 1, me.second).start()

    def to_sibling(t, k):
        unit = wall_ref.at[t, 2 * k + me.core]
        return remote(unit, unit, ms_send.at[t, k], ms_recv.at[t, k], me.sibling, me.z)

    def own_unit(t):
        unit = wall_ref.at[t, me.d]
        arrival(unit, mz_recv.at[t]).wait()
        pl.when(goes_up(t))(lambda: along_z(unit, t, 2 + t, me.z + 1).start())
        pl.when(goes_down(t))(lambda: along_z(unit, t, 2 + t, me.z - 1).start())
        plane_units(t, unit)
        to_sibling(t, me.chip).start()

    def plane_unit(t, k):
        unit = wall_ref.at[t, 2 * k + me.core]
        arrival(unit, mp_recv.at[t, k]).wait()
        return unit

    def plane_forward(t):
        unit = plane_unit(t, me.first)
        in_plane(unit, t, me.first, 2, me.second).start()
        to_sibling(t, me.first).start()

    def plane_rest(t):
        for k in (me.second, me.diagonal):
            plane_unit(t, k)
            to_sibling(t, k).start()

    plane_units(me.z, wm_ref)
    remote(wm_ref, wall_ref.at[me.z, me.d], ms_send.at[me.z, me.chip], ms_recv.at[me.z, me.chip], me.sibling, me.z).start()

    mine = pl.ds(pl.multiple_of(me.core * half, half), half)
    other = pl.ds(pl.multiple_of((1 - me.core) * half, half), half)
    far_first = 2 * (1 - me.pair) + me.pair
    far_second = 2 * (1 - me.pair) + 1 - me.pair
    blocks_in = (
        jnp.where(is_near, far_first, me.buddy),
        jnp.where(is_near, far_second, far_first),
        jnp.where(is_near, me.buddy, far_second),
    )

    def relay(n):
        j = blocks_in[n]
        part = xs_ref.at[j, mine]
        arrival(part, x_recv.at[j, me.core]).wait()
        remote(part, part, xr_send.at[1 + n, 0], x_recv.at[j, me.core], me.sibling, me.z).start()
        if n < 2:
            pl.when(is_near)(lambda: remote(part, part, xf_send.at[n], x_recv.at[j, me.core], me.d, me.buddy).start())

    own_unit(me.around[0])
    relay(0)
    relay(1)

    def small_wait(i, peer):
        arrival(smalls_ref.at[peer], sm_recv.at[peer]).wait()

    each_peer(small_wait)
    plane_count = smalls_ref[0][8:16]
    for k in range(1, dp):
        plane_count = plane_count + smalls_ref[k][8:16]
    counts[me.z] = plane_count
    for s in range(1, tp):
        remote(counts.at[me.z], counts.at[me.z], cn_send.at[s - 1], cn_recv.at[me.z], me.d, lax.rem(me.z + s, tp)).start()

    for k in range(dp):
        arrival(wqf_ref.at[k], wp_recv.at[k]).wait()
    zero = jnp.zeros((share, HEAD_DIM), BF16)
    gw = heads * HEAD_DIM
    for k in range(dp):
        w = wqf_ref[k]
        at = slice(k * share, (k + 1) * share)
        pads = []
        for m in range(3):
            cols = []
            for h in range(heads):
                cols += [w[:, m * gw + h * HEAD_DIM : m * gw + (h + 1) * HEAD_DIM], zero]
            pads.append(jnp.concatenate(cols, axis=1))
        wkp[at, :] = pads[1]
        wvp[at, :] = pads[2]
        scores[0, at, 0:384] = pads[0].astype(F32)
    wqT[...] = scores[0, 0:width, 0:384].T.astype(BF16)
    wvT[...] = wvp[...].astype(F32).T.astype(BF16)

    blocks = gw // share
    row_bias = jnp.zeros((8, 384), F32)
    col_bias = jnp.zeros((384, 8), F32)
    r_in = lax.broadcasted_iota(jnp.int32, (128, 384), 0)
    r_out = lax.broadcasted_iota(jnp.int32, (128, 384), 1)
    c_out = lax.broadcasted_iota(jnp.int32, (384, 128), 0)
    c_in = lax.broadcasted_iota(jnp.int32, (384, 128), 1)

    def padded(col):
        return (col // HEAD_DIM) * 128 + lax.rem(col, HEAD_DIM)

    for b in range(blocks):
        vecs = smalls_ref[me.group * blocks + b][0:8].astype(BF16)
        sel = jnp.logical_and(padded(r_in + b * share) == r_out, r_in < share)
        row_bias = row_bias + dot(vecs, jnp.where(sel, 1.0, 0.0).astype(BF16), 1, 0)
        sel = jnp.logical_and(padded(c_in + b * share) == c_out, c_in < share)
        col_bias = col_bias + dot(jnp.where(sel, 1.0, 0.0).astype(BF16), vecs, 1, 1)
    q_bias = col_bias[:, 0:1]
    v_bias_col = col_bias[:, 1:2]
    v_bias = row_bias[1:2, :]
    valid = smalls_ref[me.base + me.pair][12:13, 0:1]

    lane = lax.broadcasted_iota(jnp.int32, (rows, 128), 1)
    srow = lax.broadcasted_iota(jnp.int32, (128, rows), 0)

    def project(j):
        at = pl.ds(pl.multiple_of(j * rows, rows), rows)
        xb = xs_ref[j]
        keys = dot(xb, wkp[...], 1, 0)
        queries = dot(wqT[...], xb, 1, 1) + q_bias
        vals = dot(xb, wvp[...], 1, 0) + v_bias
        valsT = dot(wvT[...], xb, 1, 1) + v_bias_col
        pos = (j * rows + lax.broadcasted_iota(jnp.int32, (rows, 128), 0)).astype(F32)
        bias = jnp.where(pos < valid, 0.0, masked_score)
        for h in range(heads):
            span = slice(h * 128, (h + 1) * 128)
            vT[h * HEAD_DIM : (h + 1) * HEAD_DIM, at] = valsT[h * 128 : h * 128 + HEAD_DIM].astype(BF16)
            kA_ref[h, at, :] = jnp.where(lane == HEAD_DIM, bias, keys[:, span]).astype(BF16)
            qh = queries[span].astype(BF16) * BF16(HEAD_DIM**-0.5)
            qT_ref[h, :, at] = jnp.where(srow == HEAD_DIM, BF16(1), qh)
            v_ref[h, at, :] = vals[:, span].astype(BF16)

    arrival(xs_ref.at[me.z, pl.ds(0, half)], x_recv.at[me.z, 0]).wait()
    arrival(xs_ref.at[me.z, pl.ds(half, half)], x_recv.at[me.z, 1]).wait()
    project(me.z)
    relay(2)
    pl.when(is_near)(functools.partial(own_unit, me.around[1]))
    plane_forward(me.z)
    for j in blocks_in:
        arrival(xs_ref.at[j, other], x_recv.at[j, 1 - me.core]).wait()
        project(j)
    pl.when(is_near)(functools.partial(own_unit, me.around[2]))
    plane_forward(me.around[0])

    chunk = 256
    pieces = length // chunk

    def attend(i, _):
        j = lax.rem(me.z + 1 + i, tp)
        at = pl.ds(pl.multiple_of(j * rows, rows), rows)
        tops = []
        for h in range(heads):
            qt = qT_ref[h, :, at]
            top = None
            for c in range(pieces):
                s = dot(kA_ref[h, c * chunk : (c + 1) * chunk, :], qt, 1, 0)
                scores[h, c * chunk : (c + 1) * chunk, :] = s
                peak = jnp.max(s, axis=0, keepdims=True)
                top = peak if top is None else jnp.maximum(top, peak)
            tops.append(top)
        outs = []
        for h in range(heads):
            total, mixed = None, None
            for c in range(pieces):
                p = jnp.exp(scores[h, c * chunk : (c + 1) * chunk, :] - tops[h])
                part = jnp.sum(p, axis=0, keepdims=True)
                term = dot(vT[h * HEAD_DIM : (h + 1) * HEAD_DIM, c * chunk : (c + 1) * chunk], p.astype(BF16), 1, 0)
                total = part if total is None else total + part
                mixed = term if mixed is None else mixed + term
            mixed = mixed / total
            oT_ref[h * HEAD_DIM : (h + 1) * HEAD_DIM, at] = mixed
            lse_ref[h, :, at] = tops[h] + jnp.log(total)
            outs.append(mixed)
        o_buf[j] = jnp.concatenate(outs, axis=0).T.astype(BF16)
        here = jnp.logical_and(j == me.z, is_owner)

        @pl.when(here)
        def _():
            pltpu.make_async_copy(o_buf.at[j], oin_ref.at[me.group], o_recv.at[me.group]).start()

        @pl.when(jnp.logical_not(here))
        def _():
            remote(o_buf.at[j], oin_ref.at[me.group], o_send.at[i], o_recv.at[me.group], me.owner, j).start()

        for n in (1, 2):
            pl.when(jnp.logical_and(is_end, i == n - 1))(functools.partial(own_unit, me.around[n]))
        pl.when(i == 0)(functools.partial(plane_rest, me.z))
        pl.when(jnp.logical_and(is_near, i == 0))(functools.partial(plane_forward, me.around[1]))
        pl.when(jnp.logical_and(is_end, i == 2))(functools.partial(plane_forward, me.around[1]))
        pl.when(jnp.logical_and(is_near, i == 2))(functools.partial(plane_forward, me.around[2]))
        pl.when(jnp.logical_and(is_end, i == 3))(functools.partial(plane_forward, me.around[2]))
        return 0

    lax.fori_loop(0, tp, attend, 0)

    for t in me.around:
        plane_rest(t)

    arrival(wall_ref.at[me.z, me.d], mz_recv.at[me.z]).wait()
    for s in range(1, tp):
        t = lax.rem(me.z + s, tp)
        arrival(counts.at[t], cn_recv.at[t]).wait()
    total = counts[0]
    for t in range(1, tp):
        total = total + counts[t]
    count_ref[...] = total
    for g in range(4):
        arrival(oin_ref.at[g], o_recv.at[g]).wait()

    def sibling_units(n, _):
        t, k = n // chips, lax.rem(n, chips)
        arrival(wall_ref.at[t, 2 * k + 1 - me.core], ms_recv.at[t, k]).wait()
        to_sibling(t, k).wait_send()
        return 0

    lax.fori_loop(0, tp * chips, sibling_units, 0)

    def sent(n, _):
        t, i = n // (chips - 1), lax.rem(n, chips - 1)
        in_plane(wm_ref, t, me.chip, i, me.first).wait_send()
        return 0

    lax.fori_loop(0, tp * (chips - 1), sent, 0)
    each_peer(lambda i, peer: small_copy(i, peer).wait_send())
    for s in range(2):

        @pl.when(me.z // 2 + 2 * s != me.z)
        def _(s=s):
            remote(wq_ref, wqz.at[0], wz_send.at[s], wz_recv.at[0], me.sibling, me.z).wait_send()

        def step(i, _, s=s):
            k = lax.rem(me.chip + 1 + i, chips)

            @pl.when(2 * k + s != me.d)
            def _():
                wq_plane(s, k).wait_send()

            return 0

        lax.fori_loop(0, chips, step, 0)
    for s in range(tp - 1):
        remote(counts.at[0], counts.at[0], cn_send.at[s], cn_recv.at[0], me.sibling, me.z).wait_send()

    def z_sent(sem):
        along_z(wm_ref, 0, sem, 0).wait_send()

    pl.when(me.z > 0)(functools.partial(z_sent, 0))
    pl.when(me.z < tp - 1)(functools.partial(z_sent, 1))
    for t in range(tp):
        pl.when(jnp.logical_or(goes_up(t), goes_down(t)))(functools.partial(z_sent, 2 + t))

    def x_sent(sem):
        remote(x_ref.at[pl.ds(0, half)], xs_ref.at[0, pl.ds(0, half)], sem, x_recv.at[0, 0], me.sibling, me.z).wait_send()

    for h in range(2):
        x_sent(x_send.at[h])

        @pl.when(is_owner)
        def _(h=h):
            x_sent(xr_send.at[0, h])

    for n in range(3):
        x_sent(xr_send.at[1 + n, 0])

    @pl.when(is_near)
    def _():
        for n in range(2):
            x_sent(xf_send.at[n])

    def o_sent(i, _):
        j = lax.rem(me.z + 1 + i, tp)

        @pl.when(jnp.logical_not(jnp.logical_and(j == me.z, is_owner)))
        def _():
            remote(o_buf.at[0], oin_ref.at[0], o_send.at[i], o_recv.at[0], me.sibling, me.z).wait_send()

        return 0

    lax.fori_loop(0, tp, o_sent, 0)


def front(x, wq, wm, small, dp, tp):
    rows, width = x.shape
    length = rows * tp
    share = wq.shape[0]
    chips = dp // 2
    S = jax.ShapeDtypeStruct
    vmem = pl.BlockSpec(memory_space=pltpu.VMEM)
    anym = pl.BlockSpec(memory_space=pl.ANY)
    dma = pltpu.SemaphoreType.DMA
    return pl.pallas_call(
        front_kernel,
        name="front",
        out_shape=(
            S((4, rows, 192), BF16),
            S((tp, dp, share, wm.shape[1]), BF16),
            S((dp, 16, 128), F32),
            S((8, 128), F32),
            S((tp, rows, width), BF16),
            S((dp, share, wq.shape[1]), BF16),
            S((192, length), F32),
            S((3, 1, length), F32),
            S((3, 128, length), BF16),
            S((3, length, 128), BF16),
            S((3, length, 128), BF16),
        ),
        in_specs=[vmem] * 4,
        out_specs=(anym, anym) + (vmem,) * 9,
        scratch_shapes=[
            pltpu.VMEM((2, share, wq.shape[1]), BF16),
            pltpu.VMEM((tp, 8, 128), F32),
            pltpu.VMEM((192, length), BF16),
            pltpu.VMEM((3, length, rows), F32),
            pltpu.VMEM((tp, rows, 192), BF16),
            pltpu.VMEM((384, width), BF16),
            pltpu.VMEM((width, 384), BF16),
            pltpu.VMEM((width, 384), BF16),
            pltpu.VMEM((384, width), BF16),
            dma((dp - 1,)), dma((dp,)), dma((tp - 1,)), dma((tp,)),
            dma((2,)), dma((2,)), dma((2, chips)), dma((dp,)),
            dma((2,)), dma((tp, 2)), dma((4, 2)), dma((2,)),
            dma((tp + 2,)), dma((tp,)), dma((tp, chips - 1)), dma((tp, chips)), dma((tp, chips)), dma((tp, chips)),
            dma((tp,)), dma((4,)),
        ],
        compiler_params=pltpu.CompilerParams(
            collective_id=0, has_side_effects=True, vmem_limit_bytes=VMEM_LIMIT
        ),
    )(x, wq, wm, small)


SQRT_HALF = 0.7071067811865476
INV_SQRT_2PI = 0.3989422804014327


def norm_forward(values, gain, shift):
    centred = values - jnp.mean(values, axis=1, keepdims=True)
    inv = lax.rsqrt(jnp.mean(centred * centred, axis=1, keepdims=True) + norm_eps)
    normed = centred * inv
    return normed * gain + shift, normed, inv


def norm_backward(grad_out, normed, inv, gain):
    g = grad_out * gain
    plain = jnp.mean(g, axis=1, keepdims=True)
    mixed = jnp.mean(g * normed, axis=1, keepdims=True)
    return inv * (g - plain - normed * mixed)


def column_sum(values):
    return jnp.sum(values, axis=0, keepdims=True)


def mid_kernel(
    x_ref, teacher_ref, counted_ref, scale_ref, oin_ref, wall_ref, vec_ref, ib_ref,
    out_ref, dr1_ref, do_ref, grad_ref, small_ref, ismall_ref,
    up_ref, act_ref, f_ref, n1_ref, acc_ref, hT_ref, dfT_ref,
):
    groups = wall_ref.shape[0]
    width = x_ref.shape[1]
    gw = oin_ref.shape[2]
    inner = slice(0, width)
    outer = slice(width, 2 * width)
    mixer = slice(2 * width, 2 * width + gw)
    vec = lambda i: vec_ref[i : i + 1, :]

    acc_ref[...] = x_ref[...].astype(F32) + vec(2)
    for g in range(groups):
        acc_ref[...] += dot(oin_ref[g], wall_ref[g, :, mixer], 1, 1)
    hidden, normed1, inv1 = norm_forward(acc_ref[...], vec(3), vec(4))
    n1_ref[...] = normed1
    low = hidden.astype(BF16)
    hT_ref[...] = hidden.T.astype(BF16)
    f_ref[...] = hidden + vec(5)

    def ffn_forward(g, _):
        up = dot(low, wall_ref[g, :, inner], 1, 0) + ib_ref[g]
        up_ref[g] = up
        act = (up * (0.5 * (1.0 + lax.erf(up * SQRT_HALF)))).astype(BF16)
        act_ref[g] = act
        f_ref[...] += dot(act, wall_ref[g, :, outer], 1, 1)
        return 0

    lax.fori_loop(0, groups, ffn_forward, 0)
    final, normed2, inv2 = norm_forward(f_ref[...], vec(6), vec(7))
    out_ref[...] = final.astype(BF16)
    diff = final - teacher_ref[...].astype(F32)
    counted = counted_ref[...]
    small_ref[...] = jnp.zeros_like(small_ref)
    small_ref[6:7, 0:1] = jnp.sum(counted * jnp.sum(diff * diff, axis=1, keepdims=True), axis=0, keepdims=True)
    grad = (scale_ref[0, 0] * counted) * diff
    small_ref[4:5, :] = column_sum(grad * normed2)
    small_ref[5:6, :] = column_sum(grad)
    dr2 = norm_backward(grad, normed2, inv2, vec(6))
    small_ref[3:4, :] = column_sum(dr2)
    acc_ref[...] = dr2
    df = dr2.astype(BF16)
    dfT_ref[...] = dr2.T.astype(BF16)

    def ffn_backward(g, _):
        up = up_ref[g]
        slope = 0.5 * (1.0 + lax.erf(up * SQRT_HALF)) + up * (INV_SQRT_2PI * jnp.exp(-0.5 * up * up))
        du = (dot(df, wall_ref[g, :, outer], 1, 0) * slope).astype(BF16)
        ismall_ref[g] = column_sum(du.astype(F32))
        acc_ref[...] += dot(du, wall_ref[g, :, inner], 1, 1)
        grad_ref[g, :, inner] = dot(hT_ref[...], du, 1, 0).astype(BF16)
        grad_ref[g, :, outer] = dot(dfT_ref[...], act_ref[g], 1, 0).astype(BF16)
        return 0

    lax.fori_loop(0, groups, ffn_backward, 0)
    dh1 = acc_ref[...]
    normed1 = n1_ref[...]
    small_ref[1:2, :] = column_sum(dh1 * normed1)
    small_ref[2:3, :] = column_sum(dh1)
    dr1 = norm_backward(dh1, normed1, inv1, vec(3))
    small_ref[0:1, :] = column_sum(dr1)
    dr1_ref[...] = dr1
    da = dr1.astype(BF16)
    daT = dr1.T.astype(BF16)
    for g in range(groups):
        do_ref[g] = dot(da, wall_ref[g, :, mixer], 1, 0).astype(BF16)
        grad_ref[g, :, mixer] = dot(daT, oin_ref[g], 1, 0).astype(BF16)


def mid(x, teacher, counted, scale, oin, wall, vecs, ib):
    rows, width = x.shape
    groups = wall.shape[0]
    S = jax.ShapeDtypeStruct
    vmem = pl.BlockSpec(memory_space=pltpu.VMEM)
    return pl.pallas_call(
        mid_kernel,
        name="mid",
        out_shape=(
            S((rows, width), BF16),
            S((rows, width), F32),
            S(oin.shape, BF16),
            S(wall.shape, BF16),
            S((8, width), F32),
            S(ib.shape, F32),
        ),
        in_specs=[vmem, vmem, vmem, pl.BlockSpec(memory_space=pltpu.SMEM)] + [vmem] * 4,
        out_specs=(vmem,) * 6,
        scratch_shapes=[
            pltpu.VMEM((groups, rows, ib.shape[2]), F32),
            pltpu.VMEM((groups, rows, ib.shape[2]), BF16),
            pltpu.VMEM((rows, width), F32),
            pltpu.VMEM((rows, width), F32),
            pltpu.VMEM((rows, width), F32),
            pltpu.VMEM((width, rows), BF16),
            pltpu.VMEM((width, rows), BF16),
        ],
        compiler_params=pltpu.CompilerParams(vmem_limit_bytes=VMEM_LIMIT),
    )(x, teacher, counted, scale, oin, wall, vecs, ib)


def back_kernel(
    do_ref, grad_ref, xs_ref, wqf_ref, oT_ref, lse_ref, qT_ref, kA_ref, v_ref, pack_ref, dr1_ref,
    dx_ref, gsum_ref, qgrad_ref, small_ref,
    dof, doT, delta, qs, kT, dk, dv, dqT, dqkv,
    sib, own, pln, zsrc, zrecv, parts, pr, sj, rr, fin, qsend, qr, qz, qf, spack, srecv, zpack,
    do_send, do_recv, sb_send, sb_recv, own_sem, pl_send, pl_recv, zz_send, zz_recv,
    pr_send, pr_recv, rr_send, rr_recv, fin_send, fin_recv, qr_send, qr_recv, qf_send, qf_recv,
    sm_send, sm_recv, sz_send, sz_recv,
):
    me = Place()
    dp, tp, chips = me.dp, me.tp, me.chips
    rows, width = dx_ref.shape
    half = rows // 2
    length = rows * tp
    heads = 3
    gw = heads * HEAD_DIM
    share = width // dp
    greet(me)

    for g in range(4):
        t = 2 * me.core + g // 2
        d = me.base + g % 2
        here = jnp.logical_and(t == me.z, g % 2 == me.core)

        @pl.when(here)
        def _(g=g):
            pltpu.make_async_copy(do_ref.at[g], dof.at[me.z], do_recv.at[me.z]).start()

        @pl.when(jnp.logical_not(here))
        def _(g=g, t=t, d=d):
            remote(do_ref.at[g], dof.at[me.z], do_send.at[g], do_recv.at[me.z], d, t).start()

    def sib_copy(t):
        return remote(grad_ref.at[t, :, 1 - me.core], sib.at[t], sb_send.at[t], sb_recv.at[t], me.sibling, me.z)

    for t in range(tp):
        sib_copy(t).start()
        pltpu.make_async_copy(grad_ref.at[t, :, me.core], own.at[t], own_sem.at[t]).start()

    def pair_sum(t, _):
        arrival(own.at[t], own_sem.at[t]).wait()
        arrival(sib.at[t], sb_recv.at[t]).wait()

        def unit(k, _):
            own[t, k] = (own[t, k].astype(F32) + sib[t, k].astype(F32)).astype(BF16)
            return 0

        lax.fori_loop(0, chips, unit, 0)
        return 0

    lax.fori_loop(0, tp, pair_sum, 0)

    def plane_copy(i, t):
        k = lax.rem(me.chip + 1 + i, chips)
        return remote(own.at[t, k], pln.at[t, i], pl_send.at[t, i], pl_recv.at[t, i], 2 * k + me.core, me.z)

    def plane_start(n, _):
        plane_copy(n // tp, lax.rem(n, tp)).start()
        return 0

    lax.fori_loop(0, (chips - 1) * tp, plane_start, 0)

    def prepare(i, _):
        j = lax.rem(me.z + i, tp)
        at = pl.ds(pl.multiple_of(j * rows, rows), rows)
        arrival(dof.at[j], do_recv.at[j]).wait()
        flipped = dof[j].astype(F32).T
        doT[:, at] = flipped.astype(BF16)
        for h in range(heads):
            span = slice(h * HEAD_DIM, (h + 1) * HEAD_DIM)
            delta[h, :, at] = jnp.sum(flipped[span] * oT_ref[span, at], axis=0, keepdims=True)
            qs[h, at, :] = qT_ref[h, :, at].astype(F32).T.astype(BF16)
            kT[h, :, at] = kA_ref[h, at, :].astype(F32).T[0:HEAD_DIM, :].astype(BF16)
        return 0

    lax.fori_loop(0, tp, prepare, 0)
    chunk = 256
    for h in range(heads):
        dk[...] = jnp.zeros_like(dk)
        dv[...] = jnp.zeros_like(dv)

        def attend(j, _, h=h):
            at = pl.ds(pl.multiple_of(j * rows, rows), rows)
            span = slice(h * HEAD_DIM, (h + 1) * HEAD_DIM)
            qt, gt = qT_ref[h, :, at], doT[span, at]
            q, go = qs[h, at, :], dof[j, :, span]
            lse, dl = lse_ref[h, :, at], delta[h, :, at]
            dq = None
            for c in range(length // chunk):
                r = slice(c * chunk, (c + 1) * chunk)
                p = jnp.exp(dot(kA_ref[h, r, :], qt, 1, 0) - lse)
                dp_ = dot(v_ref[h, r, 0:HEAD_DIM], gt, 1, 0)
                ds = (p * (dp_ - dl)).astype(BF16)
                dv[r, :] += dot(p.astype(BF16), go, 1, 0)
                dk[r, :] += dot(ds, q, 1, 0)
                term = dot(kT[h, :, r], ds, 1, 0)
                dq = term if dq is None else dq + term
            dqT[span, at] = dq * HEAD_DIM**-0.5
            return 0

        lax.fori_loop(0, tp, attend, 0)
        for j in range(tp):
            at = slice(j * rows, (j + 1) * rows)
            dqkv[j, :, gw + h * HEAD_DIM : gw + (h + 1) * HEAD_DIM] = dk[at, 0:HEAD_DIM].astype(BF16)
            dqkv[j, :, 2 * gw + h * HEAD_DIM : 2 * gw + (h + 1) * HEAD_DIM] = dv[at, :].astype(BF16)

    weights = wqf_ref[...].reshape(width, 3 * gw)
    ones = jnp.ones((8, rows), BF16)
    mine = pl.ds(pl.multiple_of(me.core * half, half), half)
    other = pl.ds(pl.multiple_of((1 - me.core) * half, half), half)
    far = 2 * (1 - me.pair)

    def block_at(i):
        return jnp.where(i < 2, far + i, jnp.where(i == 2, me.buddy, me.z))

    def pr_copy(j):
        return remote(parts.at[j, other], pr.at[j], pr_send.at[j], pr_recv.at[j], me.sibling, me.z)

    def token_grads(i, sums):
        j = block_at(i)
        at = pl.ds(pl.multiple_of(j * rows, rows), rows)
        dqkv[j, :, 0:gw] = dqT[:, at].T.astype(BF16)
        flat = dqkv[j]
        parts[j] = dot(flat, weights, 1, 1).astype(BF16)
        pr_copy(j).start()
        return sums + dot(ones, flat, 1, 0)

    sums = lax.fori_loop(0, tp, token_grads, jnp.zeros((8, 3 * gw), F32))

    spack[...] = pack_ref[...]
    blocks = gw // share
    for b in range(blocks):
        spack[me.group * blocks + b, 0:1, 0:share] = sums[0:1, b * share : (b + 1) * share]
        spack[me.group * blocks + b, 1:2, 0:share] = sums[0:1, 2 * gw + b * share : 2 * gw + (b + 1) * share]

    def small_copy(i):
        peer = lax.rem(me.d + 1 + i, dp)
        return remote(spack.at[peer], srecv.at[i], sm_send.at[i], sm_recv.at[i], peer, me.z)

    def small_start(i, _):
        small_copy(i).start()
        return 0

    lax.fori_loop(0, dp - 1, small_start, 0)

    def rr_copy(j):
        return remote(sj.at[j], rr.at[j], rr_send.at[j], rr_recv.at[j], me.d, me.buddy)

    def collects(j):
        return jnp.where(j // 2 == me.pair, j, me.near_here) == me.z

    def chip_sum(i, _):
        j = block_at(i)
        arrival(pr.at[j], pr_recv.at[j]).wait()
        sj[j] = (parts[j, mine, :].astype(F32) + pr[j].astype(F32)).astype(BF16)

        @pl.when(jnp.logical_not(collects(j)))
        def _():
            rr_copy(j).start()

        return 0

    lax.fori_loop(0, tp, chip_sum, 0)

    def fin_copy(j):
        return remote(pr.at[j], fin.at[me.core], fin_send.at[j], fin_recv.at[me.core], me.owner, j)

    def lands_here(j):
        return jnp.logical_and(me.core == me.pair, j == me.z)

    total = None
    for j in range(tp):
        term = dot(xs_ref[j], dqkv[j], 0, 0)
        total = term if total is None else total + term
    qsend[...] = total.astype(BF16).reshape(dp, share, 3 * gw)

    def q_copy(peer, i):
        return remote(qsend.at[peer], qr.at[me.core, me.chip], qr_send.at[i], qr_recv.at[me.core, me.chip], peer, me.z)

    def q_start(i, _):
        peer = lax.rem(me.d + i, dp)

        @pl.when(i == 0)
        def _():
            pltpu.make_async_copy(qsend.at[peer], qr.at[me.core, me.chip], qr_recv.at[me.core, me.chip]).start()

        @pl.when(i > 0)
        def _():
            q_copy(peer, i).start()

        return 0

    lax.fori_loop(0, dp, q_start, 0)

    def pair_total(i, _):
        j = block_at(i)

        @pl.when(collects(j))
        def _():
            arrival(rr.at[j], rr_recv.at[j]).wait()
            pr[j] = (sj[j].astype(F32) + rr[j].astype(F32)).astype(BF16)

            @pl.when(lands_here(j))
            def _():
                pltpu.make_async_copy(pr.at[j], fin.at[me.core], fin_recv.at[me.core]).start()

            @pl.when(jnp.logical_not(lands_here(j)))
            def _():
                fin_copy(j).start()

        return 0

    lax.fori_loop(0, tp, pair_total, 0)

    def plane_total(t, _):
        total = own[t, me.chip].astype(F32)
        for i in range(chips - 1):
            arrival(pln.at[t, i], pl_recv.at[t, i]).wait()
            total = total + pln[t, i].astype(F32)
        zsrc[t] = total.astype(BF16)
        return 0

    lax.fori_loop(0, tp, plane_total, 0)

    def z_copy(s):
        t = lax.rem(me.z + s, tp)
        return remote(zsrc.at[t], zrecv.at[s - 1], zz_send.at[s - 1], zz_recv.at[s - 1], me.d, t)

    for s in range(1, tp):
        z_copy(s).start()

    def q_pair(s):
        return me.z // 2, 2 * me.low + s

    for s in range(2):
        total = None
        for k in range(chips):
            arrival(qr.at[s, k], qr_recv.at[s, k]).wait()
            term = qr[s, k].astype(F32)
            total = term if total is None else total + term
        qz[s] = total.astype(BF16)
        p, t = q_pair(s)

        @pl.when(t == me.z)
        def _(s=s, p=p):
            pltpu.make_async_copy(qz.at[s], qf.at[p], qf_recv.at[p]).start()

        @pl.when(t != me.z)
        def _(s=s, p=p, t=t):
            remote(qz.at[s], qf.at[p], qf_send.at[s], qf_recv.at[p], me.d, t).start()

    total = spack[me.d]
    for i in range(dp - 1):
        arrival(srecv.at[i], sm_recv.at[i]).wait()
        total = total + srecv[i]
    zpack[me.z] = total

    def sz_copy(s):
        return remote(zpack.at[me.z], zpack.at[me.z], sz_send.at[s - 1], sz_recv.at[me.z], me.d, lax.rem(me.z + s, tp))

    for s in range(1, tp):
        sz_copy(s).start()

    for h in range(2):
        arrival(fin.at[h], fin_recv.at[h]).wait()
        at = slice(h * half, (h + 1) * half)
        dx_ref[at, :] = dr1_ref[at, :] + fin[h].astype(F32)
    for p in range(2):
        arrival(qf.at[p], qf_recv.at[p]).wait()
    qgrad_ref[...] = qf[0].astype(F32) + qf[1].astype(F32)
    for s in range(1, tp):
        t = lax.rem(me.z + s, tp)
        arrival(zpack.at[t], sz_recv.at[t]).wait()
    total = zpack[0]
    for t in range(1, tp):
        total = total + zpack[t]
    small_ref[...] = total
    total = zsrc[me.z].astype(F32)
    for s in range(tp - 1):
        arrival(zrecv.at[s], zz_recv.at[s]).wait()
        total = total + zrecv[s].astype(F32)
    gsum_ref[...] = total

    for g in range(4):

        @pl.when(jnp.logical_not(jnp.logical_and(2 * me.core + g // 2 == me.z, g % 2 == me.core)))
        def _(g=g):
            remote(do_ref.at[g], dof.at[0], do_send.at[g], do_recv.at[0], me.sibling, me.z).wait_send()

    for t in range(tp):
        sib_copy(t).wait_send()
        pr_copy(t).wait_send()

        @pl.when(jnp.logical_not(collects(t)))
        def _(t=t):
            rr_copy(t).wait_send()

        @pl.when(jnp.logical_and(collects(t), jnp.logical_not(lands_here(t))))
        def _(t=t):
            fin_copy(t).wait_send()

    def plane_sent(n, _):
        plane_copy(n // tp, lax.rem(n, tp)).wait_send()
        return 0

    lax.fori_loop(0, (chips - 1) * tp, plane_sent, 0)

    def peers_sent(i, _):
        small_copy(i).wait_send()
        q_copy(lax.rem(me.d + 1 + i, dp), i + 1).wait_send()
        return 0

    lax.fori_loop(0, dp - 1, peers_sent, 0)
    for s in range(1, tp):
        z_copy(s).wait_send()
        sz_copy(s).wait_send()
    for s in range(2):
        p, t = q_pair(s)

        @pl.when(t != me.z)
        def _(s=s, p=p, t=t):
            remote(qz.at[s], qf.at[p], qf_send.at[s], qf_recv.at[p], me.d, t).wait_send()


def back(do, grad, xs, wqf, oT, lse, qT, kA, v, pack, dr1):
    tp, rows, width = xs.shape
    dp, share, qwidth = wqf.shape
    chips = dp // 2
    length = rows * tp
    half = rows // 2
    cols = grad.shape[-1]
    S = jax.ShapeDtypeStruct
    vmem = pl.BlockSpec(memory_space=pltpu.VMEM)
    anym = pl.BlockSpec(memory_space=pl.ANY)
    dma = pltpu.SemaphoreType.DMA
    V = pltpu.VMEM
    return pl.pallas_call(
        back_kernel,
        name="back",
        out_shape=(
            S((rows, width), F32),
            S((share, cols), F32),
            S((share, qwidth), F32),
            S((16, 128), F32),
        ),
        in_specs=[anym, anym] + [vmem] * 9,
        out_specs=(vmem,) * 4,
        scratch_shapes=[
            V((tp, rows, 192), BF16), V((192, length), BF16), V((3, 1, length), F32),
            V((3, length, 128), BF16), V((3, HEAD_DIM, length), BF16),
            V((length, 128), F32), V((length, HEAD_DIM), F32), V((192, length), F32), V((tp, rows, qwidth), BF16),
            V((tp, chips, share, cols), BF16), V((tp, chips, share, cols), BF16), V((tp, chips - 1, share, cols), BF16),
            V((tp, share, cols), BF16), V((tp - 1, share, cols), BF16),
            V((tp, rows, width), BF16), V((tp, half, width), BF16), V((tp, half, width), BF16), V((tp, half, width), BF16),
            V((2, half, width), BF16),
            V((dp, share, qwidth), BF16), V((2, chips, share, qwidth), BF16), V((2, share, qwidth), BF16), V((2, share, qwidth), BF16),
            V((dp, 16, 128), F32), V((dp - 1, 16, 128), F32), V((tp, 16, 128), F32),
            dma((4,)), dma((tp,)), dma((tp,)), dma((tp,)), dma((tp,)), dma((tp, chips - 1)), dma((tp, chips - 1)), dma((tp - 1,)), dma((tp - 1,)),
            dma((tp,)), dma((tp,)), dma((tp,)), dma((tp,)), dma((tp,)), dma((2,)), dma((dp,)), dma((2, chips)), dma((2,)), dma((2,)),
            dma((dp - 1,)), dma((dp - 1,)), dma((tp - 1,)), dma((tp,)),
        ],
        compiler_params=pltpu.CompilerParams(
            collective_id=1, has_side_effects=True, vmem_limit_bytes=VMEM_LIMIT
        ),
    )(do, grad, xs, wqf, oT, lse, qT, kA, v, pack, dr1)


def shards(
    tokens, teacher, lengths, loss_mask, loss_scale,
    query_weight, query_bias, key_weight, value_weight, value_bias, mixer_weight, mixer_bias,
    first_gain, first_shift, inner_weight, inner_bias, outer_weight, outer_bias, second_gain, second_shift,
):
    dp, tp = lax.axis_size("dp"), lax.axis_size("tensor")
    if dp != 8 or tp != 4:
        return plain_shards(
            tokens, teacher, lengths, loss_mask, loss_scale,
            query_weight, query_bias, key_weight, value_weight, value_bias, mixer_weight, mixer_bias,
            first_gain, first_shift, inner_weight, inner_bias, outer_weight, outer_bias, second_gain, second_shift,
        )
    z = lax.axis_index("tensor")
    rows, width = tokens.shape
    share = query_weight.shape[0]
    gw = query_weight.shape[1]
    hidden = inner_weight.shape[1]
    hshare = inner_bias.shape[0]
    hrows = -(-hshare // 128)
    pos = z * rows + jnp.arange(rows)
    counted = jnp.logical_and(pos < lengths[0], loss_mask == 1).astype(F32)
    vectors = jnp.stack(
        [query_bias, value_bias, mixer_bias, first_gain, first_shift, outer_bias, second_gain, second_shift]
    ).astype(F32)
    small = jnp.concatenate(
        [
            jnp.pad(vectors, ((0, 0), (0, 128 - share))),
            jnp.full((1, 128), jnp.sum(counted)),
            jnp.pad(inner_bias.astype(F32), (0, hrows * 128 - hshare)).reshape(hrows, 128),
            jnp.zeros((3 - hrows, 128), F32),
            jnp.full((1, 128), lengths[0].astype(F32)),
            jnp.zeros((3, 128), F32),
        ],
        axis=0,
    )
    wq = jnp.concatenate([query_weight, key_weight, value_weight], axis=1)
    wm = jnp.concatenate([inner_weight, outer_weight.T, mixer_weight.T], axis=1)
    oin, wall, smalls, count, xs, wqf, oT, lse, qT, kA, v = front(tokens, wq, wm, small, dp, tp)
    token_total = count[0, 0]
    vecs = jnp.moveaxis(smalls[:, 0:8, 0:share], 0, 1).reshape(8, width)
    ib = smalls[:, 9 : 9 + hrows, :].reshape(dp, hrows * 128)[:, :hshare].reshape(tp, 1, hidden)
    scale = (2.0 * loss_scale / (token_total * width)).reshape(1, 1)
    wall = wall.reshape(tp, width, wm.shape[1])
    layer_output, dr1, do, grad, sums, isums = mid(tokens, teacher, counted[:, None], scale, oin, wall, vecs, ib)
    pack = jnp.concatenate(
        [
            jnp.zeros((dp, 2, 128), F32),
            jnp.pad(jnp.moveaxis(sums[0:6].reshape(6, dp, share), 1, 0), ((0, 0), (0, 0), (0, 128 - share))),
            jnp.broadcast_to(sums[6, 0], (dp, 1, 128)),
            jnp.pad(isums.reshape(dp, hshare), ((0, 0), (0, hrows * 128 - hshare))).reshape(dp, hrows, 128),
            jnp.zeros((dp, 7 - hrows, 128), F32),
        ],
        axis=1,
    )
    grad = grad.reshape(tp, dp // 2, 2, share, wm.shape[1])
    input_grad, gsum, qgrad, ssum = back(do, grad, xs, wqf, oT, lse, qT, kA, v, pack, dr1)
    loss_value = ssum[8, 0] / (token_total * width)
    line = lambda i: ssum[i, :share]
    innerbias_grad = ssum[9 : 9 + hrows].reshape(-1)[:hshare]
    return (
        layer_output,
        loss_value,
        input_grad,
        qgrad[:, 0:gw],
        line(0),
        qgrad[:, gw : 2 * gw],
        qgrad[:, 2 * gw :],
        line(1),
        gsum[:, 2 * hidden :].T,
        line(2),
        line(3),
        line(4),
        gsum[:, 0:hidden],
        innerbias_grad,
        gsum[:, hidden : 2 * hidden].T,
        line(5),
        line(6),
        line(7),
    )


def in_blocks(value, dim, size):
    before, after = (value.shape[:dim], value.shape[dim + 1 :])
    return jnp.moveaxis(value.reshape(*before, size, -1, *after), dim, 0)


def summed_on_arrival(value, axis, dim):
    size = lax.axis_size(axis)
    blocks = lax.all_to_all(in_blocks(value, dim, size), axis, 0, 0, tiled=True)
    return jnp.sum(blocks.astype(jnp.float32), axis=0)


def sent_together(arrays, axis, dim, along):
    both = jnp.concatenate(arrays, axis=along)
    out, at, gathered = (summed_on_arrival(both, axis, dim), 0, [])
    for a in arrays:
        gathered.append(lax.slice_in_dim(out, at, at + a.shape[along], axis=along))
        at += a.shape[along]
    return tuple(gathered)


def contract_last(left_rows, right_rows):
    return lax.dot_general(
        left_rows, right_rows, (((1,), (1,)), ((), ())), preferred_element_type=jnp.float32
    )


def contract_first(left_rows, right_rows):
    return lax.dot_general(
        left_rows, right_rows, (((0,), (0,)), ((), ())), preferred_element_type=jnp.float32
    )


def plain_dot(left_rows, right_rows):
    return jnp.dot(left_rows, right_rows, preferred_element_type=jnp.float32)


def gelu_exact(pre_values):
    return jax.nn.gelu(pre_values, approximate=False)


def plain_norm_forward(values_in, gain_vec, shift_vec):
    centred = values_in - jnp.mean(values_in, axis=1, keepdims=True)
    inv_std = lax.rsqrt(jnp.mean(centred * centred, axis=1, keepdims=True) + norm_eps)
    normed = centred * inv_std
    return (normed * gain_vec + shift_vec, normed, inv_std)


def plain_norm_backward(grad_out, normed, inv_std, gain_vec):
    grad_normed = grad_out * gain_vec
    mean_plain = jnp.mean(grad_normed, axis=1, keepdims=True)
    mean_mixed = jnp.mean(grad_normed * normed, axis=1, keepdims=True)
    grad_in = inv_std * (grad_normed - mean_plain - normed * mean_mixed)
    return (grad_in, jnp.sum(grad_out * normed, axis=0), jnp.sum(grad_out, axis=0))


def plain_shards(
    tokens,
    teacher,
    lengths,
    loss_mask,
    loss_scale,
    query_weight,
    query_bias,
    key_weight,
    value_weight,
    value_bias,
    mixer_weight,
    mixer_bias,
    first_gain,
    first_shift,
    inner_weight,
    inner_bias,
    outer_weight,
    outer_bias,
    second_gain,
    second_shift,
):
    tp_count = lax.axis_size("tensor")
    tp_index = lax.axis_index("tensor")
    dp_count = lax.axis_size("dp")
    dp_index = lax.axis_index("dp")
    local_rows = tokens.shape[0]
    seq_len = local_rows * tp_count
    model_width = tokens.shape[1]
    head_width = query_weight.shape[1]
    hidden_width = inner_weight.shape[1]
    head_count = head_width // HEAD_DIM
    block_count = seq_len // QBLOCK
    score_scale = HEAD_DIM ** (-0.5)
    length_here = lengths[0]
    local_pos = tp_index * local_rows + jnp.arange(local_rows)
    counted = jnp.logical_and(local_pos < length_here, loss_mask == 1).astype(jnp.float32)
    count_local = jnp.sum(counted)
    small_stack = jnp.stack(
        [
            query_bias,
            value_bias,
            mixer_bias,
            first_gain,
            first_shift,
            outer_bias,
            second_gain,
            second_shift,
        ]
    )

    def fetch_params():
        return (
            lax.all_gather(query_weight, "dp", axis=0, tiled=True),
            lax.all_gather(key_weight, "dp", axis=0, tiled=True),
            lax.all_gather(value_weight, "dp", axis=0, tiled=True),
            lax.all_gather(mixer_weight, "dp", axis=1, tiled=True),
            lax.all_gather(inner_weight, "dp", axis=0, tiled=True),
            lax.all_gather(outer_weight, "dp", axis=1, tiled=True),
            lax.all_gather(small_stack, "dp", axis=1, tiled=True),
            lax.all_gather(inner_bias, "dp", axis=0, tiled=True),
        )

    def attn_gather(values_in):
        return lax.all_gather(values_in, "tensor", axis=0, tiled=True)

    def ffn_gather(values_in):
        return lax.all_gather(values_in, "tensor", axis=0, tiled=True)

    (
        query_full,
        key_full,
        value_full,
        mixer_full,
        inner_full,
        outer_full,
        small_full,
        innerb_full,
    ) = fetch_params()
    small_wide = small_full.astype(jnp.float32)
    qbias_mine = lax.dynamic_slice_in_dim(small_wide[0], tp_index * head_width, head_width)
    vbias_mine = lax.dynamic_slice_in_dim(small_wide[1], tp_index * head_width, head_width)
    inner_mine = lax.dynamic_slice_in_dim(
        innerb_full.astype(jnp.float32), tp_index * hidden_width, hidden_width
    )
    seq_rows = attn_gather(tokens)
    queries = (plain_dot(seq_rows, query_full) + qbias_mine).astype(jnp.bfloat16)
    keys_all = plain_dot(seq_rows, key_full).astype(jnp.bfloat16)
    values_all = (plain_dot(seq_rows, value_full) + vbias_mine).astype(jnp.bfloat16)
    keys_three = keys_all.reshape(seq_len, head_count, HEAD_DIM)
    values_three = values_all.reshape(seq_len, head_count, HEAD_DIM)
    key_valid = jnp.arange(seq_len) < length_here

    def score_block(query_block):
        scores = (
            jnp.einsum("qhd,khd->hqk", query_block, keys_three, preferred_element_type=jnp.float32)
            * score_scale
        )
        return jnp.where(key_valid[None, None, :], scores, masked_score)

    def forward_block(query_block):
        scores = score_block(query_block)
        row_top = jnp.max(scores, axis=2, keepdims=True)
        exp_scores = jnp.exp(scores - row_top)
        row_total = jnp.sum(exp_scores, axis=2, keepdims=True)
        prob_low = (exp_scores / row_total).astype(jnp.bfloat16)
        mixed_rows = jnp.einsum(
            "hqk,khd->qhd", prob_low, values_three, preferred_element_type=jnp.float32
        )
        return (mixed_rows.astype(jnp.bfloat16), (row_top + jnp.log(row_total))[:, :, 0])

    query_blocks = queries.reshape(block_count, QBLOCK, head_count, HEAD_DIM)
    attended, log_sums = lax.map(forward_block, query_blocks)
    attended = attended.reshape(seq_len, head_width)
    attn_out = lax.psum_scatter(
        plain_dot(attended, mixer_full).astype(jnp.bfloat16),
        "tensor",
        scatter_dimension=0,
        tiled=True,
    ).astype(jnp.float32)
    first_sum = tokens.astype(jnp.float32) + attn_out + small_wide[2]
    hidden_one, normed_one, inv_one = plain_norm_forward(first_sum, small_wide[3], small_wide[4])
    hidden_low = hidden_one.astype(jnp.bfloat16)
    ffn_rows = ffn_gather(hidden_low)
    pre_act = plain_dot(ffn_rows, inner_full) + inner_mine
    act_full, gelu_pull = jax.vjp(gelu_exact, pre_act)
    activated = act_full.astype(jnp.bfloat16)
    ffn_out = lax.psum_scatter(
        plain_dot(activated, outer_full).astype(jnp.bfloat16),
        "tensor",
        scatter_dimension=0,
        tiled=True,
    ).astype(jnp.float32)
    second_sum = hidden_one + ffn_out + small_wide[5]
    final_rows, normed_two, inv_two = plain_norm_forward(second_sum, small_wide[6], small_wide[7])
    layer_output = final_rows.astype(jnp.bfloat16)
    diff_rows = final_rows - teacher.astype(jnp.float32)
    loss_local = jnp.sum(counted * jnp.sum(diff_rows * diff_rows, axis=1))
    loss_total, token_total = lax.psum((loss_local, count_local), ("dp", "tensor"))
    grad_scale = 2.0 * loss_scale / (token_total * model_width)
    grad_final = grad_scale * counted[:, None] * diff_rows
    (
        query_full,
        key_full,
        value_full,
        mixer_full,
        inner_full,
        outer_full,
        small_full,
        innerb_full,
    ) = fetch_params()
    ffn_rows = ffn_gather(hidden_low)
    grad_second, secondgain_part, secondshift_part = plain_norm_backward(
        grad_final, normed_two, inv_two, small_wide[6]
    )
    outerbias_part = jnp.sum(grad_second, axis=0)
    grad_ffn_rows = lax.all_gather(grad_second.astype(jnp.bfloat16), "tensor", axis=0, tiled=True)
    grad_act = contract_last(grad_ffn_rows, outer_full)
    outer_local = contract_first(activated, grad_ffn_rows)
    grad_pre = gelu_pull(grad_act)[0].astype(jnp.bfloat16)
    innerbias_part = jnp.sum(grad_pre, axis=0, dtype=jnp.float32)
    inner_local = contract_first(ffn_rows, grad_pre)
    grad_hidden = lax.psum_scatter(
        contract_last(grad_pre, inner_full).astype(jnp.bfloat16),
        "tensor",
        scatter_dimension=0,
        tiled=True,
    ).astype(jnp.float32)
    inner_grad, outer_grad = (
        lax.psum_scatter(inner_local, "dp", scatter_dimension=0, tiled=True),
        lax.psum_scatter(outer_local, "dp", scatter_dimension=1, tiled=True),
    )
    grad_first, firstgain_part, firstshift_part = plain_norm_backward(
        grad_second + grad_hidden, normed_one, inv_one, small_wide[3]
    )
    mixerbias_part = jnp.sum(grad_first, axis=0)
    grad_attn_rows = lax.all_gather(grad_first.astype(jnp.bfloat16), "tensor", axis=0, tiled=True)
    grad_attended = contract_last(grad_attn_rows, mixer_full).astype(jnp.bfloat16)
    mixer_local = contract_first(attended, grad_attn_rows)
    grad_blocks = grad_attended.reshape(block_count, QBLOCK, head_count, HEAD_DIM)

    def backward_block(carried, block_in):
        key_acc, value_acc = carried
        query_block, grad_block, lse_block = block_in
        scores = score_block(query_block)
        prob_full = jnp.exp(scores - lse_block[:, :, None])
        prob_low = prob_full.astype(jnp.bfloat16)
        grad_prob = jnp.einsum(
            "qhd,khd->hqk", grad_block, values_three, preferred_element_type=jnp.float32
        )
        row_dot = jnp.sum(prob_full * grad_prob, axis=2, keepdims=True)
        grad_scores = (prob_full * (grad_prob - row_dot)).astype(jnp.bfloat16)
        grad_query = (
            jnp.einsum("hqk,khd->qhd", grad_scores, keys_three, preferred_element_type=jnp.float32)
            * score_scale
        ).astype(jnp.bfloat16)
        key_acc = (
            key_acc
            + jnp.einsum(
                "hqk,qhd->khd", grad_scores, query_block, preferred_element_type=jnp.float32
            )
            * score_scale
        )
        value_acc = value_acc + jnp.einsum(
            "hqk,qhd->khd", prob_low, grad_block, preferred_element_type=jnp.float32
        )
        return ((key_acc, value_acc), grad_query)

    zero_acc = jnp.zeros((seq_len, head_count, HEAD_DIM), jnp.float32)
    (key_acc, value_acc), grad_queries = lax.scan(
        backward_block, (zero_acc, zero_acc), (query_blocks, grad_blocks, log_sums)
    )
    grad_queries = grad_queries.reshape(seq_len, head_width)
    grad_keys = key_acc.reshape(seq_len, head_width).astype(jnp.bfloat16)
    grad_values = value_acc.reshape(seq_len, head_width).astype(jnp.bfloat16)
    seq_rows = attn_gather(tokens)
    query_local = contract_first(seq_rows, grad_queries)
    key_local = contract_first(seq_rows, grad_keys)
    value_local = contract_first(seq_rows, grad_values)
    querybias_part = jnp.sum(grad_queries, axis=0, dtype=jnp.float32)
    valuebias_part = jnp.sum(grad_values, axis=0, dtype=jnp.float32)
    total_term = contract_last(grad_queries, query_full)
    total_term = total_term + contract_last(grad_keys, key_full)
    grad_tokens = lax.psum_scatter(
        (total_term + contract_last(grad_values, value_full)).astype(jnp.bfloat16),
        "tensor",
        scatter_dimension=0,
        tiled=True,
    ).astype(jnp.float32)
    input_grad = grad_first + grad_tokens
    query_grad, key_grad, value_grad, mixer_grad = (
        *sent_together(
            (
                query_local.astype(jnp.bfloat16),
                key_local.astype(jnp.bfloat16),
                value_local.astype(jnp.bfloat16),
            ),
            "dp",
            0,
            1,
        ),
        summed_on_arrival(mixer_local.astype(jnp.bfloat16), "dp", 1),
    )

    def spread_part(part_vec, full_width):
        return lax.dynamic_update_slice_in_dim(
            jnp.zeros((full_width,), jnp.float32), part_vec, tp_index * part_vec.shape[0], 0
        )

    small_terms = jnp.stack(
        [
            spread_part(querybias_part, model_width),
            spread_part(valuebias_part, model_width),
            mixerbias_part,
            firstgain_part,
            firstshift_part,
            outerbias_part,
            secondgain_part,
            secondshift_part,
        ]
    )
    inner_terms = spread_part(innerbias_part, hidden_width * tp_count)
    small_sum, inner_sum = lax.psum((small_terms, inner_terms), ("dp", "tensor"))
    loss_value = loss_total / (token_total * model_width)
    width_share = model_width // dp_count
    small_mine = lax.dynamic_slice_in_dim(small_sum, dp_index * width_share, width_share, 1)
    hidden_share = inner_sum.shape[0] // dp_count
    innerbias_grad = lax.dynamic_slice_in_dim(inner_sum, dp_index * hidden_share, hidden_share, 0)
    return (
        layer_output,
        loss_value,
        input_grad,
        query_grad,
        small_mine[0],
        key_grad,
        value_grad,
        small_mine[1],
        mixer_grad,
        small_mine[2],
        small_mine[3],
        small_mine[4],
        inner_grad,
        innerbias_grad,
        outer_grad,
        small_mine[5],
        small_mine[6],
        small_mine[7],
    )


def solution(mesh):
    return jax.shard_map(
        shards,
        mesh=mesh,
        in_specs=(
            P(("dp", "tensor"), None),
            P(("dp", "tensor"), None),
            P("dp"),
            P(("dp", "tensor")),
            P(),
            P("dp", "tensor"),
            P("dp"),
            P("dp", "tensor"),
            P("dp", "tensor"),
            P("dp"),
            P("tensor", "dp"),
            P("dp"),
            P("dp"),
            P("dp"),
            P("dp", "tensor"),
            P("dp"),
            P("tensor", "dp"),
            P("dp"),
            P("dp"),
            P("dp"),
        ),
        out_specs=(
            P(("dp", "tensor"), None),
            P(),
            P(("dp", "tensor"), None),
            P("dp", "tensor"),
            P("dp"),
            P("dp", "tensor"),
            P("dp", "tensor"),
            P("dp"),
            P("tensor", "dp"),
            P("dp"),
            P("dp"),
            P("dp"),
            P("dp", "tensor"),
            P("dp"),
            P("tensor", "dp"),
            P("dp"),
            P("dp"),
            P("dp"),
        ),
        check_vma=False,
    )
```

```python
import functools
import jax
import jax.numpy as jnp
from jax import lax
from jax.experimental import pallas as pl
from jax.experimental.pallas import tpu as pltpu
from jax.sharding import PartitionSpec as P

HEAD_DIM = 64
QBLOCK = 512
MESH = pl.DeviceIdType.MESH
F32 = jnp.float32
BF16 = jnp.bfloat16
norm_eps = 1e-05
masked_score = -1e30
VMEM_LIMIT = 60 * 1024 * 1024


def dot(left, right, left_dim, right_dim):
    return lax.dot_general(
        left, right, (((left_dim,), (right_dim,)), ((), ())), preferred_element_type=F32
    )


def remote(src, dst, send, recv, d, t):
    return pltpu.make_async_remote_copy(
        src_ref=src,
        dst_ref=dst,
        send_sem=send,
        recv_sem=recv,
        device_id={"dp": d, "tensor": t},
        device_id_type=MESH,
    )


def arrival(dst, recv):
    return pltpu.make_async_copy(dst, dst, recv)


class Place:
    def __init__(self):
        self.dp = lax.axis_size("dp")
        self.tp = lax.axis_size("tensor")
        self.d = lax.axis_index("dp")
        self.z = lax.axis_index("tensor")
        self.core = lax.rem(self.d, 2)
        self.chip = self.d // 2
        self.chips = self.dp // 2
        self.base = self.chip * 2
        self.sibling = self.base + 1 - self.core
        self.pair = self.z // 2
        self.low = lax.rem(self.z, 2)
        self.group = 2 * self.low + self.core
        self.buddy = 2 * self.pair + 1 - self.low
        self.owner = self.base + self.pair
        self.near_here = 1 + self.pair
        self.near_there = 2 - self.pair
        side = self.chip + 1 - 2 * lax.rem(self.chip, 2)
        across = lax.rem(self.chip + 2, 4)
        self.first = jnp.where(self.core == 0, side, across)
        self.second = jnp.where(self.core == 0, across, side)
        self.diagonal = 3 - self.chip
        self.around = (self.buddy, self.near_there, 3 * (1 - self.pair))


def greet(place):
    barrier = pltpu.get_barrier_semaphore()
    count = 0
    for t in range(place.tp):
        for c in range(2):
            other = jnp.logical_not(jnp.logical_and(place.z == t, place.core == c))

            @pl.when(other)
            def _(t=t, c=c):
                pl.semaphore_signal(
                    barrier, inc=1, device_id={"dp": place.base + c, "tensor": t}, device_id_type=MESH
                )

            count += 1
    count -= 1

    def plane(i, _):
        chip = lax.rem(place.chip + 1 + i, place.chips)
        for c in range(2):
            pl.semaphore_signal(
                barrier, inc=1, device_id={"dp": chip * 2 + c, "tensor": place.z}, device_id_type=MESH
            )
        return 0

    lax.fori_loop(0, place.chips - 1, plane, 0)
    count += 2 * (place.chips - 1)
    pl.semaphore_wait(barrier, count)


def front_kernel(
    x_ref, wq_ref, wm_ref, sm_ref,
    oin_ref, wall_ref, smalls_ref, count_ref, xs_ref, wqf_ref, oT_ref, lse_ref, qT_ref, kA_ref, v_ref,
    wqz, counts, vT, scores, o_buf, wqT, wkp, wvp, wvT,
    sm_send, sm_recv, cn_send, cn_recv, wz_send, wz_recv, wp_send, wp_recv,
    x_send, x_recv, xr_send, xf_send, mz_send, mz_recv, mp_send, mp_recv, ms_send, ms_recv, o_send, o_recv,
):
    me = Place()
    dp, tp, chips = me.dp, me.tp, me.chips
    rows, width = x_ref.shape
    half = rows // 2
    length = rows * tp
    share = wq_ref.shape[0]
    heads = 3
    greet(me)

    def each_peer(f):
        def step(i, _):
            f(i, lax.rem(me.d + 1 + i, dp))
            return 0

        lax.fori_loop(0, dp - 1, step, 0)

    def small_copy(i, peer):
        return remote(sm_ref, smalls_ref.at[me.d], sm_send.at[i], sm_recv.at[me.d], peer, me.z)

    each_peer(lambda i, peer: small_copy(i, peer).start())
    smalls_ref[me.d] = sm_ref[...]

    for s in range(2):
        target = me.z // 2 + 2 * s
        src, dst = wq_ref, wqz.at[me.low]

        @pl.when(target == me.z)
        def _(s=s, dst=dst):
            pltpu.make_async_copy(wq_ref, dst, wz_recv.at[me.low]).start()

        @pl.when(target != me.z)
        def _(s=s, dst=dst, target=target):
            remote(wq_ref, dst, wz_send.at[s], wz_recv.at[me.low], me.d, target).start()

    is_near = me.z == me.near_here
    is_end = jnp.logical_not(is_near)
    pltpu.make_async_copy(wm_ref, wall_ref.at[me.z, me.d], mz_recv.at[me.z]).start()

    def along_z(unit, t, sem, to):
        return remote(unit, wall_ref.at[t, me.d], mz_send.at[sem], mz_recv.at[t], me.d, to)

    pl.when(me.z > 0)(lambda: along_z(wm_ref, me.z, 0, me.z - 1).start())
    pl.when(me.z < tp - 1)(lambda: along_z(wm_ref, me.z, 1, me.z + 1).start())

    def goes_up(t):
        return jnp.logical_and(t < me.z, me.z < tp - 1)

    def goes_down(t):
        return jnp.logical_and(t > me.z, me.z > 0)

    is_owner = me.core == me.pair
    for h in range(2):
        part = pl.ds(h * half, half)

        @pl.when(is_owner)
        def _(h=h, part=part):
            pltpu.make_async_copy(x_ref.at[part], xs_ref.at[me.z, part], x_recv.at[me.z, h]).start()
            remote(x_ref.at[part], xs_ref.at[me.z, part], x_send.at[h], x_recv.at[me.z, h], me.base + h, me.buddy).start()
            remote(x_ref.at[part], xs_ref.at[me.z, part], xr_send.at[0, h], x_recv.at[me.z, h], me.sibling, me.z).start()

        @pl.when(jnp.logical_not(is_owner))
        def _(h=h, part=part):
            remote(x_ref.at[part], xs_ref.at[me.z, part], x_send.at[h], x_recv.at[me.z, h], me.base + h, me.near_there).start()

    def wq_plane(s, k):
        dst = wqf_ref.at[me.d]
        return remote(wqz.at[s], dst, wp_send.at[s, k], wp_recv.at[me.d], 2 * k + s, me.z)

    for s in range(2):
        arrival(wqz.at[s], wz_recv.at[s]).wait()

        def step(i, _, s=s):
            k = lax.rem(me.chip + 1 + i, chips)
            here = 2 * k + s == me.d

            @pl.when(here)
            def _():
                pltpu.make_async_copy(wqz.at[s], wqf_ref.at[me.d], wp_recv.at[me.d]).start()

            @pl.when(jnp.logical_not(here))
            def _():
                wq_plane(s, k).start()

            return 0

        lax.fori_loop(0, chips, step, 0)

    def in_plane(unit, t, k, sem, to):
        return remote(unit, wall_ref.at[t, 2 * k + me.core], mp_send.at[t, sem], mp_recv.at[t, k], 2 * to + me.core, me.z)

    def plane_units(t, unit):
        in_plane(unit, t, me.chip, 0, me.first).start()
        in_plane(unit, t, me.chip, 1, me.second).start()

    def to_sibling(t, k):
        unit = wall_ref.at[t, 2 * k + me.core]
        return remote(unit, unit, ms_send.at[t, k], ms_recv.at[t, k], me.sibling, me.z)

    def own_unit(t):
        unit = wall_ref.at[t, me.d]
        arrival(unit, mz_recv.at[t]).wait()
        pl.when(goes_up(t))(lambda: along_z(unit, t, 2 + t, me.z + 1).start())
        pl.when(goes_down(t))(lambda: along_z(unit, t, 2 + t, me.z - 1).start())
        plane_units(t, unit)
        to_sibling(t, me.chip).start()

    def plane_unit(t, k):
        unit = wall_ref.at[t, 2 * k + me.core]
        arrival(unit, mp_recv.at[t, k]).wait()
        return unit

    def plane_forward(t):
        unit = plane_unit(t, me.first)
        in_plane(unit, t, me.first, 2, me.second).start()
        to_sibling(t, me.first).start()

    def plane_rest(t):
        for k in (me.second, me.diagonal):
            plane_unit(t, k)
            to_sibling(t, k).start()

    plane_units(me.z, wm_ref)
    remote(wm_ref, wall_ref.at[me.z, me.d], ms_send.at[me.z, me.chip], ms_recv.at[me.z, me.chip], me.sibling, me.z).start()

    mine = pl.ds(pl.multiple_of(me.core * half, half), half)
    other = pl.ds(pl.multiple_of((1 - me.core) * half, half), half)
    far_first = 2 * (1 - me.pair) + me.pair
    far_second = 2 * (1 - me.pair) + 1 - me.pair
    blocks_in = (
        jnp.where(is_near, far_first, me.buddy),
        jnp.where(is_near, far_second, far_first),
        jnp.where(is_near, me.buddy, far_second),
    )

    def relay(n):
        j = blocks_in[n]
        part = xs_ref.at[j, mine]
        arrival(part, x_recv.at[j, me.core]).wait()
        remote(part, part, xr_send.at[1 + n, 0], x_recv.at[j, me.core], me.sibling, me.z).start()
        if n < 2:
            pl.when(is_near)(lambda: remote(part, part, xf_send.at[n], x_recv.at[j, me.core], me.d, me.buddy).start())

    own_unit(me.around[0])
    relay(0)
    relay(1)

    def small_wait(i, peer):
        arrival(smalls_ref.at[peer], sm_recv.at[peer]).wait()

    each_peer(small_wait)
    plane_count = smalls_ref[0][8:16]
    for k in range(1, dp):
        plane_count = plane_count + smalls_ref[k][8:16]
    counts[me.z] = plane_count
    for s in range(1, tp):
        remote(counts.at[me.z], counts.at[me.z], cn_send.at[s - 1], cn_recv.at[me.z], me.d, lax.rem(me.z + s, tp)).start()

    for k in range(dp):
        arrival(wqf_ref.at[k], wp_recv.at[k]).wait()
    zero = jnp.zeros((share, HEAD_DIM), BF16)
    gw = heads * HEAD_DIM
    for k in range(dp):
        w = wqf_ref[k]
        at = slice(k * share, (k + 1) * share)
        pads = []
        for m in range(3):
            cols = []
            for h in range(heads):
                cols += [w[:, m * gw + h * HEAD_DIM : m * gw + (h + 1) * HEAD_DIM], zero]
            pads.append(jnp.concatenate(cols, axis=1))
        wkp[at, :] = pads[1]
        wvp[at, :] = pads[2]
        scores[0, at, 0:384] = pads[0].astype(F32)
    wqT[...] = scores[0, 0:width, 0:384].T.astype(BF16)
    wvT[...] = wvp[...].astype(F32).T.astype(BF16)

    blocks = gw // share
    row_bias = jnp.zeros((8, 384), F32)
    col_bias = jnp.zeros((384, 8), F32)
    r_in = lax.broadcasted_iota(jnp.int32, (128, 384), 0)
    r_out = lax.broadcasted_iota(jnp.int32, (128, 384), 1)
    c_out = lax.broadcasted_iota(jnp.int32, (384, 128), 0)
    c_in = lax.broadcasted_iota(jnp.int32, (384, 128), 1)

    def padded(col):
        return (col // HEAD_DIM) * 128 + lax.rem(col, HEAD_DIM)

    for b in range(blocks):
        vecs = smalls_ref[me.group * blocks + b][0:8].astype(BF16)
        sel = jnp.logical_and(padded(r_in + b * share) == r_out, r_in < share)
        row_bias = row_bias + dot(vecs, jnp.where(sel, 1.0, 0.0).astype(BF16), 1, 0)
        sel = jnp.logical_and(padded(c_in + b * share) == c_out, c_in < share)
        col_bias = col_bias + dot(jnp.where(sel, 1.0, 0.0).astype(BF16), vecs, 1, 1)
    q_bias = col_bias[:, 0:1]
    v_bias_col = col_bias[:, 1:2]
    v_bias = row_bias[1:2, :]
    valid = smalls_ref[me.base + me.pair][12:13, 0:1]

    lane = lax.broadcasted_iota(jnp.int32, (rows, 128), 1)
    srow = lax.broadcasted_iota(jnp.int32, (128, rows), 0)

    def project(j):
        at = pl.ds(pl.multiple_of(j * rows, rows), rows)
        xb = xs_ref[j]
        keys = dot(xb, wkp[...], 1, 0)
        queries = dot(wqT[...], xb, 1, 1) + q_bias
        vals = dot(xb, wvp[...], 1, 0) + v_bias
        valsT = dot(wvT[...], xb, 1, 1) + v_bias_col
        pos = (j * rows + lax.broadcasted_iota(jnp.int32, (rows, 128), 0)).astype(F32)
        bias = jnp.where(pos < valid, 0.0, masked_score)
        for h in range(heads):
            span = slice(h * 128, (h + 1) * 128)
            vT[h * HEAD_DIM : (h + 1) * HEAD_DIM, at] = valsT[h * 128 : h * 128 + HEAD_DIM].astype(BF16)
            kA_ref[h, at, :] = jnp.where(lane == HEAD_DIM, bias, keys[:, span]).astype(BF16)
            qh = queries[span].astype(BF16) * BF16(HEAD_DIM**-0.5)
            qT_ref[h, :, at] = jnp.where(srow == HEAD_DIM, BF16(1), qh)
            v_ref[h, at, :] = vals[:, span].astype(BF16)

    arrival(xs_ref.at[me.z, pl.ds(0, half)], x_recv.at[me.z, 0]).wait()
    arrival(xs_ref.at[me.z, pl.ds(half, half)], x_recv.at[me.z, 1]).wait()
    project(me.z)
    relay(2)
    pl.when(is_near)(functools.partial(own_unit, me.around[1]))
    plane_forward(me.z)
    for j in blocks_in:
        arrival(xs_ref.at[j, other], x_recv.at[j, 1 - me.core]).wait()
        project(j)
    pl.when(is_near)(functools.partial(own_unit, me.around[2]))
    plane_forward(me.around[0])

    chunk = 256
    pieces = length // chunk

    def attend(i, _):
        j = lax.rem(me.z + 1 + i, tp)
        at = pl.ds(pl.multiple_of(j * rows, rows), rows)
        tops = []
        for h in range(heads):
            qt = qT_ref[h, :, at]
            top = None
            for c in range(pieces):
                s = dot(kA_ref[h, c * chunk : (c + 1) * chunk, :], qt, 1, 0)
                scores[h, c * chunk : (c + 1) * chunk, :] = s
                peak = jnp.max(s, axis=0, keepdims=True)
                top = peak if top is None else jnp.maximum(top, peak)
            tops.append(top)
        outs = []
        for h in range(heads):
            total, mixed = None, None
            for c in range(pieces):
                p = jnp.exp(scores[h, c * chunk : (c + 1) * chunk, :] - tops[h])
                part = jnp.sum(p, axis=0, keepdims=True)
                term = dot(vT[h * HEAD_DIM : (h + 1) * HEAD_DIM, c * chunk : (c + 1) * chunk], p.astype(BF16), 1, 0)
                total = part if total is None else total + part
                mixed = term if mixed is None else mixed + term
            mixed = mixed / total
            oT_ref[h * HEAD_DIM : (h + 1) * HEAD_DIM, at] = mixed
            lse_ref[h, :, at] = tops[h] + jnp.log(total)
            outs.append(mixed)
        o_buf[j] = jnp.concatenate(outs, axis=0).T.astype(BF16)
        here = jnp.logical_and(j == me.z, is_owner)

        @pl.when(here)
        def _():
            pltpu.make_async_copy(o_buf.at[j], oin_ref.at[me.group], o_recv.at[me.group]).start()

        @pl.when(jnp.logical_not(here))
        def _():
            remote(o_buf.at[j], oin_ref.at[me.group], o_send.at[i], o_recv.at[me.group], me.owner, j).start()

        for n in (1, 2):
            pl.when(jnp.logical_and(is_end, i == n - 1))(functools.partial(own_unit, me.around[n]))
        pl.when(i == 0)(functools.partial(plane_rest, me.z))
        pl.when(jnp.logical_and(is_near, i == 0))(functools.partial(plane_forward, me.around[1]))
        pl.when(jnp.logical_and(is_end, i == 2))(functools.partial(plane_forward, me.around[1]))
        pl.when(jnp.logical_and(is_near, i == 2))(functools.partial(plane_forward, me.around[2]))
        pl.when(jnp.logical_and(is_end, i == 3))(functools.partial(plane_forward, me.around[2]))
        return 0

    lax.fori_loop(0, tp, attend, 0)

    for t in me.around:
        plane_rest(t)

    arrival(wall_ref.at[me.z, me.d], mz_recv.at[me.z]).wait()
    for s in range(1, tp):
        t = lax.rem(me.z + s, tp)
        arrival(counts.at[t], cn_recv.at[t]).wait()
    total = counts[0]
    for t in range(1, tp):
        total = total + counts[t]
    count_ref[...] = total
    for g in range(4):
        arrival(oin_ref.at[g], o_recv.at[g]).wait()

    def sibling_units(n, _):
        t, k = n // chips, lax.rem(n, chips)
        arrival(wall_ref.at[t, 2 * k + 1 - me.core], ms_recv.at[t, k]).wait()
        to_sibling(t, k).wait_send()
        return 0

    lax.fori_loop(0, tp * chips, sibling_units, 0)

    def sent(n, _):
        t, i = n // (chips - 1), lax.rem(n, chips - 1)
        in_plane(wm_ref, t, me.chip, i, me.first).wait_send()
        return 0

    lax.fori_loop(0, tp * (chips - 1), sent, 0)
    each_peer(lambda i, peer: small_copy(i, peer).wait_send())
    for s in range(2):

        @pl.when(me.z // 2 + 2 * s != me.z)
        def _(s=s):
            remote(wq_ref, wqz.at[0], wz_send.at[s], wz_recv.at[0], me.sibling, me.z).wait_send()

        def step(i, _, s=s):
            k = lax.rem(me.chip + 1 + i, chips)

            @pl.when(2 * k + s != me.d)
            def _():
                wq_plane(s, k).wait_send()

            return 0

        lax.fori_loop(0, chips, step, 0)
    for s in range(tp - 1):
        remote(counts.at[0], counts.at[0], cn_send.at[s], cn_recv.at[0], me.sibling, me.z).wait_send()

    def z_sent(sem):
        along_z(wm_ref, 0, sem, 0).wait_send()

    pl.when(me.z > 0)(functools.partial(z_sent, 0))
    pl.when(me.z < tp - 1)(functools.partial(z_sent, 1))
    for t in range(tp):
        pl.when(jnp.logical_or(goes_up(t), goes_down(t)))(functools.partial(z_sent, 2 + t))

    def x_sent(sem):
        remote(x_ref.at[pl.ds(0, half)], xs_ref.at[0, pl.ds(0, half)], sem, x_recv.at[0, 0], me.sibling, me.z).wait_send()

    for h in range(2):
        x_sent(x_send.at[h])

        @pl.when(is_owner)
        def _(h=h):
            x_sent(xr_send.at[0, h])

    for n in range(3):
        x_sent(xr_send.at[1 + n, 0])

    @pl.when(is_near)
    def _():
        for n in range(2):
            x_sent(xf_send.at[n])

    def o_sent(i, _):
        j = lax.rem(me.z + 1 + i, tp)

        @pl.when(jnp.logical_not(jnp.logical_and(j == me.z, is_owner)))
        def _():
            remote(o_buf.at[0], oin_ref.at[0], o_send.at[i], o_recv.at[0], me.sibling, me.z).wait_send()

        return 0

    lax.fori_loop(0, tp, o_sent, 0)


def front(x, wq, wm, small, dp, tp):
    rows, width = x.shape
    length = rows * tp
    share = wq.shape[0]
    chips = dp // 2
    S = jax.ShapeDtypeStruct
    vmem = pl.BlockSpec(memory_space=pltpu.VMEM)
    anym = pl.BlockSpec(memory_space=pl.ANY)
    dma = pltpu.SemaphoreType.DMA
    return pl.pallas_call(
        front_kernel,
        name="front",
        out_shape=(
            S((4, rows, 192), BF16),
            S((tp, dp, share, wm.shape[1]), BF16),
            S((dp, 16, 128), F32),
            S((8, 128), F32),
            S((tp, rows, width), BF16),
            S((dp, share, wq.shape[1]), BF16),
            S((192, length), F32),
            S((3, 1, length), F32),
            S((3, 128, length), BF16),
            S((3, length, 128), BF16),
            S((3, length, 128), BF16),
        ),
        in_specs=[vmem] * 4,
        out_specs=(anym, anym) + (vmem,) * 9,
        scratch_shapes=[
            pltpu.VMEM((2, share, wq.shape[1]), BF16),
            pltpu.VMEM((tp, 8, 128), F32),
            pltpu.VMEM((192, length), BF16),
            pltpu.VMEM((3, length, rows), F32),
            pltpu.VMEM((tp, rows, 192), BF16),
            pltpu.VMEM((384, width), BF16),
            pltpu.VMEM((width, 384), BF16),
            pltpu.VMEM((width, 384), BF16),
            pltpu.VMEM((384, width), BF16),
            dma((dp - 1,)), dma((dp,)), dma((tp - 1,)), dma((tp,)),
            dma((2,)), dma((2,)), dma((2, chips)), dma((dp,)),
            dma((2,)), dma((tp, 2)), dma((4, 2)), dma((2,)),
            dma((tp + 2,)), dma((tp,)), dma((tp, chips - 1)), dma((tp, chips)), dma((tp, chips)), dma((tp, chips)),
            dma((tp,)), dma((4,)),
        ],
        compiler_params=pltpu.CompilerParams(
            collective_id=0, has_side_effects=True, vmem_limit_bytes=VMEM_LIMIT
        ),
    )(x, wq, wm, small)


SQRT_HALF = 0.7071067811865476
INV_SQRT_2PI = 0.3989422804014327


def norm_forward(values, gain, shift):
    centred = values - jnp.mean(values, axis=1, keepdims=True)
    inv = lax.rsqrt(jnp.mean(centred * centred, axis=1, keepdims=True) + norm_eps)
    normed = centred * inv
    return normed * gain + shift, normed, inv


def norm_backward(grad_out, normed, inv, gain):
    g = grad_out * gain
    plain = jnp.mean(g, axis=1, keepdims=True)
    mixed = jnp.mean(g * normed, axis=1, keepdims=True)
    return inv * (g - plain - normed * mixed)


def column_sum(values):
    return jnp.sum(values, axis=0, keepdims=True)


def mid_kernel(
    x_ref, teacher_ref, counted_ref, scale_ref, oin_ref, wall_ref, vec_ref, ib_ref,
    out_ref, dr1_ref, do_ref, grad_ref, small_ref, ismall_ref,
    up_ref, act_ref, f_ref, n1_ref, acc_ref, hT_ref, dfT_ref,
):
    groups = wall_ref.shape[0]
    width = x_ref.shape[1]
    gw = oin_ref.shape[2]
    inner = slice(0, width)
    outer = slice(width, 2 * width)
    mixer = slice(2 * width, 2 * width + gw)
    vec = lambda i: vec_ref[i : i + 1, :]

    acc_ref[...] = x_ref[...].astype(F32) + vec(2)
    for g in range(groups):
        acc_ref[...] += dot(oin_ref[g], wall_ref[g, :, mixer], 1, 1)
    hidden, normed1, inv1 = norm_forward(acc_ref[...], vec(3), vec(4))
    n1_ref[...] = normed1
    low = hidden.astype(BF16)
    hT_ref[...] = hidden.T.astype(BF16)
    f_ref[...] = hidden + vec(5)

    def ffn_forward(g, _):
        up = dot(low, wall_ref[g, :, inner], 1, 0) + ib_ref[g]
        up_ref[g] = up
        act = (up * (0.5 * (1.0 + lax.erf(up * SQRT_HALF)))).astype(BF16)
        act_ref[g] = act
        f_ref[...] += dot(act, wall_ref[g, :, outer], 1, 1)
        return 0

    lax.fori_loop(0, groups, ffn_forward, 0)
    final, normed2, inv2 = norm_forward(f_ref[...], vec(6), vec(7))
    out_ref[...] = final.astype(BF16)
    diff = final - teacher_ref[...].astype(F32)
    counted = counted_ref[...]
    small_ref[...] = jnp.zeros_like(small_ref)
    small_ref[6:7, 0:1] = jnp.sum(counted * jnp.sum(diff * diff, axis=1, keepdims=True), axis=0, keepdims=True)
    grad = (scale_ref[0, 0] * counted) * diff
    small_ref[4:5, :] = column_sum(grad * normed2)
    small_ref[5:6, :] = column_sum(grad)
    dr2 = norm_backward(grad, normed2, inv2, vec(6))
    small_ref[3:4, :] = column_sum(dr2)
    acc_ref[...] = dr2
    df = dr2.astype(BF16)
    dfT_ref[...] = dr2.T.astype(BF16)

    def ffn_backward(g, _):
        up = up_ref[g]
        slope = 0.5 * (1.0 + lax.erf(up * SQRT_HALF)) + up * (INV_SQRT_2PI * jnp.exp(-0.5 * up * up))
        du = (dot(df, wall_ref[g, :, outer], 1, 0) * slope).astype(BF16)
        ismall_ref[g] = column_sum(du.astype(F32))
        acc_ref[...] += dot(du, wall_ref[g, :, inner], 1, 1)
        grad_ref[g, :, inner] = dot(hT_ref[...], du, 1, 0).astype(BF16)
        grad_ref[g, :, outer] = dot(dfT_ref[...], act_ref[g], 1, 0).astype(BF16)
        return 0

    lax.fori_loop(0, groups, ffn_backward, 0)
    dh1 = acc_ref[...]
    normed1 = n1_ref[...]
    small_ref[1:2, :] = column_sum(dh1 * normed1)
    small_ref[2:3, :] = column_sum(dh1)
    dr1 = norm_backward(dh1, normed1, inv1, vec(3))
    small_ref[0:1, :] = column_sum(dr1)
    dr1_ref[...] = dr1
    da = dr1.astype(BF16)
    daT = dr1.T.astype(BF16)
    for g in range(groups):
        do_ref[g] = dot(da, wall_ref[g, :, mixer], 1, 0).astype(BF16)
        grad_ref[g, :, mixer] = dot(daT, oin_ref[g], 1, 0).astype(BF16)


def mid(x, teacher, counted, scale, oin, wall, vecs, ib):
    rows, width = x.shape
    groups = wall.shape[0]
    S = jax.ShapeDtypeStruct
    vmem = pl.BlockSpec(memory_space=pltpu.VMEM)
    return pl.pallas_call(
        mid_kernel,
        name="mid",
        out_shape=(
            S((rows, width), BF16),
            S((rows, width), F32),
            S(oin.shape, BF16),
            S(wall.shape, BF16),
            S((8, width), F32),
            S(ib.shape, F32),
        ),
        in_specs=[vmem, vmem, vmem, pl.BlockSpec(memory_space=pltpu.SMEM)] + [vmem] * 4,
        out_specs=(vmem,) * 6,
        scratch_shapes=[
            pltpu.VMEM((groups, rows, ib.shape[2]), F32),
            pltpu.VMEM((groups, rows, ib.shape[2]), BF16),
            pltpu.VMEM((rows, width), F32),
            pltpu.VMEM((rows, width), F32),
            pltpu.VMEM((rows, width), F32),
            pltpu.VMEM((width, rows), BF16),
            pltpu.VMEM((width, rows), BF16),
        ],
        compiler_params=pltpu.CompilerParams(vmem_limit_bytes=VMEM_LIMIT),
    )(x, teacher, counted, scale, oin, wall, vecs, ib)


def back_kernel(
    do_ref, grad_ref, xs_ref, wqf_ref, oT_ref, lse_ref, qT_ref, kA_ref, v_ref, pack_ref, dr1_ref,
    dx_ref, gsum_ref, qgrad_ref, small_ref,
    dof, doT, delta, qs, kT, dk, dv, dqT, dqkv,
    sib, own, pln, zsrc, zin, parts, pr, sj, rr, fin, qsend, qr, qz, qf, spack, srecv, zpack,
    do_send, do_recv, sb_send, sb_recv, own_sem, pl_send, pl_recv, zz_send, zz_recv,
    pr_send, pr_recv, rr_send, rr_recv, fin_send, fin_recv, qr_send, qr_recv, qf_send, qf_recv,
    sm_send, sm_recv, sz_send, sz_recv,
):
    me = Place()
    dp, tp, chips = me.dp, me.tp, me.chips
    rows, width = dx_ref.shape
    half = rows // 2
    length = rows * tp
    heads = 3
    gw = heads * HEAD_DIM
    share = width // dp
    greet(me)

    for g in range(4):
        t = 2 * me.core + g // 2
        d = me.base + g % 2
        here = jnp.logical_and(t == me.z, g % 2 == me.core)

        @pl.when(here)
        def _(g=g):
            pltpu.make_async_copy(do_ref.at[g], dof.at[me.z], do_recv.at[me.z]).start()

        @pl.when(jnp.logical_not(here))
        def _(g=g, t=t, d=d):
            remote(do_ref.at[g], dof.at[me.z], do_send.at[g], do_recv.at[me.z], d, t).start()

    order = me.around[::-1] + (me.z,)

    def sib_copy(t):
        return remote(grad_ref.at[t, :, 1 - me.core], sib.at[t], sb_send.at[t], sb_recv.at[t], me.sibling, me.z)

    for t in order:
        sib_copy(t).start()
        pltpu.make_async_copy(grad_ref.at[t, :, me.core], own.at[t], own_sem.at[t]).start()

    def plane_copy(t, n):
        k = (me.diagonal, me.first, me.second)[n]
        to = (me.first, me.first, me.second)[n]
        return remote(own.at[t, k], pln.at[t, n], pl_send.at[t, n], pl_recv.at[t, n], 2 * to + me.core, me.z)

    def pair_sum(t):
        arrival(own.at[t], own_sem.at[t]).wait()
        arrival(sib.at[t], sb_recv.at[t]).wait()

        def unit(k, _):
            own[t, k] = (own[t, k].astype(F32) + sib[t, k].astype(F32)).astype(BF16)
            return 0

        lax.fori_loop(0, chips, unit, 0)
        plane_copy(t, 0).start()
        plane_copy(t, 1).start()

    def pass_on(n):
        t = order[n]
        arrival(pln.at[t, 0], pl_recv.at[t, 0]).wait()
        own[t, me.second] = (own[t, me.second].astype(F32) + pln[t, 0].astype(F32)).astype(BF16)
        plane_copy(t, 2).start()

    has_below, has_above = me.z > 0, me.z < tp - 1

    def z_copy(t):
        up = t > me.z
        to = jnp.where(up, me.z + 1, me.z - 1)
        slot = jnp.where(jnp.logical_and(to == t, jnp.logical_not(up)), tp, t)
        return remote(zsrc.at[t], zin.at[slot], zz_send.at[t], zz_recv.at[slot], me.d, to)

    def plane_total(t):
        for n in (1, 2):
            arrival(pln.at[t, n], pl_recv.at[t, n]).wait()
        return own[t, me.chip].astype(F32) + pln[t, 1].astype(F32) + pln[t, 2].astype(F32)

    def z_step(n):
        t = order[n]
        total = plane_total(t)
        comes = jnp.where(t > me.z, has_below, has_above)

        @pl.when(comes)
        def _():
            arrival(zin.at[t], zz_recv.at[t]).wait()
            zsrc[t] = (total + zin[t].astype(F32)).astype(BF16)

        @pl.when(jnp.logical_not(comes))
        def _():
            zsrc[t] = total.astype(BF16)

        z_copy(t).start()

    for t in order:
        pair_sum(t)

    is_near = me.z == me.near_here
    is_end = jnp.logical_not(is_near)
    far = 2 * (1 - me.pair)
    far_first, far_second = far + me.pair, far + 1 - me.pair

    def block_at(i):
        return jnp.where(i == 0, far_second, jnp.where(i == 1, far_first, jnp.where(i == 2, me.buddy, me.z)))

    def prepare(j, at):
        arrival(dof.at[j], do_recv.at[j]).wait()
        flipped = dof[j].astype(F32).T
        doT[:, at] = flipped.astype(BF16)
        for h in range(heads):
            span = slice(h * HEAD_DIM, (h + 1) * HEAD_DIM)
            delta[h, :, at] = jnp.sum(flipped[span] * oT_ref[span, at], axis=0, keepdims=True)
            qs[h, at, :] = qT_ref[h, :, at].astype(F32).T.astype(BF16)

    always = {(0, 1): (pass_on, 0), (0, 3): (pass_on, 1), (1, 1): (pass_on, 2), (2, 0): (pass_on, 3)}
    at_ends = {(1, 0): (z_step, 0), (1, 2): (z_step, 1), (2, 1): (z_step, 2)}
    in_middle = {(1, 2): (z_step, 0), (2, 0): (z_step, 1), (2, 2): (z_step, 2)}
    chunk = 256
    for j in range(tp):
        at = slice(j * rows, (j + 1) * rows)
        for h in range(heads):
            kT[h, :, at] = kA_ref[h, at, :].astype(F32).T[0:HEAD_DIM, :].astype(BF16)
    for h in range(heads):
        dk[...] = jnp.zeros_like(dk)
        dv[...] = jnp.zeros_like(dv)

        def attend(i, _, h=h):
            j = block_at(3 - i)
            at = pl.ds(pl.multiple_of(j * rows, rows), rows)
            if h == 0:
                prepare(j, at)
            span = slice(h * HEAD_DIM, (h + 1) * HEAD_DIM)
            qt, gt = qT_ref[h, :, at], doT[span, at]
            q, go = qs[h, at, :], dof[j, :, span]
            lse, dl = lse_ref[h, :, at], delta[h, :, at]
            dq = None
            for c in range(length // chunk):
                r = slice(c * chunk, (c + 1) * chunk)
                p = jnp.exp(dot(kA_ref[h, r, :], qt, 1, 0) - lse)
                dp_ = dot(v_ref[h, r, 0:HEAD_DIM], gt, 1, 0)
                ds = (p * (dp_ - dl)).astype(BF16)
                dv[r, :] += dot(p.astype(BF16), go, 1, 0)
                dk[r, :] += dot(ds, q, 1, 0)
                term = dot(kT[h, :, r], ds, 1, 0)
                dq = term if dq is None else dq + term
            dqT[span, at] = dq * HEAD_DIM**-0.5
            for where, hooks in ((None, always), (is_end, at_ends), (is_near, in_middle)):
                for (head, step), (act, n) in hooks.items():
                    if head == h:
                        now = i == step
                        pl.when(now if where is None else jnp.logical_and(where, now))(functools.partial(act, n))
            return 0

        lax.fori_loop(0, tp, attend, 0)
        for j in range(tp):
            at = slice(j * rows, (j + 1) * rows)
            dqkv[j, :, gw + h * HEAD_DIM : gw + (h + 1) * HEAD_DIM] = dk[at, 0:HEAD_DIM].astype(BF16)
            dqkv[j, :, 2 * gw + h * HEAD_DIM : 2 * gw + (h + 1) * HEAD_DIM] = dv[at, :].astype(BF16)

    weights = wqf_ref[...].reshape(width, 3 * gw)
    ones = jnp.ones((8, rows), BF16)
    mine = pl.ds(pl.multiple_of(me.core * half, half), half)
    other = pl.ds(pl.multiple_of((1 - me.core) * half, half), half)

    def pr_copy(j):
        return remote(parts.at[j, other], pr.at[j], pr_send.at[j], pr_recv.at[j], me.sibling, me.z)

    def rr_copy(j):
        return remote(sj.at[j], rr.at[j], rr_send.at[j], rr_recv.at[j], me.d, me.buddy)

    def collects(j):
        return jnp.where(j // 2 == me.pair, j, me.near_here) == me.z

    def chip_sum(j):
        arrival(pr.at[j], pr_recv.at[j]).wait()
        sj[j] = (parts[j, mine, :].astype(F32) + pr[j].astype(F32)).astype(BF16)
        pl.when(jnp.logical_not(collects(j)))(lambda: rr_copy(j).start())

    def token_grads(i, sums):
        j = block_at(i)
        at = pl.ds(pl.multiple_of(j * rows, rows), rows)
        dqkv[j, :, 0:gw] = dqT[:, at].T.astype(BF16)
        flat = dqkv[j]
        parts[j] = dot(flat, weights, 1, 1).astype(BF16)
        pr_copy(j).start()
        pl.when(i > 0)(lambda: chip_sum(block_at(i - 1)))
        return sums + dot(ones, flat, 1, 0)

    sums = lax.fori_loop(0, tp, token_grads, jnp.zeros((8, 3 * gw), F32))
    chip_sum(block_at(tp - 1))

    spack[...] = pack_ref[...]
    blocks = gw // share
    for b in range(blocks):
        spack[me.group * blocks + b, 0:1, 0:share] = sums[0:1, b * share : (b + 1) * share]
        spack[me.group * blocks + b, 1:2, 0:share] = sums[0:1, 2 * gw + b * share : 2 * gw + (b + 1) * share]

    def small_copy(i):
        peer = lax.rem(me.d + 1 + i, dp)
        return remote(spack.at[peer], srecv.at[i], sm_send.at[i], sm_recv.at[i], peer, me.z)

    def small_start(i, _):
        small_copy(i).start()
        return 0

    lax.fori_loop(0, dp - 1, small_start, 0)

    def fin_copy(j):
        return remote(pr.at[j], fin.at[me.core], fin_send.at[j], fin_recv.at[me.core], me.owner, j)

    def lands_here(j):
        return jnp.logical_and(me.core == me.pair, j == me.z)

    total = None
    for j in range(tp):
        term = dot(xs_ref[j], dqkv[j], 0, 0)
        total = term if total is None else total + term
    qsend[...] = total.astype(BF16).reshape(dp, share, 3 * gw)

    def q_copy(peer, i):
        return remote(qsend.at[peer], qr.at[me.core, me.chip], qr_send.at[i], qr_recv.at[me.core, me.chip], peer, me.z)

    def q_start(i, _):
        peer = lax.rem(me.d + i, dp)

        @pl.when(i == 0)
        def _():
            pltpu.make_async_copy(qsend.at[peer], qr.at[me.core, me.chip], qr_recv.at[me.core, me.chip]).start()

        @pl.when(i > 0)
        def _():
            q_copy(peer, i).start()

        return 0

    lax.fori_loop(0, dp, q_start, 0)

    def pair_total(i, _):
        j = block_at(i)

        @pl.when(collects(j))
        def _():
            arrival(rr.at[j], rr_recv.at[j]).wait()
            pr[j] = (sj[j].astype(F32) + rr[j].astype(F32)).astype(BF16)

            @pl.when(lands_here(j))
            def _():
                pltpu.make_async_copy(pr.at[j], fin.at[me.core], fin_recv.at[me.core]).start()

            @pl.when(jnp.logical_not(lands_here(j)))
            def _():
                fin_copy(j).start()

        return 0

    lax.fori_loop(0, tp, pair_total, 0)

    def q_pair(s):
        return me.z // 2, 2 * me.low + s

    for s in range(2):
        total = None
        for k in range(chips):
            arrival(qr.at[s, k], qr_recv.at[s, k]).wait()
            term = qr[s, k].astype(F32)
            total = term if total is None else total + term
        qz[s] = total.astype(BF16)
        p, t = q_pair(s)

        @pl.when(t == me.z)
        def _(s=s, p=p):
            pltpu.make_async_copy(qz.at[s], qf.at[p], qf_recv.at[p]).start()

        @pl.when(t != me.z)
        def _(s=s, p=p, t=t):
            remote(qz.at[s], qf.at[p], qf_send.at[s], qf_recv.at[p], me.d, t).start()

    total = spack[me.d]
    for i in range(dp - 1):
        arrival(srecv.at[i], sm_recv.at[i]).wait()
        total = total + srecv[i]
    zpack[me.z] = total

    def sz_copy(s):
        return remote(zpack.at[me.z], zpack.at[me.z], sz_send.at[s - 1], sz_recv.at[me.z], me.d, lax.rem(me.z + s, tp))

    for s in range(1, tp):
        sz_copy(s).start()

    for h in range(2):
        arrival(fin.at[h], fin_recv.at[h]).wait()
        at = slice(h * half, (h + 1) * half)
        dx_ref[at, :] = dr1_ref[at, :] + fin[h].astype(F32)
    for p in range(2):
        arrival(qf.at[p], qf_recv.at[p]).wait()
    qgrad_ref[...] = qf[0].astype(F32) + qf[1].astype(F32)
    for s in range(1, tp):
        t = lax.rem(me.z + s, tp)
        arrival(zpack.at[t], sz_recv.at[t]).wait()
    total = zpack[0]
    for t in range(1, tp):
        total = total + zpack[t]
    small_ref[...] = total
    gsum_ref[...] = plane_total(me.z)
    for slot, comes in ((me.z, has_below), (tp, has_above)):

        @pl.when(comes)
        def _(slot=slot):
            arrival(zin.at[slot], zz_recv.at[slot]).wait()
            gsum_ref[...] += zin[slot].astype(F32)

    for g in range(4):

        @pl.when(jnp.logical_not(jnp.logical_and(2 * me.core + g // 2 == me.z, g % 2 == me.core)))
        def _(g=g):
            remote(do_ref.at[g], dof.at[0], do_send.at[g], do_recv.at[0], me.sibling, me.z).wait_send()

    for t in range(tp):
        sib_copy(t).wait_send()
        pr_copy(t).wait_send()

        @pl.when(jnp.logical_not(collects(t)))
        def _(t=t):
            rr_copy(t).wait_send()

        @pl.when(jnp.logical_and(collects(t), jnp.logical_not(lands_here(t))))
        def _(t=t):
            fin_copy(t).wait_send()

    for t in range(tp):
        for n in range(3):
            plane_copy(t, n).wait_send()
        pl.when(t != me.z)(lambda t=t: z_copy(t).wait_send())

    def peers_sent(i, _):
        small_copy(i).wait_send()
        q_copy(lax.rem(me.d + 1 + i, dp), i + 1).wait_send()
        return 0

    lax.fori_loop(0, dp - 1, peers_sent, 0)
    for s in range(1, tp):
        sz_copy(s).wait_send()
    for s in range(2):
        p, t = q_pair(s)

        @pl.when(t != me.z)
        def _(s=s, p=p, t=t):
            remote(qz.at[s], qf.at[p], qf_send.at[s], qf_recv.at[p], me.d, t).wait_send()


def back(do, grad, xs, wqf, oT, lse, qT, kA, v, pack, dr1):
    tp, rows, width = xs.shape
    dp, share, qwidth = wqf.shape
    chips = dp // 2
    length = rows * tp
    half = rows // 2
    cols = grad.shape[-1]
    S = jax.ShapeDtypeStruct
    vmem = pl.BlockSpec(memory_space=pltpu.VMEM)
    anym = pl.BlockSpec(memory_space=pl.ANY)
    dma = pltpu.SemaphoreType.DMA
    V = pltpu.VMEM
    return pl.pallas_call(
        back_kernel,
        name="back",
        out_shape=(
            S((rows, width), F32),
            S((share, cols), F32),
            S((share, qwidth), F32),
            S((16, 128), F32),
        ),
        in_specs=[anym, anym] + [vmem] * 9,
        out_specs=(vmem,) * 4,
        scratch_shapes=[
            V((tp, rows, 192), BF16), V((192, length), BF16), V((3, 1, length), F32),
            V((3, length, 128), BF16), V((3, HEAD_DIM, length), BF16),
            V((length, 128), F32), V((length, HEAD_DIM), F32), V((192, length), F32), V((tp, rows, qwidth), BF16),
            V((tp, chips, share, cols), BF16), V((tp, chips, share, cols), BF16), V((tp, chips - 1, share, cols), BF16),
            V((tp, share, cols), BF16), V((tp + 1, share, cols), BF16),
            V((tp, rows, width), BF16), V((tp, half, width), BF16), V((tp, half, width), BF16), V((tp, half, width), BF16),
            V((2, half, width), BF16),
            V((dp, share, qwidth), BF16), V((2, chips, share, qwidth), BF16), V((2, share, qwidth), BF16), V((2, share, qwidth), BF16),
            V((dp, 16, 128), F32), V((dp - 1, 16, 128), F32), V((tp, 16, 128), F32),
            dma((4,)), dma((tp,)), dma((tp,)), dma((tp,)), dma((tp,)), dma((tp, 3)), dma((tp, 3)), dma((tp,)), dma((tp + 1,)),
            dma((tp,)), dma((tp,)), dma((tp,)), dma((tp,)), dma((tp,)), dma((2,)), dma((dp,)), dma((2, chips)), dma((2,)), dma((2,)),
            dma((dp - 1,)), dma((dp - 1,)), dma((tp - 1,)), dma((tp,)),
        ],
        compiler_params=pltpu.CompilerParams(
            collective_id=1, has_side_effects=True, vmem_limit_bytes=VMEM_LIMIT
        ),
    )(do, grad, xs, wqf, oT, lse, qT, kA, v, pack, dr1)


def shards(
    tokens, teacher, lengths, loss_mask, loss_scale,
    query_weight, query_bias, key_weight, value_weight, value_bias, mixer_weight, mixer_bias,
    first_gain, first_shift, inner_weight, inner_bias, outer_weight, outer_bias, second_gain, second_shift,
):
    dp, tp = lax.axis_size("dp"), lax.axis_size("tensor")
    if dp != 8 or tp != 4:
        return plain_shards(
            tokens, teacher, lengths, loss_mask, loss_scale,
            query_weight, query_bias, key_weight, value_weight, value_bias, mixer_weight, mixer_bias,
            first_gain, first_shift, inner_weight, inner_bias, outer_weight, outer_bias, second_gain, second_shift,
        )
    z = lax.axis_index("tensor")
    rows, width = tokens.shape
    share = query_weight.shape[0]
    gw = query_weight.shape[1]
    hidden = inner_weight.shape[1]
    hshare = inner_bias.shape[0]
    hrows = -(-hshare // 128)
    pos = z * rows + jnp.arange(rows)
    counted = jnp.logical_and(pos < lengths[0], loss_mask == 1).astype(F32)
    vectors = jnp.stack(
        [query_bias, value_bias, mixer_bias, first_gain, first_shift, outer_bias, second_gain, second_shift]
    ).astype(F32)
    small = jnp.concatenate(
        [
            jnp.pad(vectors, ((0, 0), (0, 128 - share))),
            jnp.full((1, 128), jnp.sum(counted)),
            jnp.pad(inner_bias.astype(F32), (0, hrows * 128 - hshare)).reshape(hrows, 128),
            jnp.zeros((3 - hrows, 128), F32),
            jnp.full((1, 128), lengths[0].astype(F32)),
            jnp.zeros((3, 128), F32),
        ],
        axis=0,
    )
    wq = jnp.concatenate([query_weight, key_weight, value_weight], axis=1)
    wm = jnp.concatenate([inner_weight, outer_weight.T, mixer_weight.T], axis=1)
    oin, wall, smalls, count, xs, wqf, oT, lse, qT, kA, v = front(tokens, wq, wm, small, dp, tp)
    token_total = count[0, 0]
    vecs = jnp.moveaxis(smalls[:, 0:8, 0:share], 0, 1).reshape(8, width)
    ib = smalls[:, 9 : 9 + hrows, :].reshape(dp, hrows * 128)[:, :hshare].reshape(tp, 1, hidden)
    scale = (2.0 * loss_scale / (token_total * width)).reshape(1, 1)
    wall = wall.reshape(tp, width, wm.shape[1])
    layer_output, dr1, do, grad, sums, isums = mid(tokens, teacher, counted[:, None], scale, oin, wall, vecs, ib)
    pack = jnp.concatenate(
        [
            jnp.zeros((dp, 2, 128), F32),
            jnp.pad(jnp.moveaxis(sums[0:6].reshape(6, dp, share), 1, 0), ((0, 0), (0, 0), (0, 128 - share))),
            jnp.broadcast_to(sums[6, 0], (dp, 1, 128)),
            jnp.pad(isums.reshape(dp, hshare), ((0, 0), (0, hrows * 128 - hshare))).reshape(dp, hrows, 128),
            jnp.zeros((dp, 7 - hrows, 128), F32),
        ],
        axis=1,
    )
    grad = grad.reshape(tp, dp // 2, 2, share, wm.shape[1])
    input_grad, gsum, qgrad, ssum = back(do, grad, xs, wqf, oT, lse, qT, kA, v, pack, dr1)
    loss_value = ssum[8, 0] / (token_total * width)
    line = lambda i: ssum[i, :share]
    innerbias_grad = ssum[9 : 9 + hrows].reshape(-1)[:hshare]
    return (
        layer_output,
        loss_value,
        input_grad,
        qgrad[:, 0:gw],
        line(0),
        qgrad[:, gw : 2 * gw],
        qgrad[:, 2 * gw :],
        line(1),
        gsum[:, 2 * hidden :].T,
        line(2),
        line(3),
        line(4),
        gsum[:, 0:hidden],
        innerbias_grad,
        gsum[:, hidden : 2 * hidden].T,
        line(5),
        line(6),
        line(7),
    )


def in_blocks(value, dim, size):
    before, after = (value.shape[:dim], value.shape[dim + 1 :])
    return jnp.moveaxis(value.reshape(*before, size, -1, *after), dim, 0)


def summed_on_arrival(value, axis, dim):
    size = lax.axis_size(axis)
    blocks = lax.all_to_all(in_blocks(value, dim, size), axis, 0, 0, tiled=True)
    return jnp.sum(blocks.astype(jnp.float32), axis=0)


def sent_together(arrays, axis, dim, along):
    both = jnp.concatenate(arrays, axis=along)
    out, at, gathered = (summed_on_arrival(both, axis, dim), 0, [])
    for a in arrays:
        gathered.append(lax.slice_in_dim(out, at, at + a.shape[along], axis=along))
        at += a.shape[along]
    return tuple(gathered)


def contract_last(left_rows, right_rows):
    return lax.dot_general(
        left_rows, right_rows, (((1,), (1,)), ((), ())), preferred_element_type=jnp.float32
    )


def contract_first(left_rows, right_rows):
    return lax.dot_general(
        left_rows, right_rows, (((0,), (0,)), ((), ())), preferred_element_type=jnp.float32
    )


def plain_dot(left_rows, right_rows):
    return jnp.dot(left_rows, right_rows, preferred_element_type=jnp.float32)


def gelu_exact(pre_values):
    return jax.nn.gelu(pre_values, approximate=False)


def plain_norm_forward(values_in, gain_vec, shift_vec):
    centred = values_in - jnp.mean(values_in, axis=1, keepdims=True)
    inv_std = lax.rsqrt(jnp.mean(centred * centred, axis=1, keepdims=True) + norm_eps)
    normed = centred * inv_std
    return (normed * gain_vec + shift_vec, normed, inv_std)


def plain_norm_backward(grad_out, normed, inv_std, gain_vec):
    grad_normed = grad_out * gain_vec
    mean_plain = jnp.mean(grad_normed, axis=1, keepdims=True)
    mean_mixed = jnp.mean(grad_normed * normed, axis=1, keepdims=True)
    grad_in = inv_std * (grad_normed - mean_plain - normed * mean_mixed)
    return (grad_in, jnp.sum(grad_out * normed, axis=0), jnp.sum(grad_out, axis=0))


def plain_shards(
    tokens,
    teacher,
    lengths,
    loss_mask,
    loss_scale,
    query_weight,
    query_bias,
    key_weight,
    value_weight,
    value_bias,
    mixer_weight,
    mixer_bias,
    first_gain,
    first_shift,
    inner_weight,
    inner_bias,
    outer_weight,
    outer_bias,
    second_gain,
    second_shift,
):
    tp_count = lax.axis_size("tensor")
    tp_index = lax.axis_index("tensor")
    dp_count = lax.axis_size("dp")
    dp_index = lax.axis_index("dp")
    local_rows = tokens.shape[0]
    seq_len = local_rows * tp_count
    model_width = tokens.shape[1]
    head_width = query_weight.shape[1]
    hidden_width = inner_weight.shape[1]
    head_count = head_width // HEAD_DIM
    block_count = seq_len // QBLOCK
    score_scale = HEAD_DIM ** (-0.5)
    length_here = lengths[0]
    local_pos = tp_index * local_rows + jnp.arange(local_rows)
    counted = jnp.logical_and(local_pos < length_here, loss_mask == 1).astype(jnp.float32)
    count_local = jnp.sum(counted)
    small_stack = jnp.stack(
        [
            query_bias,
            value_bias,
            mixer_bias,
            first_gain,
            first_shift,
            outer_bias,
            second_gain,
            second_shift,
        ]
    )

    def fetch_params():
        return (
            lax.all_gather(query_weight, "dp", axis=0, tiled=True),
            lax.all_gather(key_weight, "dp", axis=0, tiled=True),
            lax.all_gather(value_weight, "dp", axis=0, tiled=True),
            lax.all_gather(mixer_weight, "dp", axis=1, tiled=True),
            lax.all_gather(inner_weight, "dp", axis=0, tiled=True),
            lax.all_gather(outer_weight, "dp", axis=1, tiled=True),
            lax.all_gather(small_stack, "dp", axis=1, tiled=True),
            lax.all_gather(inner_bias, "dp", axis=0, tiled=True),
        )

    def attn_gather(values_in):
        return lax.all_gather(values_in, "tensor", axis=0, tiled=True)

    def ffn_gather(values_in):
        return lax.all_gather(values_in, "tensor", axis=0, tiled=True)

    (
        query_full,
        key_full,
        value_full,
        mixer_full,
        inner_full,
        outer_full,
        small_full,
        innerb_full,
    ) = fetch_params()
    small_wide = small_full.astype(jnp.float32)
    qbias_mine = lax.dynamic_slice_in_dim(small_wide[0], tp_index * head_width, head_width)
    vbias_mine = lax.dynamic_slice_in_dim(small_wide[1], tp_index * head_width, head_width)
    inner_mine = lax.dynamic_slice_in_dim(
        innerb_full.astype(jnp.float32), tp_index * hidden_width, hidden_width
    )
    seq_rows = attn_gather(tokens)
    queries = (plain_dot(seq_rows, query_full) + qbias_mine).astype(jnp.bfloat16)
    keys_all = plain_dot(seq_rows, key_full).astype(jnp.bfloat16)
    values_all = (plain_dot(seq_rows, value_full) + vbias_mine).astype(jnp.bfloat16)
    keys_three = keys_all.reshape(seq_len, head_count, HEAD_DIM)
    values_three = values_all.reshape(seq_len, head_count, HEAD_DIM)
    key_valid = jnp.arange(seq_len) < length_here

    def score_block(query_block):
        scores = (
            jnp.einsum("qhd,khd->hqk", query_block, keys_three, preferred_element_type=jnp.float32)
            * score_scale
        )
        return jnp.where(key_valid[None, None, :], scores, masked_score)

    def forward_block(query_block):
        scores = score_block(query_block)
        row_top = jnp.max(scores, axis=2, keepdims=True)
        exp_scores = jnp.exp(scores - row_top)
        row_total = jnp.sum(exp_scores, axis=2, keepdims=True)
        prob_low = (exp_scores / row_total).astype(jnp.bfloat16)
        mixed_rows = jnp.einsum(
            "hqk,khd->qhd", prob_low, values_three, preferred_element_type=jnp.float32
        )
        return (mixed_rows.astype(jnp.bfloat16), (row_top + jnp.log(row_total))[:, :, 0])

    query_blocks = queries.reshape(block_count, QBLOCK, head_count, HEAD_DIM)
    attended, log_sums = lax.map(forward_block, query_blocks)
    attended = attended.reshape(seq_len, head_width)
    attn_out = lax.psum_scatter(
        plain_dot(attended, mixer_full).astype(jnp.bfloat16),
        "tensor",
        scatter_dimension=0,
        tiled=True,
    ).astype(jnp.float32)
    first_sum = tokens.astype(jnp.float32) + attn_out + small_wide[2]
    hidden_one, normed_one, inv_one = plain_norm_forward(first_sum, small_wide[3], small_wide[4])
    hidden_low = hidden_one.astype(jnp.bfloat16)
    ffn_rows = ffn_gather(hidden_low)
    pre_act = plain_dot(ffn_rows, inner_full) + inner_mine
    act_full, gelu_pull = jax.vjp(gelu_exact, pre_act)
    activated = act_full.astype(jnp.bfloat16)
    ffn_out = lax.psum_scatter(
        plain_dot(activated, outer_full).astype(jnp.bfloat16),
        "tensor",
        scatter_dimension=0,
        tiled=True,
    ).astype(jnp.float32)
    second_sum = hidden_one + ffn_out + small_wide[5]
    final_rows, normed_two, inv_two = plain_norm_forward(second_sum, small_wide[6], small_wide[7])
    layer_output = final_rows.astype(jnp.bfloat16)
    diff_rows = final_rows - teacher.astype(jnp.float32)
    loss_local = jnp.sum(counted * jnp.sum(diff_rows * diff_rows, axis=1))
    loss_total, token_total = lax.psum((loss_local, count_local), ("dp", "tensor"))
    grad_scale = 2.0 * loss_scale / (token_total * model_width)
    grad_final = grad_scale * counted[:, None] * diff_rows
    (
        query_full,
        key_full,
        value_full,
        mixer_full,
        inner_full,
        outer_full,
        small_full,
        innerb_full,
    ) = fetch_params()
    ffn_rows = ffn_gather(hidden_low)
    grad_second, secondgain_part, secondshift_part = plain_norm_backward(
        grad_final, normed_two, inv_two, small_wide[6]
    )
    outerbias_part = jnp.sum(grad_second, axis=0)
    grad_ffn_rows = lax.all_gather(grad_second.astype(jnp.bfloat16), "tensor", axis=0, tiled=True)
    grad_act = contract_last(grad_ffn_rows, outer_full)
    outer_local = contract_first(activated, grad_ffn_rows)
    grad_pre = gelu_pull(grad_act)[0].astype(jnp.bfloat16)
    innerbias_part = jnp.sum(grad_pre, axis=0, dtype=jnp.float32)
    inner_local = contract_first(ffn_rows, grad_pre)
    grad_hidden = lax.psum_scatter(
        contract_last(grad_pre, inner_full).astype(jnp.bfloat16),
        "tensor",
        scatter_dimension=0,
        tiled=True,
    ).astype(jnp.float32)
    inner_grad, outer_grad = (
        lax.psum_scatter(inner_local, "dp", scatter_dimension=0, tiled=True),
        lax.psum_scatter(outer_local, "dp", scatter_dimension=1, tiled=True),
    )
    grad_first, firstgain_part, firstshift_part = plain_norm_backward(
        grad_second + grad_hidden, normed_one, inv_one, small_wide[3]
    )
    mixerbias_part = jnp.sum(grad_first, axis=0)
    grad_attn_rows = lax.all_gather(grad_first.astype(jnp.bfloat16), "tensor", axis=0, tiled=True)
    grad_attended = contract_last(grad_attn_rows, mixer_full).astype(jnp.bfloat16)
    mixer_local = contract_first(attended, grad_attn_rows)
    grad_blocks = grad_attended.reshape(block_count, QBLOCK, head_count, HEAD_DIM)

    def backward_block(carried, block_in):
        key_acc, value_acc = carried
        query_block, grad_block, lse_block = block_in
        scores = score_block(query_block)
        prob_full = jnp.exp(scores - lse_block[:, :, None])
        prob_low = prob_full.astype(jnp.bfloat16)
        grad_prob = jnp.einsum(
            "qhd,khd->hqk", grad_block, values_three, preferred_element_type=jnp.float32
        )
        row_dot = jnp.sum(prob_full * grad_prob, axis=2, keepdims=True)
        grad_scores = (prob_full * (grad_prob - row_dot)).astype(jnp.bfloat16)
        grad_query = (
            jnp.einsum("hqk,khd->qhd", grad_scores, keys_three, preferred_element_type=jnp.float32)
            * score_scale
        ).astype(jnp.bfloat16)
        key_acc = (
            key_acc
            + jnp.einsum(
                "hqk,qhd->khd", grad_scores, query_block, preferred_element_type=jnp.float32
            )
            * score_scale
        )
        value_acc = value_acc + jnp.einsum(
            "hqk,qhd->khd", prob_low, grad_block, preferred_element_type=jnp.float32
        )
        return ((key_acc, value_acc), grad_query)

    zero_acc = jnp.zeros((seq_len, head_count, HEAD_DIM), jnp.float32)
    (key_acc, value_acc), grad_queries = lax.scan(
        backward_block, (zero_acc, zero_acc), (query_blocks, grad_blocks, log_sums)
    )
    grad_queries = grad_queries.reshape(seq_len, head_width)
    grad_keys = key_acc.reshape(seq_len, head_width).astype(jnp.bfloat16)
    grad_values = value_acc.reshape(seq_len, head_width).astype(jnp.bfloat16)
    seq_rows = attn_gather(tokens)
    query_local = contract_first(seq_rows, grad_queries)
    key_local = contract_first(seq_rows, grad_keys)
    value_local = contract_first(seq_rows, grad_values)
    querybias_part = jnp.sum(grad_queries, axis=0, dtype=jnp.float32)
    valuebias_part = jnp.sum(grad_values, axis=0, dtype=jnp.float32)
    total_term = contract_last(grad_queries, query_full)
    total_term = total_term + contract_last(grad_keys, key_full)
    grad_tokens = lax.psum_scatter(
        (total_term + contract_last(grad_values, value_full)).astype(jnp.bfloat16),
        "tensor",
        scatter_dimension=0,
        tiled=True,
    ).astype(jnp.float32)
    input_grad = grad_first + grad_tokens
    query_grad, key_grad, value_grad, mixer_grad = (
        *sent_together(
            (
                query_local.astype(jnp.bfloat16),
                key_local.astype(jnp.bfloat16),
                value_local.astype(jnp.bfloat16),
            ),
            "dp",
            0,
            1,
        ),
        summed_on_arrival(mixer_local.astype(jnp.bfloat16), "dp", 1),
    )

    def spread_part(part_vec, full_width):
        return lax.dynamic_update_slice_in_dim(
            jnp.zeros((full_width,), jnp.float32), part_vec, tp_index * part_vec.shape[0], 0
        )

    small_terms = jnp.stack(
        [
            spread_part(querybias_part, model_width),
            spread_part(valuebias_part, model_width),
            mixerbias_part,
            firstgain_part,
            firstshift_part,
            outerbias_part,
            secondgain_part,
            secondshift_part,
        ]
    )
    inner_terms = spread_part(innerbias_part, hidden_width * tp_count)
    small_sum, inner_sum = lax.psum((small_terms, inner_terms), ("dp", "tensor"))
    loss_value = loss_total / (token_total * model_width)
    width_share = model_width // dp_count
    small_mine = lax.dynamic_slice_in_dim(small_sum, dp_index * width_share, width_share, 1)
    hidden_share = inner_sum.shape[0] // dp_count
    innerbias_grad = lax.dynamic_slice_in_dim(inner_sum, dp_index * hidden_share, hidden_share, 0)
    return (
        layer_output,
        loss_value,
        input_grad,
        query_grad,
        small_mine[0],
        key_grad,
        value_grad,
        small_mine[1],
        mixer_grad,
        small_mine[2],
        small_mine[3],
        small_mine[4],
        inner_grad,
        innerbias_grad,
        outer_grad,
        small_mine[5],
        small_mine[6],
        small_mine[7],
    )


def solution(mesh):
    return jax.shard_map(
        shards,
        mesh=mesh,
        in_specs=(
            P(("dp", "tensor"), None),
            P(("dp", "tensor"), None),
            P("dp"),
            P(("dp", "tensor")),
            P(),
            P("dp", "tensor"),
            P("dp"),
            P("dp", "tensor"),
            P("dp", "tensor"),
            P("dp"),
            P("tensor", "dp"),
            P("dp"),
            P("dp"),
            P("dp"),
            P("dp", "tensor"),
            P("dp"),
            P("tensor", "dp"),
            P("dp"),
            P("dp"),
            P("dp"),
        ),
        out_specs=(
            P(("dp", "tensor"), None),
            P(),
            P(("dp", "tensor"), None),
            P("dp", "tensor"),
            P("dp"),
            P("dp", "tensor"),
            P("dp", "tensor"),
            P("dp"),
            P("tensor", "dp"),
            P("dp"),
            P("dp"),
            P("dp"),
            P("dp", "tensor"),
            P("dp"),
            P("tensor", "dp"),
            P("dp"),
            P("dp"),
            P("dp"),
        ),
        check_vma=False,
    )
```

```python
import functools
import jax
import jax.numpy as jnp
from jax import lax
from jax.experimental import pallas as pl
from jax.experimental.pallas import tpu as pltpu
from jax.sharding import PartitionSpec as P

HEAD_DIM = 64
QBLOCK = 512
MESH = pl.DeviceIdType.MESH
F32 = jnp.float32
BF16 = jnp.bfloat16
norm_eps = 1e-05
masked_score = -1e30
VMEM_LIMIT = 60 * 1024 * 1024


def dot(left, right, left_dim, right_dim):
    return lax.dot_general(
        left, right, (((left_dim,), (right_dim,)), ((), ())), preferred_element_type=F32
    )


def remote(src, dst, send, recv, d, t):
    return pltpu.make_async_remote_copy(
        src_ref=src,
        dst_ref=dst,
        send_sem=send,
        recv_sem=recv,
        device_id={"dp": d, "tensor": t},
        device_id_type=MESH,
    )


def arrival(dst, recv):
    return pltpu.make_async_copy(dst, dst, recv)


class Place:
    def __init__(self):
        self.dp = lax.axis_size("dp")
        self.tp = lax.axis_size("tensor")
        self.d = lax.axis_index("dp")
        self.z = lax.axis_index("tensor")
        self.core = lax.rem(self.d, 2)
        self.chip = self.d // 2
        self.chips = self.dp // 2
        self.base = self.chip * 2
        self.sibling = self.base + 1 - self.core
        self.pair = self.z // 2
        self.low = lax.rem(self.z, 2)
        self.group = 2 * self.low + self.core
        self.buddy = 2 * self.pair + 1 - self.low
        self.owner = self.base + self.pair
        self.near_here = 1 + self.pair
        self.near_there = 2 - self.pair
        side = self.chip + 1 - 2 * lax.rem(self.chip, 2)
        across = lax.rem(self.chip + 2, 4)
        self.first = jnp.where(self.core == 0, side, across)
        self.second = jnp.where(self.core == 0, across, side)
        self.diagonal = 3 - self.chip
        self.around = (self.buddy, self.near_there, 3 * (1 - self.pair))


def greet(place):
    barrier = pltpu.get_barrier_semaphore()
    count = 0
    for t in range(place.tp):
        for c in range(2):
            other = jnp.logical_not(jnp.logical_and(place.z == t, place.core == c))

            @pl.when(other)
            def _(t=t, c=c):
                pl.semaphore_signal(
                    barrier, inc=1, device_id={"dp": place.base + c, "tensor": t}, device_id_type=MESH
                )

            count += 1
    count -= 1

    def plane(i, _):
        chip = lax.rem(place.chip + 1 + i, place.chips)
        for c in range(2):
            pl.semaphore_signal(
                barrier, inc=1, device_id={"dp": chip * 2 + c, "tensor": place.z}, device_id_type=MESH
            )
        return 0

    lax.fori_loop(0, place.chips - 1, plane, 0)
    count += 2 * (place.chips - 1)
    pl.semaphore_wait(barrier, count)


def front_kernel(
    x_ref, wq_ref, wm_ref, sm_ref,
    oin_ref, wall_ref, smalls_ref, count_ref, xs_ref, wqf_ref, oT_ref, lse_ref, qT_ref, kA_ref, v_ref,
    wqz, counts, vT, scores, o_buf, wqT, wkp, wvp, wvT,
    sm_send, sm_recv, cn_send, cn_recv, wz_send, wz_recv, wp_send, wp_recv,
    x_send, x_recv, xr_send, xf_send, mz_send, mz_recv, mp_send, mp_recv, ms_send, ms_recv, o_send, o_recv,
):
    me = Place()
    dp, tp, chips = me.dp, me.tp, me.chips
    rows, width = x_ref.shape
    half = rows // 2
    length = rows * tp
    share = wq_ref.shape[0]
    heads = 3
    greet(me)

    def each_peer(f):
        def step(i, _):
            f(i, lax.rem(me.d + 1 + i, dp))
            return 0

        lax.fori_loop(0, dp - 1, step, 0)

    def small_copy(i, peer):
        return remote(sm_ref, smalls_ref.at[me.d], sm_send.at[i], sm_recv.at[me.d], peer, me.z)

    each_peer(lambda i, peer: small_copy(i, peer).start())
    smalls_ref[me.d] = sm_ref[...]

    for s in range(2):
        target = me.z // 2 + 2 * s
        src, dst = wq_ref, wqz.at[me.low]

        @pl.when(target == me.z)
        def _(s=s, dst=dst):
            pltpu.make_async_copy(wq_ref, dst, wz_recv.at[me.low]).start()

        @pl.when(target != me.z)
        def _(s=s, dst=dst, target=target):
            remote(wq_ref, dst, wz_send.at[s], wz_recv.at[me.low], me.d, target).start()

    is_near = me.z == me.near_here
    is_end = jnp.logical_not(is_near)
    pltpu.make_async_copy(wm_ref, wall_ref.at[me.z, me.d], mz_recv.at[me.z]).start()

    def along_z(unit, t, sem, to):
        return remote(unit, wall_ref.at[t, me.d], mz_send.at[sem], mz_recv.at[t], me.d, to)

    pl.when(me.z > 0)(lambda: along_z(wm_ref, me.z, 0, me.z - 1).start())
    pl.when(me.z < tp - 1)(lambda: along_z(wm_ref, me.z, 1, me.z + 1).start())

    def goes_up(t):
        return jnp.logical_and(t < me.z, me.z < tp - 1)

    def goes_down(t):
        return jnp.logical_and(t > me.z, me.z > 0)

    is_owner = me.core == me.pair
    for h in range(2):
        part = pl.ds(h * half, half)

        @pl.when(is_owner)
        def _(h=h, part=part):
            pltpu.make_async_copy(x_ref.at[part], xs_ref.at[me.z, part], x_recv.at[me.z, h]).start()
            remote(x_ref.at[part], xs_ref.at[me.z, part], x_send.at[h], x_recv.at[me.z, h], me.base + h, me.buddy).start()
            remote(x_ref.at[part], xs_ref.at[me.z, part], xr_send.at[0, h], x_recv.at[me.z, h], me.sibling, me.z).start()

        @pl.when(jnp.logical_not(is_owner))
        def _(h=h, part=part):
            remote(x_ref.at[part], xs_ref.at[me.z, part], x_send.at[h], x_recv.at[me.z, h], me.base + h, me.near_there).start()

    def wq_plane(s, k):
        dst = wqf_ref.at[me.d]
        return remote(wqz.at[s], dst, wp_send.at[s, k], wp_recv.at[me.d], 2 * k + s, me.z)

    for s in range(2):
        arrival(wqz.at[s], wz_recv.at[s]).wait()

        def step(i, _, s=s):
            k = lax.rem(me.chip + 1 + i, chips)
            here = 2 * k + s == me.d

            @pl.when(here)
            def _():
                pltpu.make_async_copy(wqz.at[s], wqf_ref.at[me.d], wp_recv.at[me.d]).start()

            @pl.when(jnp.logical_not(here))
            def _():
                wq_plane(s, k).start()

            return 0

        lax.fori_loop(0, chips, step, 0)

    def in_plane(unit, t, k, sem, to):
        return remote(unit, wall_ref.at[t, 2 * k + me.core], mp_send.at[t, sem], mp_recv.at[t, k], 2 * to + me.core, me.z)

    def plane_units(t, unit):
        in_plane(unit, t, me.chip, 0, me.first).start()
        in_plane(unit, t, me.chip, 1, me.second).start()

    def to_sibling(t, k):
        unit = wall_ref.at[t, 2 * k + me.core]
        return remote(unit, unit, ms_send.at[t, k], ms_recv.at[t, k], me.sibling, me.z)

    def own_unit(t):
        unit = wall_ref.at[t, me.d]
        arrival(unit, mz_recv.at[t]).wait()
        pl.when(goes_up(t))(lambda: along_z(unit, t, 2 + t, me.z + 1).start())
        pl.when(goes_down(t))(lambda: along_z(unit, t, 2 + t, me.z - 1).start())
        plane_units(t, unit)
        to_sibling(t, me.chip).start()

    def plane_unit(t, k):
        unit = wall_ref.at[t, 2 * k + me.core]
        arrival(unit, mp_recv.at[t, k]).wait()
        return unit

    def plane_forward(t):
        unit = plane_unit(t, me.first)
        in_plane(unit, t, me.first, 2, me.second).start()
        to_sibling(t, me.first).start()

    def plane_rest(t):
        for k in (me.second, me.diagonal):
            plane_unit(t, k)
            to_sibling(t, k).start()

    plane_units(me.z, wm_ref)
    remote(wm_ref, wall_ref.at[me.z, me.d], ms_send.at[me.z, me.chip], ms_recv.at[me.z, me.chip], me.sibling, me.z).start()

    mine = pl.ds(pl.multiple_of(me.core * half, half), half)
    other = pl.ds(pl.multiple_of((1 - me.core) * half, half), half)
    far_first = 2 * (1 - me.pair) + me.pair
    far_second = 2 * (1 - me.pair) + 1 - me.pair
    blocks_in = (
        jnp.where(is_near, far_first, me.buddy),
        jnp.where(is_near, far_second, far_first),
        jnp.where(is_near, me.buddy, far_second),
    )

    def relay(n):
        j = blocks_in[n]
        part = xs_ref.at[j, mine]
        arrival(part, x_recv.at[j, me.core]).wait()
        remote(part, part, xr_send.at[1 + n, 0], x_recv.at[j, me.core], me.sibling, me.z).start()
        if n < 2:
            pl.when(is_near)(lambda: remote(part, part, xf_send.at[n], x_recv.at[j, me.core], me.d, me.buddy).start())

    own_unit(me.around[0])
    relay(0)
    relay(1)

    def small_wait(i, peer):
        arrival(smalls_ref.at[peer], sm_recv.at[peer]).wait()

    each_peer(small_wait)
    plane_count = smalls_ref[0][8:16]
    for k in range(1, dp):
        plane_count = plane_count + smalls_ref[k][8:16]
    counts[me.z] = plane_count
    for s in range(1, tp):
        remote(counts.at[me.z], counts.at[me.z], cn_send.at[s - 1], cn_recv.at[me.z], me.d, lax.rem(me.z + s, tp)).start()

    for k in range(dp):
        arrival(wqf_ref.at[k], wp_recv.at[k]).wait()
    zero = jnp.zeros((share, HEAD_DIM), BF16)
    gw = heads * HEAD_DIM
    for k in range(dp):
        w = wqf_ref[k]
        at = slice(k * share, (k + 1) * share)
        pads = []
        for m in range(3):
            cols = []
            for h in range(heads):
                cols += [w[:, m * gw + h * HEAD_DIM : m * gw + (h + 1) * HEAD_DIM], zero]
            pads.append(jnp.concatenate(cols, axis=1))
        wkp[at, :] = pads[1]
        wvp[at, :] = pads[2]
        scores[0, at, 0:384] = pads[0].astype(F32)
    wqT[...] = scores[0, 0:width, 0:384].T.astype(BF16)
    wvT[...] = wvp[...].astype(F32).T.astype(BF16)

    blocks = gw // share
    row_bias = jnp.zeros((8, 384), F32)
    col_bias = jnp.zeros((384, 8), F32)
    r_in = lax.broadcasted_iota(jnp.int32, (128, 384), 0)
    r_out = lax.broadcasted_iota(jnp.int32, (128, 384), 1)
    c_out = lax.broadcasted_iota(jnp.int32, (384, 128), 0)
    c_in = lax.broadcasted_iota(jnp.int32, (384, 128), 1)

    def padded(col):
        return (col // HEAD_DIM) * 128 + lax.rem(col, HEAD_DIM)

    for b in range(blocks):
        vecs = smalls_ref[me.group * blocks + b][0:8].astype(BF16)
        sel = jnp.logical_and(padded(r_in + b * share) == r_out, r_in < share)
        row_bias = row_bias + dot(vecs, jnp.where(sel, 1.0, 0.0).astype(BF16), 1, 0)
        sel = jnp.logical_and(padded(c_in + b * share) == c_out, c_in < share)
        col_bias = col_bias + dot(jnp.where(sel, 1.0, 0.0).astype(BF16), vecs, 1, 1)
    q_bias = col_bias[:, 0:1]
    v_bias_col = col_bias[:, 1:2]
    v_bias = row_bias[1:2, :]
    valid = smalls_ref[me.base + me.pair][12:13, 0:1]

    lane = lax.broadcasted_iota(jnp.int32, (rows, 128), 1)
    srow = lax.broadcasted_iota(jnp.int32, (128, rows), 0)

    def project(j):
        at = pl.ds(pl.multiple_of(j * rows, rows), rows)
        xb = xs_ref[j]
        keys = dot(xb, wkp[...], 1, 0)
        queries = dot(wqT[...], xb, 1, 1) + q_bias
        vals = dot(xb, wvp[...], 1, 0) + v_bias
        valsT = dot(wvT[...], xb, 1, 1) + v_bias_col
        pos = (j * rows + lax.broadcasted_iota(jnp.int32, (rows, 128), 0)).astype(F32)
        bias = jnp.where(pos < valid, 0.0, masked_score)
        for h in range(heads):
            span = slice(h * 128, (h + 1) * 128)
            vT[h * HEAD_DIM : (h + 1) * HEAD_DIM, at] = valsT[h * 128 : h * 128 + HEAD_DIM].astype(BF16)
            kA_ref[h, at, :] = jnp.where(lane == HEAD_DIM, bias, keys[:, span]).astype(BF16)
            qh = queries[span].astype(BF16) * BF16(HEAD_DIM**-0.5)
            qT_ref[h, :, at] = jnp.where(srow == HEAD_DIM, BF16(1), qh)
            v_ref[h, at, :] = vals[:, span].astype(BF16)

    arrival(xs_ref.at[me.z, pl.ds(0, half)], x_recv.at[me.z, 0]).wait()
    arrival(xs_ref.at[me.z, pl.ds(half, half)], x_recv.at[me.z, 1]).wait()
    project(me.z)
    relay(2)
    pl.when(is_near)(functools.partial(own_unit, me.around[1]))
    plane_forward(me.z)

    def project_next(i, _):
        j = jnp.where(i == 0, blocks_in[0], jnp.where(i == 1, blocks_in[1], blocks_in[2]))
        arrival(xs_ref.at[j, other], x_recv.at[j, 1 - me.core]).wait()
        project(j)
        return 0

    lax.fori_loop(0, tp - 1, project_next, 0)
    pl.when(is_near)(functools.partial(own_unit, me.around[2]))
    plane_forward(me.around[0])

    chunk = 256
    pieces = length // chunk

    def attend(i, _):
        j = lax.rem(me.z + 1 + i, tp)
        at = pl.ds(pl.multiple_of(j * rows, rows), rows)
        tops = []
        for h in range(heads):
            qt = qT_ref[h, :, at]
            top = None
            for c in range(pieces):
                s = dot(kA_ref[h, c * chunk : (c + 1) * chunk, :], qt, 1, 0)
                scores[h, c * chunk : (c + 1) * chunk, :] = s
                peak = jnp.max(s, axis=0, keepdims=True)
                top = peak if top is None else jnp.maximum(top, peak)
            tops.append(top)
        outs = []
        for h in range(heads):
            total, mixed = None, None
            for c in range(pieces):
                p = jnp.exp(scores[h, c * chunk : (c + 1) * chunk, :] - tops[h])
                part = jnp.sum(p, axis=0, keepdims=True)
                term = dot(vT[h * HEAD_DIM : (h + 1) * HEAD_DIM, c * chunk : (c + 1) * chunk], p.astype(BF16), 1, 0)
                total = part if total is None else total + part
                mixed = term if mixed is None else mixed + term
            mixed = mixed / total
            oT_ref[h * HEAD_DIM : (h + 1) * HEAD_DIM, at] = mixed
            lse_ref[h, :, at] = tops[h] + jnp.log(total)
            outs.append(mixed)
        o_buf[j] = jnp.concatenate(outs, axis=0).T.astype(BF16)
        here = jnp.logical_and(j == me.z, is_owner)

        @pl.when(here)
        def _():
            pltpu.make_async_copy(o_buf.at[j], oin_ref.at[me.group], o_recv.at[me.group]).start()

        @pl.when(jnp.logical_not(here))
        def _():
            remote(o_buf.at[j], oin_ref.at[me.group], o_send.at[i], o_recv.at[me.group], me.owner, j).start()

        for n in (1, 2):
            pl.when(jnp.logical_and(is_end, i == n - 1))(functools.partial(own_unit, me.around[n]))
        pl.when(i == 0)(functools.partial(plane_rest, me.z))
        pl.when(jnp.logical_and(is_near, i == 0))(functools.partial(plane_forward, me.around[1]))
        pl.when(jnp.logical_and(is_end, i == 2))(functools.partial(plane_forward, me.around[1]))
        pl.when(jnp.logical_and(is_near, i == 2))(functools.partial(plane_forward, me.around[2]))
        pl.when(jnp.logical_and(is_end, i == 3))(functools.partial(plane_forward, me.around[2]))
        return 0

    lax.fori_loop(0, tp, attend, 0)

    for t in me.around:
        plane_rest(t)

    arrival(wall_ref.at[me.z, me.d], mz_recv.at[me.z]).wait()
    for s in range(1, tp):
        t = lax.rem(me.z + s, tp)
        arrival(counts.at[t], cn_recv.at[t]).wait()
    total = counts[0]
    for t in range(1, tp):
        total = total + counts[t]
    count_ref[...] = total
    for g in range(4):
        arrival(oin_ref.at[g], o_recv.at[g]).wait()

    def sibling_units(n, _):
        t, k = n // chips, lax.rem(n, chips)
        arrival(wall_ref.at[t, 2 * k + 1 - me.core], ms_recv.at[t, k]).wait()
        to_sibling(t, k).wait_send()
        return 0

    lax.fori_loop(0, tp * chips, sibling_units, 0)

    def sent(n, _):
        t, i = n // (chips - 1), lax.rem(n, chips - 1)
        in_plane(wm_ref, t, me.chip, i, me.first).wait_send()
        return 0

    lax.fori_loop(0, tp * (chips - 1), sent, 0)
    each_peer(lambda i, peer: small_copy(i, peer).wait_send())
    for s in range(2):

        @pl.when(me.z // 2 + 2 * s != me.z)
        def _(s=s):
            remote(wq_ref, wqz.at[0], wz_send.at[s], wz_recv.at[0], me.sibling, me.z).wait_send()

        def step(i, _, s=s):
            k = lax.rem(me.chip + 1 + i, chips)

            @pl.when(2 * k + s != me.d)
            def _():
                wq_plane(s, k).wait_send()

            return 0

        lax.fori_loop(0, chips, step, 0)
    for s in range(tp - 1):
        remote(counts.at[0], counts.at[0], cn_send.at[s], cn_recv.at[0], me.sibling, me.z).wait_send()

    def z_sent(sem):
        along_z(wm_ref, 0, sem, 0).wait_send()

    pl.when(me.z > 0)(functools.partial(z_sent, 0))
    pl.when(me.z < tp - 1)(functools.partial(z_sent, 1))
    for t in range(tp):
        pl.when(jnp.logical_or(goes_up(t), goes_down(t)))(functools.partial(z_sent, 2 + t))

    def x_sent(sem):
        remote(x_ref.at[pl.ds(0, half)], xs_ref.at[0, pl.ds(0, half)], sem, x_recv.at[0, 0], me.sibling, me.z).wait_send()

    for h in range(2):
        x_sent(x_send.at[h])

        @pl.when(is_owner)
        def _(h=h):
            x_sent(xr_send.at[0, h])

    for n in range(3):
        x_sent(xr_send.at[1 + n, 0])

    @pl.when(is_near)
    def _():
        for n in range(2):
            x_sent(xf_send.at[n])

    def o_sent(i, _):
        j = lax.rem(me.z + 1 + i, tp)

        @pl.when(jnp.logical_not(jnp.logical_and(j == me.z, is_owner)))
        def _():
            remote(o_buf.at[0], oin_ref.at[0], o_send.at[i], o_recv.at[0], me.sibling, me.z).wait_send()

        return 0

    lax.fori_loop(0, tp, o_sent, 0)


def front(x, wq, wm, small, dp, tp):
    rows, width = x.shape
    length = rows * tp
    share = wq.shape[0]
    chips = dp // 2
    S = jax.ShapeDtypeStruct
    vmem = pl.BlockSpec(memory_space=pltpu.VMEM)
    anym = pl.BlockSpec(memory_space=pl.ANY)
    dma = pltpu.SemaphoreType.DMA
    return pl.pallas_call(
        front_kernel,
        name="front",
        out_shape=(
            S((4, rows, 192), BF16),
            S((tp, dp, share, wm.shape[1]), BF16),
            S((dp, 16, 128), F32),
            S((8, 128), F32),
            S((tp, rows, width), BF16),
            S((dp, share, wq.shape[1]), BF16),
            S((192, length), F32),
            S((3, 1, length), F32),
            S((3, 128, length), BF16),
            S((3, length, 128), BF16),
            S((3, length, 128), BF16),
        ),
        in_specs=[vmem] * 4,
        out_specs=(anym, anym) + (vmem,) * 9,
        scratch_shapes=[
            pltpu.VMEM((2, share, wq.shape[1]), BF16),
            pltpu.VMEM((tp, 8, 128), F32),
            pltpu.VMEM((192, length), BF16),
            pltpu.VMEM((3, length, rows), F32),
            pltpu.VMEM((tp, rows, 192), BF16),
            pltpu.VMEM((384, width), BF16),
            pltpu.VMEM((width, 384), BF16),
            pltpu.VMEM((width, 384), BF16),
            pltpu.VMEM((384, width), BF16),
            dma((dp - 1,)), dma((dp,)), dma((tp - 1,)), dma((tp,)),
            dma((2,)), dma((2,)), dma((2, chips)), dma((dp,)),
            dma((2,)), dma((tp, 2)), dma((4, 2)), dma((2,)),
            dma((tp + 2,)), dma((tp,)), dma((tp, chips - 1)), dma((tp, chips)), dma((tp, chips)), dma((tp, chips)),
            dma((tp,)), dma((4,)),
        ],
        compiler_params=pltpu.CompilerParams(
            collective_id=0, has_side_effects=True, vmem_limit_bytes=VMEM_LIMIT
        ),
    )(x, wq, wm, small)


SQRT_HALF = 0.7071067811865476
INV_SQRT_2PI = 0.3989422804014327


def norm_forward(values, gain, shift):
    centred = values - jnp.mean(values, axis=1, keepdims=True)
    inv = lax.rsqrt(jnp.mean(centred * centred, axis=1, keepdims=True) + norm_eps)
    normed = centred * inv
    return normed * gain + shift, normed, inv


def norm_backward(grad_out, normed, inv, gain):
    g = grad_out * gain
    plain = jnp.mean(g, axis=1, keepdims=True)
    mixed = jnp.mean(g * normed, axis=1, keepdims=True)
    return inv * (g - plain - normed * mixed)


def column_sum(values):
    return jnp.sum(values, axis=0, keepdims=True)


def mid_kernel(
    x_ref, teacher_ref, counted_ref, scale_ref, count_ref, oin_ref, wall_ref, smalls_ref,
    out_ref, dr1_ref, do_ref, grad_ref, pack_ref,
    slope_ref, act_ref, f_ref, n1_ref, acc_ref, hT_ref, dfT_ref, vec_ref, ib_ref, small_ref, ismall_ref,
):
    groups = wall_ref.shape[0]
    width = x_ref.shape[1]
    gw = oin_ref.shape[2]
    inner = slice(0, width)
    outer = slice(width, 2 * width)
    mixer = slice(2 * width, 2 * width + gw)
    vec = lambda i: vec_ref[i : i + 1, :]
    dp = smalls_ref.shape[0]
    share = width // dp
    per = dp // groups
    hrows = ib_ref.shape[2] // per // 128
    for d in range(dp):
        vec_ref[:, d * share : (d + 1) * share] = smalls_ref[d, 0:8, 0:share]
        for r in range(hrows):
            at = (d % per * hrows + r) * 128
            ib_ref[d // per, :, at : at + 128] = smalls_ref[d, 9 + r : 10 + r, :]

    acc_ref[...] = x_ref[...].astype(F32) + vec(2)
    for g in range(groups):
        acc_ref[...] += dot(oin_ref[g], wall_ref[g, :, mixer], 1, 1)
    hidden, normed1, inv1 = norm_forward(acc_ref[...], vec(3), vec(4))
    n1_ref[...] = normed1
    low = hidden.astype(BF16)
    hT_ref[...] = hidden.T.astype(BF16)
    f_ref[...] = hidden + vec(5)

    def ffn_forward(g, _):
        up = dot(low, wall_ref[g, :, inner], 1, 0) + ib_ref[g]
        below = 0.5 * (1.0 + lax.erf(up * SQRT_HALF))
        slope_ref[g] = below + up * (INV_SQRT_2PI * jnp.exp(-0.5 * up * up))
        act = (up * below).astype(BF16)
        act_ref[g] = act
        f_ref[...] += dot(act, wall_ref[g, :, outer], 1, 1)
        return 0

    lax.fori_loop(0, groups, ffn_forward, 0)
    final, normed2, inv2 = norm_forward(f_ref[...], vec(6), vec(7))
    out_ref[...] = final.astype(BF16)
    diff = final - teacher_ref[...].astype(F32)
    counted = counted_ref[...]
    small_ref[...] = jnp.zeros_like(small_ref)
    small_ref[6:7, 0:1] = jnp.sum(counted * jnp.sum(diff * diff, axis=1, keepdims=True), axis=0, keepdims=True)
    scale = 2.0 * scale_ref[0, 0] / (count_ref[0:1, 0:1] * width)
    grad = (scale * counted) * diff
    small_ref[4:5, :] = column_sum(grad * normed2)
    small_ref[5:6, :] = column_sum(grad)
    dr2 = norm_backward(grad, normed2, inv2, vec(6))
    small_ref[3:4, :] = column_sum(dr2)
    acc_ref[...] = dr2
    df = dr2.astype(BF16)
    dfT_ref[...] = dr2.T.astype(BF16)

    def ffn_backward(g, _):
        du = (dot(df, wall_ref[g, :, outer], 1, 0) * slope_ref[g]).astype(BF16)
        ismall_ref[g] = column_sum(du.astype(F32))
        acc_ref[...] += dot(du, wall_ref[g, :, inner], 1, 1)
        grad_ref[g, :, inner] = dot(hT_ref[...], du, 1, 0).astype(BF16)
        grad_ref[g, :, outer] = dot(dfT_ref[...], act_ref[g], 1, 0).astype(BF16)
        return 0

    lax.fori_loop(0, groups, ffn_backward, 0)
    dh1 = acc_ref[...]
    normed1 = n1_ref[...]
    small_ref[1:2, :] = column_sum(dh1 * normed1)
    small_ref[2:3, :] = column_sum(dh1)
    dr1 = norm_backward(dh1, normed1, inv1, vec(3))
    small_ref[0:1, :] = column_sum(dr1)
    dr1_ref[...] = dr1
    da = dr1.astype(BF16)
    daT = dr1.T.astype(BF16)
    for g in range(groups):
        do_ref[g] = dot(da, wall_ref[g, :, mixer], 1, 0).astype(BF16)
        grad_ref[g, :, mixer] = dot(daT, oin_ref[g], 1, 0).astype(BF16)
    pack_ref[...] = jnp.zeros_like(pack_ref)
    for d in range(dp):
        pack_ref[d, 2:8, 0:share] = small_ref[0:6, d * share : (d + 1) * share]
        pack_ref[d, 8:9, :] = jnp.broadcast_to(small_ref[6:7, 0:1], (1, 128))
        for r in range(hrows):
            at = (d % per * hrows + r) * 128
            pack_ref[d, 9 + r : 10 + r, :] = ismall_ref[d // per, :, at : at + 128]


def mid(x, teacher, counted, scale, count, oin, wall, smalls, hidden):
    rows, width = x.shape
    groups = wall.shape[0]
    S = jax.ShapeDtypeStruct
    vmem = pl.BlockSpec(memory_space=pltpu.VMEM)
    return pl.pallas_call(
        mid_kernel,
        name="mid",
        out_shape=(
            S((rows, width), BF16),
            S((rows, width), F32),
            S(oin.shape, BF16),
            S(wall.shape, BF16),
            S(smalls.shape, F32),
        ),
        in_specs=[vmem, vmem, vmem, pl.BlockSpec(memory_space=pltpu.SMEM)] + [vmem] * 4,
        out_specs=(vmem,) * 5,
        scratch_shapes=[
            pltpu.VMEM((groups, rows, hidden), F32),
            pltpu.VMEM((groups, rows, hidden), BF16),
            pltpu.VMEM((rows, width), F32),
            pltpu.VMEM((rows, width), F32),
            pltpu.VMEM((rows, width), F32),
            pltpu.VMEM((width, rows), BF16),
            pltpu.VMEM((width, rows), BF16),
            pltpu.VMEM((8, width), F32),
            pltpu.VMEM((groups, 1, hidden), F32),
            pltpu.VMEM((8, width), F32),
            pltpu.VMEM((groups, 1, hidden), F32),
        ],
        compiler_params=pltpu.CompilerParams(vmem_limit_bytes=VMEM_LIMIT),
    )(x, teacher, counted, scale, count, oin, wall, smalls)


def back_kernel(
    do_ref, grad_ref, xs_ref, wqf_ref, oT_ref, lse_ref, qT_ref, kA_ref, v_ref, pack_ref, dr1_ref,
    dx_ref, gsum_ref, qgrad_ref, small_ref,
    dof, doT, delta, qs, kT, dk, dv, dqT, dqkv,
    sib, own, pln, zsrc, zin, parts, pr, sj, rr, fin, qsend, qr, qz, qf, spack, srecv, zpack,
    do_send, do_recv, sb_send, sb_recv, own_sem, pl_send, pl_recv, zz_send, zz_recv,
    pr_send, pr_recv, rr_send, rr_recv, fin_send, fin_recv, qr_send, qr_recv, qf_send, qf_recv,
    sm_send, sm_recv, sz_send, sz_recv,
):
    me = Place()
    dp, tp, chips = me.dp, me.tp, me.chips
    rows, width = dx_ref.shape
    half = rows // 2
    length = rows * tp
    heads = 3
    gw = heads * HEAD_DIM
    share = width // dp
    greet(me)

    for g in range(4):
        t = 2 * me.core + g // 2
        d = me.base + g % 2
        here = jnp.logical_and(t == me.z, g % 2 == me.core)

        @pl.when(here)
        def _(g=g):
            pltpu.make_async_copy(do_ref.at[g], dof.at[me.z], do_recv.at[me.z]).start()

        @pl.when(jnp.logical_not(here))
        def _(g=g, t=t, d=d):
            remote(do_ref.at[g], dof.at[me.z], do_send.at[g], do_recv.at[me.z], d, t).start()

    order = me.around[::-1] + (me.z,)

    def sib_copy(t):
        return remote(grad_ref.at[t, :, 1 - me.core], sib.at[t], sb_send.at[t], sb_recv.at[t], me.sibling, me.z)

    for t in order:
        sib_copy(t).start()
        pltpu.make_async_copy(grad_ref.at[t, :, me.core], own.at[t], own_sem.at[t]).start()

    def plane_copy(t, n):
        k = (me.diagonal, me.first, me.second)[n]
        to = (me.first, me.first, me.second)[n]
        return remote(own.at[t, k], pln.at[t, n], pl_send.at[t, n], pl_recv.at[t, n], 2 * to + me.core, me.z)

    def pair_sum(t):
        arrival(own.at[t], own_sem.at[t]).wait()
        arrival(sib.at[t], sb_recv.at[t]).wait()

        def unit(k, _):
            own[t, k] = (own[t, k].astype(F32) + sib[t, k].astype(F32)).astype(BF16)
            return 0

        lax.fori_loop(0, chips, unit, 0)
        plane_copy(t, 0).start()
        plane_copy(t, 1).start()

    def pass_on(n):
        t = order[n]
        arrival(pln.at[t, 0], pl_recv.at[t, 0]).wait()
        own[t, me.second] = (own[t, me.second].astype(F32) + pln[t, 0].astype(F32)).astype(BF16)
        plane_copy(t, 2).start()

    has_below, has_above = me.z > 0, me.z < tp - 1

    def z_copy(t):
        up = t > me.z
        to = jnp.where(up, me.z + 1, me.z - 1)
        slot = jnp.where(jnp.logical_and(to == t, jnp.logical_not(up)), tp, t)
        return remote(zsrc.at[t], zin.at[slot], zz_send.at[t], zz_recv.at[slot], me.d, to)

    def plane_total(t):
        for n in (1, 2):
            arrival(pln.at[t, n], pl_recv.at[t, n]).wait()
        return own[t, me.chip].astype(F32) + pln[t, 1].astype(F32) + pln[t, 2].astype(F32)

    def z_step(n):
        t = order[n]
        total = plane_total(t)
        comes = jnp.where(t > me.z, has_below, has_above)

        @pl.when(comes)
        def _():
            arrival(zin.at[t], zz_recv.at[t]).wait()
            zsrc[t] = (total + zin[t].astype(F32)).astype(BF16)

        @pl.when(jnp.logical_not(comes))
        def _():
            zsrc[t] = total.astype(BF16)

        z_copy(t).start()

    for t in order:
        pair_sum(t)

    is_near = me.z == me.near_here
    is_end = jnp.logical_not(is_near)
    far = 2 * (1 - me.pair)
    far_first, far_second = far + me.pair, far + 1 - me.pair

    def block_at(i):
        return jnp.where(i == 0, far_second, jnp.where(i == 1, far_first, jnp.where(i == 2, me.buddy, me.z)))

    def prepare(j, at):
        arrival(dof.at[j], do_recv.at[j]).wait()
        flipped = dof[j].astype(F32).T
        doT[:, at] = flipped.astype(BF16)
        for h in range(heads):
            span = slice(h * HEAD_DIM, (h + 1) * HEAD_DIM)
            delta[h, :, at] = jnp.sum(flipped[span] * oT_ref[span, at], axis=0, keepdims=True)
            qs[h, at, :] = qT_ref[h, :, at].astype(F32).T.astype(BF16)

    always = {(0, 1): (pass_on, 0), (0, 3): (pass_on, 1), (1, 1): (pass_on, 2), (2, 0): (pass_on, 3)}
    at_ends = {(1, 0): (z_step, 0), (1, 2): (z_step, 1), (2, 1): (z_step, 2)}
    in_middle = {(1, 2): (z_step, 0), (2, 0): (z_step, 1), (2, 2): (z_step, 2)}
    chunk = 256
    def flip_keys(j, _):
        at = pl.ds(pl.multiple_of(j * rows, rows), rows)
        for h in range(heads):
            kT[h, :, at] = kA_ref[h, at, :].astype(F32).T[0:HEAD_DIM, :].astype(BF16)
        return 0

    lax.fori_loop(0, tp, flip_keys, 0)
    for h in range(heads):
        dk[...] = jnp.zeros_like(dk)
        dv[...] = jnp.zeros_like(dv)

        def attend(i, _, h=h):
            j = block_at(3 - i)
            at = pl.ds(pl.multiple_of(j * rows, rows), rows)
            if h == 0:
                prepare(j, at)
            span = slice(h * HEAD_DIM, (h + 1) * HEAD_DIM)
            qt, gt = qT_ref[h, :, at], doT[span, at]
            q, go = qs[h, at, :], dof[j, :, span]
            lse, dl = lse_ref[h, :, at], delta[h, :, at]
            dq = None
            for c in range(length // chunk):
                r = slice(c * chunk, (c + 1) * chunk)
                p = jnp.exp(dot(kA_ref[h, r, :], qt, 1, 0) - lse)
                dp_ = dot(v_ref[h, r, 0:HEAD_DIM], gt, 1, 0)
                ds = (p * (dp_ - dl)).astype(BF16)
                dv[r, :] += dot(p.astype(BF16), go, 1, 0)
                dk[r, :] += dot(ds, q, 1, 0)
                term = dot(kT[h, :, r], ds, 1, 0)
                dq = term if dq is None else dq + term
            dqT[span, at] = dq * HEAD_DIM**-0.5
            for where, hooks in ((None, always), (is_end, at_ends), (is_near, in_middle)):
                for (head, step), (act, n) in hooks.items():
                    if head == h:
                        now = i == step
                        pl.when(now if where is None else jnp.logical_and(where, now))(functools.partial(act, n))
            return 0

        lax.fori_loop(0, tp, attend, 0)
        for j in range(tp):
            at = slice(j * rows, (j + 1) * rows)
            dqkv[j, :, gw + h * HEAD_DIM : gw + (h + 1) * HEAD_DIM] = dk[at, 0:HEAD_DIM].astype(BF16)
            dqkv[j, :, 2 * gw + h * HEAD_DIM : 2 * gw + (h + 1) * HEAD_DIM] = dv[at, :].astype(BF16)

    weights = wqf_ref[...].reshape(width, 3 * gw)
    ones = jnp.ones((8, rows), BF16)
    mine = pl.ds(pl.multiple_of(me.core * half, half), half)
    other = pl.ds(pl.multiple_of((1 - me.core) * half, half), half)

    def pr_copy(j):
        return remote(parts.at[j, other], pr.at[j], pr_send.at[j], pr_recv.at[j], me.sibling, me.z)

    def rr_copy(j):
        return remote(sj.at[j], rr.at[j], rr_send.at[j], rr_recv.at[j], me.d, me.buddy)

    def collects(j):
        return jnp.where(j // 2 == me.pair, j, me.near_here) == me.z

    def chip_sum(j):
        arrival(pr.at[j], pr_recv.at[j]).wait()
        sj[j] = (parts[j, mine, :].astype(F32) + pr[j].astype(F32)).astype(BF16)
        pl.when(jnp.logical_not(collects(j)))(lambda: rr_copy(j).start())

    def token_grads(i, sums):
        j = block_at(i)
        at = pl.ds(pl.multiple_of(j * rows, rows), rows)
        dqkv[j, :, 0:gw] = dqT[:, at].T.astype(BF16)
        flat = dqkv[j]
        parts[j] = dot(flat, weights, 1, 1).astype(BF16)
        pr_copy(j).start()
        pl.when(i > 0)(lambda: chip_sum(block_at(i - 1)))
        return sums + dot(ones, flat, 1, 0)

    sums = lax.fori_loop(0, tp, token_grads, jnp.zeros((8, 3 * gw), F32))
    chip_sum(block_at(tp - 1))

    spack[...] = pack_ref[...]
    blocks = gw // share
    for b in range(blocks):
        spack[me.group * blocks + b, 0:1, 0:share] = sums[0:1, b * share : (b + 1) * share]
        spack[me.group * blocks + b, 1:2, 0:share] = sums[0:1, 2 * gw + b * share : 2 * gw + (b + 1) * share]

    def small_copy(i):
        peer = lax.rem(me.d + 1 + i, dp)
        return remote(spack.at[peer], srecv.at[i], sm_send.at[i], sm_recv.at[i], peer, me.z)

    def small_start(i, _):
        small_copy(i).start()
        return 0

    lax.fori_loop(0, dp - 1, small_start, 0)

    def fin_copy(j):
        return remote(pr.at[j], fin.at[me.core], fin_send.at[j], fin_recv.at[me.core], me.owner, j)

    def lands_here(j):
        return jnp.logical_and(me.core == me.pair, j == me.z)

    total = None
    for j in range(tp):
        term = dot(xs_ref[j], dqkv[j], 0, 0)
        total = term if total is None else total + term
    qsend[...] = total.astype(BF16).reshape(dp, share, 3 * gw)

    def q_copy(peer, i):
        return remote(qsend.at[peer], qr.at[me.core, me.chip], qr_send.at[i], qr_recv.at[me.core, me.chip], peer, me.z)

    def q_start(i, _):
        peer = lax.rem(me.d + i, dp)

        @pl.when(i == 0)
        def _():
            pltpu.make_async_copy(qsend.at[peer], qr.at[me.core, me.chip], qr_recv.at[me.core, me.chip]).start()

        @pl.when(i > 0)
        def _():
            q_copy(peer, i).start()

        return 0

    lax.fori_loop(0, dp, q_start, 0)

    def pair_total(i, _):
        j = block_at(i)

        @pl.when(collects(j))
        def _():
            arrival(rr.at[j], rr_recv.at[j]).wait()
            pr[j] = (sj[j].astype(F32) + rr[j].astype(F32)).astype(BF16)

            @pl.when(lands_here(j))
            def _():
                pltpu.make_async_copy(pr.at[j], fin.at[me.core], fin_recv.at[me.core]).start()

            @pl.when(jnp.logical_not(lands_here(j)))
            def _():
                fin_copy(j).start()

        return 0

    lax.fori_loop(0, tp, pair_total, 0)

    def q_pair(s):
        return me.z // 2, 2 * me.low + s

    for s in range(2):
        total = None
        for k in range(chips):
            arrival(qr.at[s, k], qr_recv.at[s, k]).wait()
            term = qr[s, k].astype(F32)
            total = term if total is None else total + term
        qz[s] = total.astype(BF16)
        p, t = q_pair(s)

        @pl.when(t == me.z)
        def _(s=s, p=p):
            pltpu.make_async_copy(qz.at[s], qf.at[p], qf_recv.at[p]).start()

        @pl.when(t != me.z)
        def _(s=s, p=p, t=t):
            remote(qz.at[s], qf.at[p], qf_send.at[s], qf_recv.at[p], me.d, t).start()

    total = spack[me.d]
    for i in range(dp - 1):
        arrival(srecv.at[i], sm_recv.at[i]).wait()
        total = total + srecv[i]
    zpack[me.z] = total

    def sz_copy(s):
        return remote(zpack.at[me.z], zpack.at[me.z], sz_send.at[s - 1], sz_recv.at[me.z], me.d, lax.rem(me.z + s, tp))

    for s in range(1, tp):
        sz_copy(s).start()

    for h in range(2):
        arrival(fin.at[h], fin_recv.at[h]).wait()
        at = slice(h * half, (h + 1) * half)
        dx_ref[at, :] = dr1_ref[at, :] + fin[h].astype(F32)
    for p in range(2):
        arrival(qf.at[p], qf_recv.at[p]).wait()
    qgrad_ref[...] = qf[0].astype(F32) + qf[1].astype(F32)
    for s in range(1, tp):
        t = lax.rem(me.z + s, tp)
        arrival(zpack.at[t], sz_recv.at[t]).wait()
    total = zpack[0]
    for t in range(1, tp):
        total = total + zpack[t]
    small_ref[...] = total
    gsum_ref[...] = plane_total(me.z)
    for slot, comes in ((me.z, has_below), (tp, has_above)):

        @pl.when(comes)
        def _(slot=slot):
            arrival(zin.at[slot], zz_recv.at[slot]).wait()
            gsum_ref[...] += zin[slot].astype(F32)

    for g in range(4):

        @pl.when(jnp.logical_not(jnp.logical_and(2 * me.core + g // 2 == me.z, g % 2 == me.core)))
        def _(g=g):
            remote(do_ref.at[g], dof.at[0], do_send.at[g], do_recv.at[0], me.sibling, me.z).wait_send()

    for t in range(tp):
        sib_copy(t).wait_send()
        pr_copy(t).wait_send()

        @pl.when(jnp.logical_not(collects(t)))
        def _(t=t):
            rr_copy(t).wait_send()

        @pl.when(jnp.logical_and(collects(t), jnp.logical_not(lands_here(t))))
        def _(t=t):
            fin_copy(t).wait_send()

    for t in range(tp):
        for n in range(3):
            plane_copy(t, n).wait_send()
        pl.when(t != me.z)(lambda t=t: z_copy(t).wait_send())

    def peers_sent(i, _):
        small_copy(i).wait_send()
        q_copy(lax.rem(me.d + 1 + i, dp), i + 1).wait_send()
        return 0

    lax.fori_loop(0, dp - 1, peers_sent, 0)
    for s in range(1, tp):
        sz_copy(s).wait_send()
    for s in range(2):
        p, t = q_pair(s)

        @pl.when(t != me.z)
        def _(s=s, p=p, t=t):
            remote(qz.at[s], qf.at[p], qf_send.at[s], qf_recv.at[p], me.d, t).wait_send()


def back(do, grad, xs, wqf, oT, lse, qT, kA, v, pack, dr1):
    tp, rows, width = xs.shape
    dp, share, qwidth = wqf.shape
    chips = dp // 2
    length = rows * tp
    half = rows // 2
    cols = grad.shape[-1]
    S = jax.ShapeDtypeStruct
    vmem = pl.BlockSpec(memory_space=pltpu.VMEM)
    anym = pl.BlockSpec(memory_space=pl.ANY)
    dma = pltpu.SemaphoreType.DMA
    V = pltpu.VMEM
    return pl.pallas_call(
        back_kernel,
        name="back",
        out_shape=(
            S((rows, width), F32),
            S((share, cols), F32),
            S((share, qwidth), F32),
            S((16, 128), F32),
        ),
        in_specs=[anym, anym] + [vmem] * 9,
        out_specs=(vmem,) * 4,
        scratch_shapes=[
            V((tp, rows, 192), BF16), V((192, length), BF16), V((3, 1, length), F32),
            V((3, length, 128), BF16), V((3, HEAD_DIM, length), BF16),
            V((length, 128), F32), V((length, HEAD_DIM), F32), V((192, length), F32), V((tp, rows, qwidth), BF16),
            V((tp, chips, share, cols), BF16), V((tp, chips, share, cols), BF16), V((tp, chips - 1, share, cols), BF16),
            V((tp, share, cols), BF16), V((tp + 1, share, cols), BF16),
            V((tp, rows, width), BF16), V((tp, half, width), BF16), V((tp, half, width), BF16), V((tp, half, width), BF16),
            V((2, half, width), BF16),
            V((dp, share, qwidth), BF16), V((2, chips, share, qwidth), BF16), V((2, share, qwidth), BF16), V((2, share, qwidth), BF16),
            V((dp, 16, 128), F32), V((dp - 1, 16, 128), F32), V((tp, 16, 128), F32),
            dma((4,)), dma((tp,)), dma((tp,)), dma((tp,)), dma((tp,)), dma((tp, 3)), dma((tp, 3)), dma((tp,)), dma((tp + 1,)),
            dma((tp,)), dma((tp,)), dma((tp,)), dma((tp,)), dma((tp,)), dma((2,)), dma((dp,)), dma((2, chips)), dma((2,)), dma((2,)),
            dma((dp - 1,)), dma((dp - 1,)), dma((tp - 1,)), dma((tp,)),
        ],
        compiler_params=pltpu.CompilerParams(
            collective_id=1, has_side_effects=True, vmem_limit_bytes=VMEM_LIMIT
        ),
    )(do, grad, xs, wqf, oT, lse, qT, kA, v, pack, dr1)


def pack_kernel(length_ref, mask_ref, *refs):
    vectors, (ib_ref, wq_ref, wk_ref, wv_ref, wi_ref, wo_ref, wx_ref) = refs[:8], refs[8:15]
    sm_ref, w3_ref, wm_ref, counted_ref = refs[15:]
    rows = mask_ref.shape[1]
    share, gw = wq_ref.shape
    hidden = wi_ref.shape[1]
    pos = lax.axis_index("tensor") * rows + lax.broadcasted_iota(jnp.int32, (8, rows), 1)
    mask = jnp.broadcast_to(mask_ref[...], (8, rows))
    valid = length_ref[0]
    counted = jnp.where(jnp.logical_and(pos < valid, mask == 1), 1.0, 0.0)
    counted_ref[...] = counted.T[:, 0:1]
    sm_ref[...] = jnp.zeros_like(sm_ref)
    for i, v in enumerate(vectors):
        sm_ref[i : i + 1, 0:share] = v[...].astype(F32)
    sm_ref[8:9, :] = jnp.broadcast_to(jnp.sum(counted[0:1, :], axis=1, keepdims=True), (1, 128))
    for r in range(ib_ref.shape[1] // 128):
        sm_ref[9 + r : 10 + r, :] = ib_ref[:, r * 128 : (r + 1) * 128].astype(F32)
    sm_ref[12:13, :] = jnp.full((1, 128), valid, jnp.int32).astype(F32)
    for i, w in enumerate((wq_ref, wk_ref, wv_ref)):
        w3_ref[:, i * gw : (i + 1) * gw] = w[...]
    wm_ref[:, 0:hidden] = wi_ref[...]
    wm_ref[:, hidden : 2 * hidden] = wo_ref[...].astype(F32).T.astype(BF16)
    wm_ref[:, 2 * hidden :] = wx_ref[...].astype(F32).T.astype(BF16)


def pack_inputs(lengths, mask, vectors, inner_bias, wq, wk, wv, wi, wo, wx):
    share, gw = wq.shape
    rows = mask.shape[0]
    S = jax.ShapeDtypeStruct
    vmem = pl.BlockSpec(memory_space=pltpu.VMEM)
    return pl.pallas_call(
        pack_kernel,
        name="pack_inputs",
        out_shape=(
            S((16, 128), F32),
            S((share, 3 * gw), BF16),
            S((share, 2 * wi.shape[1] + gw), BF16),
            S((rows, 1), F32),
        ),
        in_specs=[pl.BlockSpec(memory_space=pltpu.SMEM)] + [vmem] * 16,
        out_specs=(vmem,) * 4,
    )(lengths, mask.reshape(1, rows), *vectors, inner_bias.reshape(1, -1), wq, wk, wv, wi, wo, wx)


def shards(
    tokens, teacher, lengths, loss_mask, loss_scale,
    query_weight, query_bias, key_weight, value_weight, value_bias, mixer_weight, mixer_bias,
    first_gain, first_shift, inner_weight, inner_bias, outer_weight, outer_bias, second_gain, second_shift,
):
    dp, tp = lax.axis_size("dp"), lax.axis_size("tensor")
    if dp != 8 or tp != 4:
        return plain_shards(
            tokens, teacher, lengths, loss_mask, loss_scale,
            query_weight, query_bias, key_weight, value_weight, value_bias, mixer_weight, mixer_bias,
            first_gain, first_shift, inner_weight, inner_bias, outer_weight, outer_bias, second_gain, second_shift,
        )
    width = tokens.shape[1]
    share, gw = query_weight.shape
    hidden = inner_weight.shape[1]
    hshare = inner_bias.shape[0]
    hrows = hshare // 128
    rows_of = [
        v.reshape(1, -1)
        for v in (query_bias, value_bias, mixer_bias, first_gain, first_shift, outer_bias, second_gain, second_shift)
    ]
    small, wq, wm, counted = pack_inputs(
        lengths, loss_mask, rows_of, inner_bias, query_weight, key_weight, value_weight, inner_weight, outer_weight, mixer_weight
    )
    oin, wall, smalls, count, xs, wqf, oT, lse, qT, kA, v = front(tokens, wq, wm, small, dp, tp)
    token_total = count[0, 0]
    wall = wall.reshape(tp, width, wm.shape[1])
    layer_output, dr1, do, grad, pack = mid(
        tokens, teacher, counted, loss_scale.reshape(1, 1), count, oin, wall, smalls, hidden
    )
    grad = grad.reshape(tp, dp // 2, 2, share, wm.shape[1])
    input_grad, gsum, qgrad, ssum = back(do, grad, xs, wqf, oT, lse, qT, kA, v, pack, dr1)
    loss_value = ssum[8, 0] / (token_total * width)
    line = lambda i: ssum[i, :share]
    innerbias_grad = ssum[9 : 9 + hrows].reshape(-1)[:hshare]
    return (
        layer_output,
        loss_value,
        input_grad,
        qgrad[:, 0:gw],
        line(0),
        qgrad[:, gw : 2 * gw],
        qgrad[:, 2 * gw :],
        line(1),
        gsum[:, 2 * hidden :].T,
        line(2),
        line(3),
        line(4),
        gsum[:, 0:hidden],
        innerbias_grad,
        gsum[:, hidden : 2 * hidden].T,
        line(5),
        line(6),
        line(7),
    )


def in_blocks(value, dim, size):
    before, after = (value.shape[:dim], value.shape[dim + 1 :])
    return jnp.moveaxis(value.reshape(*before, size, -1, *after), dim, 0)


def summed_on_arrival(value, axis, dim):
    size = lax.axis_size(axis)
    blocks = lax.all_to_all(in_blocks(value, dim, size), axis, 0, 0, tiled=True)
    return jnp.sum(blocks.astype(jnp.float32), axis=0)


def sent_together(arrays, axis, dim, along):
    both = jnp.concatenate(arrays, axis=along)
    out, at, gathered = (summed_on_arrival(both, axis, dim), 0, [])
    for a in arrays:
        gathered.append(lax.slice_in_dim(out, at, at + a.shape[along], axis=along))
        at += a.shape[along]
    return tuple(gathered)


def contract_last(left_rows, right_rows):
    return lax.dot_general(
        left_rows, right_rows, (((1,), (1,)), ((), ())), preferred_element_type=jnp.float32
    )


def contract_first(left_rows, right_rows):
    return lax.dot_general(
        left_rows, right_rows, (((0,), (0,)), ((), ())), preferred_element_type=jnp.float32
    )


def plain_dot(left_rows, right_rows):
    return jnp.dot(left_rows, right_rows, preferred_element_type=jnp.float32)


def gelu_exact(pre_values):
    return jax.nn.gelu(pre_values, approximate=False)


def plain_norm_forward(values_in, gain_vec, shift_vec):
    centred = values_in - jnp.mean(values_in, axis=1, keepdims=True)
    inv_std = lax.rsqrt(jnp.mean(centred * centred, axis=1, keepdims=True) + norm_eps)
    normed = centred * inv_std
    return (normed * gain_vec + shift_vec, normed, inv_std)


def plain_norm_backward(grad_out, normed, inv_std, gain_vec):
    grad_normed = grad_out * gain_vec
    mean_plain = jnp.mean(grad_normed, axis=1, keepdims=True)
    mean_mixed = jnp.mean(grad_normed * normed, axis=1, keepdims=True)
    grad_in = inv_std * (grad_normed - mean_plain - normed * mean_mixed)
    return (grad_in, jnp.sum(grad_out * normed, axis=0), jnp.sum(grad_out, axis=0))


def plain_shards(
    tokens,
    teacher,
    lengths,
    loss_mask,
    loss_scale,
    query_weight,
    query_bias,
    key_weight,
    value_weight,
    value_bias,
    mixer_weight,
    mixer_bias,
    first_gain,
    first_shift,
    inner_weight,
    inner_bias,
    outer_weight,
    outer_bias,
    second_gain,
    second_shift,
):
    tp_count = lax.axis_size("tensor")
    tp_index = lax.axis_index("tensor")
    dp_count = lax.axis_size("dp")
    dp_index = lax.axis_index("dp")
    local_rows = tokens.shape[0]
    seq_len = local_rows * tp_count
    model_width = tokens.shape[1]
    head_width = query_weight.shape[1]
    hidden_width = inner_weight.shape[1]
    head_count = head_width // HEAD_DIM
    block_count = seq_len // QBLOCK
    score_scale = HEAD_DIM ** (-0.5)
    length_here = lengths[0]
    local_pos = tp_index * local_rows + jnp.arange(local_rows)
    counted = jnp.logical_and(local_pos < length_here, loss_mask == 1).astype(jnp.float32)
    count_local = jnp.sum(counted)
    small_stack = jnp.stack(
        [
            query_bias,
            value_bias,
            mixer_bias,
            first_gain,
            first_shift,
            outer_bias,
            second_gain,
            second_shift,
        ]
    )

    def fetch_params():
        return (
            lax.all_gather(query_weight, "dp", axis=0, tiled=True),
            lax.all_gather(key_weight, "dp", axis=0, tiled=True),
            lax.all_gather(value_weight, "dp", axis=0, tiled=True),
            lax.all_gather(mixer_weight, "dp", axis=1, tiled=True),
            lax.all_gather(inner_weight, "dp", axis=0, tiled=True),
            lax.all_gather(outer_weight, "dp", axis=1, tiled=True),
            lax.all_gather(small_stack, "dp", axis=1, tiled=True),
            lax.all_gather(inner_bias, "dp", axis=0, tiled=True),
        )

    def attn_gather(values_in):
        return lax.all_gather(values_in, "tensor", axis=0, tiled=True)

    def ffn_gather(values_in):
        return lax.all_gather(values_in, "tensor", axis=0, tiled=True)

    (
        query_full,
        key_full,
        value_full,
        mixer_full,
        inner_full,
        outer_full,
        small_full,
        innerb_full,
    ) = fetch_params()
    small_wide = small_full.astype(jnp.float32)
    qbias_mine = lax.dynamic_slice_in_dim(small_wide[0], tp_index * head_width, head_width)
    vbias_mine = lax.dynamic_slice_in_dim(small_wide[1], tp_index * head_width, head_width)
    inner_mine = lax.dynamic_slice_in_dim(
        innerb_full.astype(jnp.float32), tp_index * hidden_width, hidden_width
    )
    seq_rows = attn_gather(tokens)
    queries = (plain_dot(seq_rows, query_full) + qbias_mine).astype(jnp.bfloat16)
    keys_all = plain_dot(seq_rows, key_full).astype(jnp.bfloat16)
    values_all = (plain_dot(seq_rows, value_full) + vbias_mine).astype(jnp.bfloat16)
    keys_three = keys_all.reshape(seq_len, head_count, HEAD_DIM)
    values_three = values_all.reshape(seq_len, head_count, HEAD_DIM)
    key_valid = jnp.arange(seq_len) < length_here

    def score_block(query_block):
        scores = (
            jnp.einsum("qhd,khd->hqk", query_block, keys_three, preferred_element_type=jnp.float32)
            * score_scale
        )
        return jnp.where(key_valid[None, None, :], scores, masked_score)

    def forward_block(query_block):
        scores = score_block(query_block)
        row_top = jnp.max(scores, axis=2, keepdims=True)
        exp_scores = jnp.exp(scores - row_top)
        row_total = jnp.sum(exp_scores, axis=2, keepdims=True)
        prob_low = (exp_scores / row_total).astype(jnp.bfloat16)
        mixed_rows = jnp.einsum(
            "hqk,khd->qhd", prob_low, values_three, preferred_element_type=jnp.float32
        )
        return (mixed_rows.astype(jnp.bfloat16), (row_top + jnp.log(row_total))[:, :, 0])

    query_blocks = queries.reshape(block_count, QBLOCK, head_count, HEAD_DIM)
    attended, log_sums = lax.map(forward_block, query_blocks)
    attended = attended.reshape(seq_len, head_width)
    attn_out = lax.psum_scatter(
        plain_dot(attended, mixer_full).astype(jnp.bfloat16),
        "tensor",
        scatter_dimension=0,
        tiled=True,
    ).astype(jnp.float32)
    first_sum = tokens.astype(jnp.float32) + attn_out + small_wide[2]
    hidden_one, normed_one, inv_one = plain_norm_forward(first_sum, small_wide[3], small_wide[4])
    hidden_low = hidden_one.astype(jnp.bfloat16)
    ffn_rows = ffn_gather(hidden_low)
    pre_act = plain_dot(ffn_rows, inner_full) + inner_mine
    act_full, gelu_pull = jax.vjp(gelu_exact, pre_act)
    activated = act_full.astype(jnp.bfloat16)
    ffn_out = lax.psum_scatter(
        plain_dot(activated, outer_full).astype(jnp.bfloat16),
        "tensor",
        scatter_dimension=0,
        tiled=True,
    ).astype(jnp.float32)
    second_sum = hidden_one + ffn_out + small_wide[5]
    final_rows, normed_two, inv_two = plain_norm_forward(second_sum, small_wide[6], small_wide[7])
    layer_output = final_rows.astype(jnp.bfloat16)
    diff_rows = final_rows - teacher.astype(jnp.float32)
    loss_local = jnp.sum(counted * jnp.sum(diff_rows * diff_rows, axis=1))
    loss_total, token_total = lax.psum((loss_local, count_local), ("dp", "tensor"))
    grad_scale = 2.0 * loss_scale / (token_total * model_width)
    grad_final = grad_scale * counted[:, None] * diff_rows
    (
        query_full,
        key_full,
        value_full,
        mixer_full,
        inner_full,
        outer_full,
        small_full,
        innerb_full,
    ) = fetch_params()
    ffn_rows = ffn_gather(hidden_low)
    grad_second, secondgain_part, secondshift_part = plain_norm_backward(
        grad_final, normed_two, inv_two, small_wide[6]
    )
    outerbias_part = jnp.sum(grad_second, axis=0)
    grad_ffn_rows = lax.all_gather(grad_second.astype(jnp.bfloat16), "tensor", axis=0, tiled=True)
    grad_act = contract_last(grad_ffn_rows, outer_full)
    outer_local = contract_first(activated, grad_ffn_rows)
    grad_pre = gelu_pull(grad_act)[0].astype(jnp.bfloat16)
    innerbias_part = jnp.sum(grad_pre, axis=0, dtype=jnp.float32)
    inner_local = contract_first(ffn_rows, grad_pre)
    grad_hidden = lax.psum_scatter(
        contract_last(grad_pre, inner_full).astype(jnp.bfloat16),
        "tensor",
        scatter_dimension=0,
        tiled=True,
    ).astype(jnp.float32)
    inner_grad, outer_grad = (
        lax.psum_scatter(inner_local, "dp", scatter_dimension=0, tiled=True),
        lax.psum_scatter(outer_local, "dp", scatter_dimension=1, tiled=True),
    )
    grad_first, firstgain_part, firstshift_part = plain_norm_backward(
        grad_second + grad_hidden, normed_one, inv_one, small_wide[3]
    )
    mixerbias_part = jnp.sum(grad_first, axis=0)
    grad_attn_rows = lax.all_gather(grad_first.astype(jnp.bfloat16), "tensor", axis=0, tiled=True)
    grad_attended = contract_last(grad_attn_rows, mixer_full).astype(jnp.bfloat16)
    mixer_local = contract_first(attended, grad_attn_rows)
    grad_blocks = grad_attended.reshape(block_count, QBLOCK, head_count, HEAD_DIM)

    def backward_block(carried, block_in):
        key_acc, value_acc = carried
        query_block, grad_block, lse_block = block_in
        scores = score_block(query_block)
        prob_full = jnp.exp(scores - lse_block[:, :, None])
        prob_low = prob_full.astype(jnp.bfloat16)
        grad_prob = jnp.einsum(
            "qhd,khd->hqk", grad_block, values_three, preferred_element_type=jnp.float32
        )
        row_dot = jnp.sum(prob_full * grad_prob, axis=2, keepdims=True)
        grad_scores = (prob_full * (grad_prob - row_dot)).astype(jnp.bfloat16)
        grad_query = (
            jnp.einsum("hqk,khd->qhd", grad_scores, keys_three, preferred_element_type=jnp.float32)
            * score_scale
        ).astype(jnp.bfloat16)
        key_acc = (
            key_acc
            + jnp.einsum(
                "hqk,qhd->khd", grad_scores, query_block, preferred_element_type=jnp.float32
            )
            * score_scale
        )
        value_acc = value_acc + jnp.einsum(
            "hqk,qhd->khd", prob_low, grad_block, preferred_element_type=jnp.float32
        )
        return ((key_acc, value_acc), grad_query)

    zero_acc = jnp.zeros((seq_len, head_count, HEAD_DIM), jnp.float32)
    (key_acc, value_acc), grad_queries = lax.scan(
        backward_block, (zero_acc, zero_acc), (query_blocks, grad_blocks, log_sums)
    )
    grad_queries = grad_queries.reshape(seq_len, head_width)
    grad_keys = key_acc.reshape(seq_len, head_width).astype(jnp.bfloat16)
    grad_values = value_acc.reshape(seq_len, head_width).astype(jnp.bfloat16)
    seq_rows = attn_gather(tokens)
    query_local = contract_first(seq_rows, grad_queries)
    key_local = contract_first(seq_rows, grad_keys)
    value_local = contract_first(seq_rows, grad_values)
    querybias_part = jnp.sum(grad_queries, axis=0, dtype=jnp.float32)
    valuebias_part = jnp.sum(grad_values, axis=0, dtype=jnp.float32)
    total_term = contract_last(grad_queries, query_full)
    total_term = total_term + contract_last(grad_keys, key_full)
    grad_tokens = lax.psum_scatter(
        (total_term + contract_last(grad_values, value_full)).astype(jnp.bfloat16),
        "tensor",
        scatter_dimension=0,
        tiled=True,
    ).astype(jnp.float32)
    input_grad = grad_first + grad_tokens
    query_grad, key_grad, value_grad, mixer_grad = (
        *sent_together(
            (
                query_local.astype(jnp.bfloat16),
                key_local.astype(jnp.bfloat16),
                value_local.astype(jnp.bfloat16),
            ),
            "dp",
            0,
            1,
        ),
        summed_on_arrival(mixer_local.astype(jnp.bfloat16), "dp", 1),
    )

    def spread_part(part_vec, full_width):
        return lax.dynamic_update_slice_in_dim(
            jnp.zeros((full_width,), jnp.float32), part_vec, tp_index * part_vec.shape[0], 0
        )

    small_terms = jnp.stack(
        [
            spread_part(querybias_part, model_width),
            spread_part(valuebias_part, model_width),
            mixerbias_part,
            firstgain_part,
            firstshift_part,
            outerbias_part,
            secondgain_part,
            secondshift_part,
        ]
    )
    inner_terms = spread_part(innerbias_part, hidden_width * tp_count)
    small_sum, inner_sum = lax.psum((small_terms, inner_terms), ("dp", "tensor"))
    loss_value = loss_total / (token_total * model_width)
    width_share = model_width // dp_count
    small_mine = lax.dynamic_slice_in_dim(small_sum, dp_index * width_share, width_share, 1)
    hidden_share = inner_sum.shape[0] // dp_count
    innerbias_grad = lax.dynamic_slice_in_dim(inner_sum, dp_index * hidden_share, hidden_share, 0)
    return (
        layer_output,
        loss_value,
        input_grad,
        query_grad,
        small_mine[0],
        key_grad,
        value_grad,
        small_mine[1],
        mixer_grad,
        small_mine[2],
        small_mine[3],
        small_mine[4],
        inner_grad,
        innerbias_grad,
        outer_grad,
        small_mine[5],
        small_mine[6],
        small_mine[7],
    )


def solution(mesh):
    return jax.shard_map(
        shards,
        mesh=mesh,
        in_specs=(
            P(("dp", "tensor"), None),
            P(("dp", "tensor"), None),
            P("dp"),
            P(("dp", "tensor")),
            P(),
            P("dp", "tensor"),
            P("dp"),
            P("dp", "tensor"),
            P("dp", "tensor"),
            P("dp"),
            P("tensor", "dp"),
            P("dp"),
            P("dp"),
            P("dp"),
            P("dp", "tensor"),
            P("dp"),
            P("tensor", "dp"),
            P("dp"),
            P("dp"),
            P("dp"),
        ),
        out_specs=(
            P(("dp", "tensor"), None),
            P(),
            P(("dp", "tensor"), None),
            P("dp", "tensor"),
            P("dp"),
            P("dp", "tensor"),
            P("dp", "tensor"),
            P("dp"),
            P("tensor", "dp"),
            P("dp"),
            P("dp"),
            P("dp"),
            P("dp", "tensor"),
            P("dp"),
            P("tensor", "dp"),
            P("dp"),
            P("dp"),
            P("dp"),
        ),
        check_vma=False,
    )
```

```python
import functools
import jax
import jax.numpy as jnp
from jax import lax
from jax.experimental import pallas as pl
from jax.experimental.pallas import tpu as pltpu
from jax.sharding import PartitionSpec as P

HEAD_DIM = 64
QBLOCK = 512
MESH = pl.DeviceIdType.MESH
F32 = jnp.float32
BF16 = jnp.bfloat16
norm_eps = 1e-05
masked_score = -1e30
VMEM_LIMIT = 60 * 1024 * 1024


def dot(left, right, left_dim, right_dim):
    return lax.dot_general(
        left, right, (((left_dim,), (right_dim,)), ((), ())), preferred_element_type=F32
    )


def remote(src, dst, send, recv, d, t):
    return pltpu.make_async_remote_copy(
        src_ref=src,
        dst_ref=dst,
        send_sem=send,
        recv_sem=recv,
        device_id={"dp": d, "tensor": t},
        device_id_type=MESH,
    )


def arrival(dst, recv):
    return pltpu.make_async_copy(dst, dst, recv)


class Place:
    def __init__(self):
        self.dp = lax.axis_size("dp")
        self.tp = lax.axis_size("tensor")
        self.d = lax.axis_index("dp")
        self.z = lax.axis_index("tensor")
        self.core = lax.rem(self.d, 2)
        self.chip = self.d // 2
        self.chips = self.dp // 2
        self.base = self.chip * 2
        self.sibling = self.base + 1 - self.core
        self.pair = self.z // 2
        self.low = lax.rem(self.z, 2)
        self.group = 2 * self.low + self.core
        self.buddy = 2 * self.pair + 1 - self.low
        self.owner = self.base + self.pair
        self.near_here = 1 + self.pair
        self.near_there = 2 - self.pair
        side = self.chip + 1 - 2 * lax.rem(self.chip, 2)
        across = lax.rem(self.chip + 2, 4)
        self.first = jnp.where(self.core == 0, side, across)
        self.second = jnp.where(self.core == 0, across, side)
        self.diagonal = 3 - self.chip
        self.around = (self.buddy, self.near_there, 3 * (1 - self.pair))


def greet(place):
    barrier = pltpu.get_barrier_semaphore()
    count = 0
    for t in range(place.tp):
        for c in range(2):
            other = jnp.logical_not(jnp.logical_and(place.z == t, place.core == c))

            @pl.when(other)
            def _(t=t, c=c):
                pl.semaphore_signal(
                    barrier, inc=1, device_id={"dp": place.base + c, "tensor": t}, device_id_type=MESH
                )

            count += 1
    count -= 1

    def plane(i, _):
        chip = lax.rem(place.chip + 1 + i, place.chips)
        for c in range(2):
            pl.semaphore_signal(
                barrier, inc=1, device_id={"dp": chip * 2 + c, "tensor": place.z}, device_id_type=MESH
            )
        return 0

    lax.fori_loop(0, place.chips - 1, plane, 0)
    count += 2 * (place.chips - 1)
    pl.semaphore_wait(barrier, count)


def front_kernel(
    x_ref, wq_ref, wm_ref, sm_ref,
    oin_ref, wall_ref, smalls_ref, count_ref, xs_ref, wqf_ref, oT_ref, lse_ref, qT_ref, kA_ref, v_ref,
    wqz, counts, vT, scores, o_buf, wqT, wkp, wvp, wvT,
    sm_send, sm_recv, cn_send, cn_recv, wz_send, wz_recv, wp_send, wp_recv,
    x_send, x_recv, xr_send, xf_send, mz_send, mz_recv, mp_send, mp_recv, ms_send, ms_recv, o_send, o_recv,
):
    me = Place()
    dp, tp, chips = me.dp, me.tp, me.chips
    rows, width = x_ref.shape
    half = rows // 2
    length = rows * tp
    share = wq_ref.shape[0]
    heads = 3
    greet(me)

    def each_peer(f):
        def step(i, _):
            f(i, lax.rem(me.d + 1 + i, dp))
            return 0

        lax.fori_loop(0, dp - 1, step, 0)

    def small_copy(i, peer):
        return remote(sm_ref, smalls_ref.at[me.d], sm_send.at[i], sm_recv.at[me.d], peer, me.z)

    each_peer(lambda i, peer: small_copy(i, peer).start())
    smalls_ref[me.d] = sm_ref[...]

    for s in range(2):
        target = me.z // 2 + 2 * s
        src, dst = wq_ref, wqz.at[me.low]

        @pl.when(target == me.z)
        def _(s=s, dst=dst):
            pltpu.make_async_copy(wq_ref, dst, wz_recv.at[me.low]).start()

        @pl.when(target != me.z)
        def _(s=s, dst=dst, target=target):
            remote(wq_ref, dst, wz_send.at[s], wz_recv.at[me.low], me.d, target).start()

    is_near = me.z == me.near_here
    is_end = jnp.logical_not(is_near)
    pltpu.make_async_copy(wm_ref, wall_ref.at[me.z, me.d], mz_recv.at[me.z]).start()

    def along_z(unit, t, sem, to):
        return remote(unit, wall_ref.at[t, me.d], mz_send.at[sem], mz_recv.at[t], me.d, to)

    def own_along_z():
        pl.when(me.z > 0)(lambda: along_z(wm_ref, me.z, 0, me.z - 1).start())
        pl.when(me.z < tp - 1)(lambda: along_z(wm_ref, me.z, 1, me.z + 1).start())

    def goes_up(t):
        return jnp.logical_and(t < me.z, me.z < tp - 1)

    def goes_down(t):
        return jnp.logical_and(t > me.z, me.z > 0)

    is_owner = me.core == me.pair
    pl.when(is_owner)(own_along_z)
    for h in range(2):
        part = pl.ds(h * half, half)

        @pl.when(is_owner)
        def _(h=h, part=part):
            pltpu.make_async_copy(x_ref.at[part], xs_ref.at[me.z, part], x_recv.at[me.z, h]).start()
            remote(x_ref.at[part], xs_ref.at[me.z, part], x_send.at[h], x_recv.at[me.z, h], me.base + h, me.buddy).start()
            remote(x_ref.at[part], xs_ref.at[me.z, part], xr_send.at[0, h], x_recv.at[me.z, h], me.sibling, me.z).start()

        @pl.when(jnp.logical_not(is_owner))
        def _(h=h, part=part):
            remote(x_ref.at[part], xs_ref.at[me.z, part], x_send.at[h], x_recv.at[me.z, h], me.base + h, me.near_there).start()

    pl.when(jnp.logical_not(is_owner))(own_along_z)

    def wq_plane(s, k):
        dst = wqf_ref.at[me.d]
        return remote(wqz.at[s], dst, wp_send.at[s, k], wp_recv.at[me.d], 2 * k + s, me.z)

    for s in range(2):
        arrival(wqz.at[s], wz_recv.at[s]).wait()

        def step(i, _, s=s):
            k = lax.rem(me.chip + 1 + i, chips)
            here = 2 * k + s == me.d

            @pl.when(here)
            def _():
                pltpu.make_async_copy(wqz.at[s], wqf_ref.at[me.d], wp_recv.at[me.d]).start()

            @pl.when(jnp.logical_not(here))
            def _():
                wq_plane(s, k).start()

            return 0

        lax.fori_loop(0, chips, step, 0)

    def in_plane(unit, t, k, sem, to):
        return remote(unit, wall_ref.at[t, 2 * k + me.core], mp_send.at[t, sem], mp_recv.at[t, k], 2 * to + me.core, me.z)

    def plane_units(t, unit):
        in_plane(unit, t, me.chip, 0, me.first).start()
        in_plane(unit, t, me.chip, 1, me.second).start()

    def to_sibling(t, k):
        unit = wall_ref.at[t, 2 * k + me.core]
        return remote(unit, unit, ms_send.at[t, k], ms_recv.at[t, k], me.sibling, me.z)

    def own_unit(t):
        unit = wall_ref.at[t, me.d]
        arrival(unit, mz_recv.at[t]).wait()
        pl.when(goes_up(t))(lambda: along_z(unit, t, 2 + t, me.z + 1).start())
        pl.when(goes_down(t))(lambda: along_z(unit, t, 2 + t, me.z - 1).start())
        plane_units(t, unit)
        to_sibling(t, me.chip).start()

    def plane_unit(t, k):
        unit = wall_ref.at[t, 2 * k + me.core]
        arrival(unit, mp_recv.at[t, k]).wait()
        return unit

    def plane_forward(t):
        unit = plane_unit(t, me.first)
        in_plane(unit, t, me.first, 2, me.second).start()
        to_sibling(t, me.first).start()

    def plane_rest(t):
        for k in (me.second, me.diagonal):
            plane_unit(t, k)
            to_sibling(t, k).start()

    plane_units(me.z, wm_ref)
    remote(wm_ref, wall_ref.at[me.z, me.d], ms_send.at[me.z, me.chip], ms_recv.at[me.z, me.chip], me.sibling, me.z).start()

    mine = pl.ds(pl.multiple_of(me.core * half, half), half)
    other = pl.ds(pl.multiple_of((1 - me.core) * half, half), half)
    far_first = 2 * (1 - me.pair) + me.pair
    far_second = 2 * (1 - me.pair) + 1 - me.pair
    blocks_in = (
        jnp.where(is_near, far_first, me.buddy),
        jnp.where(is_near, far_second, far_first),
        jnp.where(is_near, me.buddy, far_second),
    )

    def relay(n):
        j = blocks_in[n]
        part = xs_ref.at[j, mine]
        arrival(part, x_recv.at[j, me.core]).wait()
        remote(part, part, xr_send.at[1 + n, 0], x_recv.at[j, me.core], me.sibling, me.z).start()
        if n < 2:
            pl.when(is_near)(lambda: remote(part, part, xf_send.at[n], x_recv.at[j, me.core], me.d, me.buddy).start())

    own_unit(me.around[0])
    relay(0)
    relay(1)

    def small_wait(i, peer):
        arrival(smalls_ref.at[peer], sm_recv.at[peer]).wait()

    each_peer(small_wait)
    plane_count = smalls_ref[0][8:16]
    for k in range(1, dp):
        plane_count = plane_count + smalls_ref[k][8:16]
    counts[me.z] = plane_count
    for s in range(1, tp):
        remote(counts.at[me.z], counts.at[me.z], cn_send.at[s - 1], cn_recv.at[me.z], me.d, lax.rem(me.z + s, tp)).start()

    for k in range(dp):
        arrival(wqf_ref.at[k], wp_recv.at[k]).wait()
    zero = jnp.zeros((share, HEAD_DIM), BF16)
    gw = heads * HEAD_DIM
    for k in range(dp):
        w = wqf_ref[k]
        at = slice(k * share, (k + 1) * share)
        pads = []
        for m in range(3):
            cols = []
            for h in range(heads):
                cols += [w[:, m * gw + h * HEAD_DIM : m * gw + (h + 1) * HEAD_DIM], zero]
            pads.append(jnp.concatenate(cols, axis=1))
        wkp[at, :] = pads[1]
        wvp[at, :] = pads[2]
        scores[0, at, 0:384] = pads[0].astype(F32)
    wqT[...] = scores[0, 0:width, 0:384].T.astype(BF16)
    wvT[...] = wvp[...].astype(F32).T.astype(BF16)

    blocks = gw // share
    row_bias = jnp.zeros((8, 384), F32)
    col_bias = jnp.zeros((384, 8), F32)
    r_in = lax.broadcasted_iota(jnp.int32, (128, 384), 0)
    r_out = lax.broadcasted_iota(jnp.int32, (128, 384), 1)
    c_out = lax.broadcasted_iota(jnp.int32, (384, 128), 0)
    c_in = lax.broadcasted_iota(jnp.int32, (384, 128), 1)

    def padded(col):
        return (col // HEAD_DIM) * 128 + lax.rem(col, HEAD_DIM)

    for b in range(blocks):
        vecs = smalls_ref[me.group * blocks + b][0:8].astype(BF16)
        sel = jnp.logical_and(padded(r_in + b * share) == r_out, r_in < share)
        row_bias = row_bias + dot(vecs, jnp.where(sel, 1.0, 0.0).astype(BF16), 1, 0)
        sel = jnp.logical_and(padded(c_in + b * share) == c_out, c_in < share)
        col_bias = col_bias + dot(jnp.where(sel, 1.0, 0.0).astype(BF16), vecs, 1, 1)
    q_bias = col_bias[:, 0:1]
    v_bias_col = col_bias[:, 1:2]
    v_bias = row_bias[1:2, :]
    valid = smalls_ref[me.base + me.pair][12:13, 0:1]

    lane = lax.broadcasted_iota(jnp.int32, (rows, 128), 1)
    srow = lax.broadcasted_iota(jnp.int32, (128, rows), 0)

    def project(j):
        at = pl.ds(pl.multiple_of(j * rows, rows), rows)
        xb = xs_ref[j]
        keys = dot(xb, wkp[...], 1, 0)
        queries = dot(wqT[...], xb, 1, 1) + q_bias
        vals = dot(xb, wvp[...], 1, 0) + v_bias
        valsT = dot(wvT[...], xb, 1, 1) + v_bias_col
        pos = (j * rows + lax.broadcasted_iota(jnp.int32, (rows, 128), 0)).astype(F32)
        bias = jnp.where(pos < valid, 0.0, masked_score)
        for h in range(heads):
            span = slice(h * 128, (h + 1) * 128)
            vT[h * HEAD_DIM : (h + 1) * HEAD_DIM, at] = valsT[h * 128 : h * 128 + HEAD_DIM].astype(BF16)
            kA_ref[h, at, :] = jnp.where(lane == HEAD_DIM, bias, keys[:, span]).astype(BF16)
            qh = queries[span].astype(BF16) * BF16(HEAD_DIM**-0.5)
            qT_ref[h, :, at] = jnp.where(srow == HEAD_DIM, BF16(1), qh)
            v_ref[h, at, :] = vals[:, span].astype(BF16)

    arrival(xs_ref.at[me.z, pl.ds(0, half)], x_recv.at[me.z, 0]).wait()
    arrival(xs_ref.at[me.z, pl.ds(half, half)], x_recv.at[me.z, 1]).wait()
    project(me.z)
    relay(2)
    pl.when(is_near)(functools.partial(own_unit, me.around[1]))
    plane_forward(me.z)

    def project_next(i, _):
        j = jnp.where(i == 0, blocks_in[0], jnp.where(i == 1, blocks_in[1], blocks_in[2]))
        arrival(xs_ref.at[j, other], x_recv.at[j, 1 - me.core]).wait()
        project(j)
        return 0

    lax.fori_loop(0, tp - 1, project_next, 0)
    pl.when(is_near)(functools.partial(own_unit, me.around[2]))
    plane_forward(me.around[0])

    chunk = 256
    pieces = length // chunk

    def attend(i, _):
        j = lax.rem(me.z + 1 + i, tp)
        at = pl.ds(pl.multiple_of(j * rows, rows), rows)
        tops = []
        for h in range(heads):
            qt = qT_ref[h, :, at]
            top = None
            for c in range(pieces):
                s = dot(kA_ref[h, c * chunk : (c + 1) * chunk, :], qt, 1, 0)
                scores[h, c * chunk : (c + 1) * chunk, :] = s
                peak = jnp.max(s, axis=0, keepdims=True)
                top = peak if top is None else jnp.maximum(top, peak)
            tops.append(top)
        outs = []
        for h in range(heads):
            total, mixed = None, None
            for c in range(pieces):
                p = jnp.exp(scores[h, c * chunk : (c + 1) * chunk, :] - tops[h])
                part = jnp.sum(p, axis=0, keepdims=True)
                term = dot(vT[h * HEAD_DIM : (h + 1) * HEAD_DIM, c * chunk : (c + 1) * chunk], p.astype(BF16), 1, 0)
                total = part if total is None else total + part
                mixed = term if mixed is None else mixed + term
            mixed = mixed / total
            oT_ref[h * HEAD_DIM : (h + 1) * HEAD_DIM, at] = mixed
            lse_ref[h, :, at] = tops[h] + jnp.log(total)
            outs.append(mixed)
        o_buf[j] = jnp.concatenate(outs, axis=0).T.astype(BF16)
        here = jnp.logical_and(j == me.z, is_owner)

        @pl.when(here)
        def _():
            pltpu.make_async_copy(o_buf.at[j], oin_ref.at[me.group], o_recv.at[me.group]).start()

        @pl.when(jnp.logical_not(here))
        def _():
            remote(o_buf.at[j], oin_ref.at[me.group], o_send.at[i], o_recv.at[me.group], me.owner, j).start()

        for n in (1, 2):
            pl.when(jnp.logical_and(is_end, i == n - 1))(functools.partial(own_unit, me.around[n]))
        pl.when(i == 0)(functools.partial(plane_rest, me.z))
        pl.when(jnp.logical_and(is_near, i == 0))(functools.partial(plane_forward, me.around[1]))
        pl.when(jnp.logical_and(is_end, i == 2))(functools.partial(plane_forward, me.around[1]))
        pl.when(jnp.logical_and(is_near, i == 2))(functools.partial(plane_forward, me.around[2]))
        pl.when(jnp.logical_and(is_end, i == 3))(functools.partial(plane_forward, me.around[2]))
        return 0

    lax.fori_loop(0, tp, attend, 0)

    for t in me.around:
        plane_rest(t)

    arrival(wall_ref.at[me.z, me.d], mz_recv.at[me.z]).wait()
    for s in range(1, tp):
        t = lax.rem(me.z + s, tp)
        arrival(counts.at[t], cn_recv.at[t]).wait()
    total = counts[0]
    for t in range(1, tp):
        total = total + counts[t]
    count_ref[...] = total
    for g in range(4):
        arrival(oin_ref.at[g], o_recv.at[g]).wait()

    def sibling_units(n, _):
        t, k = n // chips, lax.rem(n, chips)
        arrival(wall_ref.at[t, 2 * k + 1 - me.core], ms_recv.at[t, k]).wait()
        to_sibling(t, k).wait_send()
        return 0

    lax.fori_loop(0, tp * chips, sibling_units, 0)

    def sent(n, _):
        t, i = n // (chips - 1), lax.rem(n, chips - 1)
        in_plane(wm_ref, t, me.chip, i, me.first).wait_send()
        return 0

    lax.fori_loop(0, tp * (chips - 1), sent, 0)
    each_peer(lambda i, peer: small_copy(i, peer).wait_send())
    for s in range(2):

        @pl.when(me.z // 2 + 2 * s != me.z)
        def _(s=s):
            remote(wq_ref, wqz.at[0], wz_send.at[s], wz_recv.at[0], me.sibling, me.z).wait_send()

        def step(i, _, s=s):
            k = lax.rem(me.chip + 1 + i, chips)

            @pl.when(2 * k + s != me.d)
            def _():
                wq_plane(s, k).wait_send()

            return 0

        lax.fori_loop(0, chips, step, 0)
    for s in range(tp - 1):
        remote(counts.at[0], counts.at[0], cn_send.at[s], cn_recv.at[0], me.sibling, me.z).wait_send()

    def z_sent(sem):
        along_z(wm_ref, 0, sem, 0).wait_send()

    pl.when(me.z > 0)(functools.partial(z_sent, 0))
    pl.when(me.z < tp - 1)(functools.partial(z_sent, 1))
    for t in range(tp):
        pl.when(jnp.logical_or(goes_up(t), goes_down(t)))(functools.partial(z_sent, 2 + t))

    def x_sent(sem):
        remote(x_ref.at[pl.ds(0, half)], xs_ref.at[0, pl.ds(0, half)], sem, x_recv.at[0, 0], me.sibling, me.z).wait_send()

    for h in range(2):
        x_sent(x_send.at[h])

        @pl.when(is_owner)
        def _(h=h):
            x_sent(xr_send.at[0, h])

    for n in range(3):
        x_sent(xr_send.at[1 + n, 0])

    @pl.when(is_near)
    def _():
        for n in range(2):
            x_sent(xf_send.at[n])

    def o_sent(i, _):
        j = lax.rem(me.z + 1 + i, tp)

        @pl.when(jnp.logical_not(jnp.logical_and(j == me.z, is_owner)))
        def _():
            remote(o_buf.at[0], oin_ref.at[0], o_send.at[i], o_recv.at[0], me.sibling, me.z).wait_send()

        return 0

    lax.fori_loop(0, tp, o_sent, 0)


def front(x, wq, wm, small, dp, tp):
    rows, width = x.shape
    length = rows * tp
    share = wq.shape[0]
    chips = dp // 2
    S = jax.ShapeDtypeStruct
    vmem = pl.BlockSpec(memory_space=pltpu.VMEM)
    anym = pl.BlockSpec(memory_space=pl.ANY)
    dma = pltpu.SemaphoreType.DMA
    return pl.pallas_call(
        front_kernel,
        name="front",
        out_shape=(
            S((4, rows, 192), BF16),
            S((tp, dp, share, wm.shape[1]), BF16),
            S((dp, 16, 128), F32),
            S((8, 128), F32),
            S((tp, rows, width), BF16),
            S((dp, share, wq.shape[1]), BF16),
            S((192, length), F32),
            S((3, 1, length), F32),
            S((3, 128, length), BF16),
            S((3, length, 128), BF16),
            S((3, length, 128), BF16),
        ),
        in_specs=[vmem] * 4,
        out_specs=(anym, anym) + (vmem,) * 9,
        scratch_shapes=[
            pltpu.VMEM((2, share, wq.shape[1]), BF16),
            pltpu.VMEM((tp, 8, 128), F32),
            pltpu.VMEM((192, length), BF16),
            pltpu.VMEM((3, length, rows), F32),
            pltpu.VMEM((tp, rows, 192), BF16),
            pltpu.VMEM((384, width), BF16),
            pltpu.VMEM((width, 384), BF16),
            pltpu.VMEM((width, 384), BF16),
            pltpu.VMEM((384, width), BF16),
            dma((dp - 1,)), dma((dp,)), dma((tp - 1,)), dma((tp,)),
            dma((2,)), dma((2,)), dma((2, chips)), dma((dp,)),
            dma((2,)), dma((tp, 2)), dma((4, 2)), dma((2,)),
            dma((tp + 2,)), dma((tp,)), dma((tp, chips - 1)), dma((tp, chips)), dma((tp, chips)), dma((tp, chips)),
            dma((tp,)), dma((4,)),
        ],
        compiler_params=pltpu.CompilerParams(
            collective_id=0, has_side_effects=True, vmem_limit_bytes=VMEM_LIMIT
        ),
    )(x, wq, wm, small)


SQRT_HALF = 0.7071067811865476
INV_SQRT_2PI = 0.3989422804014327


def norm_forward(values, gain, shift):
    centred = values - jnp.mean(values, axis=1, keepdims=True)
    inv = lax.rsqrt(jnp.mean(centred * centred, axis=1, keepdims=True) + norm_eps)
    normed = centred * inv
    return normed * gain + shift, normed, inv


def norm_backward(grad_out, normed, inv, gain):
    g = grad_out * gain
    plain = jnp.mean(g, axis=1, keepdims=True)
    mixed = jnp.mean(g * normed, axis=1, keepdims=True)
    return inv * (g - plain - normed * mixed)


def column_sum(values):
    return jnp.sum(values, axis=0, keepdims=True)


def mid_kernel(
    x_ref, teacher_ref, counted_ref, scale_ref, count_ref, oin_ref, wall_ref, smalls_ref,
    out_ref, dr1_ref, do_ref, grad_ref, pack_ref,
    slope_ref, act_ref, f_ref, n1_ref, acc_ref, hT_ref, dfT_ref, vec_ref, ib_ref, small_ref, ismall_ref,
):
    groups = wall_ref.shape[0]
    width = x_ref.shape[1]
    gw = oin_ref.shape[2]
    inner = slice(0, width)
    outer = slice(width, 2 * width)
    mixer = slice(2 * width, 2 * width + gw)
    vec = lambda i: vec_ref[i : i + 1, :]
    dp = smalls_ref.shape[0]
    share = width // dp
    per = dp // groups
    hrows = ib_ref.shape[2] // per // 128
    for d in range(dp):
        vec_ref[:, d * share : (d + 1) * share] = smalls_ref[d, 0:8, 0:share]
        for r in range(hrows):
            at = (d % per * hrows + r) * 128
            ib_ref[d // per, :, at : at + 128] = smalls_ref[d, 9 + r : 10 + r, :]

    acc_ref[...] = x_ref[...].astype(F32) + vec(2)
    for g in range(groups):
        acc_ref[...] += dot(oin_ref[g], wall_ref[g, :, mixer], 1, 1)
    hidden, normed1, inv1 = norm_forward(acc_ref[...], vec(3), vec(4))
    n1_ref[...] = normed1
    low = hidden.astype(BF16)
    hT_ref[...] = hidden.T.astype(BF16)
    f_ref[...] = hidden + vec(5)

    def ffn_forward(g, _):
        up = dot(low, wall_ref[g, :, inner], 1, 0) + ib_ref[g]
        below = 0.5 * (1.0 + lax.erf(up * SQRT_HALF))
        slope_ref[g] = below + up * (INV_SQRT_2PI * jnp.exp(-0.5 * up * up))
        act = (up * below).astype(BF16)
        act_ref[g] = act
        f_ref[...] += dot(act, wall_ref[g, :, outer], 1, 1)
        return 0

    lax.fori_loop(0, groups, ffn_forward, 0)
    final, normed2, inv2 = norm_forward(f_ref[...], vec(6), vec(7))
    out_ref[...] = final.astype(BF16)
    diff = final - teacher_ref[...].astype(F32)
    counted = counted_ref[...]
    small_ref[...] = jnp.zeros_like(small_ref)
    small_ref[6:7, 0:1] = jnp.sum(counted * jnp.sum(diff * diff, axis=1, keepdims=True), axis=0, keepdims=True)
    scale = 2.0 * scale_ref[0, 0] / (count_ref[0:1, 0:1] * width)
    grad = (scale * counted) * diff
    small_ref[4:5, :] = column_sum(grad * normed2)
    small_ref[5:6, :] = column_sum(grad)
    dr2 = norm_backward(grad, normed2, inv2, vec(6))
    small_ref[3:4, :] = column_sum(dr2)
    acc_ref[...] = dr2
    df = dr2.astype(BF16)
    dfT_ref[...] = dr2.T.astype(BF16)

    def ffn_backward(g, _):
        du = (dot(df, wall_ref[g, :, outer], 1, 0) * slope_ref[g]).astype(BF16)
        ismall_ref[g] = column_sum(du.astype(F32))
        acc_ref[...] += dot(du, wall_ref[g, :, inner], 1, 1)
        grad_ref[g, :, inner] = dot(hT_ref[...], du, 1, 0).astype(BF16)
        grad_ref[g, :, outer] = dot(dfT_ref[...], act_ref[g], 1, 0).astype(BF16)
        return 0

    lax.fori_loop(0, groups, ffn_backward, 0)
    dh1 = acc_ref[...]
    normed1 = n1_ref[...]
    small_ref[1:2, :] = column_sum(dh1 * normed1)
    small_ref[2:3, :] = column_sum(dh1)
    dr1 = norm_backward(dh1, normed1, inv1, vec(3))
    small_ref[0:1, :] = column_sum(dr1)
    dr1_ref[...] = dr1
    da = dr1.astype(BF16)
    daT = dr1.T.astype(BF16)
    for g in range(groups):
        do_ref[g] = dot(da, wall_ref[g, :, mixer], 1, 0).astype(BF16)
        grad_ref[g, :, mixer] = dot(daT, oin_ref[g], 1, 0).astype(BF16)
    pack_ref[...] = jnp.zeros_like(pack_ref)
    for d in range(dp):
        pack_ref[d, 2:8, 0:share] = small_ref[0:6, d * share : (d + 1) * share]
        pack_ref[d, 8:9, :] = jnp.broadcast_to(small_ref[6:7, 0:1], (1, 128))
        for r in range(hrows):
            at = (d % per * hrows + r) * 128
            pack_ref[d, 9 + r : 10 + r, :] = ismall_ref[d // per, :, at : at + 128]


def mid(x, teacher, counted, scale, count, oin, wall, smalls, hidden):
    rows, width = x.shape
    groups = wall.shape[0]
    S = jax.ShapeDtypeStruct
    vmem = pl.BlockSpec(memory_space=pltpu.VMEM)
    return pl.pallas_call(
        mid_kernel,
        name="mid",
        out_shape=(
            S((rows, width), BF16),
            S((rows, width), F32),
            S(oin.shape, BF16),
            S(wall.shape, BF16),
            S(smalls.shape, F32),
        ),
        in_specs=[vmem, vmem, vmem, pl.BlockSpec(memory_space=pltpu.SMEM)] + [vmem] * 4,
        out_specs=(vmem,) * 5,
        scratch_shapes=[
            pltpu.VMEM((groups, rows, hidden), F32),
            pltpu.VMEM((groups, rows, hidden), BF16),
            pltpu.VMEM((rows, width), F32),
            pltpu.VMEM((rows, width), F32),
            pltpu.VMEM((rows, width), F32),
            pltpu.VMEM((width, rows), BF16),
            pltpu.VMEM((width, rows), BF16),
            pltpu.VMEM((8, width), F32),
            pltpu.VMEM((groups, 1, hidden), F32),
            pltpu.VMEM((8, width), F32),
            pltpu.VMEM((groups, 1, hidden), F32),
        ],
        compiler_params=pltpu.CompilerParams(vmem_limit_bytes=VMEM_LIMIT),
    )(x, teacher, counted, scale, count, oin, wall, smalls)


def back_kernel(
    do_ref, grad_ref, xs_ref, wqf_ref, oT_ref, lse_ref, qT_ref, kA_ref, v_ref, pack_ref,
    fin, gsum_ref, qgrad_ref, small_ref,
    dof, doT, delta, qs, kT, dk, dv, dqT, dqkv,
    sib, own, pln, zsrc, zin, parts, pr, sj, rr, qsend, qr, qz, qf, spack, srecv, zpack,
    do_send, do_recv, sb_send, sb_recv, own_sem, pl_send, pl_recv, zz_send, zz_recv,
    pr_send, pr_recv, rr_send, rr_recv, fin_send, fin_recv, qr_send, qr_recv, qf_send, qf_recv,
    sm_send, sm_recv, sz_send, sz_recv,
):
    me = Place()
    dp, tp, chips = me.dp, me.tp, me.chips
    rows, width = xs_ref.shape[1:]
    half = rows // 2
    length = rows * tp
    heads = 3
    gw = heads * HEAD_DIM
    share = width // dp
    greet(me)

    for g in range(4):
        t = 2 * me.core + g // 2
        d = me.base + g % 2
        here = jnp.logical_and(t == me.z, g % 2 == me.core)

        @pl.when(here)
        def _(g=g):
            pltpu.make_async_copy(do_ref.at[g], dof.at[me.z], do_recv.at[me.z]).start()

        @pl.when(jnp.logical_not(here))
        def _(g=g, t=t, d=d):
            remote(do_ref.at[g], dof.at[me.z], do_send.at[g], do_recv.at[me.z], d, t).start()

    order = me.around[::-1] + (me.z,)

    def sib_copy(t):
        return remote(grad_ref.at[t, :, 1 - me.core], sib.at[t], sb_send.at[t], sb_recv.at[t], me.sibling, me.z)

    for t in order:
        sib_copy(t).start()
        pltpu.make_async_copy(grad_ref.at[t, :, me.core], own.at[t], own_sem.at[t]).start()

    def plane_copy(t, n):
        k = (me.diagonal, me.first, me.second)[n]
        to = (me.first, me.first, me.second)[n]
        return remote(own.at[t, k], pln.at[t, n], pl_send.at[t, n], pl_recv.at[t, n], 2 * to + me.core, me.z)

    def pair_sum(t):
        arrival(own.at[t], own_sem.at[t]).wait()
        arrival(sib.at[t], sb_recv.at[t]).wait()

        def unit(k, _):
            own[t, k] = (own[t, k].astype(F32) + sib[t, k].astype(F32)).astype(BF16)
            return 0

        lax.fori_loop(0, chips, unit, 0)
        plane_copy(t, 0).start()
        plane_copy(t, 1).start()

    def pass_on(n):
        t = order[n]
        arrival(pln.at[t, 0], pl_recv.at[t, 0]).wait()
        own[t, me.second] = (own[t, me.second].astype(F32) + pln[t, 0].astype(F32)).astype(BF16)
        plane_copy(t, 2).start()

    has_below, has_above = me.z > 0, me.z < tp - 1

    def z_copy(t):
        up = t > me.z
        to = jnp.where(up, me.z + 1, me.z - 1)
        slot = jnp.where(jnp.logical_and(to == t, jnp.logical_not(up)), tp, t)
        return remote(zsrc.at[t], zin.at[slot], zz_send.at[t], zz_recv.at[slot], me.d, to)

    def plane_total(t):
        for n in (1, 2):
            arrival(pln.at[t, n], pl_recv.at[t, n]).wait()
        return own[t, me.chip].astype(F32) + pln[t, 1].astype(F32) + pln[t, 2].astype(F32)

    def z_step(n):
        t = order[n]
        total = plane_total(t)
        comes = jnp.where(t > me.z, has_below, has_above)

        @pl.when(comes)
        def _():
            arrival(zin.at[t], zz_recv.at[t]).wait()
            zsrc[t] = (total + zin[t].astype(F32)).astype(BF16)

        @pl.when(jnp.logical_not(comes))
        def _():
            zsrc[t] = total.astype(BF16)

        z_copy(t).start()

    for t in order:
        pair_sum(t)

    is_near = me.z == me.near_here
    is_end = jnp.logical_not(is_near)
    far = 2 * (1 - me.pair)
    far_first, far_second = far + me.pair, far + 1 - me.pair

    def block_at(i):
        return jnp.where(i == 0, far_second, jnp.where(i == 1, far_first, jnp.where(i == 2, me.buddy, me.z)))

    def prepare(j, at):
        arrival(dof.at[j], do_recv.at[j]).wait()
        flipped = dof[j].astype(F32).T
        doT[:, at] = flipped.astype(BF16)
        for h in range(heads):
            span = slice(h * HEAD_DIM, (h + 1) * HEAD_DIM)
            delta[h, :, at] = jnp.sum(flipped[span] * oT_ref[span, at], axis=0, keepdims=True)
            qs[h, at, :] = qT_ref[h, :, at].astype(F32).T.astype(BF16)

    always = {(0, 1): (pass_on, 0), (0, 3): (pass_on, 1), (1, 1): (pass_on, 2), (2, 0): (pass_on, 3)}
    at_ends = {(1, 0): (z_step, 0), (1, 2): (z_step, 1), (2, 1): (z_step, 2)}
    in_middle = {(1, 2): (z_step, 0), (2, 0): (z_step, 1), (2, 2): (z_step, 2)}
    chunk = 256
    def flip_keys(j, _):
        at = pl.ds(pl.multiple_of(j * rows, rows), rows)
        for h in range(heads):
            kT[h, :, at] = kA_ref[h, at, :].astype(F32).T[0:HEAD_DIM, :].astype(BF16)
        return 0

    lax.fori_loop(0, tp, flip_keys, 0)
    for h in range(heads):
        dk[...] = jnp.zeros_like(dk)
        dv[...] = jnp.zeros_like(dv)

        def attend(i, _, h=h):
            j = block_at(3 - i)
            at = pl.ds(pl.multiple_of(j * rows, rows), rows)
            if h == 0:
                prepare(j, at)
            span = slice(h * HEAD_DIM, (h + 1) * HEAD_DIM)
            qt, gt = qT_ref[h, :, at], doT[span, at]
            q, go = qs[h, at, :], dof[j, :, span]
            lse, dl = lse_ref[h, :, at], delta[h, :, at]
            dq = None
            for c in range(length // chunk):
                r = slice(c * chunk, (c + 1) * chunk)
                p = jnp.exp(dot(kA_ref[h, r, :], qt, 1, 0) - lse)
                dp_ = dot(v_ref[h, r, 0:HEAD_DIM], gt, 1, 0)
                ds = (p * (dp_ - dl)).astype(BF16)
                dv[r, :] += dot(p.astype(BF16), go, 1, 0)
                dk[r, :] += dot(ds, q, 1, 0)
                term = dot(kT[h, :, r], ds, 1, 0)
                dq = term if dq is None else dq + term
            dqT[span, at] = dq * HEAD_DIM**-0.5
            for where, hooks in ((None, always), (is_end, at_ends), (is_near, in_middle)):
                for (head, step), (act, n) in hooks.items():
                    if head == h:
                        now = i == step
                        pl.when(now if where is None else jnp.logical_and(where, now))(functools.partial(act, n))
            return 0

        lax.fori_loop(0, tp, attend, 0)
        for j in range(tp):
            at = slice(j * rows, (j + 1) * rows)
            dqkv[j, :, gw + h * HEAD_DIM : gw + (h + 1) * HEAD_DIM] = dk[at, 0:HEAD_DIM].astype(BF16)
            dqkv[j, :, 2 * gw + h * HEAD_DIM : 2 * gw + (h + 1) * HEAD_DIM] = dv[at, :].astype(BF16)

    weights = wqf_ref[...].reshape(width, 3 * gw)
    ones = jnp.ones((8, rows), BF16)
    mine = pl.ds(pl.multiple_of(me.core * half, half), half)
    other = pl.ds(pl.multiple_of((1 - me.core) * half, half), half)

    def pr_copy(j):
        return remote(parts.at[j, other], pr.at[j], pr_send.at[j], pr_recv.at[j], me.sibling, me.z)

    def rr_copy(j):
        return remote(sj.at[j], rr.at[j], rr_send.at[j], rr_recv.at[j], me.d, me.buddy)

    def collects(j):
        return jnp.where(j // 2 == me.pair, j, me.near_here) == me.z

    def chip_sum(j):
        arrival(pr.at[j], pr_recv.at[j]).wait()
        sj[j] = (parts[j, mine, :].astype(F32) + pr[j].astype(F32)).astype(BF16)
        pl.when(jnp.logical_not(collects(j)))(lambda: rr_copy(j).start())

    def token_grads(i, sums):
        j = block_at(i)
        at = pl.ds(pl.multiple_of(j * rows, rows), rows)
        dqkv[j, :, 0:gw] = dqT[:, at].T.astype(BF16)
        flat = dqkv[j]
        parts[j] = dot(flat, weights, 1, 1).astype(BF16)
        pr_copy(j).start()
        pl.when(i > 0)(lambda: chip_sum(block_at(i - 1)))
        return sums + dot(ones, flat, 1, 0)

    sums = lax.fori_loop(0, tp, token_grads, jnp.zeros((8, 3 * gw), F32))
    chip_sum(block_at(tp - 1))

    spack[...] = pack_ref[...]
    blocks = gw // share
    for b in range(blocks):
        spack[me.group * blocks + b, 0:1, 0:share] = sums[0:1, b * share : (b + 1) * share]
        spack[me.group * blocks + b, 1:2, 0:share] = sums[0:1, 2 * gw + b * share : 2 * gw + (b + 1) * share]

    def small_copy(i):
        peer = lax.rem(me.d + 1 + i, dp)
        return remote(spack.at[peer], srecv.at[i], sm_send.at[i], sm_recv.at[i], peer, me.z)

    def small_start(i, _):
        small_copy(i).start()
        return 0

    lax.fori_loop(0, dp - 1, small_start, 0)

    def fin_copy(j):
        return remote(pr.at[j], fin.at[me.core], fin_send.at[j], fin_recv.at[me.core], me.owner, j)

    def lands_here(j):
        return jnp.logical_and(me.core == me.pair, j == me.z)

    total = None
    for j in range(tp):
        term = dot(xs_ref[j], dqkv[j], 0, 0)
        total = term if total is None else total + term
    qsend[...] = total.astype(BF16).reshape(dp, share, 3 * gw)

    def q_copy(peer, i):
        return remote(qsend.at[peer], qr.at[me.core, me.chip], qr_send.at[i], qr_recv.at[me.core, me.chip], peer, me.z)

    def q_start(i, _):
        peer = lax.rem(me.d + i, dp)

        @pl.when(i == 0)
        def _():
            pltpu.make_async_copy(qsend.at[peer], qr.at[me.core, me.chip], qr_recv.at[me.core, me.chip]).start()

        @pl.when(i > 0)
        def _():
            q_copy(peer, i).start()

        return 0

    lax.fori_loop(0, dp, q_start, 0)

    def pair_total(i, _):
        j = block_at(i)

        @pl.when(collects(j))
        def _():
            arrival(rr.at[j], rr_recv.at[j]).wait()
            pr[j] = (sj[j].astype(F32) + rr[j].astype(F32)).astype(BF16)

            @pl.when(lands_here(j))
            def _():
                pltpu.make_async_copy(pr.at[j], fin.at[me.core], fin_recv.at[me.core]).start()

            @pl.when(jnp.logical_not(lands_here(j)))
            def _():
                fin_copy(j).start()

        return 0

    lax.fori_loop(0, tp, pair_total, 0)

    def q_pair(s):
        return me.z // 2, 2 * me.low + s

    for s in range(2):
        total = None
        for k in range(chips):
            arrival(qr.at[s, k], qr_recv.at[s, k]).wait()
            term = qr[s, k].astype(F32)
            total = term if total is None else total + term
        qz[s] = total.astype(BF16)
        p, t = q_pair(s)

        @pl.when(t == me.z)
        def _(s=s, p=p):
            pltpu.make_async_copy(qz.at[s], qf.at[p], qf_recv.at[p]).start()

        @pl.when(t != me.z)
        def _(s=s, p=p, t=t):
            remote(qz.at[s], qf.at[p], qf_send.at[s], qf_recv.at[p], me.d, t).start()

    total = spack[me.d]
    for i in range(dp - 1):
        arrival(srecv.at[i], sm_recv.at[i]).wait()
        total = total + srecv[i]
    zpack[me.z] = total

    def sz_copy(s):
        return remote(zpack.at[me.z], zpack.at[me.z], sz_send.at[s - 1], sz_recv.at[me.z], me.d, lax.rem(me.z + s, tp))

    for s in range(1, tp):
        sz_copy(s).start()

    for h in range(2):
        arrival(fin.at[h], fin_recv.at[h]).wait()
    for p in range(2):
        arrival(qf.at[p], qf_recv.at[p]).wait()
    qgrad_ref[...] = qf[0].astype(F32) + qf[1].astype(F32)
    for s in range(1, tp):
        t = lax.rem(me.z + s, tp)
        arrival(zpack.at[t], sz_recv.at[t]).wait()
    total = zpack[0]
    for t in range(1, tp):
        total = total + zpack[t]
    small_ref[...] = total
    gsum_ref[...] = plane_total(me.z)
    for slot, comes in ((me.z, has_below), (tp, has_above)):

        @pl.when(comes)
        def _(slot=slot):
            arrival(zin.at[slot], zz_recv.at[slot]).wait()
            gsum_ref[...] += zin[slot].astype(F32)

    for g in range(4):

        @pl.when(jnp.logical_not(jnp.logical_and(2 * me.core + g // 2 == me.z, g % 2 == me.core)))
        def _(g=g):
            remote(do_ref.at[g], dof.at[0], do_send.at[g], do_recv.at[0], me.sibling, me.z).wait_send()

    for t in range(tp):
        sib_copy(t).wait_send()
        pr_copy(t).wait_send()

        @pl.when(jnp.logical_not(collects(t)))
        def _(t=t):
            rr_copy(t).wait_send()

        @pl.when(jnp.logical_and(collects(t), jnp.logical_not(lands_here(t))))
        def _(t=t):
            fin_copy(t).wait_send()

    for t in range(tp):
        for n in range(3):
            plane_copy(t, n).wait_send()
        pl.when(t != me.z)(lambda t=t: z_copy(t).wait_send())

    def peers_sent(i, _):
        small_copy(i).wait_send()
        q_copy(lax.rem(me.d + 1 + i, dp), i + 1).wait_send()
        return 0

    lax.fori_loop(0, dp - 1, peers_sent, 0)
    for s in range(1, tp):
        sz_copy(s).wait_send()
    for s in range(2):
        p, t = q_pair(s)

        @pl.when(t != me.z)
        def _(s=s, p=p, t=t):
            remote(qz.at[s], qf.at[p], qf_send.at[s], qf_recv.at[p], me.d, t).wait_send()


def back(do, grad, xs, wqf, oT, lse, qT, kA, v, pack):
    tp, rows, width = xs.shape
    dp, share, qwidth = wqf.shape
    chips = dp // 2
    length = rows * tp
    half = rows // 2
    cols = grad.shape[-1]
    S = jax.ShapeDtypeStruct
    vmem = pl.BlockSpec(memory_space=pltpu.VMEM)
    anym = pl.BlockSpec(memory_space=pl.ANY)
    dma = pltpu.SemaphoreType.DMA
    V = pltpu.VMEM
    return pl.pallas_call(
        back_kernel,
        name="back",
        out_shape=(
            S((2, half, width), BF16),
            S((share, cols), F32),
            S((share, qwidth), F32),
            S((16, 128), F32),
        ),
        in_specs=[anym, anym] + [vmem] * 8,
        out_specs=(vmem,) * 4,
        scratch_shapes=[
            V((tp, rows, 192), BF16), V((192, length), BF16), V((3, 1, length), F32),
            V((3, length, 128), BF16), V((3, HEAD_DIM, length), BF16),
            V((length, 128), F32), V((length, HEAD_DIM), F32), V((192, length), F32), V((tp, rows, qwidth), BF16),
            V((tp, chips, share, cols), BF16), V((tp, chips, share, cols), BF16), V((tp, chips - 1, share, cols), BF16),
            V((tp, share, cols), BF16), V((tp + 1, share, cols), BF16),
            V((tp, rows, width), BF16), V((tp, half, width), BF16), V((tp, half, width), BF16), V((tp, half, width), BF16),
            V((dp, share, qwidth), BF16), V((2, chips, share, qwidth), BF16), V((2, share, qwidth), BF16), V((2, share, qwidth), BF16),
            V((dp, 16, 128), F32), V((dp - 1, 16, 128), F32), V((tp, 16, 128), F32),
            dma((4,)), dma((tp,)), dma((tp,)), dma((tp,)), dma((tp,)), dma((tp, 3)), dma((tp, 3)), dma((tp,)), dma((tp + 1,)),
            dma((tp,)), dma((tp,)), dma((tp,)), dma((tp,)), dma((tp,)), dma((2,)), dma((dp,)), dma((2, chips)), dma((2,)), dma((2,)),
            dma((dp - 1,)), dma((dp - 1,)), dma((tp - 1,)), dma((tp,)),
        ],
        compiler_params=pltpu.CompilerParams(
            collective_id=1, has_side_effects=True, vmem_limit_bytes=VMEM_LIMIT
        ),
    )(do, grad, xs, wqf, oT, lse, qT, kA, v, pack)


def pack_kernel(length_ref, mask_ref, *refs):
    vectors, (ib_ref, wq_ref, wk_ref, wv_ref, wi_ref, wo_ref, wx_ref) = refs[:8], refs[8:15]
    sm_ref, w3_ref, wm_ref, counted_ref = refs[15:]
    rows = mask_ref.shape[1]
    share, gw = wq_ref.shape
    hidden = wi_ref.shape[1]
    pos = lax.axis_index("tensor") * rows + lax.broadcasted_iota(jnp.int32, (8, rows), 1)
    mask = jnp.broadcast_to(mask_ref[...], (8, rows))
    valid = length_ref[0]
    counted = jnp.where(jnp.logical_and(pos < valid, mask == 1), 1.0, 0.0)
    counted_ref[...] = counted.T[:, 0:1]
    sm_ref[...] = jnp.zeros_like(sm_ref)
    for i, v in enumerate(vectors):
        sm_ref[i : i + 1, 0:share] = v[...].astype(F32)
    sm_ref[8:9, :] = jnp.broadcast_to(jnp.sum(counted[0:1, :], axis=1, keepdims=True), (1, 128))
    for r in range(ib_ref.shape[1] // 128):
        sm_ref[9 + r : 10 + r, :] = ib_ref[:, r * 128 : (r + 1) * 128].astype(F32)
    sm_ref[12:13, :] = jnp.full((1, 128), valid, jnp.int32).astype(F32)
    for i, w in enumerate((wq_ref, wk_ref, wv_ref)):
        w3_ref[:, i * gw : (i + 1) * gw] = w[...]
    wm_ref[:, 0:hidden] = wi_ref[...]
    wm_ref[:, hidden : 2 * hidden] = wo_ref[...]
    wm_ref[:, 2 * hidden :] = wx_ref[...].astype(F32).T.astype(BF16)


def pack_inputs(lengths, mask, vectors, inner_bias, wq, wk, wv, wi, wo, wx):
    share, gw = wq.shape
    rows = mask.shape[0]
    S = jax.ShapeDtypeStruct
    vmem = pl.BlockSpec(memory_space=pltpu.VMEM)
    return pl.pallas_call(
        pack_kernel,
        name="pack_inputs",
        out_shape=(
            S((16, 128), F32),
            S((share, 3 * gw), BF16),
            S((share, 2 * wi.shape[1] + gw), BF16),
            S((rows, 1), F32),
        ),
        in_specs=[pl.BlockSpec(memory_space=pltpu.SMEM)] + [vmem] * 16,
        out_specs=(vmem,) * 4,
    )(lengths, mask.reshape(1, rows), *vectors, inner_bias.reshape(1, -1), wq, wk, wv, wi, wo, wx)


def finish_kernel(
    dr1_ref, fin_ref, gsum_ref, qgrad_ref, small_ref, count_ref,
    loss_ref, dx_ref, q_ref, k_ref, v_ref, mixer_ref, inner_ref, outer_ref, ib_ref, *lines,
):
    half = fin_ref.shape[1]
    width = dr1_ref.shape[1]
    share, gw = q_ref.shape
    hidden = inner_ref.shape[1]
    loss_ref[...] = small_ref[8:9, 0:1] / (count_ref[0:1, 0:1] * width)
    for h in range(2):
        at = slice(h * half, (h + 1) * half)
        dx_ref[at, :] = dr1_ref[at, :] + fin_ref[h].astype(F32)
    for i, ref in enumerate((q_ref, k_ref, v_ref)):
        ref[...] = qgrad_ref[:, i * gw : (i + 1) * gw]
    inner_ref[...] = gsum_ref[:, 0:hidden]
    outer_ref[...] = gsum_ref[:, hidden : 2 * hidden]
    mixer_ref[...] = gsum_ref[:, 2 * hidden :].T
    for r in range(ib_ref.shape[1] // 128):
        ib_ref[:, r * 128 : (r + 1) * 128] = small_ref[9 + r : 10 + r, :]
    for i, ref in enumerate(lines):
        ref[...] = small_ref[i : i + 1, 0:share]


def finish(dr1, fin, gsum, qgrad, ssum, count, hidden, hshare):
    share = qgrad.shape[0]
    gw = qgrad.shape[1] // 3
    S = jax.ShapeDtypeStruct
    vmem = pl.BlockSpec(memory_space=pltpu.VMEM)
    shapes = [(1, 1), dr1.shape] + [(share, gw)] * 3 + [(gw, share), (share, hidden), (share, hidden), (1, hshare)]
    shapes += [(1, share)] * 8
    return pl.pallas_call(
        finish_kernel,
        name="finish",
        out_shape=tuple(S(shape, F32) for shape in shapes),
        in_specs=[vmem] * 6,
        out_specs=(vmem,) * len(shapes),
        compiler_params=pltpu.CompilerParams(vmem_limit_bytes=VMEM_LIMIT),
    )(dr1, fin, gsum, qgrad, ssum, count)


def shards(
    tokens, teacher, lengths, loss_mask, loss_scale,
    query_weight, query_bias, key_weight, value_weight, value_bias, mixer_weight, mixer_bias,
    first_gain, first_shift, inner_weight, inner_bias, outer_weight, outer_bias, second_gain, second_shift,
):
    dp, tp = lax.axis_size("dp"), lax.axis_size("tensor")
    if dp != 8 or tp != 4:
        return plain_shards(
            tokens, teacher, lengths, loss_mask, loss_scale,
            query_weight, query_bias, key_weight, value_weight, value_bias, mixer_weight, mixer_bias,
            first_gain, first_shift, inner_weight, inner_bias, outer_weight, outer_bias, second_gain, second_shift,
        )
    width = tokens.shape[1]
    share, gw = query_weight.shape
    hidden = inner_weight.shape[1]
    hshare = inner_bias.shape[0]
    hrows = hshare // 128
    rows_of = [
        v.reshape(1, -1)
        for v in (query_bias, value_bias, mixer_bias, first_gain, first_shift, outer_bias, second_gain, second_shift)
    ]
    small, wq, wm, counted = pack_inputs(
        lengths, loss_mask, rows_of, inner_bias, query_weight, key_weight, value_weight, inner_weight, outer_weight.T, mixer_weight
    )
    oin, wall, smalls, count, xs, wqf, oT, lse, qT, kA, v = front(tokens, wq, wm, small, dp, tp)
    token_total = count[0, 0]
    wall = wall.reshape(tp, width, wm.shape[1])
    layer_output, dr1, do, grad, pack = mid(
        tokens, teacher, counted, loss_scale.reshape(1, 1), count, oin, wall, smalls, hidden
    )
    grad = grad.reshape(tp, dp // 2, 2, share, wm.shape[1])
    fin, gsum, qgrad, ssum = back(do, grad, xs, wqf, oT, lse, qT, kA, v, pack)
    loss, input_grad, query_grad, key_grad, value_grad, mixer_grad, inner_grad, outer_grad, ib, *lines = finish(
        dr1, fin, gsum, qgrad, ssum, count, hidden, hshare
    )
    line = lambda i: lines[i].reshape(-1)
    return (
        layer_output,
        loss.reshape(()),
        input_grad,
        query_grad,
        line(0),
        key_grad,
        value_grad,
        line(1),
        mixer_grad,
        line(2),
        line(3),
        line(4),
        inner_grad,
        ib.reshape(-1),
        outer_grad.T,
        line(5),
        line(6),
        line(7),
    )


def in_blocks(value, dim, size):
    before, after = (value.shape[:dim], value.shape[dim + 1 :])
    return jnp.moveaxis(value.reshape(*before, size, -1, *after), dim, 0)


def summed_on_arrival(value, axis, dim):
    size = lax.axis_size(axis)
    blocks = lax.all_to_all(in_blocks(value, dim, size), axis, 0, 0, tiled=True)
    return jnp.sum(blocks.astype(jnp.float32), axis=0)


def sent_together(arrays, axis, dim, along):
    both = jnp.concatenate(arrays, axis=along)
    out, at, gathered = (summed_on_arrival(both, axis, dim), 0, [])
    for a in arrays:
        gathered.append(lax.slice_in_dim(out, at, at + a.shape[along], axis=along))
        at += a.shape[along]
    return tuple(gathered)


def contract_last(left_rows, right_rows):
    return lax.dot_general(
        left_rows, right_rows, (((1,), (1,)), ((), ())), preferred_element_type=jnp.float32
    )


def contract_first(left_rows, right_rows):
    return lax.dot_general(
        left_rows, right_rows, (((0,), (0,)), ((), ())), preferred_element_type=jnp.float32
    )


def plain_dot(left_rows, right_rows):
    return jnp.dot(left_rows, right_rows, preferred_element_type=jnp.float32)


def gelu_exact(pre_values):
    return jax.nn.gelu(pre_values, approximate=False)


def plain_norm_forward(values_in, gain_vec, shift_vec):
    centred = values_in - jnp.mean(values_in, axis=1, keepdims=True)
    inv_std = lax.rsqrt(jnp.mean(centred * centred, axis=1, keepdims=True) + norm_eps)
    normed = centred * inv_std
    return (normed * gain_vec + shift_vec, normed, inv_std)


def plain_norm_backward(grad_out, normed, inv_std, gain_vec):
    grad_normed = grad_out * gain_vec
    mean_plain = jnp.mean(grad_normed, axis=1, keepdims=True)
    mean_mixed = jnp.mean(grad_normed * normed, axis=1, keepdims=True)
    grad_in = inv_std * (grad_normed - mean_plain - normed * mean_mixed)
    return (grad_in, jnp.sum(grad_out * normed, axis=0), jnp.sum(grad_out, axis=0))


def plain_shards(
    tokens,
    teacher,
    lengths,
    loss_mask,
    loss_scale,
    query_weight,
    query_bias,
    key_weight,
    value_weight,
    value_bias,
    mixer_weight,
    mixer_bias,
    first_gain,
    first_shift,
    inner_weight,
    inner_bias,
    outer_weight,
    outer_bias,
    second_gain,
    second_shift,
):
    tp_count = lax.axis_size("tensor")
    tp_index = lax.axis_index("tensor")
    dp_count = lax.axis_size("dp")
    dp_index = lax.axis_index("dp")
    local_rows = tokens.shape[0]
    seq_len = local_rows * tp_count
    model_width = tokens.shape[1]
    head_width = query_weight.shape[1]
    hidden_width = inner_weight.shape[1]
    head_count = head_width // HEAD_DIM
    block_count = seq_len // QBLOCK
    score_scale = HEAD_DIM ** (-0.5)
    length_here = lengths[0]
    local_pos = tp_index * local_rows + jnp.arange(local_rows)
    counted = jnp.logical_and(local_pos < length_here, loss_mask == 1).astype(jnp.float32)
    count_local = jnp.sum(counted)
    small_stack = jnp.stack(
        [
            query_bias,
            value_bias,
            mixer_bias,
            first_gain,
            first_shift,
            outer_bias,
            second_gain,
            second_shift,
        ]
    )

    def fetch_params():
        return (
            lax.all_gather(query_weight, "dp", axis=0, tiled=True),
            lax.all_gather(key_weight, "dp", axis=0, tiled=True),
            lax.all_gather(value_weight, "dp", axis=0, tiled=True),
            lax.all_gather(mixer_weight, "dp", axis=1, tiled=True),
            lax.all_gather(inner_weight, "dp", axis=0, tiled=True),
            lax.all_gather(outer_weight, "dp", axis=1, tiled=True),
            lax.all_gather(small_stack, "dp", axis=1, tiled=True),
            lax.all_gather(inner_bias, "dp", axis=0, tiled=True),
        )

    def attn_gather(values_in):
        return lax.all_gather(values_in, "tensor", axis=0, tiled=True)

    def ffn_gather(values_in):
        return lax.all_gather(values_in, "tensor", axis=0, tiled=True)

    (
        query_full,
        key_full,
        value_full,
        mixer_full,
        inner_full,
        outer_full,
        small_full,
        innerb_full,
    ) = fetch_params()
    small_wide = small_full.astype(jnp.float32)
    qbias_mine = lax.dynamic_slice_in_dim(small_wide[0], tp_index * head_width, head_width)
    vbias_mine = lax.dynamic_slice_in_dim(small_wide[1], tp_index * head_width, head_width)
    inner_mine = lax.dynamic_slice_in_dim(
        innerb_full.astype(jnp.float32), tp_index * hidden_width, hidden_width
    )
    seq_rows = attn_gather(tokens)
    queries = (plain_dot(seq_rows, query_full) + qbias_mine).astype(jnp.bfloat16)
    keys_all = plain_dot(seq_rows, key_full).astype(jnp.bfloat16)
    values_all = (plain_dot(seq_rows, value_full) + vbias_mine).astype(jnp.bfloat16)
    keys_three = keys_all.reshape(seq_len, head_count, HEAD_DIM)
    values_three = values_all.reshape(seq_len, head_count, HEAD_DIM)
    key_valid = jnp.arange(seq_len) < length_here

    def score_block(query_block):
        scores = (
            jnp.einsum("qhd,khd->hqk", query_block, keys_three, preferred_element_type=jnp.float32)
            * score_scale
        )
        return jnp.where(key_valid[None, None, :], scores, masked_score)

    def forward_block(query_block):
        scores = score_block(query_block)
        row_top = jnp.max(scores, axis=2, keepdims=True)
        exp_scores = jnp.exp(scores - row_top)
        row_total = jnp.sum(exp_scores, axis=2, keepdims=True)
        prob_low = (exp_scores / row_total).astype(jnp.bfloat16)
        mixed_rows = jnp.einsum(
            "hqk,khd->qhd", prob_low, values_three, preferred_element_type=jnp.float32
        )
        return (mixed_rows.astype(jnp.bfloat16), (row_top + jnp.log(row_total))[:, :, 0])

    query_blocks = queries.reshape(block_count, QBLOCK, head_count, HEAD_DIM)
    attended, log_sums = lax.map(forward_block, query_blocks)
    attended = attended.reshape(seq_len, head_width)
    attn_out = lax.psum_scatter(
        plain_dot(attended, mixer_full).astype(jnp.bfloat16),
        "tensor",
        scatter_dimension=0,
        tiled=True,
    ).astype(jnp.float32)
    first_sum = tokens.astype(jnp.float32) + attn_out + small_wide[2]
    hidden_one, normed_one, inv_one = plain_norm_forward(first_sum, small_wide[3], small_wide[4])
    hidden_low = hidden_one.astype(jnp.bfloat16)
    ffn_rows = ffn_gather(hidden_low)
    pre_act = plain_dot(ffn_rows, inner_full) + inner_mine
    act_full, gelu_pull = jax.vjp(gelu_exact, pre_act)
    activated = act_full.astype(jnp.bfloat16)
    ffn_out = lax.psum_scatter(
        plain_dot(activated, outer_full).astype(jnp.bfloat16),
        "tensor",
        scatter_dimension=0,
        tiled=True,
    ).astype(jnp.float32)
    second_sum = hidden_one + ffn_out + small_wide[5]
    final_rows, normed_two, inv_two = plain_norm_forward(second_sum, small_wide[6], small_wide[7])
    layer_output = final_rows.astype(jnp.bfloat16)
    diff_rows = final_rows - teacher.astype(jnp.float32)
    loss_local = jnp.sum(counted * jnp.sum(diff_rows * diff_rows, axis=1))
    loss_total, token_total = lax.psum((loss_local, count_local), ("dp", "tensor"))
    grad_scale = 2.0 * loss_scale / (token_total * model_width)
    grad_final = grad_scale * counted[:, None] * diff_rows
    (
        query_full,
        key_full,
        value_full,
        mixer_full,
        inner_full,
        outer_full,
        small_full,
        innerb_full,
    ) = fetch_params()
    ffn_rows = ffn_gather(hidden_low)
    grad_second, secondgain_part, secondshift_part = plain_norm_backward(
        grad_final, normed_two, inv_two, small_wide[6]
    )
    outerbias_part = jnp.sum(grad_second, axis=0)
    grad_ffn_rows = lax.all_gather(grad_second.astype(jnp.bfloat16), "tensor", axis=0, tiled=True)
    grad_act = contract_last(grad_ffn_rows, outer_full)
    outer_local = contract_first(activated, grad_ffn_rows)
    grad_pre = gelu_pull(grad_act)[0].astype(jnp.bfloat16)
    innerbias_part = jnp.sum(grad_pre, axis=0, dtype=jnp.float32)
    inner_local = contract_first(ffn_rows, grad_pre)
    grad_hidden = lax.psum_scatter(
        contract_last(grad_pre, inner_full).astype(jnp.bfloat16),
        "tensor",
        scatter_dimension=0,
        tiled=True,
    ).astype(jnp.float32)
    inner_grad, outer_grad = (
        lax.psum_scatter(inner_local, "dp", scatter_dimension=0, tiled=True),
        lax.psum_scatter(outer_local, "dp", scatter_dimension=1, tiled=True),
    )
    grad_first, firstgain_part, firstshift_part = plain_norm_backward(
        grad_second + grad_hidden, normed_one, inv_one, small_wide[3]
    )
    mixerbias_part = jnp.sum(grad_first, axis=0)
    grad_attn_rows = lax.all_gather(grad_first.astype(jnp.bfloat16), "tensor", axis=0, tiled=True)
    grad_attended = contract_last(grad_attn_rows, mixer_full).astype(jnp.bfloat16)
    mixer_local = contract_first(attended, grad_attn_rows)
    grad_blocks = grad_attended.reshape(block_count, QBLOCK, head_count, HEAD_DIM)

    def backward_block(carried, block_in):
        key_acc, value_acc = carried
        query_block, grad_block, lse_block = block_in
        scores = score_block(query_block)
        prob_full = jnp.exp(scores - lse_block[:, :, None])
        prob_low = prob_full.astype(jnp.bfloat16)
        grad_prob = jnp.einsum(
            "qhd,khd->hqk", grad_block, values_three, preferred_element_type=jnp.float32
        )
        row_dot = jnp.sum(prob_full * grad_prob, axis=2, keepdims=True)
        grad_scores = (prob_full * (grad_prob - row_dot)).astype(jnp.bfloat16)
        grad_query = (
            jnp.einsum("hqk,khd->qhd", grad_scores, keys_three, preferred_element_type=jnp.float32)
            * score_scale
        ).astype(jnp.bfloat16)
        key_acc = (
            key_acc
            + jnp.einsum(
                "hqk,qhd->khd", grad_scores, query_block, preferred_element_type=jnp.float32
            )
            * score_scale
        )
        value_acc = value_acc + jnp.einsum(
            "hqk,qhd->khd", prob_low, grad_block, preferred_element_type=jnp.float32
        )
        return ((key_acc, value_acc), grad_query)

    zero_acc = jnp.zeros((seq_len, head_count, HEAD_DIM), jnp.float32)
    (key_acc, value_acc), grad_queries = lax.scan(
        backward_block, (zero_acc, zero_acc), (query_blocks, grad_blocks, log_sums)
    )
    grad_queries = grad_queries.reshape(seq_len, head_width)
    grad_keys = key_acc.reshape(seq_len, head_width).astype(jnp.bfloat16)
    grad_values = value_acc.reshape(seq_len, head_width).astype(jnp.bfloat16)
    seq_rows = attn_gather(tokens)
    query_local = contract_first(seq_rows, grad_queries)
    key_local = contract_first(seq_rows, grad_keys)
    value_local = contract_first(seq_rows, grad_values)
    querybias_part = jnp.sum(grad_queries, axis=0, dtype=jnp.float32)
    valuebias_part = jnp.sum(grad_values, axis=0, dtype=jnp.float32)
    total_term = contract_last(grad_queries, query_full)
    total_term = total_term + contract_last(grad_keys, key_full)
    grad_tokens = lax.psum_scatter(
        (total_term + contract_last(grad_values, value_full)).astype(jnp.bfloat16),
        "tensor",
        scatter_dimension=0,
        tiled=True,
    ).astype(jnp.float32)
    input_grad = grad_first + grad_tokens
    query_grad, key_grad, value_grad, mixer_grad = (
        *sent_together(
            (
                query_local.astype(jnp.bfloat16),
                key_local.astype(jnp.bfloat16),
                value_local.astype(jnp.bfloat16),
            ),
            "dp",
            0,
            1,
        ),
        summed_on_arrival(mixer_local.astype(jnp.bfloat16), "dp", 1),
    )

    def spread_part(part_vec, full_width):
        return lax.dynamic_update_slice_in_dim(
            jnp.zeros((full_width,), jnp.float32), part_vec, tp_index * part_vec.shape[0], 0
        )

    small_terms = jnp.stack(
        [
            spread_part(querybias_part, model_width),
            spread_part(valuebias_part, model_width),
            mixerbias_part,
            firstgain_part,
            firstshift_part,
            outerbias_part,
            secondgain_part,
            secondshift_part,
        ]
    )
    inner_terms = spread_part(innerbias_part, hidden_width * tp_count)
    small_sum, inner_sum = lax.psum((small_terms, inner_terms), ("dp", "tensor"))
    loss_value = loss_total / (token_total * model_width)
    width_share = model_width // dp_count
    small_mine = lax.dynamic_slice_in_dim(small_sum, dp_index * width_share, width_share, 1)
    hidden_share = inner_sum.shape[0] // dp_count
    innerbias_grad = lax.dynamic_slice_in_dim(inner_sum, dp_index * hidden_share, hidden_share, 0)
    return (
        layer_output,
        loss_value,
        input_grad,
        query_grad,
        small_mine[0],
        key_grad,
        value_grad,
        small_mine[1],
        mixer_grad,
        small_mine[2],
        small_mine[3],
        small_mine[4],
        inner_grad,
        innerbias_grad,
        outer_grad,
        small_mine[5],
        small_mine[6],
        small_mine[7],
    )


def solution(mesh):
    return jax.shard_map(
        shards,
        mesh=mesh,
        in_specs=(
            P(("dp", "tensor"), None),
            P(("dp", "tensor"), None),
            P("dp"),
            P(("dp", "tensor")),
            P(),
            P("dp", "tensor"),
            P("dp"),
            P("dp", "tensor"),
            P("dp", "tensor"),
            P("dp"),
            P("tensor", "dp"),
            P("dp"),
            P("dp"),
            P("dp"),
            P("dp", "tensor"),
            P("dp"),
            P("tensor", "dp"),
            P("dp"),
            P("dp"),
            P("dp"),
        ),
        out_specs=(
            P(("dp", "tensor"), None),
            P(),
            P(("dp", "tensor"), None),
            P("dp", "tensor"),
            P("dp"),
            P("dp", "tensor"),
            P("dp", "tensor"),
            P("dp"),
            P("tensor", "dp"),
            P("dp"),
            P("dp"),
            P("dp"),
            P("dp", "tensor"),
            P("dp"),
            P("tensor", "dp"),
            P("dp"),
            P("dp"),
            P("dp"),
        ),
        check_vma=False,
    )
```

```python
import functools
import jax
import jax.numpy as jnp
from jax import lax
from jax.experimental import pallas as pl
from jax.experimental.pallas import tpu as pltpu
from jax.sharding import PartitionSpec as P

HEAD_DIM = 64
QBLOCK = 512
MESH = pl.DeviceIdType.MESH
F32 = jnp.float32
BF16 = jnp.bfloat16
norm_eps = 1e-05
masked_score = -1e30
VMEM_LIMIT = 60 * 1024 * 1024


def dot(left, right, left_dim, right_dim):
    return lax.dot_general(
        left, right, (((left_dim,), (right_dim,)), ((), ())), preferred_element_type=F32
    )


def remote(src, dst, send, recv, d, t):
    return pltpu.make_async_remote_copy(
        src_ref=src,
        dst_ref=dst,
        send_sem=send,
        recv_sem=recv,
        device_id={"dp": d, "tensor": t},
        device_id_type=MESH,
    )


def arrival(dst, recv):
    return pltpu.make_async_copy(dst, dst, recv)


class Place:
    def __init__(self):
        self.dp = lax.axis_size("dp")
        self.tp = lax.axis_size("tensor")
        self.d = lax.axis_index("dp")
        self.z = lax.axis_index("tensor")
        self.core = lax.rem(self.d, 2)
        self.chip = self.d // 2
        self.chips = self.dp // 2
        self.base = self.chip * 2
        self.sibling = self.base + 1 - self.core
        self.pair = self.z // 2
        self.low = lax.rem(self.z, 2)
        self.group = 2 * self.low + self.core
        self.buddy = 2 * self.pair + 1 - self.low
        self.owner = self.base + self.pair
        self.near_here = 1 + self.pair
        self.near_there = 2 - self.pair
        side = self.chip + 1 - 2 * lax.rem(self.chip, 2)
        across = lax.rem(self.chip + 2, 4)
        self.first = jnp.where(self.core == 0, side, across)
        self.second = jnp.where(self.core == 0, across, side)
        self.diagonal = 3 - self.chip
        self.around = (self.buddy, self.near_there, 3 * (1 - self.pair))


def greet(place):
    barrier = pltpu.get_barrier_semaphore()
    count = 0
    for t in range(place.tp):
        for c in range(2):
            other = jnp.logical_not(jnp.logical_and(place.z == t, place.core == c))

            @pl.when(other)
            def _(t=t, c=c):
                pl.semaphore_signal(
                    barrier, inc=1, device_id={"dp": place.base + c, "tensor": t}, device_id_type=MESH
                )

            count += 1
    count -= 1

    def plane(i, _):
        chip = lax.rem(place.chip + 1 + i, place.chips)
        for c in range(2):
            pl.semaphore_signal(
                barrier, inc=1, device_id={"dp": chip * 2 + c, "tensor": place.z}, device_id_type=MESH
            )
        return 0

    lax.fori_loop(0, place.chips - 1, plane, 0)
    count += 2 * (place.chips - 1)
    pl.semaphore_wait(barrier, count)


def front_kernel(
    x_ref, wq_ref, wm_ref, sm_ref,
    oin_ref, wall_ref, smalls_ref, count_ref, xs_ref, wqf_ref, oT_ref, lse_ref, qT_ref, kA_ref, v_ref,
    wqz, counts, vT, scores, o_buf, wqT, wkp, wvp, wvT,
    sm_send, sm_recv, cn_send, cn_recv, wz_send, wz_recv, wp_send, wp_recv,
    x_send, x_recv, xr_send, xf_send, mz_send, mz_recv, mp_send, mp_recv, ms_send, ms_recv, o_send, o_recv,
):
    me = Place()
    dp, tp, chips = me.dp, me.tp, me.chips
    rows, width = x_ref.shape
    half = rows // 2
    length = rows * tp
    share = wq_ref.shape[0]
    heads = 3
    greet(me)

    def each_peer(f):
        def step(i, _):
            f(i, lax.rem(me.d + 1 + i, dp))
            return 0

        lax.fori_loop(0, dp - 1, step, 0)

    def small_copy(i, peer):
        return remote(sm_ref, smalls_ref.at[me.d], sm_send.at[i], sm_recv.at[me.d], peer, me.z)

    each_peer(lambda i, peer: small_copy(i, peer).start())
    smalls_ref[me.d] = sm_ref[...]

    for s in range(2):
        target = me.z // 2 + 2 * s
        src, dst = wq_ref, wqz.at[me.low]

        @pl.when(target == me.z)
        def _(s=s, dst=dst):
            pltpu.make_async_copy(wq_ref, dst, wz_recv.at[me.low]).start()

        @pl.when(target != me.z)
        def _(s=s, dst=dst, target=target):
            remote(wq_ref, dst, wz_send.at[s], wz_recv.at[me.low], me.d, target).start()

    is_near = me.z == me.near_here
    is_end = jnp.logical_not(is_near)
    pltpu.make_async_copy(wm_ref, wall_ref.at[me.z, me.d], mz_recv.at[me.z]).start()

    def along_z(unit, t, sem, to):
        return remote(unit, wall_ref.at[t, me.d], mz_send.at[sem], mz_recv.at[t], me.d, to)

    def own_along_z():
        pl.when(me.z > 0)(lambda: along_z(wm_ref, me.z, 0, me.z - 1).start())
        pl.when(me.z < tp - 1)(lambda: along_z(wm_ref, me.z, 1, me.z + 1).start())

    def goes_up(t):
        return jnp.logical_and(t < me.z, me.z < tp - 1)

    def goes_down(t):
        return jnp.logical_and(t > me.z, me.z > 0)

    is_owner = me.core == me.pair
    pl.when(is_owner)(own_along_z)
    for h in range(2):
        part = pl.ds(h * half, half)

        @pl.when(is_owner)
        def _(h=h, part=part):
            pltpu.make_async_copy(x_ref.at[part], xs_ref.at[me.z, part], x_recv.at[me.z, h]).start()
            remote(x_ref.at[part], xs_ref.at[me.z, part], x_send.at[h], x_recv.at[me.z, h], me.base + h, me.buddy).start()
            remote(x_ref.at[part], xs_ref.at[me.z, part], xr_send.at[0, h], x_recv.at[me.z, h], me.sibling, me.z).start()

        @pl.when(jnp.logical_not(is_owner))
        def _(h=h, part=part):
            remote(x_ref.at[part], xs_ref.at[me.z, part], x_send.at[h], x_recv.at[me.z, h], me.base + h, me.near_there).start()

    pl.when(jnp.logical_not(is_owner))(own_along_z)

    def wq_plane(s, k):
        dst = wqf_ref.at[me.d]
        return remote(wqz.at[s], dst, wp_send.at[s, k], wp_recv.at[me.d], 2 * k + s, me.z)

    for s in range(2):
        arrival(wqz.at[s], wz_recv.at[s]).wait()

        def step(i, _, s=s):
            k = lax.rem(me.chip + 1 + i, chips)
            here = 2 * k + s == me.d

            @pl.when(here)
            def _():
                pltpu.make_async_copy(wqz.at[s], wqf_ref.at[me.d], wp_recv.at[me.d]).start()

            @pl.when(jnp.logical_not(here))
            def _():
                wq_plane(s, k).start()

            return 0

        lax.fori_loop(0, chips, step, 0)

    def in_plane(unit, t, k, sem, to):
        return remote(unit, wall_ref.at[t, 2 * k + me.core], mp_send.at[t, sem], mp_recv.at[t, k], 2 * to + me.core, me.z)

    def plane_units(t, unit):
        in_plane(unit, t, me.chip, 0, me.first).start()
        in_plane(unit, t, me.chip, 1, me.second).start()

    def to_sibling(t, k):
        unit = wall_ref.at[t, 2 * k + me.core]
        return remote(unit, unit, ms_send.at[t, k], ms_recv.at[t, k], me.sibling, me.z)

    def own_unit(t):
        unit = wall_ref.at[t, me.d]
        arrival(unit, mz_recv.at[t]).wait()
        pl.when(goes_up(t))(lambda: along_z(unit, t, 2 + t, me.z + 1).start())
        pl.when(goes_down(t))(lambda: along_z(unit, t, 2 + t, me.z - 1).start())
        plane_units(t, unit)
        to_sibling(t, me.chip).start()

    def plane_unit(t, k):
        unit = wall_ref.at[t, 2 * k + me.core]
        arrival(unit, mp_recv.at[t, k]).wait()
        return unit

    def plane_forward(t):
        unit = plane_unit(t, me.first)
        in_plane(unit, t, me.first, 2, me.second).start()
        to_sibling(t, me.first).start()

    def plane_rest(t):
        for k in (me.second, me.diagonal):
            plane_unit(t, k)
            to_sibling(t, k).start()

    plane_units(me.z, wm_ref)
    remote(wm_ref, wall_ref.at[me.z, me.d], ms_send.at[me.z, me.chip], ms_recv.at[me.z, me.chip], me.sibling, me.z).start()

    mine = pl.ds(pl.multiple_of(me.core * half, half), half)
    other = pl.ds(pl.multiple_of((1 - me.core) * half, half), half)
    far_first = 2 * (1 - me.pair) + me.pair
    far_second = 2 * (1 - me.pair) + 1 - me.pair
    blocks_in = (
        jnp.where(is_near, far_first, me.buddy),
        jnp.where(is_near, far_second, far_first),
        jnp.where(is_near, me.buddy, far_second),
    )

    def relay(n):
        j = blocks_in[n]
        part = xs_ref.at[j, mine]
        arrival(part, x_recv.at[j, me.core]).wait()
        remote(part, part, xr_send.at[1 + n, 0], x_recv.at[j, me.core], me.sibling, me.z).start()
        if n < 2:
            pl.when(is_near)(lambda: remote(part, part, xf_send.at[n], x_recv.at[j, me.core], me.d, me.buddy).start())

    own_unit(me.around[0])
    relay(0)
    relay(1)

    def small_wait(i, peer):
        arrival(smalls_ref.at[peer], sm_recv.at[peer]).wait()

    each_peer(small_wait)
    plane_count = smalls_ref[0][8:16]
    for k in range(1, dp):
        plane_count = plane_count + smalls_ref[k][8:16]
    counts[me.z] = plane_count
    for s in range(1, tp):
        remote(counts.at[me.z], counts.at[me.z], cn_send.at[s - 1], cn_recv.at[me.z], me.d, lax.rem(me.z + s, tp)).start()

    for k in range(dp):
        arrival(wqf_ref.at[k], wp_recv.at[k]).wait()
    zero = jnp.zeros((share, HEAD_DIM), BF16)
    gw = heads * HEAD_DIM
    for k in range(dp):
        w = wqf_ref[k]
        at = slice(k * share, (k + 1) * share)
        pads = []
        for m in range(3):
            cols = []
            for h in range(heads):
                cols += [w[:, m * gw + h * HEAD_DIM : m * gw + (h + 1) * HEAD_DIM], zero]
            pads.append(jnp.concatenate(cols, axis=1))
        wkp[at, :] = pads[1]
        wvp[at, :] = pads[2]
        scores[0, at, 0:384] = pads[0].astype(F32)
    wqT[...] = scores[0, 0:width, 0:384].T.astype(BF16)
    wvT[...] = wvp[...].astype(F32).T.astype(BF16)

    blocks = gw // share
    row_bias = jnp.zeros((8, 384), F32)
    col_bias = jnp.zeros((384, 8), F32)
    r_in = lax.broadcasted_iota(jnp.int32, (128, 384), 0)
    r_out = lax.broadcasted_iota(jnp.int32, (128, 384), 1)
    c_out = lax.broadcasted_iota(jnp.int32, (384, 128), 0)
    c_in = lax.broadcasted_iota(jnp.int32, (384, 128), 1)

    def padded(col):
        return (col // HEAD_DIM) * 128 + lax.rem(col, HEAD_DIM)

    for b in range(blocks):
        vecs = smalls_ref[me.group * blocks + b][0:8].astype(BF16)
        sel = jnp.logical_and(padded(r_in + b * share) == r_out, r_in < share)
        row_bias = row_bias + dot(vecs, jnp.where(sel, 1.0, 0.0).astype(BF16), 1, 0)
        sel = jnp.logical_and(padded(c_in + b * share) == c_out, c_in < share)
        col_bias = col_bias + dot(jnp.where(sel, 1.0, 0.0).astype(BF16), vecs, 1, 1)
    q_bias = col_bias[:, 0:1]
    v_bias_col = col_bias[:, 1:2]
    v_bias = row_bias[1:2, :]
    valid = smalls_ref[me.base + me.pair][12:13, 0:1]

    lane = lax.broadcasted_iota(jnp.int32, (rows, 128), 1)
    srow = lax.broadcasted_iota(jnp.int32, (128, rows), 0)

    def project(j):
        at = pl.ds(pl.multiple_of(j * rows, rows), rows)
        xb = xs_ref[j]
        keys = dot(xb, wkp[...], 1, 0)
        queries = dot(wqT[...], xb, 1, 1) + q_bias
        vals = dot(xb, wvp[...], 1, 0) + v_bias
        valsT = dot(wvT[...], xb, 1, 1) + v_bias_col
        pos = (j * rows + lax.broadcasted_iota(jnp.int32, (rows, 128), 0)).astype(F32)
        bias = jnp.where(pos < valid, 0.0, masked_score)
        for h in range(heads):
            span = slice(h * 128, (h + 1) * 128)
            vT[h * HEAD_DIM : (h + 1) * HEAD_DIM, at] = valsT[h * 128 : h * 128 + HEAD_DIM].astype(BF16)
            kA_ref[h, at, :] = jnp.where(lane == HEAD_DIM, bias, keys[:, span]).astype(BF16)
            qh = queries[span].astype(BF16) * BF16(HEAD_DIM**-0.5)
            qT_ref[h, :, at] = jnp.where(srow == HEAD_DIM, BF16(1), qh)
            v_ref[h, at, :] = vals[:, span].astype(BF16)

    arrival(xs_ref.at[me.z, pl.ds(0, half)], x_recv.at[me.z, 0]).wait()
    arrival(xs_ref.at[me.z, pl.ds(half, half)], x_recv.at[me.z, 1]).wait()
    project(me.z)
    relay(2)
    pl.when(is_near)(functools.partial(own_unit, me.around[1]))
    plane_forward(me.z)

    def project_next(i, _):
        j = jnp.where(i == 0, blocks_in[0], jnp.where(i == 1, blocks_in[1], blocks_in[2]))
        arrival(xs_ref.at[j, other], x_recv.at[j, 1 - me.core]).wait()
        project(j)
        return 0

    lax.fori_loop(0, tp - 1, project_next, 0)
    pl.when(is_near)(functools.partial(own_unit, me.around[2]))
    plane_forward(me.around[0])

    chunk = 256
    pieces = length // chunk

    def attend(i, _):
        j = lax.rem(me.z + 1 + i, tp)
        at = pl.ds(pl.multiple_of(j * rows, rows), rows)
        tops = []
        for h in range(heads):
            qt = qT_ref[h, :, at]
            top = None
            for c in range(pieces):
                s = dot(kA_ref[h, c * chunk : (c + 1) * chunk, :], qt, 1, 0)
                scores[h, c * chunk : (c + 1) * chunk, :] = s
                peak = jnp.max(s, axis=0, keepdims=True)
                top = peak if top is None else jnp.maximum(top, peak)
            tops.append(top)
        outs = []
        for h in range(heads):
            total, mixed = None, None
            for c in range(pieces):
                p = jnp.exp(scores[h, c * chunk : (c + 1) * chunk, :] - tops[h])
                part = jnp.sum(p, axis=0, keepdims=True)
                term = dot(vT[h * HEAD_DIM : (h + 1) * HEAD_DIM, c * chunk : (c + 1) * chunk], p.astype(BF16), 1, 0)
                total = part if total is None else total + part
                mixed = term if mixed is None else mixed + term
            mixed = mixed / total
            oT_ref[h * HEAD_DIM : (h + 1) * HEAD_DIM, at] = mixed
            lse_ref[h, :, at] = tops[h] + jnp.log(total)
            outs.append(mixed)
        o_buf[j] = jnp.concatenate(outs, axis=0).T.astype(BF16)
        here = jnp.logical_and(j == me.z, is_owner)

        @pl.when(here)
        def _():
            pltpu.make_async_copy(o_buf.at[j], oin_ref.at[me.group], o_recv.at[me.group]).start()

        @pl.when(jnp.logical_not(here))
        def _():
            remote(o_buf.at[j], oin_ref.at[me.group], o_send.at[i], o_recv.at[me.group], me.owner, j).start()

        for n in (1, 2):
            pl.when(jnp.logical_and(is_end, i == n - 1))(functools.partial(own_unit, me.around[n]))
        pl.when(i == 0)(functools.partial(plane_rest, me.z))
        pl.when(jnp.logical_and(is_near, i == 0))(functools.partial(plane_forward, me.around[1]))
        pl.when(jnp.logical_and(is_end, i == 2))(functools.partial(plane_forward, me.around[1]))
        pl.when(jnp.logical_and(is_near, i == 2))(functools.partial(plane_forward, me.around[2]))
        pl.when(jnp.logical_and(is_end, i == 3))(functools.partial(plane_forward, me.around[2]))
        return 0

    lax.fori_loop(0, tp, attend, 0)

    for t in me.around:
        plane_rest(t)

    arrival(wall_ref.at[me.z, me.d], mz_recv.at[me.z]).wait()
    for s in range(1, tp):
        t = lax.rem(me.z + s, tp)
        arrival(counts.at[t], cn_recv.at[t]).wait()
    total = counts[0]
    for t in range(1, tp):
        total = total + counts[t]
    count_ref[...] = total
    for g in range(4):
        arrival(oin_ref.at[g], o_recv.at[g]).wait()

    def sibling_units(n, _):
        t, k = n // chips, lax.rem(n, chips)
        arrival(wall_ref.at[t, 2 * k + 1 - me.core], ms_recv.at[t, k]).wait()
        to_sibling(t, k).wait_send()
        return 0

    lax.fori_loop(0, tp * chips, sibling_units, 0)

    def sent(n, _):
        t, i = n // (chips - 1), lax.rem(n, chips - 1)
        in_plane(wm_ref, t, me.chip, i, me.first).wait_send()
        return 0

    lax.fori_loop(0, tp * (chips - 1), sent, 0)
    each_peer(lambda i, peer: small_copy(i, peer).wait_send())
    for s in range(2):

        @pl.when(me.z // 2 + 2 * s != me.z)
        def _(s=s):
            remote(wq_ref, wqz.at[0], wz_send.at[s], wz_recv.at[0], me.sibling, me.z).wait_send()

        def step(i, _, s=s):
            k = lax.rem(me.chip + 1 + i, chips)

            @pl.when(2 * k + s != me.d)
            def _():
                wq_plane(s, k).wait_send()

            return 0

        lax.fori_loop(0, chips, step, 0)
    for s in range(tp - 1):
        remote(counts.at[0], counts.at[0], cn_send.at[s], cn_recv.at[0], me.sibling, me.z).wait_send()

    def z_sent(sem):
        along_z(wm_ref, 0, sem, 0).wait_send()

    pl.when(me.z > 0)(functools.partial(z_sent, 0))
    pl.when(me.z < tp - 1)(functools.partial(z_sent, 1))
    for t in range(tp):
        pl.when(jnp.logical_or(goes_up(t), goes_down(t)))(functools.partial(z_sent, 2 + t))

    def x_sent(sem):
        remote(x_ref.at[pl.ds(0, half)], xs_ref.at[0, pl.ds(0, half)], sem, x_recv.at[0, 0], me.sibling, me.z).wait_send()

    for h in range(2):
        x_sent(x_send.at[h])

        @pl.when(is_owner)
        def _(h=h):
            x_sent(xr_send.at[0, h])

    for n in range(3):
        x_sent(xr_send.at[1 + n, 0])

    @pl.when(is_near)
    def _():
        for n in range(2):
            x_sent(xf_send.at[n])

    def o_sent(i, _):
        j = lax.rem(me.z + 1 + i, tp)

        @pl.when(jnp.logical_not(jnp.logical_and(j == me.z, is_owner)))
        def _():
            remote(o_buf.at[0], oin_ref.at[0], o_send.at[i], o_recv.at[0], me.sibling, me.z).wait_send()

        return 0

    lax.fori_loop(0, tp, o_sent, 0)


def front(x, wq, wm, small, dp, tp):
    rows, width = x.shape
    length = rows * tp
    share = wq.shape[0]
    chips = dp // 2
    S = jax.ShapeDtypeStruct
    vmem = pl.BlockSpec(memory_space=pltpu.VMEM)
    anym = pl.BlockSpec(memory_space=pl.ANY)
    dma = pltpu.SemaphoreType.DMA
    return pl.pallas_call(
        front_kernel,
        name="front",
        out_shape=(
            S((4, rows, 192), BF16),
            S((tp, dp, share, wm.shape[1]), BF16),
            S((dp, 16, 128), F32),
            S((8, 128), F32),
            S((tp, rows, width), BF16),
            S((dp, share, wq.shape[1]), BF16),
            S((192, length), F32),
            S((3, 1, length), F32),
            S((3, 128, length), BF16),
            S((3, length, 128), BF16),
            S((3, length, 128), BF16),
        ),
        in_specs=[vmem] * 4,
        out_specs=(anym, anym) + (vmem,) * 9,
        scratch_shapes=[
            pltpu.VMEM((2, share, wq.shape[1]), BF16),
            pltpu.VMEM((tp, 8, 128), F32),
            pltpu.VMEM((192, length), BF16),
            pltpu.VMEM((3, length, rows), F32),
            pltpu.VMEM((tp, rows, 192), BF16),
            pltpu.VMEM((384, width), BF16),
            pltpu.VMEM((width, 384), BF16),
            pltpu.VMEM((width, 384), BF16),
            pltpu.VMEM((384, width), BF16),
            dma((dp - 1,)), dma((dp,)), dma((tp - 1,)), dma((tp,)),
            dma((2,)), dma((2,)), dma((2, chips)), dma((dp,)),
            dma((2,)), dma((tp, 2)), dma((4, 2)), dma((2,)),
            dma((tp + 2,)), dma((tp,)), dma((tp, chips - 1)), dma((tp, chips)), dma((tp, chips)), dma((tp, chips)),
            dma((tp,)), dma((4,)),
        ],
        compiler_params=pltpu.CompilerParams(
            collective_id=0, has_side_effects=True, vmem_limit_bytes=VMEM_LIMIT
        ),
    )(x, wq, wm, small)


SQRT_HALF = 0.7071067811865476
INV_SQRT_2PI = 0.3989422804014327


def norm_forward(values, gain, shift):
    centred = values - jnp.mean(values, axis=1, keepdims=True)
    inv = lax.rsqrt(jnp.mean(centred * centred, axis=1, keepdims=True) + norm_eps)
    normed = centred * inv
    return normed * gain + shift, normed, inv


def norm_backward(grad_out, normed, inv, gain):
    g = grad_out * gain
    plain = jnp.mean(g, axis=1, keepdims=True)
    mixed = jnp.mean(g * normed, axis=1, keepdims=True)
    return inv * (g - plain - normed * mixed)


def column_sum(values):
    return jnp.sum(values, axis=0, keepdims=True)


def mid_kernel(
    x_ref, teacher_ref, counted_ref, scale_ref, count_ref, oin_ref, wall_ref, smalls_ref,
    out_ref, dr1_ref, do_ref, grad_ref, pack_ref,
    slope_ref, act_ref, f_ref, n1_ref, acc_ref, hT_ref, dfT_ref, vec_ref, ib_ref, small_ref, ismall_ref,
):
    groups = wall_ref.shape[0]
    width = x_ref.shape[1]
    gw = oin_ref.shape[2]
    inner = slice(0, width)
    outer = slice(width, 2 * width)
    mixer = slice(2 * width, 2 * width + gw)
    vec = lambda i: vec_ref[i : i + 1, :]
    dp = smalls_ref.shape[0]
    share = width // dp
    per = dp // groups
    hrows = ib_ref.shape[2] // per // 128
    for d in range(dp):
        vec_ref[:, d * share : (d + 1) * share] = smalls_ref[d, 0:8, 0:share]
        for r in range(hrows):
            at = (d % per * hrows + r) * 128
            ib_ref[d // per, :, at : at + 128] = smalls_ref[d, 9 + r : 10 + r, :]

    acc_ref[...] = x_ref[...].astype(F32) + vec(2)
    for g in range(groups):
        acc_ref[...] += dot(oin_ref[g], wall_ref[g, :, mixer], 1, 1)
    hidden, normed1, inv1 = norm_forward(acc_ref[...], vec(3), vec(4))
    n1_ref[...] = normed1
    low = hidden.astype(BF16)
    hT_ref[...] = hidden.T.astype(BF16)
    f_ref[...] = hidden + vec(5)

    def ffn_forward(g, _):
        up = dot(low, wall_ref[g, :, inner], 1, 0) + ib_ref[g]
        below = 0.5 * (1.0 + lax.erf(up * SQRT_HALF))
        slope_ref[g] = below + up * (INV_SQRT_2PI * jnp.exp(-0.5 * up * up))
        act = (up * below).astype(BF16)
        act_ref[g] = act
        f_ref[...] += dot(act, wall_ref[g, :, outer], 1, 1)
        return 0

    lax.fori_loop(0, groups, ffn_forward, 0)
    final, normed2, inv2 = norm_forward(f_ref[...], vec(6), vec(7))
    out_ref[...] = final.astype(BF16)
    diff = final - teacher_ref[...].astype(F32)
    counted = counted_ref[...]
    small_ref[...] = jnp.zeros_like(small_ref)
    small_ref[6:7, 0:1] = jnp.sum(counted * jnp.sum(diff * diff, axis=1, keepdims=True), axis=0, keepdims=True)
    scale = 2.0 * scale_ref[0, 0] / (count_ref[0:1, 0:1] * width)
    grad = (scale * counted) * diff
    small_ref[4:5, :] = column_sum(grad * normed2)
    small_ref[5:6, :] = column_sum(grad)
    dr2 = norm_backward(grad, normed2, inv2, vec(6))
    small_ref[3:4, :] = column_sum(dr2)
    acc_ref[...] = dr2
    df = dr2.astype(BF16)
    dfT_ref[...] = dr2.T.astype(BF16)

    def ffn_backward(g, _):
        du = (dot(df, wall_ref[g, :, outer], 1, 0) * slope_ref[g]).astype(BF16)
        ismall_ref[g] = column_sum(du.astype(F32))
        acc_ref[...] += dot(du, wall_ref[g, :, inner], 1, 1)
        grad_ref[g, :, inner] = dot(hT_ref[...], du, 1, 0).astype(BF16)
        grad_ref[g, :, outer] = dot(dfT_ref[...], act_ref[g], 1, 0).astype(BF16)
        return 0

    lax.fori_loop(0, groups, ffn_backward, 0)
    dh1 = acc_ref[...]
    normed1 = n1_ref[...]
    small_ref[1:2, :] = column_sum(dh1 * normed1)
    small_ref[2:3, :] = column_sum(dh1)
    dr1 = norm_backward(dh1, normed1, inv1, vec(3))
    small_ref[0:1, :] = column_sum(dr1)
    dr1_ref[...] = dr1
    da = dr1.astype(BF16)
    daT = dr1.T.astype(BF16)
    for g in range(groups):
        do_ref[g] = dot(da, wall_ref[g, :, mixer], 1, 0).astype(BF16)
        grad_ref[g, :, mixer] = dot(daT, oin_ref[g], 1, 0).astype(BF16)
    pack_ref[...] = jnp.zeros_like(pack_ref)
    for d in range(dp):
        pack_ref[d, 2:8, 0:share] = small_ref[0:6, d * share : (d + 1) * share]
        pack_ref[d, 8:9, :] = jnp.broadcast_to(small_ref[6:7, 0:1], (1, 128))
        for r in range(hrows):
            at = (d % per * hrows + r) * 128
            pack_ref[d, 9 + r : 10 + r, :] = ismall_ref[d // per, :, at : at + 128]


def mid(x, teacher, counted, scale, count, oin, wall, smalls, hidden):
    rows, width = x.shape
    groups = wall.shape[0]
    S = jax.ShapeDtypeStruct
    vmem = pl.BlockSpec(memory_space=pltpu.VMEM)
    return pl.pallas_call(
        mid_kernel,
        name="mid",
        out_shape=(
            S((rows, width), BF16),
            S((rows, width), F32),
            S(oin.shape, BF16),
            S(wall.shape, BF16),
            S(smalls.shape, F32),
        ),
        in_specs=[vmem, vmem, vmem, pl.BlockSpec(memory_space=pltpu.SMEM)] + [vmem] * 4,
        out_specs=(vmem,) * 5,
        scratch_shapes=[
            pltpu.VMEM((groups, rows, hidden), F32),
            pltpu.VMEM((groups, rows, hidden), BF16),
            pltpu.VMEM((rows, width), F32),
            pltpu.VMEM((rows, width), F32),
            pltpu.VMEM((rows, width), F32),
            pltpu.VMEM((width, rows), BF16),
            pltpu.VMEM((width, rows), BF16),
            pltpu.VMEM((8, width), F32),
            pltpu.VMEM((groups, 1, hidden), F32),
            pltpu.VMEM((8, width), F32),
            pltpu.VMEM((groups, 1, hidden), F32),
        ],
        compiler_params=pltpu.CompilerParams(vmem_limit_bytes=VMEM_LIMIT),
    )(x, teacher, counted, scale, count, oin, wall, smalls)


def back_kernel(
    do_ref, grad_ref, xs_ref, wqf_ref, oT_ref, lse_ref, qT_ref, kA_ref, v_ref, pack_ref,
    fin, gsum_ref, qgrad_ref, small_ref,
    dof, doT, delta, qs, kT, dk, dv, dqT, dqkv,
    sib, own, pln, zsrc, zin, parts, pr, sj, rr, qsend, qr, qz, qf, spack, srecv, zpack,
    do_send, do_recv, sb_send, sb_recv, own_sem, pl_send, pl_recv, zz_send, zz_recv,
    pr_send, pr_recv, rr_send, rr_recv, fin_send, fin_recv, qr_send, qr_recv, qf_send, qf_recv,
    sm_send, sm_recv, sz_send, sz_recv,
):
    me = Place()
    dp, tp, chips = me.dp, me.tp, me.chips
    rows, width = xs_ref.shape[1:]
    half = rows // 2
    length = rows * tp
    heads = 3
    gw = heads * HEAD_DIM
    share = width // dp
    greet(me)

    for g in range(4):
        t = 2 * me.core + g // 2
        d = me.base + g % 2
        here = jnp.logical_and(t == me.z, g % 2 == me.core)

        @pl.when(here)
        def _(g=g):
            pltpu.make_async_copy(do_ref.at[g], dof.at[me.z], do_recv.at[me.z]).start()

        @pl.when(jnp.logical_not(here))
        def _(g=g, t=t, d=d):
            remote(do_ref.at[g], dof.at[me.z], do_send.at[g], do_recv.at[me.z], d, t).start()

    order = me.around[::-1] + (me.z,)

    def sib_copy(t):
        return remote(grad_ref.at[t, :, 1 - me.core], sib.at[t], sb_send.at[t], sb_recv.at[t], me.sibling, me.z)

    for t in order:
        sib_copy(t).start()
        pltpu.make_async_copy(grad_ref.at[t, :, me.core], own.at[t], own_sem.at[t]).start()

    def plane_copy(t, n):
        k = (me.diagonal, me.first, me.second)[n]
        to = (me.first, me.first, me.second)[n]
        return remote(own.at[t, k], pln.at[t, n], pl_send.at[t, n], pl_recv.at[t, n], 2 * to + me.core, me.z)

    def pair_sum(t):
        arrival(own.at[t], own_sem.at[t]).wait()
        arrival(sib.at[t], sb_recv.at[t]).wait()

        def unit(k, _):
            own[t, k] = (own[t, k].astype(F32) + sib[t, k].astype(F32)).astype(BF16)
            return 0

        lax.fori_loop(0, chips, unit, 0)
        plane_copy(t, 0).start()
        plane_copy(t, 1).start()

    def pass_on(n):
        t = order[n]
        arrival(pln.at[t, 0], pl_recv.at[t, 0]).wait()
        own[t, me.second] = (own[t, me.second].astype(F32) + pln[t, 0].astype(F32)).astype(BF16)
        plane_copy(t, 2).start()

    has_below, has_above = me.z > 0, me.z < tp - 1

    def z_copy(t):
        up = t > me.z
        to = jnp.where(up, me.z + 1, me.z - 1)
        slot = jnp.where(jnp.logical_and(to == t, jnp.logical_not(up)), tp, t)
        return remote(zsrc.at[t], zin.at[slot], zz_send.at[t], zz_recv.at[slot], me.d, to)

    def plane_total(t):
        for n in (1, 2):
            arrival(pln.at[t, n], pl_recv.at[t, n]).wait()
        return own[t, me.chip].astype(F32) + pln[t, 1].astype(F32) + pln[t, 2].astype(F32)

    def z_step(n):
        t = order[n]
        total = plane_total(t)
        comes = jnp.where(t > me.z, has_below, has_above)

        @pl.when(comes)
        def _():
            arrival(zin.at[t], zz_recv.at[t]).wait()
            zsrc[t] = (total + zin[t].astype(F32)).astype(BF16)

        @pl.when(jnp.logical_not(comes))
        def _():
            zsrc[t] = total.astype(BF16)

        z_copy(t).start()

    for t in order[:2]:
        pair_sum(t)

    def pair_step(n):
        pair_sum(order[n])

    is_near = me.z == me.near_here
    is_end = jnp.logical_not(is_near)
    far = 2 * (1 - me.pair)
    far_first, far_second = far + me.pair, far + 1 - me.pair

    def block_at(i):
        return jnp.where(i == 0, far_second, jnp.where(i == 1, far_first, jnp.where(i == 2, me.buddy, me.z)))

    def prepare(j, at):
        arrival(dof.at[j], do_recv.at[j]).wait()
        flipped = dof[j].astype(F32).T
        doT[:, at] = flipped.astype(BF16)
        for h in range(heads):
            span = slice(h * HEAD_DIM, (h + 1) * HEAD_DIM)
            delta[h, :, at] = jnp.sum(flipped[span] * oT_ref[span, at], axis=0, keepdims=True)
            qs[h, at, :] = qT_ref[h, :, at].astype(F32).T.astype(BF16)

    always = {(0, 0): (pair_step, 2), (0, 2): (pair_step, 3), (0, 1): (pass_on, 0), (0, 3): (pass_on, 1), (1, 1): (pass_on, 2), (2, 0): (pass_on, 3)}
    at_ends = {(1, 0): (z_step, 0), (1, 2): (z_step, 1), (2, 1): (z_step, 2)}
    in_middle = {(1, 2): (z_step, 0), (2, 0): (z_step, 1), (2, 2): (z_step, 2)}
    chunk = 256
    def flip_keys(j, _):
        at = pl.ds(pl.multiple_of(j * rows, rows), rows)
        for h in range(heads):
            kT[h, :, at] = kA_ref[h, at, :].astype(F32).T[0:HEAD_DIM, :].astype(BF16)
        return 0

    lax.fori_loop(0, tp, flip_keys, 0)
    for h in range(heads):
        dk[...] = jnp.zeros_like(dk)
        dv[...] = jnp.zeros_like(dv)

        def attend(i, _, h=h):
            j = block_at(3 - i)
            at = pl.ds(pl.multiple_of(j * rows, rows), rows)
            if h == 0:
                prepare(j, at)
            span = slice(h * HEAD_DIM, (h + 1) * HEAD_DIM)
            qt, gt = qT_ref[h, :, at], doT[span, at]
            q, go = qs[h, at, :], dof[j, :, span]
            lse, dl = lse_ref[h, :, at], delta[h, :, at]
            dq = None
            for c in range(length // chunk):
                r = slice(c * chunk, (c + 1) * chunk)
                p = jnp.exp(dot(kA_ref[h, r, :], qt, 1, 0) - lse)
                dp_ = dot(v_ref[h, r, 0:HEAD_DIM], gt, 1, 0)
                ds = (p * (dp_ - dl)).astype(BF16)
                dv[r, :] += dot(p.astype(BF16), go, 1, 0)
                dk[r, :] += dot(ds, q, 1, 0)
                term = dot(kT[h, :, r], ds, 1, 0)
                dq = term if dq is None else dq + term
            dqT[span, at] = dq * HEAD_DIM**-0.5
            for where, hooks in ((None, always), (is_end, at_ends), (is_near, in_middle)):
                for (head, step), (act, n) in hooks.items():
                    if head == h:
                        now = i == step
                        pl.when(now if where is None else jnp.logical_and(where, now))(functools.partial(act, n))
            return 0

        lax.fori_loop(0, tp, attend, 0)
        for j in range(tp):
            at = slice(j * rows, (j + 1) * rows)
            dqkv[j, :, gw + h * HEAD_DIM : gw + (h + 1) * HEAD_DIM] = dk[at, 0:HEAD_DIM].astype(BF16)
            dqkv[j, :, 2 * gw + h * HEAD_DIM : 2 * gw + (h + 1) * HEAD_DIM] = dv[at, :].astype(BF16)

    weights = wqf_ref[...].reshape(width, 3 * gw)
    ones = jnp.ones((8, rows), BF16)
    mine = pl.ds(pl.multiple_of(me.core * half, half), half)
    other = pl.ds(pl.multiple_of((1 - me.core) * half, half), half)

    def pr_copy(j):
        return remote(parts.at[j, other], pr.at[j], pr_send.at[j], pr_recv.at[j], me.sibling, me.z)

    def rr_copy(j):
        return remote(sj.at[j], rr.at[j], rr_send.at[j], rr_recv.at[j], me.d, me.buddy)

    def collects(j):
        return jnp.where(j // 2 == me.pair, j, me.near_here) == me.z

    def chip_sum(j):
        arrival(pr.at[j], pr_recv.at[j]).wait()
        sj[j] = (parts[j, mine, :].astype(F32) + pr[j].astype(F32)).astype(BF16)
        pl.when(jnp.logical_not(collects(j)))(lambda: rr_copy(j).start())

    def token_grads(i, sums):
        j = block_at(i)
        at = pl.ds(pl.multiple_of(j * rows, rows), rows)
        dqkv[j, :, 0:gw] = dqT[:, at].T.astype(BF16)
        flat = dqkv[j]
        parts[j] = dot(flat, weights, 1, 1).astype(BF16)
        pr_copy(j).start()
        pl.when(i > 0)(lambda: chip_sum(block_at(i - 1)))
        return sums + dot(ones, flat, 1, 0)

    sums = lax.fori_loop(0, tp, token_grads, jnp.zeros((8, 3 * gw), F32))
    chip_sum(block_at(tp - 1))

    spack[...] = pack_ref[...]
    blocks = gw // share
    for b in range(blocks):
        spack[me.group * blocks + b, 0:1, 0:share] = sums[0:1, b * share : (b + 1) * share]
        spack[me.group * blocks + b, 1:2, 0:share] = sums[0:1, 2 * gw + b * share : 2 * gw + (b + 1) * share]

    def small_copy(i):
        peer = lax.rem(me.d + 1 + i, dp)
        return remote(spack.at[peer], srecv.at[i], sm_send.at[i], sm_recv.at[i], peer, me.z)

    def small_start(i, _):
        small_copy(i).start()
        return 0

    lax.fori_loop(0, dp - 1, small_start, 0)

    def fin_copy(j):
        return remote(pr.at[j], fin.at[me.core], fin_send.at[j], fin_recv.at[me.core], me.owner, j)

    def lands_here(j):
        return jnp.logical_and(me.core == me.pair, j == me.z)

    total = None
    for j in range(tp):
        term = dot(xs_ref[j], dqkv[j], 0, 0)
        total = term if total is None else total + term
    qsend[...] = total.astype(BF16).reshape(dp, share, 3 * gw)

    def q_copy(peer, i):
        return remote(qsend.at[peer], qr.at[me.core, me.chip], qr_send.at[i], qr_recv.at[me.core, me.chip], peer, me.z)

    def q_start(i, _):
        peer = lax.rem(me.d + i, dp)

        @pl.when(i == 0)
        def _():
            pltpu.make_async_copy(qsend.at[peer], qr.at[me.core, me.chip], qr_recv.at[me.core, me.chip]).start()

        @pl.when(i > 0)
        def _():
            q_copy(peer, i).start()

        return 0

    lax.fori_loop(0, dp, q_start, 0)

    def pair_total(i, _):
        j = block_at(i)

        @pl.when(collects(j))
        def _():
            arrival(rr.at[j], rr_recv.at[j]).wait()
            pr[j] = (sj[j].astype(F32) + rr[j].astype(F32)).astype(BF16)

            @pl.when(lands_here(j))
            def _():
                pltpu.make_async_copy(pr.at[j], fin.at[me.core], fin_recv.at[me.core]).start()

            @pl.when(jnp.logical_not(lands_here(j)))
            def _():
                fin_copy(j).start()

        return 0

    lax.fori_loop(0, tp, pair_total, 0)

    def q_pair(s):
        return me.z // 2, 2 * me.low + s

    for s in range(2):
        total = None
        for k in range(chips):
            arrival(qr.at[s, k], qr_recv.at[s, k]).wait()
            term = qr[s, k].astype(F32)
            total = term if total is None else total + term
        qz[s] = total.astype(BF16)
        p, t = q_pair(s)

        @pl.when(t == me.z)
        def _(s=s, p=p):
            pltpu.make_async_copy(qz.at[s], qf.at[p], qf_recv.at[p]).start()

        @pl.when(t != me.z)
        def _(s=s, p=p, t=t):
            remote(qz.at[s], qf.at[p], qf_send.at[s], qf_recv.at[p], me.d, t).start()

    total = spack[me.d]
    for i in range(dp - 1):
        arrival(srecv.at[i], sm_recv.at[i]).wait()
        total = total + srecv[i]
    zpack[me.z] = total

    def sz_copy(s):
        return remote(zpack.at[me.z], zpack.at[me.z], sz_send.at[s - 1], sz_recv.at[me.z], me.d, lax.rem(me.z + s, tp))

    for s in range(1, tp):
        sz_copy(s).start()

    for h in range(2):
        arrival(fin.at[h], fin_recv.at[h]).wait()
    for p in range(2):
        arrival(qf.at[p], qf_recv.at[p]).wait()
    qgrad_ref[...] = qf[0].astype(F32) + qf[1].astype(F32)
    for s in range(1, tp):
        t = lax.rem(me.z + s, tp)
        arrival(zpack.at[t], sz_recv.at[t]).wait()
    total = zpack[0]
    for t in range(1, tp):
        total = total + zpack[t]
    small_ref[...] = total
    gsum_ref[...] = plane_total(me.z)
    for slot, comes in ((me.z, has_below), (tp, has_above)):

        @pl.when(comes)
        def _(slot=slot):
            arrival(zin.at[slot], zz_recv.at[slot]).wait()
            gsum_ref[...] += zin[slot].astype(F32)

    for g in range(4):

        @pl.when(jnp.logical_not(jnp.logical_and(2 * me.core + g // 2 == me.z, g % 2 == me.core)))
        def _(g=g):
            remote(do_ref.at[g], dof.at[0], do_send.at[g], do_recv.at[0], me.sibling, me.z).wait_send()

    for t in range(tp):
        sib_copy(t).wait_send()
        pr_copy(t).wait_send()

        @pl.when(jnp.logical_not(collects(t)))
        def _(t=t):
            rr_copy(t).wait_send()

        @pl.when(jnp.logical_and(collects(t), jnp.logical_not(lands_here(t))))
        def _(t=t):
            fin_copy(t).wait_send()

    for t in range(tp):
        for n in range(3):
            plane_copy(t, n).wait_send()
        pl.when(t != me.z)(lambda t=t: z_copy(t).wait_send())

    def peers_sent(i, _):
        small_copy(i).wait_send()
        q_copy(lax.rem(me.d + 1 + i, dp), i + 1).wait_send()
        return 0

    lax.fori_loop(0, dp - 1, peers_sent, 0)
    for s in range(1, tp):
        sz_copy(s).wait_send()
    for s in range(2):
        p, t = q_pair(s)

        @pl.when(t != me.z)
        def _(s=s, p=p, t=t):
            remote(qz.at[s], qf.at[p], qf_send.at[s], qf_recv.at[p], me.d, t).wait_send()


def back(do, grad, xs, wqf, oT, lse, qT, kA, v, pack):
    tp, rows, width = xs.shape
    dp, share, qwidth = wqf.shape
    chips = dp // 2
    length = rows * tp
    half = rows // 2
    cols = grad.shape[-1]
    S = jax.ShapeDtypeStruct
    vmem = pl.BlockSpec(memory_space=pltpu.VMEM)
    anym = pl.BlockSpec(memory_space=pl.ANY)
    dma = pltpu.SemaphoreType.DMA
    V = pltpu.VMEM
    return pl.pallas_call(
        back_kernel,
        name="back",
        out_shape=(
            S((2, half, width), BF16),
            S((share, cols), F32),
            S((share, qwidth), F32),
            S((16, 128), F32),
        ),
        in_specs=[anym, anym] + [vmem] * 8,
        out_specs=(vmem,) * 4,
        scratch_shapes=[
            V((tp, rows, 192), BF16), V((192, length), BF16), V((3, 1, length), F32),
            V((3, length, 128), BF16), V((3, HEAD_DIM, length), BF16),
            V((length, 128), F32), V((length, HEAD_DIM), F32), V((192, length), F32), V((tp, rows, qwidth), BF16),
            V((tp, chips, share, cols), BF16), V((tp, chips, share, cols), BF16), V((tp, chips - 1, share, cols), BF16),
            V((tp, share, cols), BF16), V((tp + 1, share, cols), BF16),
            V((tp, rows, width), BF16), V((tp, half, width), BF16), V((tp, half, width), BF16), V((tp, half, width), BF16),
            V((dp, share, qwidth), BF16), V((2, chips, share, qwidth), BF16), V((2, share, qwidth), BF16), V((2, share, qwidth), BF16),
            V((dp, 16, 128), F32), V((dp - 1, 16, 128), F32), V((tp, 16, 128), F32),
            dma((4,)), dma((tp,)), dma((tp,)), dma((tp,)), dma((tp,)), dma((tp, 3)), dma((tp, 3)), dma((tp,)), dma((tp + 1,)),
            dma((tp,)), dma((tp,)), dma((tp,)), dma((tp,)), dma((tp,)), dma((2,)), dma((dp,)), dma((2, chips)), dma((2,)), dma((2,)),
            dma((dp - 1,)), dma((dp - 1,)), dma((tp - 1,)), dma((tp,)),
        ],
        compiler_params=pltpu.CompilerParams(
            collective_id=1, has_side_effects=True, vmem_limit_bytes=VMEM_LIMIT
        ),
    )(do, grad, xs, wqf, oT, lse, qT, kA, v, pack)


def pack_kernel(length_ref, mask_ref, *refs):
    vectors, (ib_ref, wq_ref, wk_ref, wv_ref, wi_ref, wo_ref, wx_ref) = refs[:8], refs[8:15]
    sm_ref, w3_ref, wm_ref, counted_ref = refs[15:]
    rows = mask_ref.shape[1]
    share, gw = wq_ref.shape
    hidden = wi_ref.shape[1]
    pos = lax.axis_index("tensor") * rows + lax.broadcasted_iota(jnp.int32, (8, rows), 1)
    mask = jnp.broadcast_to(mask_ref[...], (8, rows))
    valid = length_ref[0]
    counted = jnp.where(jnp.logical_and(pos < valid, mask == 1), 1.0, 0.0)
    counted_ref[...] = counted.T[:, 0:1]
    sm_ref[...] = jnp.zeros_like(sm_ref)
    for i, v in enumerate(vectors):
        sm_ref[i : i + 1, 0:share] = v[...].astype(F32)
    sm_ref[8:9, :] = jnp.broadcast_to(jnp.sum(counted[0:1, :], axis=1, keepdims=True), (1, 128))
    for r in range(ib_ref.shape[1] // 128):
        sm_ref[9 + r : 10 + r, :] = ib_ref[:, r * 128 : (r + 1) * 128].astype(F32)
    sm_ref[12:13, :] = jnp.full((1, 128), valid, jnp.int32).astype(F32)
    for i, w in enumerate((wq_ref, wk_ref, wv_ref)):
        w3_ref[:, i * gw : (i + 1) * gw] = w[...]
    wm_ref[:, 0:hidden] = wi_ref[...]
    wm_ref[:, hidden : 2 * hidden] = wo_ref[...]
    wm_ref[:, 2 * hidden :] = wx_ref[...].astype(F32).T.astype(BF16)


def pack_inputs(lengths, mask, vectors, inner_bias, wq, wk, wv, wi, wo, wx):
    share, gw = wq.shape
    rows = mask.shape[0]
    S = jax.ShapeDtypeStruct
    vmem = pl.BlockSpec(memory_space=pltpu.VMEM)
    return pl.pallas_call(
        pack_kernel,
        name="pack_inputs",
        out_shape=(
            S((16, 128), F32),
            S((share, 3 * gw), BF16),
            S((share, 2 * wi.shape[1] + gw), BF16),
            S((rows, 1), F32),
        ),
        in_specs=[pl.BlockSpec(memory_space=pltpu.SMEM)] + [vmem] * 16,
        out_specs=(vmem,) * 4,
    )(lengths, mask.reshape(1, rows), *vectors, inner_bias.reshape(1, -1), wq, wk, wv, wi, wo, wx)


def finish_kernel(
    dr1_ref, fin_ref, gsum_ref, qgrad_ref, small_ref, count_ref,
    loss_ref, dx_ref, q_ref, k_ref, v_ref, mixer_ref, inner_ref, outer_ref, ib_ref, *lines,
):
    half = fin_ref.shape[1]
    width = dr1_ref.shape[1]
    share, gw = q_ref.shape
    hidden = inner_ref.shape[1]
    loss_ref[...] = small_ref[8:9, 0:1] / (count_ref[0:1, 0:1] * width)
    for h in range(2):
        at = slice(h * half, (h + 1) * half)
        dx_ref[at, :] = dr1_ref[at, :] + fin_ref[h].astype(F32)
    for i, ref in enumerate((q_ref, k_ref, v_ref)):
        ref[...] = qgrad_ref[:, i * gw : (i + 1) * gw]
    inner_ref[...] = gsum_ref[:, 0:hidden]
    outer_ref[...] = gsum_ref[:, hidden : 2 * hidden]
    mixer_ref[...] = gsum_ref[:, 2 * hidden :].T
    for r in range(ib_ref.shape[1] // 128):
        ib_ref[:, r * 128 : (r + 1) * 128] = small_ref[9 + r : 10 + r, :]
    for i, ref in enumerate(lines):
        ref[...] = small_ref[i : i + 1, 0:share]


def finish(dr1, fin, gsum, qgrad, ssum, count, hidden, hshare):
    share = qgrad.shape[0]
    gw = qgrad.shape[1] // 3
    S = jax.ShapeDtypeStruct
    vmem = pl.BlockSpec(memory_space=pltpu.VMEM)
    shapes = [(1, 1), dr1.shape] + [(share, gw)] * 3 + [(gw, share), (share, hidden), (share, hidden), (1, hshare)]
    shapes += [(1, share)] * 8
    return pl.pallas_call(
        finish_kernel,
        name="finish",
        out_shape=tuple(S(shape, F32) for shape in shapes),
        in_specs=[vmem] * 6,
        out_specs=(vmem,) * len(shapes),
        compiler_params=pltpu.CompilerParams(vmem_limit_bytes=VMEM_LIMIT),
    )(dr1, fin, gsum, qgrad, ssum, count)


def shards(
    tokens, teacher, lengths, loss_mask, loss_scale,
    query_weight, query_bias, key_weight, value_weight, value_bias, mixer_weight, mixer_bias,
    first_gain, first_shift, inner_weight, inner_bias, outer_weight, outer_bias, second_gain, second_shift,
):
    dp, tp = lax.axis_size("dp"), lax.axis_size("tensor")
    if dp != 8 or tp != 4:
        return plain_shards(
            tokens, teacher, lengths, loss_mask, loss_scale,
            query_weight, query_bias, key_weight, value_weight, value_bias, mixer_weight, mixer_bias,
            first_gain, first_shift, inner_weight, inner_bias, outer_weight, outer_bias, second_gain, second_shift,
        )
    width = tokens.shape[1]
    share, gw = query_weight.shape
    hidden = inner_weight.shape[1]
    hshare = inner_bias.shape[0]
    hrows = hshare // 128
    rows_of = [
        v.reshape(1, -1)
        for v in (query_bias, value_bias, mixer_bias, first_gain, first_shift, outer_bias, second_gain, second_shift)
    ]
    small, wq, wm, counted = pack_inputs(
        lengths, loss_mask, rows_of, inner_bias, query_weight, key_weight, value_weight, inner_weight, outer_weight.T, mixer_weight
    )
    oin, wall, smalls, count, xs, wqf, oT, lse, qT, kA, v = front(tokens, wq, wm, small, dp, tp)
    token_total = count[0, 0]
    wall = wall.reshape(tp, width, wm.shape[1])
    layer_output, dr1, do, grad, pack = mid(
        tokens, teacher, counted, loss_scale.reshape(1, 1), count, oin, wall, smalls, hidden
    )
    grad = grad.reshape(tp, dp // 2, 2, share, wm.shape[1])
    fin, gsum, qgrad, ssum = back(do, grad, xs, wqf, oT, lse, qT, kA, v, pack)
    loss, input_grad, query_grad, key_grad, value_grad, mixer_grad, inner_grad, outer_grad, ib, *lines = finish(
        dr1, fin, gsum, qgrad, ssum, count, hidden, hshare
    )
    line = lambda i: lines[i].reshape(-1)
    return (
        layer_output,
        loss.reshape(()),
        input_grad,
        query_grad,
        line(0),
        key_grad,
        value_grad,
        line(1),
        mixer_grad,
        line(2),
        line(3),
        line(4),
        inner_grad,
        ib.reshape(-1),
        outer_grad.T,
        line(5),
        line(6),
        line(7),
    )


def in_blocks(value, dim, size):
    before, after = (value.shape[:dim], value.shape[dim + 1 :])
    return jnp.moveaxis(value.reshape(*before, size, -1, *after), dim, 0)


def summed_on_arrival(value, axis, dim):
    size = lax.axis_size(axis)
    blocks = lax.all_to_all(in_blocks(value, dim, size), axis, 0, 0, tiled=True)
    return jnp.sum(blocks.astype(jnp.float32), axis=0)


def sent_together(arrays, axis, dim, along):
    both = jnp.concatenate(arrays, axis=along)
    out, at, gathered = (summed_on_arrival(both, axis, dim), 0, [])
    for a in arrays:
        gathered.append(lax.slice_in_dim(out, at, at + a.shape[along], axis=along))
        at += a.shape[along]
    return tuple(gathered)


def contract_last(left_rows, right_rows):
    return lax.dot_general(
        left_rows, right_rows, (((1,), (1,)), ((), ())), preferred_element_type=jnp.float32
    )


def contract_first(left_rows, right_rows):
    return lax.dot_general(
        left_rows, right_rows, (((0,), (0,)), ((), ())), preferred_element_type=jnp.float32
    )


def plain_dot(left_rows, right_rows):
    return jnp.dot(left_rows, right_rows, preferred_element_type=jnp.float32)


def gelu_exact(pre_values):
    return jax.nn.gelu(pre_values, approximate=False)


def plain_norm_forward(values_in, gain_vec, shift_vec):
    centred = values_in - jnp.mean(values_in, axis=1, keepdims=True)
    inv_std = lax.rsqrt(jnp.mean(centred * centred, axis=1, keepdims=True) + norm_eps)
    normed = centred * inv_std
    return (normed * gain_vec + shift_vec, normed, inv_std)


def plain_norm_backward(grad_out, normed, inv_std, gain_vec):
    grad_normed = grad_out * gain_vec
    mean_plain = jnp.mean(grad_normed, axis=1, keepdims=True)
    mean_mixed = jnp.mean(grad_normed * normed, axis=1, keepdims=True)
    grad_in = inv_std * (grad_normed - mean_plain - normed * mean_mixed)
    return (grad_in, jnp.sum(grad_out * normed, axis=0), jnp.sum(grad_out, axis=0))


def plain_shards(
    tokens,
    teacher,
    lengths,
    loss_mask,
    loss_scale,
    query_weight,
    query_bias,
    key_weight,
    value_weight,
    value_bias,
    mixer_weight,
    mixer_bias,
    first_gain,
    first_shift,
    inner_weight,
    inner_bias,
    outer_weight,
    outer_bias,
    second_gain,
    second_shift,
):
    tp_count = lax.axis_size("tensor")
    tp_index = lax.axis_index("tensor")
    dp_count = lax.axis_size("dp")
    dp_index = lax.axis_index("dp")
    local_rows = tokens.shape[0]
    seq_len = local_rows * tp_count
    model_width = tokens.shape[1]
    head_width = query_weight.shape[1]
    hidden_width = inner_weight.shape[1]
    head_count = head_width // HEAD_DIM
    block_count = seq_len // QBLOCK
    score_scale = HEAD_DIM ** (-0.5)
    length_here = lengths[0]
    local_pos = tp_index * local_rows + jnp.arange(local_rows)
    counted = jnp.logical_and(local_pos < length_here, loss_mask == 1).astype(jnp.float32)
    count_local = jnp.sum(counted)
    small_stack = jnp.stack(
        [
            query_bias,
            value_bias,
            mixer_bias,
            first_gain,
            first_shift,
            outer_bias,
            second_gain,
            second_shift,
        ]
    )

    def fetch_params():
        return (
            lax.all_gather(query_weight, "dp", axis=0, tiled=True),
            lax.all_gather(key_weight, "dp", axis=0, tiled=True),
            lax.all_gather(value_weight, "dp", axis=0, tiled=True),
            lax.all_gather(mixer_weight, "dp", axis=1, tiled=True),
            lax.all_gather(inner_weight, "dp", axis=0, tiled=True),
            lax.all_gather(outer_weight, "dp", axis=1, tiled=True),
            lax.all_gather(small_stack, "dp", axis=1, tiled=True),
            lax.all_gather(inner_bias, "dp", axis=0, tiled=True),
        )

    def attn_gather(values_in):
        return lax.all_gather(values_in, "tensor", axis=0, tiled=True)

    def ffn_gather(values_in):
        return lax.all_gather(values_in, "tensor", axis=0, tiled=True)

    (
        query_full,
        key_full,
        value_full,
        mixer_full,
        inner_full,
        outer_full,
        small_full,
        innerb_full,
    ) = fetch_params()
    small_wide = small_full.astype(jnp.float32)
    qbias_mine = lax.dynamic_slice_in_dim(small_wide[0], tp_index * head_width, head_width)
    vbias_mine = lax.dynamic_slice_in_dim(small_wide[1], tp_index * head_width, head_width)
    inner_mine = lax.dynamic_slice_in_dim(
        innerb_full.astype(jnp.float32), tp_index * hidden_width, hidden_width
    )
    seq_rows = attn_gather(tokens)
    queries = (plain_dot(seq_rows, query_full) + qbias_mine).astype(jnp.bfloat16)
    keys_all = plain_dot(seq_rows, key_full).astype(jnp.bfloat16)
    values_all = (plain_dot(seq_rows, value_full) + vbias_mine).astype(jnp.bfloat16)
    keys_three = keys_all.reshape(seq_len, head_count, HEAD_DIM)
    values_three = values_all.reshape(seq_len, head_count, HEAD_DIM)
    key_valid = jnp.arange(seq_len) < length_here

    def score_block(query_block):
        scores = (
            jnp.einsum("qhd,khd->hqk", query_block, keys_three, preferred_element_type=jnp.float32)
            * score_scale
        )
        return jnp.where(key_valid[None, None, :], scores, masked_score)

    def forward_block(query_block):
        scores = score_block(query_block)
        row_top = jnp.max(scores, axis=2, keepdims=True)
        exp_scores = jnp.exp(scores - row_top)
        row_total = jnp.sum(exp_scores, axis=2, keepdims=True)
        prob_low = (exp_scores / row_total).astype(jnp.bfloat16)
        mixed_rows = jnp.einsum(
            "hqk,khd->qhd", prob_low, values_three, preferred_element_type=jnp.float32
        )
        return (mixed_rows.astype(jnp.bfloat16), (row_top + jnp.log(row_total))[:, :, 0])

    query_blocks = queries.reshape(block_count, QBLOCK, head_count, HEAD_DIM)
    attended, log_sums = lax.map(forward_block, query_blocks)
    attended = attended.reshape(seq_len, head_width)
    attn_out = lax.psum_scatter(
        plain_dot(attended, mixer_full).astype(jnp.bfloat16),
        "tensor",
        scatter_dimension=0,
        tiled=True,
    ).astype(jnp.float32)
    first_sum = tokens.astype(jnp.float32) + attn_out + small_wide[2]
    hidden_one, normed_one, inv_one = plain_norm_forward(first_sum, small_wide[3], small_wide[4])
    hidden_low = hidden_one.astype(jnp.bfloat16)
    ffn_rows = ffn_gather(hidden_low)
    pre_act = plain_dot(ffn_rows, inner_full) + inner_mine
    act_full, gelu_pull = jax.vjp(gelu_exact, pre_act)
    activated = act_full.astype(jnp.bfloat16)
    ffn_out = lax.psum_scatter(
        plain_dot(activated, outer_full).astype(jnp.bfloat16),
        "tensor",
        scatter_dimension=0,
        tiled=True,
    ).astype(jnp.float32)
    second_sum = hidden_one + ffn_out + small_wide[5]
    final_rows, normed_two, inv_two = plain_norm_forward(second_sum, small_wide[6], small_wide[7])
    layer_output = final_rows.astype(jnp.bfloat16)
    diff_rows = final_rows - teacher.astype(jnp.float32)
    loss_local = jnp.sum(counted * jnp.sum(diff_rows * diff_rows, axis=1))
    loss_total, token_total = lax.psum((loss_local, count_local), ("dp", "tensor"))
    grad_scale = 2.0 * loss_scale / (token_total * model_width)
    grad_final = grad_scale * counted[:, None] * diff_rows
    (
        query_full,
        key_full,
        value_full,
        mixer_full,
        inner_full,
        outer_full,
        small_full,
        innerb_full,
    ) = fetch_params()
    ffn_rows = ffn_gather(hidden_low)
    grad_second, secondgain_part, secondshift_part = plain_norm_backward(
        grad_final, normed_two, inv_two, small_wide[6]
    )
    outerbias_part = jnp.sum(grad_second, axis=0)
    grad_ffn_rows = lax.all_gather(grad_second.astype(jnp.bfloat16), "tensor", axis=0, tiled=True)
    grad_act = contract_last(grad_ffn_rows, outer_full)
    outer_local = contract_first(activated, grad_ffn_rows)
    grad_pre = gelu_pull(grad_act)[0].astype(jnp.bfloat16)
    innerbias_part = jnp.sum(grad_pre, axis=0, dtype=jnp.float32)
    inner_local = contract_first(ffn_rows, grad_pre)
    grad_hidden = lax.psum_scatter(
        contract_last(grad_pre, inner_full).astype(jnp.bfloat16),
        "tensor",
        scatter_dimension=0,
        tiled=True,
    ).astype(jnp.float32)
    inner_grad, outer_grad = (
        lax.psum_scatter(inner_local, "dp", scatter_dimension=0, tiled=True),
        lax.psum_scatter(outer_local, "dp", scatter_dimension=1, tiled=True),
    )
    grad_first, firstgain_part, firstshift_part = plain_norm_backward(
        grad_second + grad_hidden, normed_one, inv_one, small_wide[3]
    )
    mixerbias_part = jnp.sum(grad_first, axis=0)
    grad_attn_rows = lax.all_gather(grad_first.astype(jnp.bfloat16), "tensor", axis=0, tiled=True)
    grad_attended = contract_last(grad_attn_rows, mixer_full).astype(jnp.bfloat16)
    mixer_local = contract_first(attended, grad_attn_rows)
    grad_blocks = grad_attended.reshape(block_count, QBLOCK, head_count, HEAD_DIM)

    def backward_block(carried, block_in):
        key_acc, value_acc = carried
        query_block, grad_block, lse_block = block_in
        scores = score_block(query_block)
        prob_full = jnp.exp(scores - lse_block[:, :, None])
        prob_low = prob_full.astype(jnp.bfloat16)
        grad_prob = jnp.einsum(
            "qhd,khd->hqk", grad_block, values_three, preferred_element_type=jnp.float32
        )
        row_dot = jnp.sum(prob_full * grad_prob, axis=2, keepdims=True)
        grad_scores = (prob_full * (grad_prob - row_dot)).astype(jnp.bfloat16)
        grad_query = (
            jnp.einsum("hqk,khd->qhd", grad_scores, keys_three, preferred_element_type=jnp.float32)
            * score_scale
        ).astype(jnp.bfloat16)
        key_acc = (
            key_acc
            + jnp.einsum(
                "hqk,qhd->khd", grad_scores, query_block, preferred_element_type=jnp.float32
            )
            * score_scale
        )
        value_acc = value_acc + jnp.einsum(
            "hqk,qhd->khd", prob_low, grad_block, preferred_element_type=jnp.float32
        )
        return ((key_acc, value_acc), grad_query)

    zero_acc = jnp.zeros((seq_len, head_count, HEAD_DIM), jnp.float32)
    (key_acc, value_acc), grad_queries = lax.scan(
        backward_block, (zero_acc, zero_acc), (query_blocks, grad_blocks, log_sums)
    )
    grad_queries = grad_queries.reshape(seq_len, head_width)
    grad_keys = key_acc.reshape(seq_len, head_width).astype(jnp.bfloat16)
    grad_values = value_acc.reshape(seq_len, head_width).astype(jnp.bfloat16)
    seq_rows = attn_gather(tokens)
    query_local = contract_first(seq_rows, grad_queries)
    key_local = contract_first(seq_rows, grad_keys)
    value_local = contract_first(seq_rows, grad_values)
    querybias_part = jnp.sum(grad_queries, axis=0, dtype=jnp.float32)
    valuebias_part = jnp.sum(grad_values, axis=0, dtype=jnp.float32)
    total_term = contract_last(grad_queries, query_full)
    total_term = total_term + contract_last(grad_keys, key_full)
    grad_tokens = lax.psum_scatter(
        (total_term + contract_last(grad_values, value_full)).astype(jnp.bfloat16),
        "tensor",
        scatter_dimension=0,
        tiled=True,
    ).astype(jnp.float32)
    input_grad = grad_first + grad_tokens
    query_grad, key_grad, value_grad, mixer_grad = (
        *sent_together(
            (
                query_local.astype(jnp.bfloat16),
                key_local.astype(jnp.bfloat16),
                value_local.astype(jnp.bfloat16),
            ),
            "dp",
            0,
            1,
        ),
        summed_on_arrival(mixer_local.astype(jnp.bfloat16), "dp", 1),
    )

    def spread_part(part_vec, full_width):
        return lax.dynamic_update_slice_in_dim(
            jnp.zeros((full_width,), jnp.float32), part_vec, tp_index * part_vec.shape[0], 0
        )

    small_terms = jnp.stack(
        [
            spread_part(querybias_part, model_width),
            spread_part(valuebias_part, model_width),
            mixerbias_part,
            firstgain_part,
            firstshift_part,
            outerbias_part,
            secondgain_part,
            secondshift_part,
        ]
    )
    inner_terms = spread_part(innerbias_part, hidden_width * tp_count)
    small_sum, inner_sum = lax.psum((small_terms, inner_terms), ("dp", "tensor"))
    loss_value = loss_total / (token_total * model_width)
    width_share = model_width // dp_count
    small_mine = lax.dynamic_slice_in_dim(small_sum, dp_index * width_share, width_share, 1)
    hidden_share = inner_sum.shape[0] // dp_count
    innerbias_grad = lax.dynamic_slice_in_dim(inner_sum, dp_index * hidden_share, hidden_share, 0)
    return (
        layer_output,
        loss_value,
        input_grad,
        query_grad,
        small_mine[0],
        key_grad,
        value_grad,
        small_mine[1],
        mixer_grad,
        small_mine[2],
        small_mine[3],
        small_mine[4],
        inner_grad,
        innerbias_grad,
        outer_grad,
        small_mine[5],
        small_mine[6],
        small_mine[7],
    )


def solution(mesh):
    return jax.shard_map(
        shards,
        mesh=mesh,
        in_specs=(
            P(("dp", "tensor"), None),
            P(("dp", "tensor"), None),
            P("dp"),
            P(("dp", "tensor")),
            P(),
            P("dp", "tensor"),
            P("dp"),
            P("dp", "tensor"),
            P("dp", "tensor"),
            P("dp"),
            P("tensor", "dp"),
            P("dp"),
            P("dp"),
            P("dp"),
            P("dp", "tensor"),
            P("dp"),
            P("tensor", "dp"),
            P("dp"),
            P("dp"),
            P("dp"),
        ),
        out_specs=(
            P(("dp", "tensor"), None),
            P(),
            P(("dp", "tensor"), None),
            P("dp", "tensor"),
            P("dp"),
            P("dp", "tensor"),
            P("dp", "tensor"),
            P("dp"),
            P("tensor", "dp"),
            P("dp"),
            P("dp"),
            P("dp"),
            P("dp", "tensor"),
            P("dp"),
            P("tensor", "dp"),
            P("dp"),
            P("dp"),
            P("dp"),
        ),
        check_vma=False,
    )
```
